32 devices in a mesh: head: 4 (over x, core), blk: 8 (over z, y).
Axes of the slice: x: 2, y: 2, z: 4, core: 2. Of those that a mesh axis runs over, the one named last changes fastest.
Arguments:
- inputs: bfloat16 [2, 2048, 768], P(None, ('blk', 'head')), may hold values from -6 to 6
- time_embed: float32 [2, 128], replicated, may hold values from -6 to 6
- segments: int32 [2, 2048], P(None, ('blk', 'head')), may hold values from 0 to 15, never falling along the last dimension, each value on 1 to 1280 neighbouring positions
- valid_mask: int32 [2, 2048], P(None, ('blk', 'head')), may hold values from 0 to 1
- teacher: bfloat16 [2, 2048, 768], P(None, ('blk', 'head')), may hold values from -6 to 6
- ada_weight: bfloat16 [128, 4608], P(None, ('head', 'blk')), may hold values from -0.25 to 0.25
- ada_bias: bfloat16 [4608], P(('head', 'blk')), may hold values from -3 to 3
- gain_attn: bfloat16 [768], P(('head', 'blk')), may hold values from 0.5 to 1.5
- qkv_weight: bfloat16 [768, 2304], P(('head', 'blk')), may hold values from -0.21875 to 0.21875
- out_weight: bfloat16 [768, 768], P(('head', 'blk')), may hold values from -3 to 3
- gain_mlp: bfloat16 [768], P(('head', 'blk')), may hold values from 0.5 to 1.5
- up_weight: bfloat16 [768, 3072], P(('head', 'blk')), may hold values from -0.21875 to 0.21875
- up_bias: bfloat16 [3072], P(('head', 'blk')), may hold values from -3 to 3
- down_weight: bfloat16 [3072, 768], P(('head', 'blk')), may hold values from -0.109375 to 0.109375
- down_bias: bfloat16 [768], P(('head', 'blk')), may hold values from -3 to 3
Outputs:
- output: bfloat16 [2, 2048, 768], P(None, ('blk', 'head'))
- loss_value: float32 [], replicated
- grad_input: float32 [2, 2048, 768], P(None, ('blk', 'head'))
- grad_ada_weight: float32 [128, 4608], P(None, ('head', 'blk'))
- grad_ada_bias: float32 [4608], P(('head', 'blk'))
- grad_gain_attn: float32 [768], P(('head', 'blk'))
- grad_qkv_weight: float32 [768, 2304], P(('head', 'blk'))
- grad_out_weight: float32 [768, 768], P(('head', 'blk'))
- grad_gain_mlp: float32 [768], P(('head', 'blk'))
- grad_up_weight: float32 [768, 3072], P(('head', 'blk'))
- grad_up_bias: float32 [3072], P(('head', 'blk'))
- grad_down_weight: float32 [3072, 768], P(('head', 'blk'))
- grad_down_bias: float32 [768], P(('head', 'blk'))
The draws below stay inside these ranges and needn't reach their ends.
Inputs may be any that keep to these rules, and one draw needn't show every extreme that they name: `segments`: documents are numbered from 0 along each sequence, never falling; a document has 1 to 1280 tokens, and one has exactly that many.
All inputs are finite; a program needn't handle non-finite values.
Results may differ from the reference program's by a relative error of at most 0.019.
Values may be sent and summed in bfloat16 or wider, within the bound.
No kernel may reach another device: no remote copies, remote signals or barrier semaphores. Data moves between devices by JAX's collectives and lax.ppermute only.
A program may use at most 576 MiB of HBM per device.

```python
import math
import jax
import jax.numpy as jnp
import numpy as np
from jax import lax

D = 768
HEADS = 12
HEAD_DIM = 64
FF = 3072
COND = 128
SEQS = 2
TOK = 64
ROWS = 256
LEN = 2048
N_HEAD = 4


def draw_valid_mask(key, part):
    position = jnp.arange(LEN, dtype=jnp.int32)
    group_index = position // TOK % N_HEAD
    threshold = 150 + 600 * group_index // max(N_HEAD - 1, 1) + 100 * position // LEN
    sampled = jax.random.randint(key, (SEQS, LEN), 0, 1000, dtype=jnp.int32)
    return (sampled < threshold[None, :]).astype(jnp.int32)


def steps_of(key, extent, cuts, least, top_value):
    def one(dim, shards_of):
        heights = jax.random.uniform(jax.random.fold_in(jax.random.fold_in(key, 6), dim), (shards_of,), jnp.float32, least / len(cuts), top_value / len(cuts))
        return jnp.repeat(jnp.exp(heights), extent[dim] // shards_of).reshape((-1,) + (1,) * (len(extent) - dim - 1))

    factor_of = one(*cuts[0])
    for cut in cuts[1:]:
        factor_of = factor_of * one(*cut)
    return factor_of


def length_profile(count, total, reach, slope):
    portions = [(1 << 20) // math.isqrt(grade ** slope) + 1 for grade in range(2, count + 1)]
    surplus, given = total - reach - (count - 1), [1] * (count - 1)
    while surplus > 0:
        free = [i for i in range(count - 1) if given[i] < reach]
        whole, remaining = sum([portions[i] for i in free]), surplus
        for i in free:
            more = min(reach - given[i], max(1, remaining * portions[i] // whole), surplus)
            given[i] = given[i] + more
            surplus = surplus - more
    return np.array([reach] + given)


def uneven_parts(own_key, count, total, limit, slope):
    if count == 2:
        one = jax.random.randint(own_key, (), max(1, total - limit), min(limit, total - 1) + 1)
        return jnp.stack([one, total - one])
    sizes = jnp.asarray(length_profile(count, total, limit, slope), jnp.int32)
    pairs = (count - 1) // 2
    giver, sink = sizes[1:1 + 2 * pairs:2], sizes[2:2 + 2 * pairs:2]
    margin = jnp.minimum(giver - 1, limit - sink)
    moved = jax.random.randint(jax.random.fold_in(own_key, 1), (pairs,), 0, 1 << 20) % (margin + 1)
    sizes = sizes.at[1:1 + 2 * pairs:2].set(giver - moved).at[2:2 + 2 * pairs:2].set(sink + moved)
    return sizes[jax.random.permutation(jax.random.fold_in(own_key, 2), count)]


def normal_values(rng, extent, spread, reach, cuts=(), kind=jnp.bfloat16):
    array = jax.random.normal(rng, extent, jnp.float32) * spread
    if len(cuts) > 0:
        array = steps_of(rng, extent, cuts, -0.22, 0.18) * array
    return jnp.clip(array, min=-reach, max=reach).astype(kind)


def setup_inputs(seed: int = 0) -> dict:
    key_of = jax.random.split(jax.random.key(seed), 16)
    return {
        "inputs": normal_values(key_of[0], (SEQS, LEN, D), 1.0, 6.0, ((1, 32),)),
        "time_embed": normal_values(key_of[1], (SEQS, COND), 1.0, 6.0, (), jnp.float32),
        "segments": jax.vmap(lambda own: jnp.searchsorted(jnp.cumsum(uneven_parts(own, max(16, LEN // 256), LEN, LEN // 2 + ROWS, 2)), jnp.arange(LEN), side="right"))(jax.random.split(key_of[2], SEQS)).reshape((SEQS, LEN)).astype(jnp.int32),
        "valid_mask": draw_valid_mask(jax.random.fold_in(key_of[15], 71), 0),
        "teacher": normal_values(key_of[4], (SEQS, LEN, D), 1.0, 6.0, ((1, 32),)),
        "ada_weight": normal_values(key_of[5], (COND, 6 * D), (4 * COND) ** -0.5, 0.25, ((1, 32),)),
        "ada_bias": normal_values(key_of[6], (6 * D,), 0.5, 3.0, ((0, 32),)),
        "gain_attn": jnp.clip(1.0 + 0.1 * jax.random.normal(key_of[7], (D,), jnp.float32), 0.5, 1.5).astype(jnp.bfloat16),
        "qkv_weight": normal_values(key_of[8], (D, 3 * D), D ** -0.5, 0.21875, ((0, 32),)),
        "out_weight": normal_values(key_of[9], (D, D), (max(1, D // 192)) ** -0.5, 3.0, ((0, 32),)),
        "gain_mlp": jnp.clip(1.0 + 0.1 * jax.random.normal(key_of[10], (D,), jnp.float32), 0.5, 1.5).astype(jnp.bfloat16),
        "up_weight": normal_values(key_of[11], (D, FF), D ** -0.5, 0.21875, ((0, 32),)),
        "up_bias": normal_values(key_of[12], (FF,), 0.5, 3.0, ((0, 32),)),
        "down_weight": normal_values(key_of[13], (FF, D), FF ** -0.5, 0.109375, ((0, 32),)),
        "down_bias": normal_values(key_of[14], (D,), 0.5, 3.0, ((0, 32),)),
    }


precise = lax.Precision.HIGHEST

@jax.custom_vjp
def low(v):
    return lax.optimization_barrier(v.astype(jnp.bfloat16)).astype(jnp.float32)

@jax.custom_vjp
def low_back(v):
    return v

def low_keep(v):
    return (low(v), None)

def low_pass(kept, grad):
    return (grad,)

def back_keep(v):
    return (v, None)

def back_low(kept, grad):
    return (low(grad),)
low.defvjp(low_keep, low_pass)
low_back.defvjp(back_keep, back_low)

def matmul(left, right):
    return jnp.matmul(left, right, precision=precise)

def normalize(hidden):
    average = lax.optimization_barrier(jnp.mean(hidden, axis=-1, keepdims=True))
    centred = hidden - average
    variance = lax.optimization_barrier(jnp.mean(centred * centred, axis=-1, keepdims=True))
    return centred * lax.rsqrt(variance + 1e-05)

def attend(queries, key_rows, value_rows, doc_ids):
    total_rows = queries.shape[0]
    block_rows = 512 if total_rows % 512 == 0 else total_rows
    query_blocks = queries.reshape(total_rows // block_rows, block_rows, HEADS, HEAD_DIM)
    doc_blocks = doc_ids.reshape(total_rows // block_rows, block_rows)
    scale_factor = HEAD_DIM ** (-0.5)

    def one_block(blocks_in):
        query_part, doc_part = blocks_in
        scores = jnp.einsum('qhe,khe->hqk', query_part, key_rows, precision=precise) * scale_factor
        scores = low_back(scores)
        allowed = (doc_part[:, None] == doc_ids[None, :])[None]
        scores = jnp.where(allowed, scores, -1e+30)
        row_max = lax.optimization_barrier(jnp.max(scores, axis=-1, keepdims=True))
        exponent = jnp.exp(scores - row_max)
        probabilities = low(exponent / lax.optimization_barrier(jnp.sum(exponent, axis=-1, keepdims=True)))
        return jnp.einsum('hqk,khe->qhe', probabilities, value_rows, precision=precise)
    result = lax.map(jax.checkpoint(one_block), (query_blocks, doc_blocks))
    return result.reshape(total_rows, HEADS * HEAD_DIM)

def layer(inputs, ada_weight, ada_bias, gain_attn, qkv_weight, out_weight, gain_mlp, up_weight, up_bias, down_weight, down_bias, time_embed, segments, mask_float, teacher, valid_total):
    modulation = matmul(time_embed, ada_weight) + ada_bias
    pieces = modulation.reshape(SEQS, 6, 1, D)
    shift_attn = pieces[:, 0]
    scale_attn = pieces[:, 1]
    gate_attn = pieces[:, 2]
    shift_mlp = pieces[:, 3]
    scale_mlp = pieces[:, 4]
    gate_mlp = pieces[:, 5]
    entered = low(normalize(inputs) * gain_attn * (1.0 + scale_attn) + shift_attn)
    triple = low_back(low(matmul(entered, qkv_weight))).reshape(SEQS, LEN, 3, HEADS, HEAD_DIM)
    attended = jnp.stack([attend(triple[sequence, :, 0], triple[sequence, :, 1], triple[sequence, :, 2], segments[sequence]) for sequence in range(SEQS)])
    attended = low_back(low(attended))
    branch = low_back(matmul(attended, out_weight))
    hidden = inputs + gate_attn * branch
    moved = low(normalize(hidden) * gain_mlp * (1.0 + scale_mlp) + shift_mlp)
    upper_in = low_back(matmul(moved, up_weight) + up_bias)
    active = low(jax.nn.gelu(upper_in, approximate=True))
    lower_out = low_back(matmul(active, down_weight) + down_bias)
    final_state = hidden + gate_mlp * lower_out
    mismatch = final_state - teacher
    error_total = jnp.sum(mask_float[:, :, None] * mismatch * mismatch)
    objective = error_total * (SEQS * LEN / (2.0 * valid_total))
    return ((final_state, objective), error_total)

def reference(inputs, time_embed, segments, valid_mask, teacher, ada_weight, ada_bias, gain_attn, qkv_weight, out_weight, gain_mlp, up_weight, up_bias, down_weight, down_bias):
    mask_float = valid_mask.astype(jnp.float32)
    valid_total = jnp.sum(mask_float)
    teacher_float = teacher.astype(jnp.float32)
    params = (inputs.astype(jnp.float32), ada_weight.astype(jnp.float32), ada_bias.astype(jnp.float32), gain_attn.astype(jnp.float32), qkv_weight.astype(jnp.float32), out_weight.astype(jnp.float32), gain_mlp.astype(jnp.float32), up_weight.astype(jnp.float32), up_bias.astype(jnp.float32), down_weight.astype(jnp.float32), down_bias.astype(jnp.float32))

    def wrapped(*params_in):
        return layer(*params_in, time_embed, segments, mask_float, teacher_float, valid_total)
    outcome, pullback, error_total = jax.vjp(wrapped, *params, has_aux=True)
    final_state, objective = outcome
    gradients = pullback((jnp.zeros_like(final_state), jnp.ones_like(objective)))
    loss_value = error_total / (valid_total * D)
    return (final_state.astype(jnp.bfloat16), loss_value, gradients[0], gradients[1], gradients[2], gradients[3], gradients[4], gradients[5], gradients[6], gradients[7], gradients[8], gradients[9], gradients[10])
```

```python
from functools import partial

import jax
import jax.numpy as jnp
from jax import lax
from jax.experimental import pallas as pl
from jax.experimental.pallas import tpu as pltpu
from jax.sharding import Mesh, PartitionSpec as P

HEADS = 12
HEAD_DIM = 64
GROUPS = 4
WIDTH = HEADS // GROUPS * HEAD_DIM
EVERY = ("hx", "hc", "rb", "sz", "sy")
SPOT = ("sz", "sy")
bf16 = jnp.bfloat16
f32 = jnp.float32
precise = lax.Precision.HIGHEST


def normalize(hidden):
    average = jnp.mean(hidden, axis=-1, keepdims=True)
    centred = hidden - average
    variance = jnp.mean(centred * centred, axis=-1, keepdims=True)
    inverse = lax.rsqrt(variance + 1e-05)
    return (centred * inverse, inverse)


def norm_back(upstream, normed, inverse):
    first_mean = jnp.mean(upstream, axis=-1, keepdims=True)
    second_mean = jnp.mean(upstream * normed, axis=-1, keepdims=True)
    return inverse * (upstream - first_mean - normed * second_mean)


def swap(value, axis):
    return lax.ppermute(value, axis, [(0, 1), (1, 0)])


def turn(value, axis, step):
    size = lax.axis_size(axis)
    return lax.ppermute(value, axis, [(i, (i - step) % size) for i in range(size)])


def place():
    return jnp.stack([lax.axis_index(name) for name in ("hx", "hc", "sz", "sy")]).astype(jnp.int32)


def piece_copies(place_ref, halves, whole, sems, inward):
    hx, hc, sz, sy = (place_ref[i] for i in range(4))
    rows, half = halves[0].shape[-2:]
    copies = []
    for side in range(2):
        for core in range(2):
            for second in range(2):
                for first in range(2):
                    for deep in range(4):
                        across, down = (first, second) if side == 0 else (second, first)
                        spot = (((hx ^ across) * 2 + (hc ^ core)) * 4 + lax.rem(sz + deep, 4)) * 2 + (sy ^ down)
                        near = halves[side].at[core, second, first, deep]
                        far = whole.at[spot, :, pl.ds(side * half, half)]
                        source, target = (near, far) if inward else (far, near)
                        copies.append(pltpu.make_async_copy(source, target, sems.at[len(copies)]))
    for copy in copies:
        copy.start()
    for copy in copies:
        copy.wait()


def join_kernel(place_ref, left, right, whole, sems):
    piece_copies(place_ref, (left, right), whole, sems, True)


def part_kernel(place_ref, whole, left, right, sems):
    piece_copies(place_ref, (left, right), whole, sems, False)


ANY = pl.BlockSpec(memory_space=pl.ANY)
SMEM = pl.BlockSpec(memory_space=pltpu.SMEM)


def join(here, left, right):
    rows, half = left.shape[-2:]
    return pl.pallas_call(
        join_kernel,
        out_shape=jax.ShapeDtypeStruct((32, rows, half * 2), left.dtype),
        in_specs=[SMEM, ANY, ANY],
        out_specs=ANY,
        scratch_shapes=[pltpu.SemaphoreType.DMA((64,))],
    )(here, left, right).reshape(rows * 32, half * 2)


def part(here, whole):
    rows, half = whole.shape[0] // 32, whole.shape[1] // 2
    side = jax.ShapeDtypeStruct((2, 2, 2, 4, rows, half), whole.dtype)
    return pl.pallas_call(
        part_kernel,
        out_shape=(side, side),
        in_specs=[SMEM, ANY],
        out_specs=(ANY, ANY),
        scratch_shapes=[pltpu.SemaphoreType.DMA((64,))],
    )(here, whole.reshape(32, rows, half * 2))


def gather_rows(here, shard):
    if lax.axis_size("rb") > 1:
        return lax.all_gather(shard, EVERY, axis=0, tiled=True)
    half = shard.shape[1] // 2
    sides = []
    for side, order in ((0, ("hx", "sy")), (1, ("sy", "hx"))):
        mine = shard[:, side * half : (side + 1) * half]
        level = jnp.stack([mine] + [turn(mine, "sz", k) for k in (1, 2, 3)])
        for axis in order + ("hc",):
            level = jnp.stack([level, swap(level, axis)])
        sides.append(level)
    return join(here, *sides)


def scatter_rows(here, whole):
    if lax.axis_size("rb") > 1:
        return lax.psum_scatter(whole, EVERY, scatter_dimension=0, tiled=True)
    sides = part(here, whole.astype(bf16))
    out = []
    for side, order in ((0, ("hx", "sy")), (1, ("sy", "hx"))):
        level = sides[side]
        for axis in ("hc",) + order[::-1]:
            total = level[0].astype(f32) + swap(level[1].astype(bf16), axis).astype(f32)
            level = total
        total = level[0]
        for k in (1, 2, 3):
            total = total + turn(level[k].astype(bf16), "sz", -k).astype(f32)
        out.append(total)
    return jnp.concatenate(out, axis=1)


def on_device(
    inputs,
    time_embed,
    segments,
    valid_mask,
    teacher,
    ada_weight,
    ada_bias,
    gain_attn,
    qkv_weight,
    out_weight,
    gain_mlp,
    up_weight,
    up_bias,
    down_weight,
    down_bias,
):
    seqs, tokens, width = inputs.shape
    hidden_units = up_weight.shape[1]
    parts = lax.axis_size("rb")
    devices = 32 * parts
    length = tokens * devices
    queries = 8 * tokens
    heads_here = HEADS // GROUPS
    scale_factor = HEAD_DIM ** (-0.5)
    here = place()
    hx, hc, rb = lax.axis_index("hx"), lax.axis_index("hc"), lax.axis_index("rb")
    spot = lax.axis_index("sz") * 2 + lax.axis_index("sy")
    own_seq = spot // GROUPS

    own_modulation = jnp.dot(
        time_embed, ada_weight.astype(f32), precision=precise
    ) + ada_bias.astype(f32)
    mask_float = valid_mask.astype(f32)
    fields = [
        own_modulation.reshape(-1),
        gain_attn.astype(f32),
        gain_mlp.astype(f32),
        up_bias.astype(f32),
        down_bias.astype(f32),
        segments.astype(f32).reshape(-1),
        jnp.sum(mask_float).reshape(1),
    ]
    sizes = [field.shape[0] for field in fields]
    packed = jnp.concatenate(fields)
    everyone = lax.all_to_all(
        jnp.broadcast_to(packed, (devices, packed.shape[0])), EVERY, 0, 0, tiled=True
    )
    columns = []
    begin = 0
    for size in sizes:
        columns.append(everyone[:, begin : begin + size])
        begin += size
    modulation = columns[0].reshape(devices, seqs, -1).transpose(1, 0, 2).reshape(seqs, -1)
    gain_one, gain_two, full_up_bias, full_down_bias = (c.reshape(-1) for c in columns[1:5])
    docs = columns[5].reshape(2, 2, parts, 8, seqs, tokens)
    count_all = jnp.sum(columns[6])
    pieces = modulation.reshape(seqs, 6, 1, width)
    shift_attn, scale_attn, gate_attn, shift_mlp, scale_mlp, gate_mlp = (
        pieces[:, i] for i in range(6)
    )

    full_qkv = gather_rows(here, qkv_weight)
    full_out = gather_rows(here, out_weight)
    full_up = gather_rows(here, up_weight)
    full_down = gather_rows(here, down_weight)

    residual = inputs.astype(f32)
    normed_one, inverse_one = normalize(residual)
    scaled_one = normed_one * gain_one
    entered = (scaled_one * (1.0 + scale_attn) + shift_attn).astype(bf16)
    triple = jnp.einsum("std,df->stf", entered, full_qkv, preferred_element_type=f32).astype(bf16)
    leave = (
        triple.reshape(seqs, tokens, 3, GROUPS, WIDTH)
        .transpose(0, 3, 2, 1, 4)
        .reshape(8, 3, tokens, WIDTH)
    )
    came = lax.all_to_all(leave, SPOT, 0, 0, tiled=True)
    came = came.transpose(1, 0, 2, 3).reshape(3, queries, WIDTH)
    query_rows = came[0]
    pair = came[1:]
    if parts > 1:
        pair = lax.all_gather(pair, "rb", axis=1, tiled=True)
    for axis in ("hx", "hc"):
        pair = jnp.stack([pair, swap(pair, axis)], axis=1)

    def heads_first(value):
        return value.reshape(-1, heads_here, HEAD_DIM).transpose(1, 0, 2)

    query_three = heads_first(query_rows)
    key_three = heads_first(pair[0])
    value_three = heads_first(pair[1])
    docs_here = lax.dynamic_index_in_dim(docs, own_seq, 4, keepdims=False)
    docs_here = jnp.where(hx == 1, docs_here[::-1], docs_here)
    docs_here = jnp.where(hc == 1, docs_here[:, ::-1], docs_here)
    key_docs = docs_here.transpose(1, 0, 2, 3, 4).reshape(-1)
    query_docs = lax.dynamic_index_in_dim(docs_here[0, 0], rb, 0, keepdims=False).reshape(-1)
    allowed = (query_docs[:, None] == key_docs[None, :])[None]
    scores = (
        jnp.einsum("hqe,hke->hqk", query_three, key_three, preferred_element_type=f32)
        * scale_factor
    )
    masked = jnp.where(allowed, scores, -1e30)
    row_max = jnp.max(masked, axis=-1)
    exponent = jnp.where(allowed, jnp.exp(scores - row_max[..., None]), 0.0)
    denominator = jnp.sum(exponent, axis=-1)
    numerator = jnp.einsum(
        "hqk,hke->hqe", exponent.astype(bf16), value_three, preferred_element_type=f32
    )
    attention = numerator / denominator[..., None]
    log_total = row_max + jnp.log(denominator)

    def rows_first(value):
        return value.astype(bf16).transpose(1, 0, 2).reshape(-1, WIDTH)

    def to_owner(rows):
        back = lax.all_to_all(rows.reshape(8, tokens, WIDTH), SPOT, 0, 0, tiled=True)
        return (
            back.reshape(seqs, GROUPS, tokens, WIDTH)
            .transpose(0, 2, 1, 3)
            .reshape(seqs, tokens, width)
        )

    mixed = to_owner(rows_first(attention))
    branch = jnp.einsum("std,de->ste", mixed, full_out, preferred_element_type=f32)
    hidden = residual + gate_attn * branch
    normed_two, inverse_two = normalize(hidden)
    scaled_two = normed_two * gain_two
    moved = (scaled_two * (1.0 + scale_mlp) + shift_mlp).astype(bf16)
    upper_in = jnp.einsum("std,df->stf", moved, full_up, preferred_element_type=f32) + full_up_bias
    active = jax.nn.gelu(upper_in, approximate=True).astype(bf16)
    lower_out = (
        jnp.einsum("stf,fd->std", active, full_down, preferred_element_type=f32) + full_down_bias
    )
    final_state = hidden + gate_mlp * lower_out
    mismatch = final_state - teacher.astype(f32)
    error_here = jnp.sum(mask_float[:, :, None] * mismatch * mismatch)
    grad_final = seqs * length / count_all * mask_float[:, :, None] * mismatch
    grad_lower = (gate_mlp * grad_final).astype(bf16)
    grad_gate_mlp = jnp.sum(grad_final * lower_out, axis=1)
    grad_down_weight = jnp.einsum("stf,std->fd", active, grad_lower, preferred_element_type=f32)
    grad_down_bias = jnp.sum(grad_lower.astype(f32), axis=(0, 1))
    grad_active = jnp.einsum("std,fd->stf", grad_lower, full_down, preferred_element_type=f32)
    unused_value, gelu_back = jax.vjp(partial(jax.nn.gelu, approximate=True), upper_in)
    grad_upper = gelu_back(grad_active)[0].astype(bf16)
    grad_up_weight = jnp.einsum("std,stf->df", moved, grad_upper, preferred_element_type=f32)
    grad_up_bias = jnp.sum(grad_upper.astype(f32), axis=(0, 1))
    grad_moved = jnp.einsum("stf,df->std", grad_upper, full_up, preferred_element_type=f32)
    grad_shift_mlp = jnp.sum(grad_moved, axis=1)
    grad_scale_mlp = jnp.sum(grad_moved * scaled_two, axis=1)
    grad_scaled_two = grad_moved * (1.0 + scale_mlp)
    grad_gain_mlp = jnp.sum(grad_scaled_two * normed_two, axis=(0, 1))
    grad_hidden = grad_final + norm_back(grad_scaled_two * gain_two, normed_two, inverse_two)
    grad_branch = (gate_attn * grad_hidden).astype(bf16)
    grad_gate_attn = jnp.sum(grad_hidden * branch, axis=1)
    grad_out_weight = jnp.einsum("ste,std->ed", mixed, grad_branch, preferred_element_type=f32)
    grad_mixed = jnp.einsum(
        "std,ed->ste", grad_branch, full_out, preferred_element_type=f32
    ).astype(bf16)
    grad_leave = (
        grad_mixed.reshape(seqs, tokens, GROUPS, WIDTH)
        .transpose(0, 2, 1, 3)
        .reshape(8, tokens, WIDTH)
    )
    grad_rows = lax.all_to_all(grad_leave, SPOT, 0, 0, tiled=True).reshape(queries, WIDTH)
    grad_three = heads_first(grad_rows)
    row_delta = jnp.sum(grad_three.astype(f32) * attention, axis=-1)

    shard_out = scatter_rows(here, grad_out_weight)
    shard_up = scatter_rows(here, grad_up_weight)
    shard_down = scatter_rows(here, grad_down_weight)

    probabilities = jnp.where(allowed, jnp.exp(scores - log_total[..., None]), 0.0)
    grad_probs = jnp.einsum("hqe,hke->hqk", grad_three, value_three, preferred_element_type=f32)
    grad_scores = (probabilities * (grad_probs - row_delta[..., None])).astype(bf16)
    grad_query = (
        jnp.einsum("hqk,hke->hqe", grad_scores, key_three, preferred_element_type=f32)
        * scale_factor
    )
    grad_value = jnp.einsum(
        "hqk,hqe->hke", probabilities.astype(bf16), grad_three, preferred_element_type=f32
    )
    grad_key = (
        jnp.einsum("hqk,hqe->hke", grad_scores, query_three, preferred_element_type=f32)
        * scale_factor
    )
    grad_pair = jnp.stack([rows_first(grad_key), rows_first(grad_value)]).reshape(
        2, 2, 2, parts * queries, WIDTH
    )
    for axis in ("hc", "hx"):
        grad_pair = (
            grad_pair[:, 0].astype(f32) + swap(grad_pair[:, 1].astype(bf16), axis).astype(f32)
        )
    if parts > 1:
        grad_pair = lax.psum_scatter(grad_pair, "rb", scatter_dimension=1, tiled=True)
    home = jnp.concatenate([rows_first(grad_query)[None], grad_pair.astype(bf16)])
    home = home.reshape(3, 8, tokens, WIDTH).transpose(1, 0, 2, 3)
    home = lax.all_to_all(home, SPOT, 0, 0, tiled=True)
    grad_flat = (
        home.reshape(seqs, GROUPS, 3, tokens, WIDTH)
        .transpose(0, 3, 2, 1, 4)
        .reshape(seqs, tokens, 3 * width)
    )
    grad_qkv_weight = jnp.einsum("std,stf->df", entered, grad_flat, preferred_element_type=f32)
    shard_qkv = scatter_rows(here, grad_qkv_weight)
    grad_entered = jnp.einsum("stf,df->std", grad_flat, full_qkv, preferred_element_type=f32)
    grad_shift_attn = jnp.sum(grad_entered, axis=1)
    grad_scale_attn = jnp.sum(grad_entered * scaled_one, axis=1)
    grad_scaled_one = grad_entered * (1.0 + scale_attn)
    grad_gain_attn = jnp.sum(grad_scaled_one * normed_one, axis=(0, 1))
    grad_input = grad_hidden + norm_back(grad_scaled_one * gain_one, normed_one, inverse_one)
    grad_modulation = jnp.stack(
        [
            grad_shift_attn,
            grad_scale_attn,
            grad_gate_attn,
            grad_shift_mlp,
            grad_scale_mlp,
            grad_gate_mlp,
        ],
        axis=1,
    ).reshape(seqs, devices, -1)
    sums = [
        grad_modulation.transpose(1, 0, 2).reshape(devices, -1),
        grad_gain_attn.reshape(devices, -1),
        grad_gain_mlp.reshape(devices, -1),
        grad_up_bias.reshape(devices, -1),
        grad_down_bias.reshape(devices, -1),
        jnp.broadcast_to(error_here, (devices, 1)),
    ]
    sizes = [value.shape[1] for value in sums]
    added = jnp.sum(
        lax.all_to_all(jnp.concatenate(sums, axis=1), EVERY, 0, 0, tiled=True), axis=0
    )
    owned = []
    begin = 0
    for size in sizes:
        owned.append(added[begin : begin + size])
        begin += size
    own_grad = owned[0].reshape(seqs, -1)
    grad_ada_weight = jnp.sum(time_embed[:, :, None] * own_grad[:, None, :], axis=0)
    loss_value = owned[5][0] / (count_all * width)
    return (
        final_state.astype(bf16),
        loss_value,
        grad_input,
        grad_ada_weight,
        jnp.sum(own_grad, axis=0),
        owned[1],
        shard_qkv,
        shard_out,
        owned[2],
        shard_up,
        owned[3],
        shard_down,
        owned[4],
    )


def solution(mesh):
    blocks = mesh.shape["blk"]
    fine = Mesh(mesh.devices.reshape(2, 2, blocks // 8, 4, 2), EVERY)
    tokens = ("rb", "sz", "sy", "hx", "hc")
    return jax.shard_map(
        on_device,
        mesh=fine,
        in_specs=(
            P(None, tokens, None),
            P(),
            P(None, tokens),
            P(None, tokens),
            P(None, tokens, None),
            P(None, EVERY),
            P(EVERY),
            P(EVERY),
            P(EVERY, None),
            P(EVERY, None),
            P(EVERY),
            P(EVERY, None),
            P(EVERY),
            P(EVERY, None),
            P(EVERY),
        ),
        out_specs=(
            P(None, tokens, None),
            P(),
            P(None, tokens, None),
            P(None, EVERY),
            P(EVERY),
            P(EVERY),
            P(EVERY, None),
            P(EVERY, None),
            P(EVERY),
            P(EVERY, None),
            P(EVERY),
            P(EVERY, None),
            P(EVERY),
        ),
        check_vma=False,
    )
```

```python
from functools import partial

import jax
import jax.numpy as jnp
from jax import lax
from jax.experimental import pallas as pl
from jax.experimental.pallas import tpu as pltpu
from jax.sharding import Mesh, PartitionSpec as P

HEADS = 12
HEAD_DIM = 64
GROUPS = 4
WIDTH = HEADS // GROUPS * HEAD_DIM
EVERY = ("hx", "hc", "rb", "sz", "sy")
SPOT = ("sz", "sy")
bf16 = jnp.bfloat16
f32 = jnp.float32
precise = lax.Precision.HIGHEST


def normalize(hidden):
    average = jnp.mean(hidden, axis=-1, keepdims=True)
    centred = hidden - average
    variance = jnp.mean(centred * centred, axis=-1, keepdims=True)
    inverse = lax.rsqrt(variance + 1e-05)
    return (centred * inverse, inverse)


def norm_back(upstream, normed, inverse):
    first_mean = jnp.mean(upstream, axis=-1, keepdims=True)
    second_mean = jnp.mean(upstream * normed, axis=-1, keepdims=True)
    return inverse * (upstream - first_mean - normed * second_mean)


def swap(value, axis):
    return lax.ppermute(value, axis, [(0, 1), (1, 0)])


def turn(value, axis, step):
    size = lax.axis_size(axis)
    return lax.ppermute(value, axis, [(i, (i - step) % size) for i in range(size)])


def place():
    return jnp.stack([lax.axis_index(name) for name in ("hx", "hc", "sz", "sy")]).astype(jnp.int32)


def piece_copies(place_ref, halves, whole, sems, inward):
    hx, hc, sz, sy = (place_ref[i] for i in range(4))
    rows, half = halves[0].shape[-2:]
    copies = []
    for side in range(2):
        for core in range(2):
            for second in range(2):
                for first in range(2):
                    for deep in range(4):
                        across, down = (first, second) if side == 0 else (second, first)
                        spot = (((hx ^ across) * 2 + (hc ^ core)) * 4 + lax.rem(sz + deep, 4)) * 2 + (sy ^ down)
                        near = halves[side].at[core, second, first, deep]
                        far = whole.at[spot, :, pl.ds(side * half, half)]
                        source, target = (near, far) if inward else (far, near)
                        copies.append(pltpu.make_async_copy(source, target, sems.at[len(copies)]))
    for copy in copies:
        copy.start()
    for copy in copies:
        copy.wait()


def join_kernel(place_ref, left, right, whole, sems):
    piece_copies(place_ref, (left, right), whole, sems, True)


def part_kernel(place_ref, whole, left, right, sems):
    piece_copies(place_ref, (left, right), whole, sems, False)


ANY = pl.BlockSpec(memory_space=pl.ANY)
SMEM = pl.BlockSpec(memory_space=pltpu.SMEM)
VMEM = pl.BlockSpec(memory_space=pltpu.VMEM)


def join(here, left, right):
    rows, half = left.shape[-2:]
    return pl.pallas_call(
        join_kernel,
        out_shape=jax.ShapeDtypeStruct((32, rows, half * 2), left.dtype),
        in_specs=[SMEM, ANY, ANY],
        out_specs=VMEM,
        scratch_shapes=[pltpu.SemaphoreType.DMA((64,))],
        compiler_params=pltpu.CompilerParams(vmem_limit_bytes=40 << 20),
    )(here, left, right).reshape(rows * 32, half * 2)


def part(here, whole):
    rows, half = whole.shape[0] // 32, whole.shape[1] // 2
    side = jax.ShapeDtypeStruct((2, 2, 2, 4, rows, half), whole.dtype)
    return pl.pallas_call(
        part_kernel,
        out_shape=(side, side),
        in_specs=[SMEM, VMEM],
        out_specs=(ANY, ANY),
        scratch_shapes=[pltpu.SemaphoreType.DMA((64,))],
        compiler_params=pltpu.CompilerParams(vmem_limit_bytes=40 << 20),
    )(here, whole.reshape(32, rows, half * 2))


def gather_rows(here, shard):
    if lax.axis_size("rb") > 1:
        return lax.all_gather(shard, EVERY, axis=0, tiled=True)
    half = shard.shape[1] // 2
    sides = []
    for side, order in ((0, ("hx", "sy")), (1, ("sy", "hx"))):
        mine = shard[:, side * half : (side + 1) * half]
        level = jnp.stack([mine] + [turn(mine, "sz", k) for k in (1, 2, 3)])
        for axis in order + ("hc",):
            level = jnp.stack([level, swap(level, axis)])
        sides.append(level)
    return join(here, *sides)


def scatter_rows(here, whole):
    if lax.axis_size("rb") > 1:
        return lax.psum_scatter(whole, EVERY, scatter_dimension=0, tiled=True)
    sides = part(here, whole.astype(bf16))
    out = []
    for side, order in ((0, ("hx", "sy")), (1, ("sy", "hx"))):
        level = sides[side]
        for axis in ("hc",) + order[::-1]:
            total = level[0].astype(f32) + swap(level[1].astype(bf16), axis).astype(f32)
            level = total
        total = level[0]
        for k in (1, 2, 3):
            total = total + turn(level[k].astype(bf16), "sz", -k).astype(f32)
        out.append(total)
    return jnp.concatenate(out, axis=1)


def on_device(
    inputs,
    time_embed,
    segments,
    valid_mask,
    teacher,
    ada_weight,
    ada_bias,
    gain_attn,
    qkv_weight,
    out_weight,
    gain_mlp,
    up_weight,
    up_bias,
    down_weight,
    down_bias,
):
    seqs, tokens, width = inputs.shape
    hidden_units = up_weight.shape[1]
    parts = lax.axis_size("rb")
    devices = 32 * parts
    length = tokens * devices
    queries = 8 * tokens
    heads_here = HEADS // GROUPS
    scale_factor = HEAD_DIM ** (-0.5)
    here = place()
    hx, hc, rb = lax.axis_index("hx"), lax.axis_index("hc"), lax.axis_index("rb")
    spot = lax.axis_index("sz") * 2 + lax.axis_index("sy")
    own_seq = spot // GROUPS

    own_modulation = jnp.dot(
        time_embed, ada_weight.astype(f32), precision=precise
    ) + ada_bias.astype(f32)
    mask_float = valid_mask.astype(f32)
    fields = [
        own_modulation.reshape(-1),
        gain_attn.astype(f32),
        gain_mlp.astype(f32),
        up_bias.astype(f32),
        down_bias.astype(f32),
        segments.astype(f32).reshape(-1),
        jnp.sum(mask_float).reshape(1),
    ]
    sizes = [field.shape[0] for field in fields]
    packed = jnp.concatenate(fields)
    everyone = lax.all_to_all(
        jnp.broadcast_to(packed, (devices, packed.shape[0])), EVERY, 0, 0, tiled=True
    )
    columns = []
    begin = 0
    for size in sizes:
        columns.append(everyone[:, begin : begin + size])
        begin += size
    modulation = columns[0].reshape(devices, seqs, -1).transpose(1, 0, 2).reshape(seqs, -1)
    gain_one, gain_two, full_up_bias, full_down_bias = (c.reshape(-1) for c in columns[1:5])
    docs = columns[5].reshape(2, 2, parts, 8, seqs, tokens)
    count_all = jnp.sum(columns[6])
    pieces = modulation.reshape(seqs, 6, 1, width)
    shift_attn, scale_attn, gate_attn, shift_mlp, scale_mlp, gate_mlp = (
        pieces[:, i] for i in range(6)
    )

    full_qkv = gather_rows(here, qkv_weight)
    full_out = gather_rows(here, out_weight)
    full_up = gather_rows(here, up_weight)
    full_down = gather_rows(here, down_weight)

    residual = inputs.astype(f32)
    normed_one, inverse_one = normalize(residual)
    scaled_one = normed_one * gain_one
    entered = (scaled_one * (1.0 + scale_attn) + shift_attn).astype(bf16)
    triple = jnp.einsum("std,df->stf", entered, full_qkv, preferred_element_type=f32).astype(bf16)
    leave = (
        triple.reshape(seqs, tokens, 3, GROUPS, WIDTH)
        .transpose(0, 3, 2, 1, 4)
        .reshape(8, 3, tokens, WIDTH)
    )
    came = lax.all_to_all(leave, SPOT, 0, 0, tiled=True)
    came = came.transpose(1, 0, 2, 3).reshape(3, queries, WIDTH)
    query_rows = came[0]
    pair = came[1:]
    if parts > 1:
        pair = lax.all_gather(pair, "rb", axis=1, tiled=True)
    for axis in ("hx", "hc"):
        pair = jnp.stack([pair, swap(pair, axis)], axis=1)

    def heads_first(value):
        return value.reshape(-1, heads_here, HEAD_DIM).transpose(1, 0, 2)

    query_three = heads_first(query_rows)
    key_three = heads_first(pair[0])
    value_three = heads_first(pair[1])
    docs_here = lax.dynamic_index_in_dim(docs, own_seq, 4, keepdims=False)
    docs_here = jnp.where(hx == 1, docs_here[::-1], docs_here)
    docs_here = jnp.where(hc == 1, docs_here[:, ::-1], docs_here)
    key_docs = docs_here.transpose(1, 0, 2, 3, 4).reshape(-1)
    query_docs = lax.dynamic_index_in_dim(docs_here[0, 0], rb, 0, keepdims=False).reshape(-1)
    allowed = (query_docs[:, None] == key_docs[None, :])[None]
    scores = (
        jnp.einsum("hqe,hke->hqk", query_three, key_three, preferred_element_type=f32)
        * scale_factor
    )
    masked = jnp.where(allowed, scores, -1e30)
    row_max = jnp.max(masked, axis=-1)
    exponent = jnp.where(allowed, jnp.exp(scores - row_max[..., None]), 0.0)
    denominator = jnp.sum(exponent, axis=-1)
    numerator = jnp.einsum(
        "hqk,hke->hqe", exponent.astype(bf16), value_three, preferred_element_type=f32
    )
    attention = numerator / denominator[..., None]
    log_total = row_max + jnp.log(denominator)

    def rows_first(value):
        return value.astype(bf16).transpose(1, 0, 2).reshape(-1, WIDTH)

    def to_owner(rows):
        back = lax.all_to_all(rows.reshape(8, tokens, WIDTH), SPOT, 0, 0, tiled=True)
        return (
            back.reshape(seqs, GROUPS, tokens, WIDTH)
            .transpose(0, 2, 1, 3)
            .reshape(seqs, tokens, width)
        )

    mixed = to_owner(rows_first(attention))
    branch = jnp.einsum("std,de->ste", mixed, full_out, preferred_element_type=f32)
    hidden = residual + gate_attn * branch
    normed_two, inverse_two = normalize(hidden)
    scaled_two = normed_two * gain_two
    moved = (scaled_two * (1.0 + scale_mlp) + shift_mlp).astype(bf16)
    upper_in = jnp.einsum("std,df->stf", moved, full_up, preferred_element_type=f32) + full_up_bias
    active = jax.nn.gelu(upper_in, approximate=True).astype(bf16)
    lower_out = (
        jnp.einsum("stf,fd->std", active, full_down, preferred_element_type=f32) + full_down_bias
    )
    final_state = hidden + gate_mlp * lower_out
    mismatch = final_state - teacher.astype(f32)
    error_here = jnp.sum(mask_float[:, :, None] * mismatch * mismatch)
    grad_final = seqs * length / count_all * mask_float[:, :, None] * mismatch
    grad_lower = (gate_mlp * grad_final).astype(bf16)
    grad_gate_mlp = jnp.sum(grad_final * lower_out, axis=1)
    grad_down_weight = jnp.einsum("stf,std->fd", active, grad_lower, preferred_element_type=f32)
    grad_down_bias = jnp.sum(grad_lower.astype(f32), axis=(0, 1))
    grad_active = jnp.einsum("std,fd->stf", grad_lower, full_down, preferred_element_type=f32)
    unused_value, gelu_back = jax.vjp(partial(jax.nn.gelu, approximate=True), upper_in)
    grad_upper = gelu_back(grad_active)[0].astype(bf16)
    grad_up_weight = jnp.einsum("std,stf->df", moved, grad_upper, preferred_element_type=f32)
    grad_up_bias = jnp.sum(grad_upper.astype(f32), axis=(0, 1))
    grad_moved = jnp.einsum("stf,df->std", grad_upper, full_up, preferred_element_type=f32)
    grad_shift_mlp = jnp.sum(grad_moved, axis=1)
    grad_scale_mlp = jnp.sum(grad_moved * scaled_two, axis=1)
    grad_scaled_two = grad_moved * (1.0 + scale_mlp)
    grad_gain_mlp = jnp.sum(grad_scaled_two * normed_two, axis=(0, 1))
    grad_hidden = grad_final + norm_back(grad_scaled_two * gain_two, normed_two, inverse_two)
    grad_branch = (gate_attn * grad_hidden).astype(bf16)
    grad_gate_attn = jnp.sum(grad_hidden * branch, axis=1)
    grad_out_weight = jnp.einsum("ste,std->ed", mixed, grad_branch, preferred_element_type=f32)
    grad_mixed = jnp.einsum(
        "std,ed->ste", grad_branch, full_out, preferred_element_type=f32
    ).astype(bf16)
    grad_leave = (
        grad_mixed.reshape(seqs, tokens, GROUPS, WIDTH)
        .transpose(0, 2, 1, 3)
        .reshape(8, tokens, WIDTH)
    )
    grad_rows = lax.all_to_all(grad_leave, SPOT, 0, 0, tiled=True).reshape(queries, WIDTH)
    grad_three = heads_first(grad_rows)
    row_delta = jnp.sum(grad_three.astype(f32) * attention, axis=-1)

    shard_out = scatter_rows(here, grad_out_weight)
    shard_up = scatter_rows(here, grad_up_weight)
    shard_down = scatter_rows(here, grad_down_weight)

    probabilities = jnp.where(allowed, jnp.exp(scores - log_total[..., None]), 0.0)
    grad_probs = jnp.einsum("hqe,hke->hqk", grad_three, value_three, preferred_element_type=f32)
    grad_scores = (probabilities * (grad_probs - row_delta[..., None])).astype(bf16)
    grad_query = (
        jnp.einsum("hqk,hke->hqe", grad_scores, key_three, preferred_element_type=f32)
        * scale_factor
    )
    grad_value = jnp.einsum(
        "hqk,hqe->hke", probabilities.astype(bf16), grad_three, preferred_element_type=f32
    )
    grad_key = (
        jnp.einsum("hqk,hqe->hke", grad_scores, query_three, preferred_element_type=f32)
        * scale_factor
    )
    grad_pair = jnp.stack([rows_first(grad_key), rows_first(grad_value)]).reshape(
        2, 2, 2, parts * queries, WIDTH
    )
    for axis in ("hc", "hx"):
        grad_pair = (
            grad_pair[:, 0].astype(f32) + swap(grad_pair[:, 1].astype(bf16), axis).astype(f32)
        )
    if parts > 1:
        grad_pair = lax.psum_scatter(grad_pair, "rb", scatter_dimension=1, tiled=True)
    home = jnp.concatenate([rows_first(grad_query)[None], grad_pair.astype(bf16)])
    home = home.reshape(3, 8, tokens, WIDTH).transpose(1, 0, 2, 3)
    home = lax.all_to_all(home, SPOT, 0, 0, tiled=True)
    grad_flat = (
        home.reshape(seqs, GROUPS, 3, tokens, WIDTH)
        .transpose(0, 3, 2, 1, 4)
        .reshape(seqs, tokens, 3 * width)
    )
    grad_qkv_weight = jnp.einsum("std,stf->df", entered, grad_flat, preferred_element_type=f32)
    shard_qkv = scatter_rows(here, grad_qkv_weight)
    grad_entered = jnp.einsum("stf,df->std", grad_flat, full_qkv, preferred_element_type=f32)
    grad_shift_attn = jnp.sum(grad_entered, axis=1)
    grad_scale_attn = jnp.sum(grad_entered * scaled_one, axis=1)
    grad_scaled_one = grad_entered * (1.0 + scale_attn)
    grad_gain_attn = jnp.sum(grad_scaled_one * normed_one, axis=(0, 1))
    grad_input = grad_hidden + norm_back(grad_scaled_one * gain_one, normed_one, inverse_one)
    grad_modulation = jnp.stack(
        [
            grad_shift_attn,
            grad_scale_attn,
            grad_gate_attn,
            grad_shift_mlp,
            grad_scale_mlp,
            grad_gate_mlp,
        ],
        axis=1,
    ).reshape(seqs, devices, -1)
    sums = [
        grad_modulation.transpose(1, 0, 2).reshape(devices, -1),
        grad_gain_attn.reshape(devices, -1),
        grad_gain_mlp.reshape(devices, -1),
        grad_up_bias.reshape(devices, -1),
        grad_down_bias.reshape(devices, -1),
        jnp.broadcast_to(error_here, (devices, 1)),
    ]
    sizes = [value.shape[1] for value in sums]
    added = jnp.sum(
        lax.all_to_all(jnp.concatenate(sums, axis=1), EVERY, 0, 0, tiled=True), axis=0
    )
    owned = []
    begin = 0
    for size in sizes:
        owned.append(added[begin : begin + size])
        begin += size
    own_grad = owned[0].reshape(seqs, -1)
    grad_ada_weight = jnp.sum(time_embed[:, :, None] * own_grad[:, None, :], axis=0)
    loss_value = owned[5][0] / (count_all * width)
    return (
        final_state.astype(bf16),
        loss_value,
        grad_input,
        grad_ada_weight,
        jnp.sum(own_grad, axis=0),
        owned[1],
        shard_qkv,
        shard_out,
        owned[2],
        shard_up,
        owned[3],
        shard_down,
        owned[4],
    )


def solution(mesh):
    blocks = mesh.shape["blk"]
    fine = Mesh(mesh.devices.reshape(2, 2, blocks // 8, 4, 2), EVERY)
    tokens = ("rb", "sz", "sy", "hx", "hc")
    return jax.shard_map(
        on_device,
        mesh=fine,
        in_specs=(
            P(None, tokens, None),
            P(),
            P(None, tokens),
            P(None, tokens),
            P(None, tokens, None),
            P(None, EVERY),
            P(EVERY),
            P(EVERY),
            P(EVERY, None),
            P(EVERY, None),
            P(EVERY),
            P(EVERY, None),
            P(EVERY),
            P(EVERY, None),
            P(EVERY),
        ),
        out_specs=(
            P(None, tokens, None),
            P(),
            P(None, tokens, None),
            P(None, EVERY),
            P(EVERY),
            P(EVERY),
            P(EVERY, None),
            P(EVERY, None),
            P(EVERY),
            P(EVERY, None),
            P(EVERY),
            P(EVERY, None),
            P(EVERY),
        ),
        check_vma=False,
    )
```

```python
from functools import partial

import jax
import jax.numpy as jnp
from jax import lax
from jax.experimental import pallas as pl
from jax.experimental.pallas import tpu as pltpu
from jax.sharding import Mesh, PartitionSpec as P

HEADS = 12
HEAD_DIM = 64
GROUPS = 4
WIDTH = HEADS // GROUPS * HEAD_DIM
EVERY = ("hx", "hc", "rb", "sz", "sy")
SPOT = ("sz", "sy")
bf16 = jnp.bfloat16
f32 = jnp.float32
precise = lax.Precision.HIGHEST


def normalize(hidden):
    average = jnp.mean(hidden, axis=-1, keepdims=True)
    centred = hidden - average
    variance = jnp.mean(centred * centred, axis=-1, keepdims=True)
    inverse = lax.rsqrt(variance + 1e-05)
    return (centred * inverse, inverse)


def dot(left, right):
    return jnp.dot(left, right, preferred_element_type=f32)


def dot_nt(left, right):
    return lax.dot_general(left, right, (((1,), (1,)), ((), ())), preferred_element_type=f32)


def norm_back(upstream, normed, inverse):
    first_mean = jnp.mean(upstream, axis=-1, keepdims=True)
    second_mean = jnp.mean(upstream * normed, axis=-1, keepdims=True)
    return inverse * (upstream - first_mean - normed * second_mean)


def swap(value, axis):
    return lax.ppermute(value, axis, [(0, 1), (1, 0)])


def turn(value, axis, step):
    size = lax.axis_size(axis)
    return lax.ppermute(value, axis, [(i, (i - step) % size) for i in range(size)])


def place():
    return jnp.stack([lax.axis_index(name) for name in ("hx", "hc", "sz", "sy")]).astype(jnp.int32)


ANY = pl.BlockSpec(memory_space=pl.ANY)
SMEM = pl.BlockSpec(memory_space=pltpu.SMEM)
VMEM = pl.BlockSpec(memory_space=pltpu.VMEM)


def run_all(copies):
    for copy in copies:
        copy.start()
    for copy in copies:
        copy.wait()


def join_kernel(place_ref, left, right, whole, sems):
    hx, hc, sz, sy = (place_ref[i] for i in range(4))
    half = left.shape[-1]
    copies = []
    for side, pieces in enumerate((left, right)):
        for core in range(2):
            for second in range(2):
                for first in range(2):
                    for deep in range(4):
                        across, down = (first, second) if side == 0 else (second, first)
                        block = (hx ^ across) * 2 + (hc ^ core)
                        spot = (block * 4 + lax.rem(sz + deep, 4)) * 2 + (sy ^ down)
                        copies.append(
                            pltpu.make_async_copy(
                                pieces.at[core, second, first, deep],
                                whole.at[spot, :, pl.ds(side * half, half)],
                                sems.at[len(copies)],
                            )
                        )
    run_all(copies)


def join(here, left, right):
    rows, half = left.shape[-2:]
    return pl.pallas_call(
        join_kernel,
        out_shape=jax.ShapeDtypeStruct((32, rows, half * 2), left.dtype),
        in_specs=[SMEM, ANY, ANY],
        out_specs=VMEM,
        scratch_shapes=[pltpu.SemaphoreType.DMA((64,))],
        compiler_params=pltpu.CompilerParams(vmem_limit_bytes=40 << 20),
    )(here, left, right).reshape(rows * 32, half * 2)


def gather_rows(here, shard):
    if lax.axis_size("rb") > 1:
        return lax.all_gather(shard, EVERY, axis=0, tiled=True)
    half = shard.shape[1] // 2
    sides = []
    deep = jnp.stack([shard] + [turn(shard, "sz", k) for k in (1, 2, 3)])
    for side, order in ((0, ("hx", "sy")), (1, ("sy", "hx"))):
        level = deep[:, :, side * half : (side + 1) * half]
        for axis in order + ("hc",):
            level = jnp.stack([level, swap(level, axis)])
        sides.append(level)
    return join(here, *sides)


def piece_copies(place_ref, blocks, keep, send, sems, side, columns=None):
    hx, sz, sy = place_ref[0], place_ref[2], place_ref[3]
    copies = []
    for second in range(2):
        for first in range(2):
            for deep in range(4):
                across, down = (first, second) if side == 0 else (second, first)
                spot = ((hx ^ across) * 4 + lax.rem(sz + deep, 4)) * 2 + (sy ^ down)
                source = blocks.at[spot] if columns is None else blocks.at[spot, :, columns]
                target = (keep, send)[second].at[first, deep]
                copies.append(pltpu.make_async_copy(source, target, sems.at[side, len(copies)]))
    for copy in copies:
        copy.start()
    return copies


ORDERS = (("sy", "hx"), ("hx", "sy"))


def collect(keep, send, order):
    total = keep.astype(f32) + swap(send, order[0]).astype(f32)
    total = total[0] + swap(total[1].astype(bf16), order[1]).astype(f32)
    result = total[0]
    for k in (1, 2, 3):
        result = result + turn(total[k].astype(bf16), "sz", -k).astype(f32)
    return result


def put_rows(leave_ref, slot, which, rows):
    tokens = rows.shape[0]
    if which == 0:
        leave_ref[slot, pl.ds(tokens, tokens // 2), pl.ds(0, WIDTH)] = rows[: tokens // 2]
        leave_ref[slot, pl.ds(tokens, tokens // 2), pl.ds(WIDTH, WIDTH)] = rows[tokens // 2 :]
    else:
        leave_ref[slot, pl.ds(0, tokens), pl.ds((which - 1) * WIDTH, WIDTH)] = rows


def enter_kernel(x_ref, mod_ref, gain_ref, weight_ref, entered_ref, leave_ref):
    seqs, tokens, width = x_ref.shape
    for s in range(seqs):
        normed = normalize(x_ref[s].astype(f32))[0]
        value = normed * gain_ref[...] * (1.0 + mod_ref[s, 1:2]) + mod_ref[s, 0:1]
        entered_ref[pl.ds(s * tokens, tokens), :] = value.astype(bf16)
    entered = entered_ref[...]
    for which in range(3):
        triple = dot(entered, weight_ref[:, pl.ds(which * width, width)]).astype(bf16)
        for s in range(seqs):
            for g in range(GROUPS):
                rows = triple[s * tokens : (s + 1) * tokens, g * WIDTH : (g + 1) * WIDTH]
                put_rows(leave_ref, s * GROUPS + g, which, rows)


def enter(inputs, pieces, gain, weight):
    seqs, tokens, width = inputs.shape
    return pl.pallas_call(
        enter_kernel,
        out_shape=(
            jax.ShapeDtypeStruct((seqs * tokens, width), bf16),
            jax.ShapeDtypeStruct((8, tokens + tokens // 2, 2 * WIDTH), bf16),
        ),
        in_specs=[VMEM] * 4,
        out_specs=(VMEM, VMEM),
        compiler_params=pltpu.CompilerParams(vmem_limit_bytes=40 << 20),
    )(inputs, pieces, gain, weight)


def head_lanes(rows, head):
    lane = lax.broadcasted_iota(jnp.int32, (rows, WIDTH), 1)
    return (lane >= head * HEAD_DIM) & (lane < (head + 1) * HEAD_DIM)


def load_pairs(pair_ref, slot, first_row, half):
    value = pair_ref[slot, pl.ds(first_row, half), :]
    return value[:, :WIDTH], value[:, WIDTH:]


def spread_heads(pair_ref, first_row, half, target, factor):
    heads = target.shape[0]
    zero = jnp.zeros((half, WIDTH), bf16)
    for slot in range(8):
        for part, rows in enumerate(load_pairs(pair_ref, slot, first_row, half)):
            rows = (rows.astype(f32) * factor).astype(bf16)
            for h in range(heads):
                target[h, pl.ds((slot * 2 + part) * half, half), :] = jnp.where(
                    head_lanes(half, h), rows, zero
                )


def fetch(step, pair_refs, starts, pair_sc):
    for ref, (begin, end) in zip(pair_refs, starts):
        @pl.when((step >= begin) & (step < end))
        def take(ref=ref):
            pair_sc[...] = ref[...]


def forward_kernel(
    starts, came_ref, first_ref, second_ref, third_ref, key_docs_ref, query_docs_ref,
    out_ref, turned_ref, total_ref, query_sc, pair_sc, top_sc, sum_sc, acc_sc,
):
    step = pl.program_id(0)
    heads, queries = query_sc.shape[:2]
    half = out_ref.shape[1]

    @pl.when(step == 0)
    def start():
        spread_heads(came_ref, 2 * half, half, query_sc, HEAD_DIM ** (-0.5))
        top_sc[...] = jnp.full(top_sc.shape, -1e30, f32)
        sum_sc[...] = jnp.zeros(sum_sc.shape, f32)
        acc_sc[...] = jnp.zeros(acc_sc.shape, f32)

    fetch(step, (first_ref, second_ref, third_ref), starts, pair_sc)
    key_part = pair_sc[:, :WIDTH]
    value_turned = pair_sc[:, WIDTH:].T
    allowed = key_docs_ref[...] == query_docs_ref[...]
    for h in range(heads):
        rows = pl.ds(h * HEAD_DIM, HEAD_DIM)
        scores = jnp.where(allowed, dot_nt(key_part, query_sc[h]), -1e30)
        old = top_sc[h : h + 1]
        new = jnp.maximum(old, jnp.max(scores, axis=0, keepdims=True))
        exponent = jnp.exp(scores - new)
        fade = jnp.exp(old - new)
        top_sc[h : h + 1] = new
        sum_sc[h : h + 1] = sum_sc[h : h + 1] * fade + jnp.sum(exponent, axis=0, keepdims=True)
        acc_sc[rows] = acc_sc[rows] * fade + dot(
            value_turned[h * HEAD_DIM : (h + 1) * HEAD_DIM], exponent.astype(bf16)
        )

    @pl.when(step == pl.num_programs(0) - 1)
    def finish():
        total_ref[...] = jnp.zeros(total_ref.shape, f32)
        for h in range(heads):
            rows = pl.ds(h * HEAD_DIM, HEAD_DIM)
            turned_ref[rows] = acc_sc[rows] / sum_sc[h : h + 1]
            total_ref[h : h + 1] = top_sc[h : h + 1] + jnp.log(sum_sc[h : h + 1])
        whole = turned_ref[...].T.astype(bf16)
        for slot in range(8):
            for part in range(2):
                begin = (slot * 2 + part) * half
                out_ref[slot, :, pl.ds(part * WIDTH, WIDTH)] = whole[begin : begin + half]


def pair_specs(pairs, chunk):
    specs, starts, begin = [], [], 0
    for pair in pairs:
        count = pair.shape[0] // chunk
        specs.append(
            pl.BlockSpec(
                (chunk, 2 * WIDTH),
                lambda i, begin=begin, count=count: (jnp.clip(i - begin, 0, count - 1), 0),
            )
        )
        starts.append((begin, begin + count))
        begin += count
    return specs, starts, begin


def whole_spec(shape):
    return pl.BlockSpec(shape, lambda i: (0,) * len(shape))


def attend(came, pairs, key_docs, query_docs):
    slots, rows, columns = came.shape
    half = rows // 3
    queries = slots * 2 * half
    heads = WIDTH // HEAD_DIM
    chunk = 512
    specs, starts, steps = pair_specs(pairs, chunk)
    outs = (
        jax.ShapeDtypeStruct((slots, half, columns), bf16),
        jax.ShapeDtypeStruct((WIDTH, queries), f32),
        jax.ShapeDtypeStruct((8, queries), f32),
    )
    return pl.pallas_call(
        partial(forward_kernel, starts),
        grid=(steps,),
        out_shape=outs,
        in_specs=[
            whole_spec(came.shape),
            *specs,
            pl.BlockSpec((chunk, 1), lambda i: (i, 0)),
            whole_spec(query_docs.shape),
        ],
        out_specs=tuple(whole_spec(o.shape) for o in outs),
        scratch_shapes=[
            pltpu.VMEM((heads, queries, WIDTH), bf16),
            pltpu.VMEM((chunk, 2 * WIDTH), bf16),
            pltpu.VMEM((8, queries), f32),
            pltpu.VMEM((8, queries), f32),
            pltpu.VMEM((WIDTH, queries), f32),
        ],
        compiler_params=pltpu.CompilerParams(vmem_limit_bytes=48 << 20),
    )(came, *pairs, key_docs, query_docs)


def backward_kernel(
    starts, came_ref, grad_ref, first_ref, second_ref, third_ref, key_docs_ref, query_docs_ref,
    turned_ref, total_ref, query_out, keep_ref, send_ref,
    query_sc, grad_sc, pair_sc, delta_sc, acc_sc,
):
    step = pl.program_id(0)
    heads, queries = query_sc.shape[:2]
    half = query_out.shape[1]

    @pl.when(step == 0)
    def start():
        spread_heads(came_ref, 2 * half, half, query_sc, HEAD_DIM ** (-0.5))
        spread_heads(grad_ref, 0, half, grad_sc, 1.0)
        acc_sc[...] = jnp.zeros(acc_sc.shape, f32)
        for h in range(heads):
            rows = slice(h * HEAD_DIM, (h + 1) * HEAD_DIM)
            turned = grad_sc[h].astype(f32).T
            delta_sc[h : h + 1] = jnp.sum(turned[rows] * turned_ref[rows], axis=0, keepdims=True)

    fetch(step, (first_ref, second_ref, third_ref), starts, pair_sc)
    key_part = pair_sc[:, :WIDTH]
    value_part = pair_sc[:, WIDTH:]
    key_turned = key_part.T
    allowed = key_docs_ref[...] == query_docs_ref[...]
    grad_key = grad_value = None
    for h in range(heads):
        rows = pl.ds(h * HEAD_DIM, HEAD_DIM)
        query, grad = query_sc[h], grad_sc[h]
        scores = jnp.where(allowed, dot_nt(key_part, query), -1e30)
        probabilities = jnp.exp(scores - total_ref[h : h + 1])
        slope = dot_nt(value_part, grad) - delta_sc[h : h + 1]
        grad_scores = (probabilities * slope).astype(bf16)
        value_term = dot(probabilities.astype(bf16), grad)
        key_term = dot(grad_scores, query)
        grad_value = value_term if grad_value is None else grad_value + value_term
        grad_key = key_term if grad_key is None else grad_key + key_term
        acc_sc[rows] = acc_sc[rows] + dot(
            key_turned[h * HEAD_DIM : (h + 1) * HEAD_DIM], grad_scores
        )
    middle = pl.num_programs(0) // 2

    @pl.when(step < middle)
    def mine():
        keep_ref[:, pl.ds(0, WIDTH)] = grad_key
        keep_ref[:, pl.ds(WIDTH, WIDTH)] = grad_value

    @pl.when(step >= middle)
    def theirs():
        send_ref[:, pl.ds(0, WIDTH)] = grad_key.astype(bf16)
        send_ref[:, pl.ds(WIDTH, WIDTH)] = grad_value.astype(bf16)

    @pl.when(step == pl.num_programs(0) - 1)
    def finish():
        whole = (acc_sc[...] * HEAD_DIM ** (-0.5)).T.astype(bf16)
        for slot in range(8):
            for part in range(2):
                begin = (slot * 2 + part) * half
                query_out[slot, :, pl.ds(part * WIDTH, WIDTH)] = whole[begin : begin + half]


def attend_back(came, grad, pairs, key_docs, query_docs, turned, total):
    slots, rows, columns = came.shape
    half = rows // 3
    queries = slots * 2 * half
    heads = WIDTH // HEAD_DIM
    chunk = 512
    specs, starts, steps = pair_specs(pairs, chunk)
    middle = steps // 2
    return pl.pallas_call(
        partial(backward_kernel, starts),
        grid=(steps,),
        out_shape=(
            jax.ShapeDtypeStruct((slots, half, columns), bf16),
            jax.ShapeDtypeStruct((middle * chunk, columns), f32),
            jax.ShapeDtypeStruct((middle * chunk, columns), bf16),
        ),
        in_specs=[
            whole_spec(came.shape),
            whole_spec(grad.shape),
            *specs,
            pl.BlockSpec((chunk, 1), lambda i: (i, 0)),
            whole_spec(query_docs.shape),
            whole_spec(turned.shape),
            whole_spec(total.shape),
        ],
        out_specs=(
            whole_spec((slots, half, columns)),
            pl.BlockSpec((chunk, columns), lambda i: (jnp.minimum(i, middle - 1), 0)),
            pl.BlockSpec((chunk, columns), lambda i: (jnp.maximum(i - middle, 0), 0)),
        ),
        scratch_shapes=[
            pltpu.VMEM((heads, queries, WIDTH), bf16),
            pltpu.VMEM((heads, queries, WIDTH), bf16),
            pltpu.VMEM((chunk, 2 * WIDTH), bf16),
            pltpu.VMEM((8, queries), f32),
            pltpu.VMEM((WIDTH, queries), f32),
        ],
        compiler_params=pltpu.CompilerParams(vmem_limit_bytes=48 << 20),
    )(came, grad, *pairs, key_docs, query_docs, turned, total)


def middle_kernel(
    came_ref, x_ref, teacher_ref, mask_ref, weight_ref, mod_ref, gain_ref, up_bias_ref,
    down_bias_ref, out_ref, up_hbm, down_hbm,
    final_ref, hidden_ref, leave_ref, pack_ref, sums_ref, up_sc, down_sc, slope_sc, sems,
):
    seqs, tokens, width = x_ref.shape
    units = up_sc.shape[1]
    rows = seqs * tokens
    half = tokens // 2
    up_copy = pltpu.make_async_copy(up_hbm, up_sc, sems.at[0])
    down_copy = pltpu.make_async_copy(down_hbm, down_sc, sems.at[1])
    up_copy.start()
    down_copy.start()

    def wide(index):
        return jnp.concatenate(
            [jnp.broadcast_to(mod_ref[s, index : index + 1], (tokens, width)) for s in range(seqs)]
        )

    def add_rows(first, value):
        for s in range(seqs):
            sums_ref[first + s : first + s + 1] = jnp.sum(
                value[s * tokens : (s + 1) * tokens], axis=0, keepdims=True
            )

    for s in range(seqs):
        for g in range(GROUPS):
            left, right = load_pairs(came_ref, s * GROUPS + g, 0, half)
            columns = pl.ds(g * WIDTH, WIDTH)
            pack_ref[pl.ds(s * tokens, half), columns] = left
            pack_ref[pl.ds(s * tokens + half, half), columns] = right
    mixed = pack_ref[:, pl.ds(0, width)]
    residual = jnp.concatenate([x_ref[s].astype(f32) for s in range(seqs)])
    branch = dot(mixed, out_ref[...])
    hidden = residual + wide(2) * branch
    normed, inverse = normalize(hidden)
    scaled = normed * gain_ref[...]
    moved = (scaled * (1.0 + wide(4)) + wide(3)).astype(bf16)
    pack_ref[:, pl.ds(width, width)] = moved
    up_copy.wait()
    lower = None
    for f in range(units // width):
        columns = pl.ds(f * width, width)
        u = dot(moved, up_sc[:, columns]) + up_bias_ref[:, columns]
        square = u * u
        t = jnp.tanh(0.7978845608028654 * (u + 0.044715 * u * square))
        active = (0.5 * u * (1.0 + t)).astype(bf16)
        slope_sc[:, columns] = 0.5 * (1.0 + t) + 0.5 * u * (1.0 - t * t) * 0.7978845608028654 * (
            1.0 + 0.134145 * square
        )
        pack_ref[:, pl.ds(2 * width + f * width, width)] = active
        if f == 0:
            down_copy.wait()
        term = dot(active, down_sc[columns, :])
        lower = term if lower is None else lower + term
    lower = lower + down_bias_ref[...]
    gate = wide(5)
    final = hidden + gate * lower
    for s in range(seqs):
        final_ref[s] = final[s * tokens : (s + 1) * tokens].astype(bf16)
    teacher = jnp.concatenate([teacher_ref[s].astype(f32) for s in range(seqs)])
    mismatch = final - teacher
    sums_ref[14:15] = jnp.sum(mask_ref[...] * mismatch * mismatch, axis=0, keepdims=True)
    sums_ref[15:16] = jnp.zeros((1, width), f32)
    grad_final = weight_ref[...] * mismatch
    add_rows(6, grad_final * lower)
    grad_lower = (gate * grad_final).astype(bf16)
    base = 2 * width + units
    pack_ref[:, pl.ds(base + width + units, width)] = grad_lower
    sums_ref[9:10] = jnp.sum(grad_lower.astype(f32), axis=0, keepdims=True)
    grad_moved = None
    for f in range(units // width):
        columns = pl.ds(f * width, width)
        grad_active = dot_nt(grad_lower, down_sc[columns, :])
        grad_upper = (grad_active * slope_sc[:, columns]).astype(bf16)
        pack_ref[:, pl.ds(base + width + f * width, width)] = grad_upper
        sums_ref[10 + f : 11 + f] = jnp.sum(grad_upper.astype(f32), axis=0, keepdims=True)
        term = dot_nt(grad_upper, up_sc[:, columns])
        grad_moved = term if grad_moved is None else grad_moved + term
    add_rows(2, grad_moved)
    add_rows(4, grad_moved * scaled)
    grad_scaled = grad_moved * (1.0 + wide(4))
    sums_ref[8:9] = jnp.sum(grad_scaled * normed, axis=0, keepdims=True)
    grad_hidden = grad_final + norm_back(grad_scaled * gain_ref[...], normed, inverse)
    hidden_ref[...] = grad_hidden
    add_rows(0, grad_hidden * branch)
    grad_branch = (wide(2) * grad_hidden).astype(bf16)
    pack_ref[:, pl.ds(base, width)] = grad_branch
    grad_mixed = dot_nt(grad_branch, out_ref[...]).astype(bf16)
    for s in range(seqs):
        for g in range(GROUPS):
            piece = grad_mixed[s * tokens : (s + 1) * tokens, g * WIDTH : (g + 1) * WIDTH]
            leave_ref[s * GROUPS + g, :, pl.ds(0, WIDTH)] = piece[:half]
            leave_ref[s * GROUPS + g, :, pl.ds(WIDTH, WIDTH)] = piece[half:]


def middle(came, inputs, teacher, mask, weight, pieces, gain, up_bias, down_bias, out, up, down):
    seqs, tokens, width = inputs.shape
    units = up.shape[1]
    rows = seqs * tokens
    return pl.pallas_call(
        middle_kernel,
        out_shape=(
            jax.ShapeDtypeStruct((seqs, tokens, width), bf16),
            jax.ShapeDtypeStruct((rows, width), f32),
            jax.ShapeDtypeStruct(came.shape, bf16),
            jax.ShapeDtypeStruct((rows, 4 * width + 2 * units), bf16),
            jax.ShapeDtypeStruct((16, width), f32),
        ),
        in_specs=[VMEM] * 10 + [ANY] * 2,
        out_specs=(VMEM,) * 5,
        scratch_shapes=[
            pltpu.VMEM((width, units), bf16),
            pltpu.VMEM((units, width), bf16),
            pltpu.VMEM((rows, units), f32),
            pltpu.SemaphoreType.DMA((2,)),
        ],
        compiler_params=pltpu.CompilerParams(vmem_limit_bytes=56 << 20),
    )(came, inputs, teacher, mask, weight, pieces, gain, up_bias, down_bias, out, up, down)


def weights_kernel(
    place_ref, own_ref, other_ref, keep_a, send_a, keep_b, send_b, left_sc, right_sc, a_sc, b_sc, sems
):
    rows, width = own_ref.shape[0], a_sc.shape[-1]
    units = 4 * width
    hc = place_ref[1]
    base = 2 * width + units
    for which, ref in enumerate((own_ref, other_ref)):
        left_sc[:, pl.ds(which * rows, rows)] = ref[:, pl.ds(0, base)].T
        right_sc[pl.ds(which * rows, rows), :] = ref[:, pl.ds(base, base)]
    for hx in range(2):
        begin = pl.multiple_of(hx * 384 + hc * 192, 64)
        for j in range(5):
            offset = 0 if j == 0 else width
            value = dot(left_sc[pl.ds(begin + offset, 192), :], right_sc[:, pl.ds(j * width, width)])
            for i in range(8):
                a_sc[hx * 8 + i, j] = value[i * 24 : (i + 1) * 24].astype(bf16)
    copies = piece_copies(place_ref, a_sc, keep_a, send_a, sems, 0)
    for hx in range(2):
        begin = pl.multiple_of(2 * width + hx * 1536 + hc * 768, 256)
        value = dot(left_sc[pl.ds(begin, 768), :], right_sc[:, pl.ds(width + units, width)])
        for i in range(8):
            for j in range(4):
                first = i * 96 + j * 24
                b_sc[hx * 8 + i, j] = value[first : first + 24].astype(bf16)
    copies += piece_copies(place_ref, b_sc, keep_b, send_b, sems, 1)
    for copy in copies:
        copy.wait()


def weight_terms(here, own, other, width):
    rows, total = own.shape
    a = jax.ShapeDtypeStruct((2, 4, 5, 24, width), bf16)
    b = jax.ShapeDtypeStruct((2, 4, 4, 24, width), bf16)
    return pl.pallas_call(
        weights_kernel,
        out_shape=(a, a, b, b),
        in_specs=[SMEM, VMEM, VMEM],
        out_specs=(ANY,) * 4,
        scratch_shapes=[
            pltpu.VMEM((total // 2, 2 * rows), bf16),
            pltpu.VMEM((2 * rows, total // 2), bf16),
            pltpu.VMEM((16, 5, 24, width), bf16),
            pltpu.VMEM((16, 4, 24, width), bf16),
            pltpu.SemaphoreType.DMA((2, 16)),
        ],
        compiler_params=pltpu.CompilerParams(vmem_limit_bytes=56 << 20),
    )(here, own, other)


def flat_rows(came_ref, target, first_row, seqs, tokens, width):
    half = tokens // 2
    for s in range(seqs):
        for g in range(GROUPS):
            slot = s * GROUPS + g
            row = first_row + s * tokens
            left, right = load_pairs(came_ref, slot, tokens, half)
            target[pl.ds(row, half), pl.ds(g * WIDTH, WIDTH)] = left
            target[pl.ds(row + half, half), pl.ds(g * WIDTH, WIDTH)] = right
            left, right = load_pairs(came_ref, slot, 0, tokens)
            target[pl.ds(row, tokens), pl.ds(width + g * WIDTH, WIDTH)] = left
            target[pl.ds(row, tokens), pl.ds(2 * width + g * WIDTH, WIDTH)] = right


def qkv_kernel(
    seqs, place_ref, entered_ref, entered_other, own_ref, other_ref,
    keep_a, send_a, keep_b, send_b, left_sc, right_sc, block_sc, sems,
):
    rows, width = entered_ref.shape
    hc = place_ref[1]
    for which, (left, right) in enumerate(((entered_ref, own_ref), (entered_other, other_ref))):
        left_sc[:, pl.ds(which * rows, rows)] = left[...].T
        flat_rows(right, right_sc, which * rows, seqs, rows // seqs, width)
    for hx in range(2):
        begin = pl.multiple_of(hx * 384 + hc * 192, 64)
        for j in range(3):
            value = dot(left_sc[pl.ds(begin, 192), :], right_sc[:, pl.ds(j * width, width)])
            for i in range(8):
                block_sc[hx * 8 + i, :, pl.ds(j * width, width)] = value[
                    i * 24 : (i + 1) * 24
                ].astype(bf16)
    half = 3 * width // 2
    copies = piece_copies(place_ref, block_sc, keep_a, send_a, sems, 0, pl.ds(0, half))
    copies += piece_copies(place_ref, block_sc, keep_b, send_b, sems, 1, pl.ds(half, half))
    for copy in copies:
        copy.wait()


def qkv_terms(here, seqs, entered, entered_other, own, other):
    rows, width = entered.shape
    side = jax.ShapeDtypeStruct((2, 4, 24, 3 * width // 2), bf16)
    return pl.pallas_call(
        partial(qkv_kernel, seqs),
        out_shape=(side,) * 4,
        in_specs=[SMEM] + [VMEM] * 4,
        out_specs=(ANY,) * 4,
        scratch_shapes=[
            pltpu.VMEM((width, 2 * rows), bf16),
            pltpu.VMEM((2 * rows, 3 * width), bf16),
            pltpu.VMEM((16, 24, 3 * width), bf16),
            pltpu.SemaphoreType.DMA((2, 16)),
        ],
        compiler_params=pltpu.CompilerParams(vmem_limit_bytes=40 << 20),
    )(here, entered, entered_other, own, other)


def leave_kernel(
    came_ref, x_ref, hidden_ref, mod_ref, gain_ref, weight_ref, grad_ref, sums_ref, flat_ref
):
    seqs, tokens, width = x_ref.shape
    flat_rows(came_ref, flat_ref, 0, seqs, tokens, width)
    grad_entered = None
    for which in range(3):
        columns = pl.ds(which * width, width)
        term = dot_nt(flat_ref[:, columns], weight_ref[:, columns])
        grad_entered = term if grad_entered is None else grad_entered + term
    sums_ref[...] = jnp.zeros(sums_ref.shape, f32)
    gain_sum = None
    for s in range(seqs):
        normed, inverse = normalize(x_ref[s].astype(f32))
        rows = slice(s * tokens, (s + 1) * tokens)
        grad = grad_entered[rows]
        sums_ref[s : s + 1] = jnp.sum(grad, axis=0, keepdims=True)
        sums_ref[2 + s : 3 + s] = jnp.sum(grad * (normed * gain_ref[...]), axis=0, keepdims=True)
        grad_scaled = grad * (1.0 + mod_ref[s, 1:2])
        term = jnp.sum(grad_scaled * normed, axis=0, keepdims=True)
        gain_sum = term if gain_sum is None else gain_sum + term
        grad_ref[s] = hidden_ref[rows] + norm_back(grad_scaled * gain_ref[...], normed, inverse)
    sums_ref[4:5] = gain_sum


def leave(came, inputs, grad_hidden, pieces, gain, weight):
    seqs, tokens, width = inputs.shape
    return pl.pallas_call(
        leave_kernel,
        out_shape=(
            jax.ShapeDtypeStruct((seqs, tokens, width), f32),
            jax.ShapeDtypeStruct((8, width), f32),
            jax.ShapeDtypeStruct((seqs * tokens, 3 * width), bf16),
        ),
        in_specs=[VMEM] * 6,
        out_specs=(VMEM,) * 3,
        compiler_params=pltpu.CompilerParams(vmem_limit_bytes=40 << 20),
    )(came, inputs, grad_hidden, pieces, gain, weight)


def exchange(rows):
    return lax.all_to_all(rows, SPOT, 0, 0, tiled=True)


def on_device(
    inputs,
    time_embed,
    segments,
    valid_mask,
    teacher,
    ada_weight,
    ada_bias,
    gain_attn,
    qkv_weight,
    out_weight,
    gain_mlp,
    up_weight,
    up_bias,
    down_weight,
    down_bias,
):
    seqs, tokens, width = inputs.shape
    units = up_weight.shape[1]
    parts = lax.axis_size("rb")
    devices = 32 * parts
    length = tokens * devices
    queries = 8 * tokens
    here = place()
    hx, hc, rb = lax.axis_index("hx"), lax.axis_index("hc"), lax.axis_index("rb")
    own_seq = (lax.axis_index("sz") * 2 + lax.axis_index("sy")) // GROUPS

    own_modulation = jnp.dot(
        time_embed, ada_weight.astype(f32), precision=precise
    ) + ada_bias.astype(f32)
    mask_float = valid_mask.astype(f32)
    fields = [
        own_modulation.reshape(-1),
        gain_attn.astype(f32),
        gain_mlp.astype(f32),
        up_bias.astype(f32),
        down_bias.astype(f32),
        segments.astype(f32).reshape(-1),
        jnp.sum(mask_float).reshape(1),
    ]
    sizes = [field.shape[0] for field in fields]
    packed = jnp.concatenate(fields)
    everyone = lax.all_to_all(
        jnp.broadcast_to(packed, (devices, packed.shape[0])), EVERY, 0, 0, tiled=True
    )
    columns = []
    begin = 0
    for size in sizes:
        columns.append(everyone[:, begin : begin + size])
        begin += size
    modulation = columns[0].reshape(devices, seqs, -1).transpose(1, 0, 2)
    pieces = modulation.reshape(seqs, 6, width)
    gain_one, gain_two, full_up_bias, full_down_bias = (c.reshape(1, -1) for c in columns[1:5])
    docs = columns[5].reshape(2, 2, parts, 8, seqs, tokens)
    count_all = jnp.sum(columns[6])

    full_qkv = gather_rows(here, qkv_weight)
    if parts > 1:
        full_out, full_up, full_down = (
            lax.all_gather(w, EVERY, axis=0, tiled=True)
            for w in (out_weight, up_weight, down_weight)
        )
    else:
        later = jnp.concatenate(
            [out_weight[None]]
            + [up_weight[None, :, j * width : (j + 1) * width] for j in range(4)]
            + [down_weight.reshape(4, 24, width)]
        )
        later = lax.all_gather(later, EVERY, axis=0, tiled=False)
        full_out = later[:, 0].reshape(width, width)
        full_up = later[:, 1:5].transpose(0, 2, 1, 3).reshape(width, units)
        full_down = later[:, 5:].reshape(units, width)

    entered, leaving = enter(inputs, pieces, gain_one, full_qkv)
    came = exchange(leaving)
    pair = came[:, :tokens].reshape(queries, 2 * WIDTH)
    if parts > 1:
        pair = lax.all_gather(pair, "rb", axis=0, tiled=True)
    pair_x = swap(pair, "hx")
    pair_c = jnp.concatenate([swap(pair, "hc"), swap(pair_x, "hc")])
    pairs = (pair, pair_x, pair_c)

    docs_here = lax.dynamic_index_in_dim(docs, own_seq, 4, keepdims=False)
    docs_here = jnp.where(hx == 1, docs_here[::-1], docs_here)
    docs_here = jnp.where(hc == 1, docs_here[:, ::-1], docs_here)
    key_docs = docs_here.transpose(1, 0, 2, 3, 4).reshape(-1, 1)
    query_docs = lax.dynamic_index_in_dim(docs_here[0, 0], rb, 0, keepdims=False).reshape(1, -1)
    attended, turned, total = attend(came, pairs, key_docs, query_docs)

    mask_column = mask_float.reshape(-1, 1)
    final, grad_hidden, grad_leaving, pack, sums = middle(
        exchange(attended),
        inputs,
        teacher,
        mask_column,
        mask_column * (seqs * length / count_all),
        pieces,
        gain_two,
        full_up_bias,
        full_down_bias,
        full_out,
        full_up,
        full_down,
    )
    grad_came = exchange(grad_leaving)
    if parts == 1:
        terms = weight_terms(here, pack, swap(pack, "hc"), width)
        side_a = collect(terms[0], terms[1], ORDERS[0])
        side_b = collect(terms[2], terms[3], ORDERS[1])
        shard_out = side_a[0]
        shard_up = side_a[1:].transpose(1, 0, 2).reshape(24, units)
        shard_down = side_b.reshape(96, width)
    else:
        base = 2 * width + units
        ends = (base + width, base + width + units)
        shard_out, shard_up, shard_down = (
            lax.psum_scatter(
                jnp.einsum("tk,tn->kn", left, right, preferred_element_type=f32),
                EVERY,
                scatter_dimension=0,
                tiled=True,
            )
            for left, right in (
                (pack[:, :width], pack[:, base : ends[0]]),
                (pack[:, width : 2 * width], pack[:, ends[0] : ends[1]]),
                (pack[:, 2 * width : base], pack[:, ends[1] :]),
            )
        )

    grad_query, keep, send = attend_back(
        came, grad_came, pairs, key_docs, query_docs, turned, total
    )
    grad_pair = keep + swap(send, "hc").astype(f32)
    middle_row = grad_pair.shape[0] // 2
    grad_pair = grad_pair[:middle_row] + swap(grad_pair[middle_row:].astype(bf16), "hx").astype(f32)
    if parts > 1:
        grad_pair = lax.psum_scatter(grad_pair, "rb", scatter_dimension=0, tiled=True)
    home = exchange(
        jnp.concatenate(
            [grad_pair.astype(bf16).reshape(8, tokens, 2 * WIDTH), grad_query], axis=1
        )
    )
    grad_input, sums_one, flat = leave(home, inputs, grad_hidden, pieces, gain_one, full_qkv)
    if parts == 1:
        terms = qkv_terms(here, seqs, entered, swap(entered, "hc"), home, swap(home, "hc"))
        shard_qkv = jnp.concatenate(
            [collect(terms[0], terms[1], ORDERS[0]), collect(terms[2], terms[3], ORDERS[1])],
            axis=1,
        )
    else:
        shard_qkv = lax.psum_scatter(
            jnp.einsum("tk,tn->kn", entered, flat, preferred_element_type=f32),
            EVERY,
            scatter_dimension=0,
            tiled=True,
        )
    grad_modulation = jnp.stack(
        [
            jnp.stack([sums_one[s], sums_one[2 + s], sums[s], sums[2 + s], sums[4 + s], sums[6 + s]])
            for s in range(seqs)
        ]
    ).reshape(seqs, devices, -1)
    fields = [
        grad_modulation.transpose(1, 0, 2).reshape(devices, -1),
        sums_one[4].reshape(devices, -1),
        sums[8].reshape(devices, -1),
        sums[10:14].reshape(devices, -1),
        sums[9].reshape(devices, -1),
        jnp.broadcast_to(jnp.sum(sums[14]), (devices, 1)),
    ]
    sizes = [value.shape[1] for value in fields]
    added = jnp.sum(
        lax.all_to_all(jnp.concatenate(fields, axis=1), EVERY, 0, 0, tiled=True), axis=0
    )
    owned = []
    begin = 0
    for size in sizes:
        owned.append(added[begin : begin + size])
        begin += size
    own_grad = owned[0].reshape(seqs, -1)
    grad_ada_weight = jnp.sum(time_embed[:, :, None] * own_grad[:, None, :], axis=0)
    loss_value = owned[5][0] / (count_all * width)
    return (
        final,
        loss_value,
        grad_input,
        grad_ada_weight,
        jnp.sum(own_grad, axis=0),
        owned[1],
        shard_qkv,
        shard_out,
        owned[2],
        shard_up,
        owned[3],
        shard_down,
        owned[4],
    )


def solution(mesh):
    blocks = mesh.shape["blk"]
    fine = Mesh(mesh.devices.reshape(2, 2, blocks // 8, 4, 2), EVERY)
    tokens = ("rb", "sz", "sy", "hx", "hc")
    return jax.shard_map(
        on_device,
        mesh=fine,
        in_specs=(
            P(None, tokens, None),
            P(),
            P(None, tokens),
            P(None, tokens),
            P(None, tokens, None),
            P(None, EVERY),
            P(EVERY),
            P(EVERY),
            P(EVERY, None),
            P(EVERY, None),
            P(EVERY),
            P(EVERY, None),
            P(EVERY),
            P(EVERY, None),
            P(EVERY),
        ),
        out_specs=(
            P(None, tokens, None),
            P(),
            P(None, tokens, None),
            P(None, EVERY),
            P(EVERY),
            P(EVERY),
            P(EVERY, None),
            P(EVERY, None),
            P(EVERY),
            P(EVERY, None),
            P(EVERY),
            P(EVERY, None),
            P(EVERY),
        ),
        check_vma=False,
    )
```

```python
from functools import partial

import jax
import jax.numpy as jnp
from jax import lax
from jax.experimental import pallas as pl
from jax.experimental.pallas import tpu as pltpu
from jax.sharding import Mesh, PartitionSpec as P

HEADS = 12
HEAD_DIM = 64
GROUPS = 4
WIDTH = HEADS // GROUPS * HEAD_DIM
EVERY = ("hx", "hc", "rb", "sz", "sy")
SPOT = ("sz", "sy")
bf16 = jnp.bfloat16
f32 = jnp.float32
precise = lax.Precision.HIGHEST


def normalize(hidden):
    average = jnp.mean(hidden, axis=-1, keepdims=True)
    centred = hidden - average
    variance = jnp.mean(centred * centred, axis=-1, keepdims=True)
    inverse = lax.rsqrt(variance + 1e-05)
    return (centred * inverse, inverse)


def dot(left, right):
    return jnp.dot(left, right, preferred_element_type=f32)


def dot_nt(left, right):
    return lax.dot_general(left, right, (((1,), (1,)), ((), ())), preferred_element_type=f32)


def norm_back(upstream, normed, inverse):
    first_mean = jnp.mean(upstream, axis=-1, keepdims=True)
    second_mean = jnp.mean(upstream * normed, axis=-1, keepdims=True)
    return inverse * (upstream - first_mean - normed * second_mean)


def swap(value, axis):
    return lax.ppermute(value, axis, [(0, 1), (1, 0)])


def turn(value, axis, step):
    size = lax.axis_size(axis)
    return lax.ppermute(value, axis, [(i, (i - step) % size) for i in range(size)])


def place():
    return jnp.stack([lax.axis_index(name) for name in ("hx", "hc", "sz", "sy", "rb")]).astype(
        jnp.int32
    )


ANY = pl.BlockSpec(memory_space=pl.ANY)
SMEM = pl.BlockSpec(memory_space=pltpu.SMEM)
VMEM = pl.BlockSpec(memory_space=pltpu.VMEM)


def run_all(copies):
    for copy in copies:
        copy.start()
    for copy in copies:
        copy.wait()


def join_kernel(place_ref, left, left_other, right, right_other, whole, sems):
    hx, hc, sz, sy = (place_ref[i] for i in range(4))
    half = left.shape[-1]
    copies = []
    for side, cores in enumerate(((left, left_other), (right, right_other))):
        for core, pieces in enumerate(cores):
            for second in range(2):
                for first in range(2):
                    for deep in range(4):
                        across, down = (first, second) if side == 0 else (second, first)
                        block = (hx ^ across) * 2 + (hc ^ core)
                        spot = (block * 4 + lax.rem(sz + deep, 4)) * 2 + (sy ^ down)
                        copies.append(
                            pltpu.make_async_copy(
                                pieces.at[second, first, deep],
                                whole.at[spot, :, pl.ds(side * half, half)],
                                sems.at[len(copies)],
                            )
                        )
    run_all(copies)


def join(here, *sides):
    rows, half = sides[0].shape[-2:]
    return pl.pallas_call(
        join_kernel,
        out_shape=jax.ShapeDtypeStruct((32, rows, half * 2), bf16),
        in_specs=[SMEM] + [ANY] * 4,
        out_specs=VMEM,
        scratch_shapes=[pltpu.SemaphoreType.DMA((64,))],
        compiler_params=pltpu.CompilerParams(vmem_limit_bytes=40 << 20),
    )(here, *sides).reshape(rows * 32, half * 2)


def gather_rows(here, shard, first):
    half = shard.shape[1] // 2
    sides = []
    deep = jnp.stack([shard] + [turn(shard, "sz", k) for k in (1, 2, 3)])
    deep, first = lax.optimization_barrier((deep, first))
    for side, order in ((0, ("hx", "sy")), (1, ("sy", "hx"))):
        level = deep[:, :, side * half : (side + 1) * half]
        for axis in order:
            level = jnp.stack([level, swap(level, axis)])
        sides += [level, swap(level, "hc")]
    return join(here, *sides), first


def piece_copies(place_ref, blocks, keep, send, sems, side, columns=None):
    hx, sz, sy = place_ref[0], place_ref[2], place_ref[3]
    copies = []
    for second in range(2):
        for first in range(2):
            for deep in range(4):
                across, down = (first, second) if side == 0 else (second, first)
                spot = ((hx ^ across) * 4 + lax.rem(sz + deep, 4)) * 2 + (sy ^ down)
                source = blocks.at[spot] if columns is None else blocks.at[spot, :, columns]
                target = (keep, send)[second].at[first, deep]
                copies.append(pltpu.make_async_copy(source, target, sems.at[side, len(copies)]))
    for copy in copies:
        copy.start()
    return copies


ORDERS = (("sy", "hx"), ("hx", "sy"))


def reduce_first(keep, send, order):
    return keep.astype(f32) + swap(send, order[0]).astype(f32)


def reduce_second(total, order):
    return total[0] + swap(total[1].astype(bf16), order[1]).astype(f32)


def reduce_third(total):
    result = total[0]
    for k in (1, 2, 3):
        result = result + turn(total[k].astype(bf16), "sz", -k).astype(f32)
    return result


def enter_kernel(x_ref, mod_ref, gains_ref, weight_ref, entered_ref, pair_ref, query_ref):
    seqs, tokens, width = x_ref.shape
    half = tokens // 2
    for s in range(seqs):
        normed = normalize(x_ref[s].astype(f32))[0]
        shift, scale = (mod_ref[s : s + 1, pl.ds(i * width, width)] for i in (0, 1))
        value = normed * gains_ref[0:1] * (1.0 + scale) + shift
        entered_ref[pl.ds(s * tokens, tokens), :] = value.astype(bf16)
    entered = entered_ref[...]
    for which in (1, 2, 0):
        triple = dot(entered, weight_ref[:, pl.ds(which * width, width)]).astype(bf16)
        for s in range(seqs):
            for g in range(GROUPS):
                rows = triple[s * tokens : (s + 1) * tokens, g * WIDTH : (g + 1) * WIDTH]
                slot = s * GROUPS + g
                if which == 0:
                    query_ref[slot, :, pl.ds(0, WIDTH)] = rows[:half]
                    query_ref[slot, :, pl.ds(WIDTH, WIDTH)] = rows[half:]
                else:
                    pair_ref[slot, :, pl.ds((which - 1) * WIDTH, WIDTH)] = rows


def enter(inputs, modulation, gains, weight):
    seqs, tokens, width = inputs.shape
    return pl.pallas_call(
        enter_kernel,
        out_shape=(
            jax.ShapeDtypeStruct((seqs * tokens, width), bf16),
            jax.ShapeDtypeStruct((8, tokens, 2 * WIDTH), bf16),
            jax.ShapeDtypeStruct((8, tokens // 2, 2 * WIDTH), bf16),
        ),
        in_specs=[VMEM] * 4,
        out_specs=(VMEM,) * 3,
        compiler_params=pltpu.CompilerParams(vmem_limit_bytes=40 << 20),
    )(inputs, modulation, gains, weight)


def head_lanes(rows, head):
    lane = lax.broadcasted_iota(jnp.int32, (rows, WIDTH), 1)
    return (lane >= head * HEAD_DIM) & (lane < (head + 1) * HEAD_DIM)


def load_pairs(pair_ref, slot, first_row, half):
    value = pair_ref[slot, pl.ds(first_row, half), :]
    return value[:, :WIDTH], value[:, WIDTH:]


def spread_heads(pair_ref, first_row, half, target, factor):
    heads = target.shape[0]
    zero = jnp.zeros((half, WIDTH), bf16)
    for slot in range(8):
        for part, rows in enumerate(load_pairs(pair_ref, slot, first_row, half)):
            rows = (rows.astype(f32) * factor).astype(bf16)
            for h in range(heads):
                target[h, pl.ds((slot * 2 + part) * half, half), :] = jnp.where(
                    head_lanes(half, h), rows, zero
                )


def fetch(step, pair_refs, starts, pair_sc):
    for ref, (begin, end) in zip(pair_refs, starts):
        @pl.when((step >= begin) & (step < end))
        def take(ref=ref):
            pair_sc[...] = ref[...]


def forward_kernel(
    starts, came_ref, first_ref, second_ref, third_ref, fourth_ref, key_docs_ref, query_docs_ref,
    out_ref, turned_ref, total_ref, query_sc, pair_sc, top_sc, sum_sc, acc_sc,
):
    step = pl.program_id(0)
    heads, queries = query_sc.shape[:2]
    half = out_ref.shape[1]

    @pl.when(step == 0)
    def start():
        spread_heads(came_ref, 0, half, query_sc, HEAD_DIM ** (-0.5))
        top_sc[...] = jnp.full(top_sc.shape, -1e30, f32)
        sum_sc[...] = jnp.zeros(sum_sc.shape, f32)
        acc_sc[...] = jnp.zeros(acc_sc.shape, f32)

    fetch(step, (first_ref, second_ref, third_ref, fourth_ref), starts, pair_sc)
    key_part = pair_sc[:, :WIDTH]
    value_turned = pair_sc[:, WIDTH:].T
    allowed = key_docs_ref[...] == query_docs_ref[...]
    for h in range(heads):
        rows = pl.ds(h * HEAD_DIM, HEAD_DIM)
        scores = jnp.where(allowed, dot_nt(key_part, query_sc[h]), -1e30)
        old = top_sc[h : h + 1]
        new = jnp.maximum(old, jnp.max(scores, axis=0, keepdims=True))
        exponent = jnp.exp(scores - new)
        fade = jnp.exp(old - new)
        top_sc[h : h + 1] = new
        sum_sc[h : h + 1] = sum_sc[h : h + 1] * fade + jnp.sum(exponent, axis=0, keepdims=True)
        acc_sc[rows] = acc_sc[rows] * fade + dot(
            value_turned[h * HEAD_DIM : (h + 1) * HEAD_DIM], exponent.astype(bf16)
        )

    @pl.when(step == pl.num_programs(0) - 1)
    def finish():
        total_ref[...] = jnp.zeros(total_ref.shape, f32)
        for h in range(heads):
            rows = pl.ds(h * HEAD_DIM, HEAD_DIM)
            turned_ref[rows] = acc_sc[rows] / sum_sc[h : h + 1]
            total_ref[h : h + 1] = top_sc[h : h + 1] + jnp.log(sum_sc[h : h + 1])
        whole = turned_ref[...].T.astype(bf16)
        for slot in range(8):
            for part in range(2):
                begin = (slot * 2 + part) * half
                out_ref[slot, :, pl.ds(part * WIDTH, WIDTH)] = whole[begin : begin + half]


def pair_specs(pairs, chunk):
    specs, starts, begin = [], [], 0
    for pair in pairs:
        count = pair.shape[0] // chunk
        specs.append(
            pl.BlockSpec(
                (chunk, 2 * WIDTH),
                lambda i, begin=begin, count=count: (jnp.clip(i - begin, 0, count - 1), 0),
            )
        )
        starts.append((begin, begin + count))
        begin += count
    return specs, starts, begin


def whole_spec(shape):
    return pl.BlockSpec(shape, lambda i: (0,) * len(shape))


def attend(came, pairs, key_docs, query_docs):
    slots, half, columns = came.shape
    queries = slots * 2 * half
    heads = WIDTH // HEAD_DIM
    chunk = 512
    specs, starts, steps = pair_specs(pairs, chunk)
    outs = (
        jax.ShapeDtypeStruct((slots, half, columns), bf16),
        jax.ShapeDtypeStruct((WIDTH, queries), f32),
        jax.ShapeDtypeStruct((8, queries), f32),
    )
    return pl.pallas_call(
        partial(forward_kernel, starts),
        grid=(steps,),
        out_shape=outs,
        in_specs=[
            whole_spec(came.shape),
            *specs,
            pl.BlockSpec((chunk, 1), lambda i: (i, 0)),
            whole_spec(query_docs.shape),
        ],
        out_specs=tuple(whole_spec(o.shape) for o in outs),
        scratch_shapes=[
            pltpu.VMEM((heads, queries, WIDTH), bf16),
            pltpu.VMEM((chunk, 2 * WIDTH), bf16),
            pltpu.VMEM((8, queries), f32),
            pltpu.VMEM((8, queries), f32),
            pltpu.VMEM((WIDTH, queries), f32),
        ],
        compiler_params=pltpu.CompilerParams(vmem_limit_bytes=48 << 20),
    )(came, *pairs, key_docs, query_docs)


def backward_kernel(
    starts, came_ref, grad_ref, first_ref, second_ref, third_ref, fourth_ref, key_docs_ref, query_docs_ref,
    turned_ref, total_ref, query_out, keep_ref, send_ref,
    query_sc, grad_sc, pair_sc, delta_sc, acc_sc,
):
    step = pl.program_id(0)
    heads, queries = query_sc.shape[:2]
    half = query_out.shape[1]

    @pl.when(step == 0)
    def start():
        spread_heads(came_ref, 0, half, query_sc, HEAD_DIM ** (-0.5))
        spread_heads(grad_ref, 0, half, grad_sc, 1.0)
        acc_sc[...] = jnp.zeros(acc_sc.shape, f32)
        for h in range(heads):
            rows = slice(h * HEAD_DIM, (h + 1) * HEAD_DIM)
            turned = grad_sc[h].astype(f32).T
            delta_sc[h : h + 1] = jnp.sum(turned[rows] * turned_ref[rows], axis=0, keepdims=True)

    fetch(step, (first_ref, second_ref, third_ref, fourth_ref), starts, pair_sc)
    key_part = pair_sc[:, :WIDTH]
    value_part = pair_sc[:, WIDTH:]
    key_turned = key_part.T
    allowed = key_docs_ref[...] == query_docs_ref[...]
    grad_key = grad_value = None
    for h in range(heads):
        rows = pl.ds(h * HEAD_DIM, HEAD_DIM)
        query, grad = query_sc[h], grad_sc[h]
        scores = jnp.where(allowed, dot_nt(key_part, query), -1e30)
        probabilities = jnp.exp(scores - total_ref[h : h + 1])
        slope = dot_nt(value_part, grad) - delta_sc[h : h + 1]
        grad_scores = (probabilities * slope).astype(bf16)
        value_term = dot(probabilities.astype(bf16), grad)
        key_term = dot(grad_scores, query)
        grad_value = value_term if grad_value is None else grad_value + value_term
        grad_key = key_term if grad_key is None else grad_key + key_term
        acc_sc[rows] = acc_sc[rows] + dot(
            key_turned[h * HEAD_DIM : (h + 1) * HEAD_DIM], grad_scores
        )
    middle = pl.num_programs(0) // 2

    @pl.when(step < middle)
    def mine():
        keep_ref[:, pl.ds(0, WIDTH)] = grad_key
        keep_ref[:, pl.ds(WIDTH, WIDTH)] = grad_value

    @pl.when(step >= middle)
    def theirs():
        send_ref[:, pl.ds(0, WIDTH)] = grad_key.astype(bf16)
        send_ref[:, pl.ds(WIDTH, WIDTH)] = grad_value.astype(bf16)

    @pl.when(step == pl.num_programs(0) - 1)
    def finish():
        whole = (acc_sc[...] * HEAD_DIM ** (-0.5)).T.astype(bf16)
        for slot in range(8):
            for part in range(2):
                begin = (slot * 2 + part) * half
                query_out[slot, :, pl.ds(part * WIDTH, WIDTH)] = whole[begin : begin + half]


def attend_back(came, grad, pairs, key_docs, query_docs, turned, total):
    slots, half, columns = came.shape
    queries = slots * 2 * half
    heads = WIDTH // HEAD_DIM
    chunk = 512
    specs, starts, steps = pair_specs(pairs, chunk)
    middle = steps // 2
    return pl.pallas_call(
        partial(backward_kernel, starts),
        grid=(steps,),
        out_shape=(
            jax.ShapeDtypeStruct((slots, half, columns), bf16),
            jax.ShapeDtypeStruct((middle * chunk, columns), f32),
            jax.ShapeDtypeStruct((middle * chunk, columns), bf16),
        ),
        in_specs=[
            whole_spec(came.shape),
            whole_spec(grad.shape),
            *specs,
            pl.BlockSpec((chunk, 1), lambda i: (i, 0)),
            whole_spec(query_docs.shape),
            whole_spec(turned.shape),
            whole_spec(total.shape),
        ],
        out_specs=(
            whole_spec((slots, half, columns)),
            pl.BlockSpec((chunk, columns), lambda i: (jnp.minimum(i, middle - 1), 0)),
            pl.BlockSpec((chunk, columns), lambda i: (jnp.maximum(i - middle, 0), 0)),
        ),
        scratch_shapes=[
            pltpu.VMEM((heads, queries, WIDTH), bf16),
            pltpu.VMEM((heads, queries, WIDTH), bf16),
            pltpu.VMEM((chunk, 2 * WIDTH), bf16),
            pltpu.VMEM((8, queries), f32),
            pltpu.VMEM((WIDTH, queries), f32),
        ],
        compiler_params=pltpu.CompilerParams(vmem_limit_bytes=48 << 20),
    )(came, grad, *pairs, key_docs, query_docs, turned, total)


def middle_kernel(
    gathered, came_ref, x_ref, teacher_ref, mask_ref, mod_ref, gains_ref, up_bias_ref, *refs
):
    if gathered:
        later_hbm, *refs = refs
    else:
        out_hbm, up_hbm, down_hbm, *refs = refs
    final_ref, hidden_ref, leave_ref, pack_ref, sums_ref, *refs = refs
    out_sc, up_sc, down_sc, slope_sc, *refs = refs
    if gathered:
        block_sc, sems = refs
    else:
        (sems,) = refs

    seqs, tokens, width = x_ref.shape
    units = up_sc.shape[1]
    rows = seqs * tokens
    half = tokens // 2
    if gathered:
        copies = [
            pltpu.make_async_copy(later_hbm.at[:, j], block_sc.at[j], sems.at[j]) for j in range(9)
        ]
    else:
        copies = [
            pltpu.make_async_copy(source, target, sems.at[i])
            for i, (source, target) in enumerate(
                ((out_hbm, out_sc), (up_hbm, up_sc), (down_hbm, down_sc))
            )
        ]
    for copy in copies:
        copy.start()

    def settle(j):
        if not gathered:
            if j < 2 or j == 5:
                copies[(0, 1, None, None, None, 2)[j]].wait()
            return
        copies[j].wait()
        for i in range(32):
            value = block_sc[j, i]
            if j == 0:
                out_sc[pl.ds(i * 24, 24), :] = value
            elif j < 5:
                up_sc[pl.ds(i * 24, 24), pl.ds((j - 1) * width, width)] = value
            else:
                down_sc[pl.ds(i * 96 + (j - 5) * 24, 24), :] = value

    def wide(index):
        return jnp.concatenate(
            [
                jnp.broadcast_to(
                    mod_ref[s : s + 1, pl.ds(index * width, width)], (tokens, width)
                )
                for s in range(seqs)
            ]
        )

    def add_rows(first, value):
        for s in range(seqs):
            sums_ref[first + s : first + s + 1] = jnp.sum(
                value[s * tokens : (s + 1) * tokens], axis=0, keepdims=True
            )

    for s in range(seqs):
        for g in range(GROUPS):
            left, right = load_pairs(came_ref, s * GROUPS + g, 0, half)
            columns = pl.ds(g * WIDTH, WIDTH)
            pack_ref[pl.ds(s * tokens, half), columns] = left
            pack_ref[pl.ds(s * tokens + half, half), columns] = right
    mixed = pack_ref[:, pl.ds(0, width)]
    residual = jnp.concatenate([x_ref[s].astype(f32) for s in range(seqs)])
    settle(0)
    branch = dot(mixed, out_sc[...])
    hidden = residual + wide(2) * branch
    normed, inverse = normalize(hidden)
    scaled = normed * gains_ref[1:2]
    moved = (scaled * (1.0 + wide(4)) + wide(3)).astype(bf16)
    pack_ref[:, pl.ds(width, width)] = moved
    for j in range(1, 9):
        settle(j)
    lower = None
    for f in range(units // width):
        columns = pl.ds(f * width, width)
        u = dot(moved, up_sc[:, columns]) + up_bias_ref[0:1, columns]
        square = u * u
        t = jnp.tanh(0.7978845608028654 * (u + 0.044715 * u * square))
        active = (0.5 * u * (1.0 + t)).astype(bf16)
        slope_sc[:, columns] = 0.5 * (1.0 + t) + 0.5 * u * (1.0 - t * t) * 0.7978845608028654 * (
            1.0 + 0.134145 * square
        )
        pack_ref[:, pl.ds(2 * width + f * width, width)] = active
        term = dot(active, down_sc[columns, :])
        lower = term if lower is None else lower + term
    lower = lower + gains_ref[2:3]
    gate = wide(5)
    final = hidden + gate * lower
    for s in range(seqs):
        final_ref[s] = final[s * tokens : (s + 1) * tokens].astype(bf16)
    teacher = jnp.concatenate([teacher_ref[s].astype(f32) for s in range(seqs)])
    mismatch = final - teacher
    sums_ref[14:15] = jnp.sum(
        mask_ref[:, 0:1] * mismatch * mismatch, axis=0, keepdims=True
    )
    sums_ref[15:16] = jnp.zeros((1, width), f32)
    grad_final = mask_ref[:, 1:2] * mismatch
    add_rows(6, grad_final * lower)
    grad_lower = (gate * grad_final).astype(bf16)
    base = 2 * width + units
    pack_ref[:, pl.ds(base + width + units, width)] = grad_lower
    sums_ref[9:10] = jnp.sum(grad_lower.astype(f32), axis=0, keepdims=True)
    grad_moved = None
    for f in range(units // width):
        columns = pl.ds(f * width, width)
        grad_active = dot_nt(grad_lower, down_sc[columns, :])
        grad_upper = (grad_active * slope_sc[:, columns]).astype(bf16)
        pack_ref[:, pl.ds(base + width + f * width, width)] = grad_upper
        sums_ref[10 + f : 11 + f] = jnp.sum(grad_upper.astype(f32), axis=0, keepdims=True)
        term = dot_nt(grad_upper, up_sc[:, columns])
        grad_moved = term if grad_moved is None else grad_moved + term
    add_rows(2, grad_moved)
    add_rows(4, grad_moved * scaled)
    grad_scaled = grad_moved * (1.0 + wide(4))
    sums_ref[8:9] = jnp.sum(grad_scaled * normed, axis=0, keepdims=True)
    grad_hidden = grad_final + norm_back(grad_scaled * gains_ref[1:2], normed, inverse)
    hidden_ref[...] = grad_hidden
    add_rows(0, grad_hidden * branch)
    grad_branch = (wide(2) * grad_hidden).astype(bf16)
    pack_ref[:, pl.ds(base, width)] = grad_branch
    grad_mixed = dot_nt(grad_branch, out_sc[...]).astype(bf16)
    for s in range(seqs):
        for g in range(GROUPS):
            piece = grad_mixed[s * tokens : (s + 1) * tokens, g * WIDTH : (g + 1) * WIDTH]
            leave_ref[s * GROUPS + g, :, pl.ds(0, WIDTH)] = piece[:half]
            leave_ref[s * GROUPS + g, :, pl.ds(WIDTH, WIDTH)] = piece[half:]


def middle(came, inputs, teacher, masks, modulation, gains, up_bias, later):
    seqs, tokens, width = inputs.shape
    units = up_bias.shape[1]
    rows = seqs * tokens
    gathered = len(later) == 1
    scratch = [
        pltpu.VMEM((width, width), bf16),
        pltpu.VMEM((width, units), bf16),
        pltpu.VMEM((units, width), bf16),
        pltpu.VMEM((rows, units), f32),
    ]
    if gathered:
        scratch.append(pltpu.VMEM((9, 32, 24, width), bf16))
    return pl.pallas_call(
        partial(middle_kernel, gathered),
        out_shape=(
            jax.ShapeDtypeStruct((seqs, tokens, width), bf16),
            jax.ShapeDtypeStruct((rows, width), f32),
            jax.ShapeDtypeStruct(came.shape, bf16),
            jax.ShapeDtypeStruct((rows, 4 * width + 2 * units), bf16),
            jax.ShapeDtypeStruct((16, width), f32),
        ),
        in_specs=[VMEM] * 7 + [ANY] * len(later),
        out_specs=(VMEM,) * 5,
        scratch_shapes=scratch + [pltpu.SemaphoreType.DMA((9,))],
        compiler_params=pltpu.CompilerParams(vmem_limit_bytes=60 << 20),
    )(came, inputs, teacher, masks, modulation, gains, up_bias, *later)


def weights_kernel(
    place_ref, own_ref, other_ref, keep_a, send_a, keep_b, send_b, left_sc, right_sc, a_sc, b_sc, sems
):
    rows, width = own_ref.shape[0], a_sc.shape[-1]
    units = 4 * width
    hc = place_ref[1]
    base = 2 * width + units
    for which, ref in enumerate((own_ref, other_ref)):
        left_sc[:, pl.ds(which * rows, rows)] = ref[:, pl.ds(0, base)].T
        right_sc[pl.ds(which * rows, rows), :] = ref[:, pl.ds(base, base)]
    for hx in range(2):
        begin = pl.multiple_of(hx * 384 + hc * 192, 64)
        for j in range(5):
            offset = 0 if j == 0 else width
            value = dot(left_sc[pl.ds(begin + offset, 192), :], right_sc[:, pl.ds(j * width, width)])
            for i in range(8):
                a_sc[hx * 8 + i, j] = value[i * 24 : (i + 1) * 24].astype(bf16)
    copies = piece_copies(place_ref, a_sc, keep_a, send_a, sems, 0)
    for hx in range(2):
        begin = pl.multiple_of(2 * width + hx * 1536 + hc * 768, 256)
        value = dot(left_sc[pl.ds(begin, 768), :], right_sc[:, pl.ds(width + units, width)])
        for i in range(8):
            for j in range(4):
                first = i * 96 + j * 24
                b_sc[hx * 8 + i, j] = value[first : first + 24].astype(bf16)
    copies += piece_copies(place_ref, b_sc, keep_b, send_b, sems, 1)
    for copy in copies:
        copy.wait()


def weight_terms(here, own, other, width):
    rows, total = own.shape
    a = jax.ShapeDtypeStruct((2, 4, 5, 24, width), bf16)
    b = jax.ShapeDtypeStruct((2, 4, 4, 24, width), bf16)
    return pl.pallas_call(
        weights_kernel,
        out_shape=(a, a, b, b),
        in_specs=[SMEM, VMEM, VMEM],
        out_specs=(ANY,) * 4,
        scratch_shapes=[
            pltpu.VMEM((total // 2, 2 * rows), bf16),
            pltpu.VMEM((2 * rows, total // 2), bf16),
            pltpu.VMEM((16, 5, 24, width), bf16),
            pltpu.VMEM((16, 4, 24, width), bf16),
            pltpu.SemaphoreType.DMA((2, 16)),
        ],
        compiler_params=pltpu.CompilerParams(vmem_limit_bytes=56 << 20),
    )(here, own, other)


def flat_rows(query_ref, pair_ref, target, first_row, seqs, tokens, width):
    half = tokens // 2
    for s in range(seqs):
        for g in range(GROUPS):
            slot = s * GROUPS + g
            row = first_row + s * tokens
            left, right = load_pairs(query_ref, slot, 0, half)
            target[pl.ds(row, half), pl.ds(g * WIDTH, WIDTH)] = left
            target[pl.ds(row + half, half), pl.ds(g * WIDTH, WIDTH)] = right
            left, right = load_pairs(pair_ref, slot, 0, tokens)
            target[pl.ds(row, tokens), pl.ds(width + g * WIDTH, WIDTH)] = left
            target[pl.ds(row, tokens), pl.ds(2 * width + g * WIDTH, WIDTH)] = right


def qkv_kernel(
    seqs, place_ref, entered_ref, entered_other, query_ref, query_other, pair_ref, pair_other,
    keep_a, send_a, keep_b, send_b, left_sc, right_sc, block_sc, sems,
):
    rows, width = entered_ref.shape
    hc = place_ref[1]
    both = ((entered_ref, query_ref, pair_ref), (entered_other, query_other, pair_other))
    for which, (left, query, pair) in enumerate(both):
        left_sc[:, pl.ds(which * rows, rows)] = left[...].T
        flat_rows(query, pair, right_sc, which * rows, seqs, rows // seqs, width)
    for hx in range(2):
        begin = pl.multiple_of(hx * 384 + hc * 192, 64)
        for j in range(3):
            value = dot(left_sc[pl.ds(begin, 192), :], right_sc[:, pl.ds(j * width, width)])
            for i in range(8):
                block_sc[hx * 8 + i, :, pl.ds(j * width, width)] = value[
                    i * 24 : (i + 1) * 24
                ].astype(bf16)
    half = 3 * width // 2
    copies = piece_copies(place_ref, block_sc, keep_a, send_a, sems, 0, pl.ds(0, half))
    copies += piece_copies(place_ref, block_sc, keep_b, send_b, sems, 1, pl.ds(half, half))
    for copy in copies:
        copy.wait()


def qkv_terms(here, seqs, *values):
    rows, width = values[0].shape
    side = jax.ShapeDtypeStruct((2, 4, 24, 3 * width // 2), bf16)
    return pl.pallas_call(
        partial(qkv_kernel, seqs),
        out_shape=(side,) * 4,
        in_specs=[SMEM] + [VMEM] * 6,
        out_specs=(ANY,) * 4,
        scratch_shapes=[
            pltpu.VMEM((width, 2 * rows), bf16),
            pltpu.VMEM((2 * rows, 3 * width), bf16),
            pltpu.VMEM((16, 24, 3 * width), bf16),
            pltpu.SemaphoreType.DMA((2, 16)),
        ],
        compiler_params=pltpu.CompilerParams(vmem_limit_bytes=40 << 20),
    )(here, *values)


def leave_kernel(
    query_ref, pair_ref, x_ref, hidden_ref, mod_ref, gains_ref, weight_ref, middle_ref,
    grad_ref, small_ref, flat_ref,
):
    seqs, tokens, width = x_ref.shape
    devices = small_ref.shape[0]
    flat_rows(query_ref, pair_ref, flat_ref, 0, seqs, tokens, width)
    grad_entered = None
    for which in range(3):
        columns = pl.ds(which * width, width)
        term = dot_nt(flat_ref[:, columns], weight_ref[:, columns])
        grad_entered = term if grad_entered is None else grad_entered + term
    gain_sum = None
    sums = []
    for s in range(seqs):
        normed, inverse = normalize(x_ref[s].astype(f32))
        rows = slice(s * tokens, (s + 1) * tokens)
        grad = grad_entered[rows]
        shift_sum = jnp.sum(grad, axis=0, keepdims=True)
        scale_sum = jnp.sum(grad * (normed * gains_ref[0:1]), axis=0, keepdims=True)
        grad_scaled = grad * (1.0 + mod_ref[s : s + 1, pl.ds(width, width)])
        term = jnp.sum(grad_scaled * normed, axis=0, keepdims=True)
        gain_sum = term if gain_sum is None else gain_sum + term
        grad_ref[s] = hidden_ref[rows] + norm_back(grad_scaled * gains_ref[0:1], normed, inverse)
        later = [middle_ref[i + s : i + s + 1] for i in (0, 2, 4, 6)]
        sums.append(jnp.concatenate([shift_sum, scale_sum, *later], axis=1))
    up_bias = jnp.concatenate([middle_ref[i : i + 1] for i in range(10, 14)], axis=1)
    fields = [*sums, gain_sum, middle_ref[8:9], up_bias, middle_ref[9:10]]
    error = jnp.sum(middle_ref[14:15], axis=1, keepdims=True)
    small_ref[...] = jnp.zeros(small_ref.shape, f32)
    begin = 0
    for field in fields:
        size = field.shape[1] // devices
        for i in range(devices):
            small_ref[i : i + 1, pl.ds(begin, size)] = field[:, i * size : (i + 1) * size]
        begin += size
    small_ref[:, pl.ds(begin, 1)] = jnp.broadcast_to(error, (devices, 1))


def leave(query, pair, inputs, grad_hidden, modulation, gains, weight, sums, devices):
    seqs, tokens, width = inputs.shape
    return pl.pallas_call(
        leave_kernel,
        out_shape=(
            jax.ShapeDtypeStruct((seqs, tokens, width), f32),
            jax.ShapeDtypeStruct((devices, 512), f32),
            jax.ShapeDtypeStruct((seqs * tokens, 3 * width), bf16),
        ),
        in_specs=[VMEM] * 8,
        out_specs=(VMEM,) * 3,
        compiler_params=pltpu.CompilerParams(vmem_limit_bytes=40 << 20),
    )(query, pair, inputs, grad_hidden, modulation, gains, weight, sums)


def unpack_kernel(
    parts, sizes, factor, place_ref, every_ref, valid_ref,
    mod_ref, gains_ref, up_ref, key_docs_ref, query_docs_ref, masks_ref,
):
    devices = every_ref.shape[0]
    seqs, tokens = valid_ref.shape
    size_mod, size_gain, size_up = sizes
    mod_ref[...] = jnp.zeros(mod_ref.shape, f32)
    gains_ref[...] = jnp.zeros(gains_ref.shape, f32)
    up_ref[...] = jnp.zeros(up_ref.shape, f32)
    begin = 0
    targets = [(mod_ref, s, size_mod) for s in range(seqs)]
    targets += [(gains_ref, 0, size_gain), (gains_ref, 1, size_gain)]
    targets += [(up_ref, 0, size_up), (gains_ref, 2, size_gain)]
    for target, row, size in targets:
        for i in range(devices):
            target[row : row + 1, pl.ds(i * size, size)] = every_ref[
                i : i + 1, pl.ds(begin, size)
            ]
        begin += size
    hx, hc, sz, sy, rb = (place_ref[i] for i in range(5))
    second = sz * 2 + sy >= GROUPS
    row = 0
    for core in range(2):
        for across in range(2):
            for part in range(parts):
                block = ((hx ^ across) * 2 + (hc ^ core)) * parts + part
                lines = every_ref[pl.ds(pl.multiple_of(block * 8, 8), 8), pl.ds(begin, 2 * tokens)]
                lines = jnp.where(second, lines[:, tokens:], lines[:, :tokens])
                turned = lines.T
                for spot in range(8):
                    key_docs_ref[pl.ds(row, tokens), :] = turned[:, spot : spot + 1]
                    row += tokens
    lines = every_ref[
        pl.ds(pl.multiple_of(((hx * 2 + hc) * parts + rb) * 8, 8), 8), pl.ds(begin, 2 * tokens)
    ]
    lines = jnp.where(second, lines[:, tokens:], lines[:, :tokens])
    for spot in range(8):
        query_docs_ref[:, pl.ds(spot * tokens, tokens)] = lines[spot : spot + 1]
    begin += 2 * tokens
    count = jnp.sum(every_ref[:, pl.ds(begin, 1)], axis=0, keepdims=True)
    gains_ref[3:4, pl.ds(0, 1)] = count
    turned = valid_ref[...].astype(f32).T
    for s in range(seqs):
        rows = pl.ds(s * tokens, tokens)
        masks_ref[rows, pl.ds(0, 1)] = turned[:, s : s + 1]
        masks_ref[rows, pl.ds(1, 1)] = turned[:, s : s + 1] * (factor / count)


def unpack(here, every, valid_mask, width, units, parts, length):
    seqs, tokens = valid_mask.shape
    devices = every.shape[0]
    sizes = (6 * width // devices, width // devices, units // devices)
    return pl.pallas_call(
        partial(unpack_kernel, parts, sizes, float(seqs * length)),
        out_shape=(
            jax.ShapeDtypeStruct((8, 6 * width), f32),
            jax.ShapeDtypeStruct((8, width), f32),
            jax.ShapeDtypeStruct((8, units), f32),
            jax.ShapeDtypeStruct((4 * parts * 8 * tokens, 1), f32),
            jax.ShapeDtypeStruct((1, 8 * tokens), f32),
            jax.ShapeDtypeStruct((seqs * tokens, 2), f32),
        ),
        in_specs=[SMEM, VMEM, VMEM],
        out_specs=(VMEM,) * 6,
        compiler_params=pltpu.CompilerParams(vmem_limit_bytes=40 << 20),
    )(here, every, valid_mask)


def block_kernel(out_ref, up_ref, down_ref, later_ref):
    width = out_ref.shape[1]
    later_ref[0] = out_ref[...]
    for j in range(4):
        later_ref[1 + j] = up_ref[:, pl.ds(j * width, width)]
        later_ref[5 + j] = down_ref[pl.ds(j * 24, 24), :]


def block(out_weight, up_weight, down_weight):
    width = out_weight.shape[1]
    return pl.pallas_call(
        block_kernel,
        out_shape=jax.ShapeDtypeStruct((9, 24, width), bf16),
        in_specs=[VMEM] * 3,
        out_specs=VMEM,
    )(out_weight, up_weight, down_weight)


def exchange(rows):
    return lax.all_to_all(rows, SPOT, 0, 0, tiled=True)


def on_device(
    inputs,
    time_embed,
    segments,
    valid_mask,
    teacher,
    ada_weight,
    ada_bias,
    gain_attn,
    qkv_weight,
    out_weight,
    gain_mlp,
    up_weight,
    up_bias,
    down_weight,
    down_bias,
):
    seqs, tokens, width = inputs.shape
    units = up_weight.shape[1]
    parts = lax.axis_size("rb")
    devices = 32 * parts
    length = tokens * devices
    queries = 8 * tokens
    here = place()

    own_modulation = jnp.dot(
        time_embed, ada_weight.astype(f32), precision=precise
    ) + ada_bias.astype(f32)
    fields = [
        own_modulation.reshape(-1),
        gain_attn.astype(f32),
        gain_mlp.astype(f32),
        up_bias.astype(f32),
        down_bias.astype(f32),
        segments.astype(f32).reshape(-1),
        jnp.sum(valid_mask.astype(f32)).reshape(1),
    ]
    packed = jnp.concatenate(fields)
    packed = jnp.pad(packed, (0, -packed.shape[0] % 128))
    every = lax.all_to_all(
        jnp.broadcast_to(packed, (devices, packed.shape[0])), EVERY, 0, 0, tiled=True
    )
    if parts > 1:
        full_qkv, *later = (
            lax.all_gather(w, EVERY, axis=0, tiled=True)
            for w in (qkv_weight, out_weight, up_weight, down_weight)
        )
    else:
        later = [
            lax.all_gather(block(out_weight, up_weight, down_weight), EVERY, axis=0, tiled=False)
        ]
        full_qkv, every = gather_rows(here, qkv_weight, every)
    modulation, gains, full_up_bias, key_docs, query_docs, masks = unpack(
        here, every, valid_mask, width, units, parts, length
    )
    count_all = gains[3, 0]

    entered, pair, query = enter(inputs, modulation, gains, full_qkv)
    pair = exchange(pair).reshape(queries, 2 * WIDTH)
    query = exchange(query)
    if parts > 1:
        pair = lax.all_gather(pair, "rb", axis=0, tiled=True)
    pair_x = swap(pair, "hx")
    pairs = (pair, pair_x, swap(pair, "hc"), swap(pair_x, "hc"))
    attended, turned, total = attend(query, pairs, key_docs, query_docs)

    final, grad_hidden, grad_leaving, pack, sums = middle(
        exchange(attended), inputs, teacher, masks, modulation, gains, full_up_bias, later
    )
    grad_came = exchange(grad_leaving)
    if parts == 1:
        terms = weight_terms(here, pack, swap(pack, "hc"), width)
        grad_came, terms = lax.optimization_barrier((grad_came, terms))
        first_a = reduce_first(terms[0], terms[1], ORDERS[0])
        first_b = reduce_first(terms[2], terms[3], ORDERS[1])

    grad_query, keep, send = attend_back(
        query, grad_came, pairs, key_docs, query_docs, turned, total
    )
    home_query = exchange(grad_query)
    grad_pair = keep + swap(send, "hc").astype(f32)
    middle_row = grad_pair.shape[0] // 2
    grad_pair = grad_pair[:middle_row] + swap(grad_pair[middle_row:].astype(bf16), "hx").astype(f32)
    if parts > 1:
        grad_pair = lax.psum_scatter(grad_pair, "rb", scatter_dimension=0, tiled=True)
    grad_pair = grad_pair.astype(bf16).reshape(8, tokens, 2 * WIDTH)
    if parts == 1:
        grad_pair, first_a, first_b = lax.optimization_barrier((grad_pair, first_a, first_b))
        second_a = reduce_second(first_a, ORDERS[0])
        second_b = reduce_second(first_b, ORDERS[1])
    home_pair = exchange(grad_pair)
    grad_input, small, flat = leave(
        home_query, home_pair, inputs, grad_hidden, modulation, gains, full_qkv, sums, devices
    )
    if parts == 1:
        others = swap(entered, "hc"), swap(home_query, "hc"), swap(home_pair, "hc")
        others, second_a, second_b = lax.optimization_barrier((others, second_a, second_b))
        terms = qkv_terms(
            here, seqs, entered, others[0], home_query, others[1], home_pair, others[2]
        )
        shard_qkv = jnp.concatenate(
            [
                reduce_third(reduce_second(reduce_first(keep, send, order), order))
                for keep, send, order in zip(terms[::2], terms[1::2], ORDERS)
            ],
            axis=1,
        )
        side_a = reduce_third(second_a)
        side_b = reduce_third(second_b)
        shard_out = side_a[0]
        shard_up = side_a[1:].transpose(1, 0, 2).reshape(24, units)
        shard_down = side_b.reshape(96, width)
    else:
        base = 2 * width + units
        ends = (base + width, base + width + units)
        shard_qkv, shard_out, shard_up, shard_down = (
            lax.psum_scatter(
                jnp.einsum("tk,tn->kn", left, right, preferred_element_type=f32),
                EVERY,
                scatter_dimension=0,
                tiled=True,
            )
            for left, right in (
                (entered, flat),
                (pack[:, :width], pack[:, base : ends[0]]),
                (pack[:, width : 2 * width], pack[:, ends[0] : ends[1]]),
                (pack[:, 2 * width : base], pack[:, ends[1] :]),
            )
        )
    added = jnp.sum(lax.all_to_all(small, EVERY, 0, 0, tiled=True), axis=0)
    owned = []
    begin = 0
    sizes = [6 * width // devices * seqs] + [size // devices for size in (width, width, units, width)]
    for size in sizes + [1]:
        owned.append(added[begin : begin + size])
        begin += size
    own_grad = owned[0].reshape(seqs, -1)
    grad_ada_weight = jnp.sum(time_embed[:, :, None] * own_grad[:, None, :], axis=0)
    loss_value = owned[5][0] / (count_all * width)
    return (
        final,
        loss_value,
        grad_input,
        grad_ada_weight,
        jnp.sum(own_grad, axis=0),
        owned[1],
        shard_qkv,
        shard_out,
        owned[2],
        shard_up,
        owned[3],
        shard_down,
        owned[4],
    )


def solution(mesh):
    blocks = mesh.shape["blk"]
    fine = Mesh(mesh.devices.reshape(2, 2, blocks // 8, 4, 2), EVERY)
    tokens = ("rb", "sz", "sy", "hx", "hc")
    return jax.shard_map(
        on_device,
        mesh=fine,
        in_specs=(
            P(None, tokens, None),
            P(),
            P(None, tokens),
            P(None, tokens),
            P(None, tokens, None),
            P(None, EVERY),
            P(EVERY),
            P(EVERY),
            P(EVERY, None),
            P(EVERY, None),
            P(EVERY),
            P(EVERY, None),
            P(EVERY),
            P(EVERY, None),
            P(EVERY),
        ),
        out_specs=(
            P(None, tokens, None),
            P(),
            P(None, tokens, None),
            P(None, EVERY),
            P(EVERY),
            P(EVERY),
            P(EVERY, None),
            P(EVERY, None),
            P(EVERY),
            P(EVERY, None),
            P(EVERY),
            P(EVERY, None),
            P(EVERY),
        ),
        check_vma=False,
    )
```

```python
from functools import partial

import jax
import jax.numpy as jnp
from jax import lax
from jax.experimental import pallas as pl
from jax.experimental.pallas import tpu as pltpu
from jax.sharding import Mesh, PartitionSpec as P

HEADS = 12
HEAD_DIM = 64
GROUPS = 4
WIDTH = HEADS // GROUPS * HEAD_DIM
EVERY = ("hx", "hc", "rb", "sz", "sy")
SPOT = ("sz", "sy")
bf16 = jnp.bfloat16
f32 = jnp.float32
precise = lax.Precision.HIGHEST


def normalize(hidden):
    average = jnp.mean(hidden, axis=-1, keepdims=True)
    centred = hidden - average
    variance = jnp.mean(centred * centred, axis=-1, keepdims=True)
    inverse = lax.rsqrt(variance + 1e-05)
    return (centred * inverse, inverse)


def dot(left, right):
    return jnp.dot(left, right, preferred_element_type=f32)


def dot_nt(left, right):
    return lax.dot_general(left, right, (((1,), (1,)), ((), ())), preferred_element_type=f32)


def norm_back(upstream, normed, inverse):
    first_mean = jnp.mean(upstream, axis=-1, keepdims=True)
    second_mean = jnp.mean(upstream * normed, axis=-1, keepdims=True)
    return inverse * (upstream - first_mean - normed * second_mean)


def swap(value, axis):
    return lax.ppermute(value, axis, [(0, 1), (1, 0)])


def turn(value, axis, step):
    size = lax.axis_size(axis)
    return lax.ppermute(value, axis, [(i, (i - step) % size) for i in range(size)])


def place():
    return jnp.stack([lax.axis_index(name) for name in ("hx", "hc", "sz", "sy", "rb")]).astype(
        jnp.int32
    )


ANY = pl.BlockSpec(memory_space=pl.ANY)
SMEM = pl.BlockSpec(memory_space=pltpu.SMEM)
VMEM = pl.BlockSpec(memory_space=pltpu.VMEM)


def hbm(value):
    return pltpu.with_memory_space_constraint(value, pltpu.HBM)


def whole_spec(shape):
    return pl.BlockSpec(shape, lambda *_: (0,) * len(shape))


def single(kernel, outs, values, scratch=(), limit=40, place=None, raw=0, raw_out=False):
    blocked = len(values) - raw
    specs = [whole_spec(v.shape) for v in values[:blocked]] + [ANY] * raw
    values = [hbm(v) for v in values]
    if place is not None:
        specs, values = [SMEM] + specs, [place] + values
    return pl.pallas_call(
        kernel,
        grid=(1,),
        out_shape=tuple(jax.ShapeDtypeStruct(*o) for o in outs),
        in_specs=specs,
        out_specs=tuple(ANY if raw_out else whole_spec(o[0]) for o in outs),
        scratch_shapes=list(scratch),
        compiler_params=pltpu.CompilerParams(vmem_limit_bytes=limit << 20),
    )(*values)


def run_all(copies):
    for copy in copies:
        copy.start()
    for copy in copies:
        copy.wait()


def join_kernel(place_ref, left, left_other, right, right_other, whole, sems):
    hx, hc, sz, sy = (place_ref[i] for i in range(4))
    half = left.shape[-1]
    copies = []
    for side, cores in enumerate(((left, left_other), (right, right_other))):
        for core, pieces in enumerate(cores):
            for second in range(2):
                for first in range(2):
                    for deep in range(4):
                        across, down = (first, second) if side == 0 else (second, first)
                        block = (hx ^ across) * 2 + (hc ^ core)
                        spot = (block * 4 + lax.rem(sz + deep, 4)) * 2 + (sy ^ down)
                        copies.append(
                            pltpu.make_async_copy(
                                pieces.at[second, first, deep],
                                whole.at[spot, :, pl.ds(side * half, half)],
                                sems.at[len(copies)],
                            )
                        )
    run_all(copies)


def join(here, *sides):
    rows, half = sides[0].shape[-2:]
    (whole,) = single(
        join_kernel,
        [((32, rows, half * 2), bf16)],
        sides,
        [pltpu.SemaphoreType.DMA((64,))],
        place=here,
        raw=4,
    )
    return whole.reshape(rows * 32, half * 2)


def gather_rows(here, shard, every, use):
    half = shard.shape[1] // 2
    sides = []
    deep = jnp.stack([shard] + [turn(shard, "sz", k) for k in (1, 2, 3)])
    orders = (("hx", "sy"), ("sy", "hx"))
    levels = [deep[:, :, :half], deep[:, :, half:]]
    levels = [jnp.stack([v, swap(v, order[0])]) for v, order in zip(levels, orders)]
    levels, every = lax.optimization_barrier((levels, every))
    levels = [jnp.stack([v, swap(v, order[1])]) for v, order in zip(levels, orders)]
    used = use(every)
    levels, used = lax.optimization_barrier((levels, used))
    for level in levels:
        sides += [level, swap(level, "hc")]
    return join(here, *sides), used


def piece_copies(place_ref, blocks, keep, send, sems, side, columns):
    hx, sz, sy = place_ref[0], place_ref[2], place_ref[3]
    copies = []
    for second in range(2):
        for first in range(2):
            for deep in range(4):
                across, down = (first, second) if side == 0 else (second, first)
                spot = ((hx ^ across) * 4 + lax.rem(sz + deep, 4)) * 2 + (sy ^ down)
                source = blocks.at[(spot,) + (slice(None),) * (len(blocks.shape) - 2) + (columns,)]
                target = (keep, send)[second].at[first, deep]
                copies.append(pltpu.make_async_copy(source, target, sems.at[len(copies)]))
    for copy in copies:
        copy.start()
    return copies


ORDERS = (("sy", "hx"), ("hx", "sy"))
COLUMN_GROUPS = ((1, 0), (2, 0), (1, 1), (2, 1))


def second_send(keep, recv):
    return (keep[1].astype(f32) + recv[1].astype(f32)).astype(bf16)


def second_total(keep, recv, recv_second):
    return keep[0].astype(f32) + recv[0].astype(f32) + recv_second.astype(f32)


def third_recvs(total):
    return [turn(total[k].astype(bf16), "sz", -k) for k in (1, 2, 3)]


def third_total(total, recvs):
    result = total[0]
    for recv in recvs:
        result = result + recv.astype(f32)
    return result


def enter_kernel(x_ref, mod_ref, gains_ref, weight_ref, entered_ref, pair_ref, query_ref):
    seqs, tokens, width = x_ref.shape
    half = tokens // 2
    for s in range(seqs):
        normed = normalize(x_ref[s].astype(f32))[0]
        shift, scale = (mod_ref[s : s + 1, pl.ds(i * width, width)] for i in (0, 1))
        value = normed * gains_ref[0:1] * (1.0 + scale) + shift
        entered_ref[pl.ds(s * tokens, tokens), :] = value.astype(bf16)
    entered = entered_ref[...]
    for which in (1, 2, 0):
        triple = dot(entered, weight_ref[:, pl.ds(which * width, width)]).astype(bf16)
        for s in range(seqs):
            for g in range(GROUPS):
                rows = triple[s * tokens : (s + 1) * tokens, g * WIDTH : (g + 1) * WIDTH]
                slot = s * GROUPS + g
                if which == 0:
                    query_ref[slot, :, pl.ds(0, WIDTH)] = rows[:half]
                    query_ref[slot, :, pl.ds(WIDTH, WIDTH)] = rows[half:]
                else:
                    pair_ref[slot, :, pl.ds((which - 1) * WIDTH, WIDTH)] = rows


def enter(inputs, modulation, gains, weight):
    seqs, tokens, width = inputs.shape
    return single(
        enter_kernel,
        [
            ((seqs * tokens, width), bf16),
            ((8, tokens, 2 * WIDTH), bf16),
            ((8, tokens // 2, 2 * WIDTH), bf16),
        ],
        [inputs, modulation, gains, weight],
    )


def head_lanes(rows, head):
    lane = lax.broadcasted_iota(jnp.int32, (rows, WIDTH), 1)
    return (lane >= head * HEAD_DIM) & (lane < (head + 1) * HEAD_DIM)


def load_pairs(pair_ref, slot, first_row, half):
    value = pair_ref[slot, pl.ds(first_row, half), :]
    return value[:, :WIDTH], value[:, WIDTH:]


def spread_heads(pair_ref, first_row, half, target, factor):
    heads = target.shape[0]
    zero = jnp.zeros((half, WIDTH), bf16)
    for slot in range(8):
        for part, rows in enumerate(load_pairs(pair_ref, slot, first_row, half)):
            rows = (rows.astype(f32) * factor).astype(bf16)
            for h in range(heads):
                target[h, pl.ds((slot * 2 + part) * half, half), :] = jnp.where(
                    head_lanes(half, h), rows, zero
                )


def fetch(step, pair_refs, starts, pair_sc):
    for ref, (begin, end) in zip(pair_refs, starts):
        @pl.when((step >= begin) & (step < end))
        def take(ref=ref):
            pair_sc[...] = ref[...]


def forward_kernel(
    starts, came_ref, first_ref, second_ref, third_ref, fourth_ref, key_docs_ref, query_docs_ref,
    out_ref, turned_ref, total_ref, query_sc, pair_sc, top_sc, sum_sc, acc_sc,
):
    step = pl.program_id(0)
    heads, queries = query_sc.shape[:2]
    half = out_ref.shape[1]

    @pl.when(step == 0)
    def start():
        spread_heads(came_ref, 0, half, query_sc, HEAD_DIM ** (-0.5))
        top_sc[...] = jnp.full(top_sc.shape, -1e30, f32)
        sum_sc[...] = jnp.zeros(sum_sc.shape, f32)
        acc_sc[...] = jnp.zeros(acc_sc.shape, f32)

    fetch(step, (first_ref, second_ref, third_ref, fourth_ref), starts, pair_sc)
    key_part = pair_sc[:, :WIDTH]
    value_turned = pair_sc[:, WIDTH:].T
    allowed = key_docs_ref[...] == query_docs_ref[...]
    for h in range(heads):
        rows = pl.ds(h * HEAD_DIM, HEAD_DIM)
        scores = jnp.where(allowed, dot_nt(key_part, query_sc[h]), -1e30)
        old = top_sc[h : h + 1]
        new = jnp.maximum(old, jnp.max(scores, axis=0, keepdims=True))
        exponent = jnp.exp(scores - new)
        fade = jnp.exp(old - new)
        top_sc[h : h + 1] = new
        sum_sc[h : h + 1] = sum_sc[h : h + 1] * fade + jnp.sum(exponent, axis=0, keepdims=True)
        acc_sc[rows] = acc_sc[rows] * fade + dot(
            value_turned[h * HEAD_DIM : (h + 1) * HEAD_DIM], exponent.astype(bf16)
        )

    @pl.when(step == pl.num_programs(0) - 1)
    def finish():
        total_ref[...] = jnp.zeros(total_ref.shape, f32)
        for h in range(heads):
            rows = pl.ds(h * HEAD_DIM, HEAD_DIM)
            turned_ref[rows] = acc_sc[rows] / sum_sc[h : h + 1]
            total_ref[h : h + 1] = top_sc[h : h + 1] + jnp.log(sum_sc[h : h + 1])
        whole = turned_ref[...].T.astype(bf16)
        for slot in range(8):
            for part in range(2):
                begin = (slot * 2 + part) * half
                out_ref[slot, :, pl.ds(part * WIDTH, WIDTH)] = whole[begin : begin + half]


def pair_specs(pairs, chunk):
    specs, starts, begin = [], [], 0
    for pair in pairs:
        count = pair.shape[0] // chunk
        specs.append(
            pl.BlockSpec(
                (chunk, 2 * WIDTH),
                lambda i, begin=begin, count=count: (jnp.clip(i - begin, 0, count - 1), 0),
            )
        )
        starts.append((begin, begin + count))
        begin += count
    return specs, starts, begin


def attend(came, pairs, key_docs, query_docs):
    slots, half, columns = came.shape
    queries = slots * 2 * half
    heads = WIDTH // HEAD_DIM
    chunk = 512
    specs, starts, steps = pair_specs(pairs, chunk)
    outs = (
        jax.ShapeDtypeStruct((slots, half, columns), bf16),
        jax.ShapeDtypeStruct((WIDTH, queries), f32),
        jax.ShapeDtypeStruct((8, queries), f32),
    )
    return pl.pallas_call(
        partial(forward_kernel, starts),
        grid=(steps,),
        out_shape=outs,
        in_specs=[
            whole_spec(came.shape),
            *specs,
            pl.BlockSpec((chunk, 1), lambda i: (i, 0)),
            whole_spec(query_docs.shape),
        ],
        out_specs=tuple(whole_spec(o.shape) for o in outs),
        scratch_shapes=[
            pltpu.VMEM((heads, queries, WIDTH), bf16),
            pltpu.VMEM((chunk, 2 * WIDTH), bf16),
            pltpu.VMEM((8, queries), f32),
            pltpu.VMEM((8, queries), f32),
            pltpu.VMEM((WIDTH, queries), f32),
        ],
        compiler_params=pltpu.CompilerParams(vmem_limit_bytes=48 << 20),
    )(*map(hbm, (came, *pairs, key_docs, query_docs)))


def backward_kernel(
    starts, came_ref, grad_ref, first_ref, second_ref, third_ref, fourth_ref, key_docs_ref, query_docs_ref,
    turned_ref, total_ref, query_out, keep_ref, keep_other, send_ref,
    query_sc, grad_sc, pair_sc, delta_sc, acc_sc,
):
    step = pl.program_id(0)
    heads, queries = query_sc.shape[:2]
    half = query_out.shape[1]

    @pl.when(step == 0)
    def start():
        spread_heads(came_ref, 0, half, query_sc, HEAD_DIM ** (-0.5))
        spread_heads(grad_ref, 0, half, grad_sc, 1.0)
        acc_sc[...] = jnp.zeros(acc_sc.shape, f32)
        for h in range(heads):
            rows = slice(h * HEAD_DIM, (h + 1) * HEAD_DIM)
            turned = grad_sc[h].astype(f32).T
            delta_sc[h : h + 1] = jnp.sum(turned[rows] * turned_ref[rows], axis=0, keepdims=True)

    fetch(step, (first_ref, second_ref, third_ref, fourth_ref), starts, pair_sc)
    key_part = pair_sc[:, :WIDTH]
    value_part = pair_sc[:, WIDTH:]
    key_turned = key_part.T
    allowed = key_docs_ref[...] == query_docs_ref[...]
    grad_key = grad_value = None
    for h in range(heads):
        rows = pl.ds(h * HEAD_DIM, HEAD_DIM)
        query, grad = query_sc[h], grad_sc[h]
        scores = jnp.where(allowed, dot_nt(key_part, query), -1e30)
        probabilities = jnp.exp(scores - total_ref[h : h + 1])
        slope = dot_nt(value_part, grad) - delta_sc[h : h + 1]
        grad_scores = (probabilities * slope).astype(bf16)
        value_term = dot(probabilities.astype(bf16), grad)
        key_term = dot(grad_scores, query)
        grad_value = value_term if grad_value is None else grad_value + value_term
        grad_key = key_term if grad_key is None else grad_key + key_term
        acc_sc[rows] = acc_sc[rows] + dot(
            key_turned[h * HEAD_DIM : (h + 1) * HEAD_DIM], grad_scores
        )
    quarter = pl.num_programs(0) // 4
    middle = 2 * quarter

    for number, ref in enumerate((keep_ref, keep_other)):
        @pl.when((step >= number * quarter) & (step < (number + 1) * quarter))
        def mine(ref=ref):
            ref[:, pl.ds(0, WIDTH)] = grad_key
            ref[:, pl.ds(WIDTH, WIDTH)] = grad_value

    @pl.when(step >= middle)
    def theirs():
        send_ref[:, pl.ds(0, WIDTH)] = grad_key.astype(bf16)
        send_ref[:, pl.ds(WIDTH, WIDTH)] = grad_value.astype(bf16)

    @pl.when(step == pl.num_programs(0) - 1)
    def finish():
        whole = (acc_sc[...] * HEAD_DIM ** (-0.5)).T.astype(bf16)
        for slot in range(8):
            for part in range(2):
                begin = (slot * 2 + part) * half
                query_out[slot, :, pl.ds(part * WIDTH, WIDTH)] = whole[begin : begin + half]


def attend_back(came, grad, pairs, key_docs, query_docs, turned, total):
    slots, half, columns = came.shape
    queries = slots * 2 * half
    heads = WIDTH // HEAD_DIM
    chunk = 512
    specs, starts, steps = pair_specs(pairs, chunk)
    quarter = steps // 4
    middle = 2 * quarter
    return pl.pallas_call(
        partial(backward_kernel, starts),
        grid=(steps,),
        out_shape=(
            jax.ShapeDtypeStruct((slots, half, columns), bf16),
            jax.ShapeDtypeStruct((quarter * chunk, columns), f32),
            jax.ShapeDtypeStruct((quarter * chunk, columns), f32),
            jax.ShapeDtypeStruct((middle * chunk, columns), bf16),
        ),
        in_specs=[
            whole_spec(came.shape),
            whole_spec(grad.shape),
            *specs,
            pl.BlockSpec((chunk, 1), lambda i: (i, 0)),
            whole_spec(query_docs.shape),
            whole_spec(turned.shape),
            whole_spec(total.shape),
        ],
        out_specs=(
            whole_spec((slots, half, columns)),
            pl.BlockSpec((chunk, columns), lambda i: (jnp.minimum(i, quarter - 1), 0)),
            pl.BlockSpec((chunk, columns), lambda i: (jnp.clip(i - quarter, 0, quarter - 1), 0)),
            pl.BlockSpec((chunk, columns), lambda i: (jnp.maximum(i - middle, 0), 0)),
        ),
        scratch_shapes=[
            pltpu.VMEM((heads, queries, WIDTH), bf16),
            pltpu.VMEM((heads, queries, WIDTH), bf16),
            pltpu.VMEM((chunk, 2 * WIDTH), bf16),
            pltpu.VMEM((8, queries), f32),
            pltpu.VMEM((WIDTH, queries), f32),
        ],
        compiler_params=pltpu.CompilerParams(vmem_limit_bytes=48 << 20),
    )(*map(hbm, (came, grad, *pairs, key_docs, query_docs, turned, total)))


def middle_kernel(
    gathered, came_ref, x_ref, teacher_ref, mask_ref, mod_ref, gains_ref, up_bias_ref, *refs
):
    if gathered:
        later_hbm, *refs = refs
    else:
        out_hbm, up_hbm, down_hbm, *refs = refs
    final_ref, hidden_ref, leave_ref, pack_ref, sums_ref, *refs = refs
    out_sc, up_sc, down_sc, slope_sc, *refs = refs
    if gathered:
        block_sc, sems = refs
    else:
        (sems,) = refs

    seqs, tokens, width = x_ref.shape
    units = up_sc.shape[1]
    rows = seqs * tokens
    half = tokens // 2
    if gathered:
        copies = [
            pltpu.make_async_copy(later_hbm.at[:, j], block_sc.at[j], sems.at[j]) for j in range(9)
        ]
    else:
        copies = [
            pltpu.make_async_copy(source, target, sems.at[i])
            for i, (source, target) in enumerate(
                ((out_hbm, out_sc), (up_hbm, up_sc), (down_hbm, down_sc))
            )
        ]
    for copy in copies:
        copy.start()

    def settle(j):
        if not gathered:
            if j < 2 or j == 5:
                copies[(0, 1, None, None, None, 2)[j]].wait()
            return
        copies[j].wait()
        for i in range(32):
            value = block_sc[j, i]
            if j == 0:
                out_sc[pl.ds(i * 24, 24), :] = value
            elif j < 5:
                up_sc[pl.ds(i * 24, 24), pl.ds((j - 1) * width, width)] = value
            else:
                down_sc[pl.ds(i * 96 + (j - 5) * 24, 24), :] = value

    def wide(index):
        return jnp.concatenate(
            [
                jnp.broadcast_to(
                    mod_ref[s : s + 1, pl.ds(index * width, width)], (tokens, width)
                )
                for s in range(seqs)
            ]
        )

    def add_rows(first, value):
        for s in range(seqs):
            sums_ref[first + s : first + s + 1] = jnp.sum(
                value[s * tokens : (s + 1) * tokens], axis=0, keepdims=True
            )

    for s in range(seqs):
        for g in range(GROUPS):
            left, right = load_pairs(came_ref, s * GROUPS + g, 0, half)
            columns = pl.ds(g * WIDTH, WIDTH)
            pack_ref[pl.ds(s * tokens, half), columns] = left
            pack_ref[pl.ds(s * tokens + half, half), columns] = right
    mixed = pack_ref[:, pl.ds(0, width)]
    residual = jnp.concatenate([x_ref[s].astype(f32) for s in range(seqs)])
    settle(0)
    branch = dot(mixed, out_sc[...])
    hidden = residual + wide(2) * branch
    normed, inverse = normalize(hidden)
    scaled = normed * gains_ref[1:2]
    moved = (scaled * (1.0 + wide(4)) + wide(3)).astype(bf16)
    pack_ref[:, pl.ds(width, width)] = moved
    for j in range(1, 9):
        settle(j)
    lower = None
    for f in range(units // width):
        columns = pl.ds(f * width, width)
        u = dot(moved, up_sc[:, columns]) + up_bias_ref[0:1, columns]
        square = u * u
        t = jnp.tanh(0.7978845608028654 * (u + 0.044715 * u * square))
        active = (0.5 * u * (1.0 + t)).astype(bf16)
        slope_sc[:, columns] = 0.5 * (1.0 + t) + 0.5 * u * (1.0 - t * t) * 0.7978845608028654 * (
            1.0 + 0.134145 * square
        )
        pack_ref[:, pl.ds(2 * width + f * width, width)] = active
        term = dot(active, down_sc[columns, :])
        lower = term if lower is None else lower + term
    lower = lower + gains_ref[2:3]
    gate = wide(5)
    final = hidden + gate * lower
    for s in range(seqs):
        final_ref[s] = final[s * tokens : (s + 1) * tokens].astype(bf16)
    teacher = jnp.concatenate([teacher_ref[s].astype(f32) for s in range(seqs)])
    mismatch = final - teacher
    sums_ref[14:15] = jnp.sum(
        mask_ref[:, 0:1] * mismatch * mismatch, axis=0, keepdims=True
    )
    sums_ref[15:16] = jnp.zeros((1, width), f32)
    grad_final = mask_ref[:, 1:2] * mismatch
    add_rows(6, grad_final * lower)
    grad_lower = (gate * grad_final).astype(bf16)
    base = 2 * width + units
    pack_ref[:, pl.ds(base + width + units, width)] = grad_lower
    sums_ref[9:10] = jnp.sum(grad_lower.astype(f32), axis=0, keepdims=True)
    grad_moved = None
    for f in range(units // width):
        columns = pl.ds(f * width, width)
        grad_active = dot_nt(grad_lower, down_sc[columns, :])
        grad_upper = (grad_active * slope_sc[:, columns]).astype(bf16)
        pack_ref[:, pl.ds(base + width + f * width, width)] = grad_upper
        sums_ref[10 + f : 11 + f] = jnp.sum(grad_upper.astype(f32), axis=0, keepdims=True)
        term = dot_nt(grad_upper, up_sc[:, columns])
        grad_moved = term if grad_moved is None else grad_moved + term
    add_rows(2, grad_moved)
    add_rows(4, grad_moved * scaled)
    grad_scaled = grad_moved * (1.0 + wide(4))
    sums_ref[8:9] = jnp.sum(grad_scaled * normed, axis=0, keepdims=True)
    grad_hidden = grad_final + norm_back(grad_scaled * gains_ref[1:2], normed, inverse)
    hidden_ref[...] = grad_hidden
    add_rows(0, grad_hidden * branch)
    grad_branch = (wide(2) * grad_hidden).astype(bf16)
    pack_ref[:, pl.ds(base, width)] = grad_branch
    grad_mixed = dot_nt(grad_branch, out_sc[...]).astype(bf16)
    for s in range(seqs):
        for g in range(GROUPS):
            piece = grad_mixed[s * tokens : (s + 1) * tokens, g * WIDTH : (g + 1) * WIDTH]
            leave_ref[s * GROUPS + g, :, pl.ds(0, WIDTH)] = piece[:half]
            leave_ref[s * GROUPS + g, :, pl.ds(WIDTH, WIDTH)] = piece[half:]


def middle(came, inputs, teacher, masks, modulation, gains, up_bias, later):
    seqs, tokens, width = inputs.shape
    units = up_bias.shape[1]
    rows = seqs * tokens
    gathered = len(later) == 1
    scratch = [
        pltpu.VMEM((width, width), bf16),
        pltpu.VMEM((width, units), bf16),
        pltpu.VMEM((units, width), bf16),
        pltpu.VMEM((rows, units), f32),
    ]
    if gathered:
        scratch.append(pltpu.VMEM((9, 32, 24, width), bf16))
    return single(
        partial(middle_kernel, gathered),
        [
            ((seqs, tokens, width), bf16),
            ((rows, width), f32),
            (came.shape, bf16),
            ((rows, 4 * width + 2 * units), bf16),
            ((16, width), f32),
        ],
        [came, inputs, teacher, masks, modulation, gains, up_bias, *later],
        scratch + [pltpu.SemaphoreType.DMA((9,))],
        limit=60,
        raw=len(later),
    )


def weights_kernel(
    place_ref, own_ref, other_ref, *refs
):
    *groups, left_sc, right_sc, block_sc, sems = refs
    rows, width = own_ref.shape[0], block_sc.shape[-1]
    units = 4 * width
    hc = place_ref[1]
    base = 2 * width + units
    for which, ref in enumerate((own_ref, other_ref)):
        left_sc[:, pl.ds(which * rows, rows)] = ref[:, pl.ds(0, base)].T
        right_sc[pl.ds(which * rows, rows), :] = ref[:, pl.ds(base, base)]
    for hx in range(2):
        begin = pl.multiple_of(hx * 384 + hc * 192, 64)
        for j in range(5):
            offset = 0 if j == 0 else width
            value = dot(left_sc[pl.ds(begin + offset, 192), :], right_sc[:, pl.ds(j * width, width)])
            for i in range(8):
                block_sc[hx * 8 + i, j] = value[i * 24 : (i + 1) * 24].astype(bf16)
        begin = pl.multiple_of(2 * width + hx * 1536 + hc * 768, 256)
        value = dot(left_sc[pl.ds(begin, 768), :], right_sc[:, pl.ds(width + units, width)])
        for i in range(8):
            for j in range(4):
                first = i * 96 + j * 24
                block_sc[hx * 8 + i, 5 + j] = value[first : first + 24].astype(bf16)
    copies = []
    begin = 0
    for number, (_, side) in enumerate(COLUMN_GROUPS):
        keep, send = groups[2 * number : 2 * number + 2]
        columns = pl.ds(begin, keep.shape[-1])
        copies += piece_copies(place_ref, block_sc, keep, send, sems.at[number], side, columns)
        begin += keep.shape[-1]
    for copy in copies:
        copy.wait()


def weight_terms(here, own, other, width):
    rows, total = own.shape
    return single(
        weights_kernel,
        [((2, 4, 9, 24, 128 * size), bf16) for size, _ in COLUMN_GROUPS for _ in range(2)],
        [own, other],
        [
            pltpu.VMEM((total // 2, 2 * rows), bf16),
            pltpu.VMEM((2 * rows, total // 2), bf16),
            pltpu.VMEM((16, 9, 24, width), bf16),
            pltpu.SemaphoreType.DMA((len(COLUMN_GROUPS), 16)),
        ],
        limit=56,
        place=here,
        raw_out=True,
    )


def flat_rows(home_ref, target, first_row, seqs, tokens, width):
    half = tokens // 2
    for s in range(seqs):
        for g in range(GROUPS):
            slot = s * GROUPS + g
            row = first_row + s * tokens
            left, right = load_pairs(home_ref, slot, tokens, half)
            target[pl.ds(row, half), pl.ds(g * WIDTH, WIDTH)] = left
            target[pl.ds(row + half, half), pl.ds(g * WIDTH, WIDTH)] = right
            left, right = load_pairs(home_ref, slot, 0, tokens)
            target[pl.ds(row, tokens), pl.ds(width + g * WIDTH, WIDTH)] = left
            target[pl.ds(row, tokens), pl.ds(2 * width + g * WIDTH, WIDTH)] = right


def qkv_kernel(
    seqs, place_ref, entered_ref, entered_other, home_ref, home_other,
    keep_a, send_a, keep_b, send_b, left_sc, right_sc, block_sc, sems,
):
    rows, width = entered_ref.shape
    hc = place_ref[1]
    for which, (left, home) in enumerate(((entered_ref, home_ref), (entered_other, home_other))):
        left_sc[:, pl.ds(which * rows, rows)] = left[...].T
        flat_rows(home, right_sc, which * rows, seqs, rows // seqs, width)
    for hx in range(2):
        begin = pl.multiple_of(hx * 384 + hc * 192, 64)
        for j in range(3):
            value = dot(left_sc[pl.ds(begin, 192), :], right_sc[:, pl.ds(j * width, width)])
            for i in range(8):
                block_sc[hx * 8 + i, :, pl.ds(j * width, width)] = value[
                    i * 24 : (i + 1) * 24
                ].astype(bf16)
    half = 3 * width // 2
    copies = piece_copies(place_ref, block_sc, keep_a, send_a, sems.at[0], 0, pl.ds(0, half))
    copies += piece_copies(place_ref, block_sc, keep_b, send_b, sems.at[1], 1, pl.ds(half, half))
    for copy in copies:
        copy.wait()


def qkv_terms(here, seqs, *values):
    rows, width = values[0].shape
    return single(
        partial(qkv_kernel, seqs),
        [((2, 4, 24, 3 * width // 2), bf16)] * 4,
        values,
        [
            pltpu.VMEM((width, 2 * rows), bf16),
            pltpu.VMEM((2 * rows, 3 * width), bf16),
            pltpu.VMEM((16, 24, 3 * width), bf16),
            pltpu.SemaphoreType.DMA((2, 16)),
        ],
        place=here,
        raw_out=True,
    )


def leave_kernel(
    home_ref, x_ref, hidden_ref, mod_ref, gains_ref, weight_ref, middle_ref,
    grad_ref, small_ref, flat_ref,
):
    seqs, tokens, width = x_ref.shape
    devices = small_ref.shape[0]
    flat_rows(home_ref, flat_ref, 0, seqs, tokens, width)
    grad_entered = None
    for which in range(3):
        columns = pl.ds(which * width, width)
        term = dot_nt(flat_ref[:, columns], weight_ref[:, columns])
        grad_entered = term if grad_entered is None else grad_entered + term
    gain_sum = None
    sums = []
    for s in range(seqs):
        normed, inverse = normalize(x_ref[s].astype(f32))
        rows = slice(s * tokens, (s + 1) * tokens)
        grad = grad_entered[rows]
        shift_sum = jnp.sum(grad, axis=0, keepdims=True)
        scale_sum = jnp.sum(grad * (normed * gains_ref[0:1]), axis=0, keepdims=True)
        grad_scaled = grad * (1.0 + mod_ref[s : s + 1, pl.ds(width, width)])
        term = jnp.sum(grad_scaled * normed, axis=0, keepdims=True)
        gain_sum = term if gain_sum is None else gain_sum + term
        grad_ref[s] = hidden_ref[rows] + norm_back(grad_scaled * gains_ref[0:1], normed, inverse)
        later = [middle_ref[i + s : i + s + 1] for i in (0, 2, 4, 6)]
        sums.append(jnp.concatenate([shift_sum, scale_sum, *later], axis=1))
    up_bias = jnp.concatenate([middle_ref[i : i + 1] for i in range(10, 14)], axis=1)
    fields = [*sums, gain_sum, middle_ref[8:9], up_bias, middle_ref[9:10]]
    error = jnp.sum(middle_ref[14:15], axis=1, keepdims=True)
    small_ref[...] = jnp.zeros(small_ref.shape, f32)
    begin = 0
    for field in fields:
        size = field.shape[1] // devices
        for i in range(devices):
            small_ref[i : i + 1, pl.ds(begin, size)] = field[:, i * size : (i + 1) * size]
        begin += size
    small_ref[:, pl.ds(begin, 1)] = jnp.broadcast_to(error, (devices, 1))


def leave(home, inputs, grad_hidden, modulation, gains, weight, sums, devices):
    seqs, tokens, width = inputs.shape
    return single(
        leave_kernel,
        [
            ((seqs, tokens, width), f32),
            ((devices, 512), f32),
            ((seqs * tokens, 3 * width), bf16),
        ],
        [home, inputs, grad_hidden, modulation, gains, weight, sums],
    )


def unpack_kernel(
    parts, sizes, factor, place_ref, every_ref, valid_ref,
    mod_ref, gains_ref, up_ref, key_docs_ref, query_docs_ref, masks_ref,
):
    devices = every_ref.shape[0]
    seqs, tokens = valid_ref.shape
    size_mod, size_gain, size_up = sizes
    mod_ref[...] = jnp.zeros(mod_ref.shape, f32)
    gains_ref[...] = jnp.zeros(gains_ref.shape, f32)
    up_ref[...] = jnp.zeros(up_ref.shape, f32)
    begin = 0
    targets = [(mod_ref, s, size_mod) for s in range(seqs)]
    targets += [(gains_ref, 0, size_gain), (gains_ref, 1, size_gain)]
    targets += [(up_ref, 0, size_up), (gains_ref, 2, size_gain)]
    for target, row, size in targets:
        for i in range(devices):
            target[row : row + 1, pl.ds(i * size, size)] = every_ref[
                i : i + 1, pl.ds(begin, size)
            ]
        begin += size
    hx, hc, sz, sy, rb = (place_ref[i] for i in range(5))
    second = sz * 2 + sy >= GROUPS
    row = 0
    for core in range(2):
        for across in range(2):
            for part in range(parts):
                block = ((hx ^ across) * 2 + (hc ^ core)) * parts + part
                lines = every_ref[pl.ds(pl.multiple_of(block * 8, 8), 8), pl.ds(begin, 2 * tokens)]
                lines = jnp.where(second, lines[:, tokens:], lines[:, :tokens])
                turned = lines.T
                for spot in range(8):
                    key_docs_ref[pl.ds(row, tokens), :] = turned[:, spot : spot + 1]
                    row += tokens
    lines = every_ref[
        pl.ds(pl.multiple_of(((hx * 2 + hc) * parts + rb) * 8, 8), 8), pl.ds(begin, 2 * tokens)
    ]
    lines = jnp.where(second, lines[:, tokens:], lines[:, :tokens])
    for spot in range(8):
        query_docs_ref[:, pl.ds(spot * tokens, tokens)] = lines[spot : spot + 1]
    begin += 2 * tokens
    count = jnp.sum(every_ref[:, pl.ds(begin, 1)], axis=0, keepdims=True)
    gains_ref[3:4, pl.ds(0, 1)] = count
    turned = valid_ref[...].astype(f32).T
    for s in range(seqs):
        rows = pl.ds(s * tokens, tokens)
        masks_ref[rows, pl.ds(0, 1)] = turned[:, s : s + 1]
        masks_ref[rows, pl.ds(1, 1)] = turned[:, s : s + 1] * (factor / count)


def unpack(here, every, valid_mask, width, units, parts, length):
    seqs, tokens = valid_mask.shape
    devices = every.shape[0]
    sizes = (6 * width // devices, width // devices, units // devices)
    return single(
        partial(unpack_kernel, parts, sizes, float(seqs * length)),
        [
            ((8, 6 * width), f32),
            ((8, width), f32),
            ((8, units), f32),
            ((4 * parts * 8 * tokens, 1), f32),
            ((1, 8 * tokens), f32),
            ((seqs * tokens, 2), f32),
        ],
        [every, valid_mask],
        place=here,
    )


def begin_kernel(embed_ref, ada_ref, vectors_ref, segments_ref, valid_ref, *refs):
    *weights, packed_ref = refs[:-1] if len(refs) > 1 else refs
    seqs, tokens = segments_ref.shape
    modulation = jnp.dot(
        embed_ref[...], ada_ref[...].astype(f32), precision=precise, preferred_element_type=f32
    )
    size = modulation.shape[1]
    modulation = modulation + vectors_ref[:, pl.ds(0, size)]
    rest = vectors_ref.shape[1] - size
    count = jnp.sum(valid_ref[...].astype(f32), axis=1, keepdims=True)
    count = jnp.sum(count, axis=0, keepdims=True)
    fields = [modulation[s : s + 1] for s in range(seqs)]
    fields.append(vectors_ref[:, pl.ds(size, rest)])
    fields += [segments_ref[s : s + 1, :].astype(f32) for s in range(seqs)]
    fields.append(count)
    packed_ref[...] = jnp.zeros(packed_ref.shape, f32)
    begin = 0
    for field in fields:
        columns = pl.ds(begin, field.shape[1])
        packed_ref[:, columns] = jnp.broadcast_to(
            field, (packed_ref.shape[0], field.shape[1])
        )
        begin += field.shape[1]
    if weights:
        out_ref, up_ref, down_ref = weights
        later_ref = refs[-1]
        width = out_ref.shape[1]
        later_ref[0] = out_ref[...]
        for j in range(4):
            later_ref[1 + j] = up_ref[:, pl.ds(j * width, width)]
            later_ref[5 + j] = down_ref[pl.ds(j * 24, 24), :]


def begin_with(time_embed, ada_weight, vectors, segments, valid_mask, weights, devices):
    seqs, tokens = segments.shape
    columns = seqs * ada_weight.shape[1] + vectors.shape[1] - ada_weight.shape[1] + seqs * tokens + 1
    outs = [((devices, columns + -columns % 128), f32)]
    if weights:
        outs.append(((9, 24, weights[0].shape[1]), bf16))
    return single(
        begin_kernel, outs, [time_embed, ada_weight, vectors, segments, valid_mask, *weights]
    )


def after(value, *others):
    return lax.optimization_barrier((value, others))[0]


def exchange(rows):
    return lax.all_to_all(rows, SPOT, 0, 0, tiled=True)


def on_device(
    inputs,
    time_embed,
    segments,
    valid_mask,
    teacher,
    ada_weight,
    ada_bias,
    gain_attn,
    qkv_weight,
    out_weight,
    gain_mlp,
    up_weight,
    up_bias,
    down_weight,
    down_bias,
):
    seqs, tokens, width = inputs.shape
    units = up_weight.shape[1]
    parts = lax.axis_size("rb")
    devices = 32 * parts
    length = tokens * devices
    queries = 8 * tokens
    here = place()

    vectors = jnp.concatenate([ada_bias, gain_attn, gain_mlp, up_bias, down_bias])
    vectors = vectors.astype(f32).reshape(1, -1)
    weights = [] if parts > 1 else [out_weight, up_weight, down_weight]
    packed, *later = begin_with(
        time_embed, ada_weight, vectors, segments, valid_mask, weights, devices
    )
    every = lax.all_to_all(packed, EVERY, 0, 0, tiled=True)
    if parts > 1:
        full_qkv, *later = (
            lax.all_gather(w, EVERY, axis=0, tiled=True)
            for w in (qkv_weight, out_weight, up_weight, down_weight)
        )
    else:
        later = [lax.all_gather(later[0], EVERY, axis=0, tiled=False)]
        shard, packed = lax.optimization_barrier((qkv_weight, packed))

    def use(every):
        return unpack(here, every, valid_mask, width, units, parts, length)

    if parts > 1:
        used = use(every)
    else:
        full_qkv, used = gather_rows(here, shard, every, use)
    modulation, gains, full_up_bias, key_docs, query_docs, masks = used
    count_all = gains[3, 0]

    entered, pair, query = enter(inputs, modulation, gains, full_qkv)
    pair = exchange(pair).reshape(queries, 2 * WIDTH)
    query = exchange(query)
    if parts > 1:
        pair = lax.all_gather(pair, "rb", axis=0, tiled=True)
    pair_x = swap(pair, "hx")
    pair_x, query = lax.optimization_barrier((pair_x, query))
    pairs = (pair, pair_x, swap(pair, "hc"), swap(pair_x, "hc"))
    attended, turned, total = attend(query, pairs, key_docs, query_docs)

    final, grad_hidden, grad_leaving, pack, sums = middle(
        exchange(attended), inputs, teacher, masks, modulation, gains, full_up_bias, later
    )
    grad_came = exchange(grad_leaving)
    if parts == 1:
        terms = weight_terms(here, pack, swap(pack, "hc"), width)
        grad_came, terms = lax.optimization_barrier((grad_came, terms))
        held = terms[::2]
        firsts = [
            swap(send, ORDERS[side][0]) for send, (_, side) in zip(terms[1::2], COLUMN_GROUPS)
        ]

    grad_query, keep, keep_x, send = attend_back(
        query, grad_came, pairs, key_docs, query_docs, turned, total
    )
    if parts == 1:
        send, firsts[0], firsts[2] = lax.optimization_barrier((send, firsts[0], firsts[2]))
    recv = swap(send, "hc")
    own_rows = keep.shape[0]
    send_x = (keep_x + recv[own_rows:].astype(f32)).astype(bf16)
    grad_pair = keep + recv[:own_rows].astype(f32) + swap(send_x, "hx").astype(f32)
    if parts > 1:
        grad_pair = lax.psum_scatter(grad_pair, "rb", scatter_dimension=0, tiled=True)
    home = jnp.concatenate(
        [grad_pair.astype(bf16).reshape(8, tokens, 2 * WIDTH), grad_query], axis=1
    )
    if parts == 1:
        home, firsts[1] = lax.optimization_barrier((home, firsts[1]))
        seconds = [
            swap(
                jnp.concatenate(
                    [
                        second_send(keep, recv)
                        for keep, recv, (_, own) in zip(held, firsts, COLUMN_GROUPS)
                        if own == side
                    ],
                    axis=3,
                ),
                ORDERS[side][1],
            )
            for side in (0, 1)
        ]
    home = exchange(home)
    if parts == 1:
        others = swap(entered, "hc"), swap(home, "hc")
        terms = qkv_terms(here, seqs, entered, others[0], home, others[1])
        seconds = after(seconds, terms)
        second = jnp.concatenate(
            [
                keep[0].astype(f32) + recv[0].astype(f32)
                for keep, recv in zip(held, firsts)
            ],
            axis=3,
        ) + jnp.concatenate(seconds, axis=3).astype(f32)
        third = third_recvs(second)
        recvs = [swap(send, order[0]) for send, order in zip(terms[1::2], ORDERS)]
        home = after(home, recvs)
        second_qkv = jnp.concatenate(
            [
                second_total(keep, recv, swap(second_send(keep, recv), order[1]))
                for keep, recv, order in zip(terms[::2], recvs, ORDERS)
            ],
            axis=2,
        )
        third, third_qkv = lax.optimization_barrier((third, third_recvs(second_qkv)))
        owned_later = third_total(second, third)
        shard_qkv = third_total(second_qkv, third_qkv)
        shard_out = owned_later[0]
        shard_up = owned_later[1:5].transpose(1, 0, 2).reshape(24, units)
        shard_down = owned_later[5:].reshape(96, width)
    grad_input, small, flat = leave(
        home, inputs, grad_hidden, modulation, gains, full_qkv, sums, devices
    )
    if parts > 1:
        base = 2 * width + units
        ends = (base + width, base + width + units)
        shard_qkv, shard_out, shard_up, shard_down = (
            lax.psum_scatter(
                jnp.einsum("tk,tn->kn", left, right, preferred_element_type=f32),
                EVERY,
                scatter_dimension=0,
                tiled=True,
            )
            for left, right in (
                (entered, flat),
                (pack[:, :width], pack[:, base : ends[0]]),
                (pack[:, width : 2 * width], pack[:, ends[0] : ends[1]]),
                (pack[:, 2 * width : base], pack[:, ends[1] :]),
            )
        )
    small = lax.all_to_all(small, EVERY, 0, 0, tiled=True)
    if parts == 1:
        small = after(small, second_qkv)
    added = jnp.sum(small, axis=0)
    owned = []
    begin = 0
    sizes = [6 * width // devices * seqs] + [size // devices for size in (width, width, units, width)]
    for size in sizes + [1]:
        owned.append(added[begin : begin + size])
        begin += size
    own_grad = owned[0].reshape(seqs, -1)
    grad_ada_weight = jnp.sum(time_embed[:, :, None] * own_grad[:, None, :], axis=0)
    loss_value = owned[5][0] / (count_all * width)
    return (
        final,
        loss_value,
        grad_input,
        grad_ada_weight,
        jnp.sum(own_grad, axis=0),
        owned[1],
        shard_qkv,
        shard_out,
        owned[2],
        shard_up,
        owned[3],
        shard_down,
        owned[4],
    )


def solution(mesh):
    blocks = mesh.shape["blk"]
    fine = Mesh(mesh.devices.reshape(2, 2, blocks // 8, 4, 2), EVERY)
    tokens = ("rb", "sz", "sy", "hx", "hc")
    return jax.shard_map(
        on_device,
        mesh=fine,
        in_specs=(
            P(None, tokens, None),
            P(),
            P(None, tokens),
            P(None, tokens),
            P(None, tokens, None),
            P(None, EVERY),
            P(EVERY),
            P(EVERY),
            P(EVERY, None),
            P(EVERY, None),
            P(EVERY),
            P(EVERY, None),
            P(EVERY),
            P(EVERY, None),
            P(EVERY),
        ),
        out_specs=(
            P(None, tokens, None),
            P(),
            P(None, tokens, None),
            P(None, EVERY),
            P(EVERY),
            P(EVERY),
            P(EVERY, None),
            P(EVERY, None),
            P(EVERY),
            P(EVERY, None),
            P(EVERY),
            P(EVERY, None),
            P(EVERY),
        ),
        check_vma=False,
    )
```

```python
from functools import partial

import jax
import jax.numpy as jnp
from jax import lax
from jax.experimental import pallas as pl
from jax.experimental.pallas import tpu as pltpu
from jax.sharding import Mesh, PartitionSpec as P

HEADS = 12
HEAD_DIM = 64
GROUPS = 4
WIDTH = HEADS // GROUPS * HEAD_DIM
EVERY = ("hx", "hc", "rb", "sz", "sy")
SPOT = ("sz", "sy")
bf16 = jnp.bfloat16
f32 = jnp.float32
precise = lax.Precision.HIGHEST


def normalize(hidden):
    average = jnp.mean(hidden, axis=-1, keepdims=True)
    centred = hidden - average
    variance = jnp.mean(centred * centred, axis=-1, keepdims=True)
    inverse = lax.rsqrt(variance + 1e-05)
    return (centred * inverse, inverse)


def dot(left, right):
    return jnp.dot(left, right, preferred_element_type=f32)


def dot_nt(left, right):
    return lax.dot_general(left, right, (((1,), (1,)), ((), ())), preferred_element_type=f32)


def norm_back(upstream, normed, inverse):
    first_mean = jnp.mean(upstream, axis=-1, keepdims=True)
    second_mean = jnp.mean(upstream * normed, axis=-1, keepdims=True)
    return inverse * (upstream - first_mean - normed * second_mean)


def swap(value, axis):
    return lax.ppermute(value, axis, [(0, 1), (1, 0)])


def turn(value, axis, step):
    size = lax.axis_size(axis)
    return lax.ppermute(value, axis, [(i, (i - step) % size) for i in range(size)])


def place():
    return jnp.stack([lax.axis_index(name) for name in ("hx", "hc", "sz", "sy", "rb")]).astype(
        jnp.int32
    )


ANY = pl.BlockSpec(memory_space=pl.ANY)
SMEM = pl.BlockSpec(memory_space=pltpu.SMEM)
VMEM = pl.BlockSpec(memory_space=pltpu.VMEM)


def hbm(value):
    return pltpu.with_memory_space_constraint(value, pltpu.HBM)


def whole_spec(shape):
    return pl.BlockSpec(shape, lambda *_: (0,) * len(shape))


def result(shape, kind, free=False):
    return jax.ShapeDtypeStruct(shape, kind) if free else pltpu.HBM(shape, kind)


def single(kernel, outs, values, raw=(), held=(), scratch=(), limit=40, place=None, raw_outs=0):
    specs = [whole_spec(v.shape) for v in values] + [ANY] * len(raw) + [VMEM] * len(held)
    values = [hbm(v) for v in values] + list(raw) + list(held)
    blocked_outs = len(outs) - raw_outs
    if place is not None:
        specs, values = [SMEM] + specs, [place] + values
    return pl.pallas_call(
        kernel,
        grid=(1,),
        out_shape=tuple(result(*o) for o in outs),
        in_specs=specs,
        out_specs=tuple(
            whole_spec(o[0]) if i < blocked_outs else ANY for i, o in enumerate(outs)
        ),
        scratch_shapes=list(scratch),
        compiler_params=pltpu.CompilerParams(vmem_limit_bytes=limit << 20),
    )(*values)


def join_copies(place_ref, sides, blocks, sems):
    hx, hc, sz, sy = (place_ref[i] for i in range(4))
    half = sides[0].shape[-1]
    copies = []
    for number, pieces in enumerate(sides):
        side, core = divmod(number, 2)
        for second in range(2):
            for first in range(2):
                for deep in range(4):
                    across, down = (first, second) if side == 0 else (second, first)
                    block = (hx ^ across) * 2 + (hc ^ core)
                    spot = (block * 4 + lax.rem(sz + deep, 4)) * 2 + (sy ^ down)
                    copies.append(
                        pltpu.make_async_copy(
                            pieces.at[second, first, deep],
                            blocks.at[spot, :, pl.ds(side * half, half)],
                            sems.at[len(copies)],
                        )
                    )
    return copies


def gather_rows(here, shard, every, use):
    half = shard.shape[1] // 2
    sides = []
    deep = jnp.stack([shard] + [turn(shard, "sz", k) for k in (1, 2, 3)])
    orders = (("hx", "sy"), ("sy", "hx"))
    levels = [deep[:, :, :half], deep[:, :, half:]]
    levels = [jnp.stack([v, swap(v, order[0])]) for v, order in zip(levels, orders)]
    levels, every = lax.optimization_barrier((levels, every))
    levels = [jnp.stack([v, swap(v, order[1])]) for v, order in zip(levels, orders)]
    used = use(every)
    levels, used = lax.optimization_barrier((levels, used))
    for level in levels:
        sides += [level, swap(level, "hc")]
    return sides, used


def piece_copies(place_ref, blocks, keep, send, sems, side, columns):
    hx, sz, sy = place_ref[0], place_ref[2], place_ref[3]
    copies = []
    for second in range(2):
        for first in range(2):
            for deep in range(4):
                across, down = (first, second) if side == 0 else (second, first)
                spot = ((hx ^ across) * 4 + lax.rem(sz + deep, 4)) * 2 + (sy ^ down)
                source = blocks.at[(spot,) + (slice(None),) * (len(blocks.shape) - 2) + (columns,)]
                target = (keep, send)[second].at[first, deep]
                copies.append(pltpu.make_async_copy(source, target, sems.at[len(copies)]))
    for copy in copies:
        copy.start()
    return copies


ORDERS = (("sy", "hx"), ("hx", "sy"))
COLUMN_GROUPS = ((1, 0), (2, 0), (1, 1), (2, 1))


def second_send(keep, recv):
    return (keep[1].astype(f32) + recv[1].astype(f32)).astype(bf16)


def second_total(keep, recv, recv_second):
    return keep[0].astype(f32) + recv[0].astype(f32) + recv_second.astype(f32)


def third_recvs(total):
    return [turn(total[k].astype(bf16), "sz", -k) for k in (1, 2, 3)]


def third_total(total, recvs):
    result = total[0]
    for recv in recvs:
        result = result + recv.astype(f32)
    return result


def enter_kernel(place_ref, x_ref, mod_ref, gains_ref, *refs):
    *sides, entered_ref, pair_ref, query_ref, whole_ref, block_sc, weight_sc, sems, sem = refs
    seqs, tokens, width = x_ref.shape
    half = tokens // 2
    pieced = len(sides) > 1
    if pieced:
        copies = join_copies(place_ref, sides, block_sc, sems)
    else:
        copies = [pltpu.make_async_copy(sides[0], weight_sc, sem)]
    for copy in copies:
        copy.start()
    for s in range(seqs):
        normed = normalize(x_ref[s].astype(f32))[0]
        shift, scale = (mod_ref[s : s + 1, pl.ds(i * width, width)] for i in (0, 1))
        value = normed * gains_ref[0:1] * (1.0 + scale) + shift
        entered_ref[pl.ds(s * tokens, tokens), :] = value.astype(bf16)
    entered = entered_ref[...]
    for copy in copies:
        copy.wait()
    if pieced:
        rows = block_sc.shape[1]
        for i in range(block_sc.shape[0]):
            weight_sc[pl.ds(i * rows, rows), :] = block_sc[i]
    leaving = pltpu.make_async_copy(weight_sc, whole_ref, sem)
    leaving.start()
    for which in (1, 2, 0):
        triple = dot(entered, weight_sc[:, pl.ds(which * width, width)])
        if which == 0:
            triple = triple * HEAD_DIM ** (-0.5)
        triple = triple.astype(bf16)
        for s in range(seqs):
            for g in range(GROUPS):
                rows = triple[s * tokens : (s + 1) * tokens, g * WIDTH : (g + 1) * WIDTH]
                slot = s * GROUPS + g
                if which == 0:
                    query_ref[slot, :, pl.ds(0, WIDTH)] = rows[:half]
                    query_ref[slot, :, pl.ds(WIDTH, WIDTH)] = rows[half:]
                else:
                    pair_ref[slot, :, pl.ds((which - 1) * WIDTH, WIDTH)] = rows
    leaving.wait()


def enter(here, inputs, modulation, gains, sides):
    seqs, tokens, width = inputs.shape
    rows = sides[0].shape[-2] if len(sides) > 1 else width // 32
    return single(
        enter_kernel,
        [
            ((seqs * tokens, width), bf16),
            ((8, tokens, 2 * WIDTH), bf16, True),
            ((8, tokens // 2, 2 * WIDTH), bf16, True),
            ((width, 3 * width), bf16),
        ],
        [inputs, modulation, gains],
        raw=sides,
        scratch=[
            pltpu.VMEM((32, rows, 3 * width), bf16),
            pltpu.VMEM((width, 3 * width), bf16),
            pltpu.SemaphoreType.DMA((64,)),
            pltpu.SemaphoreType.DMA,
        ],
        place=here,
        raw_outs=1,
    )


def load_pairs(pair_ref, slot, first_row, half):
    value = pair_ref[slot, pl.ds(first_row, half), :]
    return value[:, :WIDTH], value[:, WIDTH:]


def key_column(docs_ref, step):
    row = docs_ref[pl.ds(step, 1), :]
    return jnp.broadcast_to(row, (8, row.shape[1])).T[:, 0:1]


def gather_pairs(pair_ref, target):
    half = pair_ref.shape[1]
    for slot in range(pair_ref.shape[0]):
        for part, rows in enumerate(load_pairs(pair_ref, slot, 0, half)):
            target[pl.ds((slot * 2 + part) * half, half), :] = rows


def spread_heads(rows, target):
    lane = lax.broadcasted_iota(jnp.int32, (1, WIDTH), 1)
    for h in range(target.shape[0]):
        own = (lane >= h * HEAD_DIM) & (lane < (h + 1) * HEAD_DIM)
        target[h] = rows * jnp.where(own, 1.0, 0.0).astype(bf16)


def fetch(step, pair_refs, starts, pair_sc):
    for ref, (begin, end) in zip(pair_refs, starts):
        @pl.when((step >= begin) & (step < end))
        def take(ref=ref):
            pair_sc[...] = ref[...]


def forward_kernel(
    starts, came_ref, first_ref, second_ref, third_ref, fourth_ref, key_docs_ref, query_docs_ref,
    out_ref, turned_ref, total_ref, query_sc, flat_sc, pair_sc, top_sc, sum_sc, acc_sc,
):
    step = pl.program_id(0)
    heads, queries = query_sc.shape[:2]
    half = out_ref.shape[1]

    @pl.when(step == 0)
    def start():
        gather_pairs(came_ref, flat_sc)
        spread_heads(flat_sc[...], query_sc)
        top_sc[...] = jnp.full(top_sc.shape, -1e30, f32)
        sum_sc[...] = jnp.zeros(sum_sc.shape, f32)
        acc_sc[...] = jnp.zeros(acc_sc.shape, f32)

    fetch(step, (first_ref, second_ref, third_ref, fourth_ref), starts, pair_sc)
    key_part = pair_sc[:, :WIDTH]
    value_turned = pair_sc[:, WIDTH:].T
    allowed = key_column(key_docs_ref, step) == query_docs_ref[...]
    old = [top_sc[h : h + 1] for h in range(heads)]
    raw = [dot_nt(key_part, query_sc[h]) for h in range(heads)]
    scores = [jnp.where(allowed, value, -1e30) for value in raw]
    new = [jnp.maximum(o, jnp.max(v, axis=0, keepdims=True)) for o, v in zip(old, scores)]
    exponent = [jnp.exp(v - n) for v, n in zip(scores, new)]
    terms = [
        dot(value_turned[h * HEAD_DIM : (h + 1) * HEAD_DIM], exponent[h].astype(bf16))
        for h in range(heads)
    ]
    sums = [jnp.sum(v, axis=0, keepdims=True) for v in exponent]
    for h in range(heads):
        rows = pl.ds(h * HEAD_DIM, HEAD_DIM)
        fade = jnp.exp(old[h] - new[h])
        top_sc[h : h + 1] = new[h]
        sum_sc[h : h + 1] = sum_sc[h : h + 1] * fade + sums[h]
        acc_sc[rows] = acc_sc[rows] * fade + terms[h]

    @pl.when(step == pl.num_programs(0) - 1)
    def finish():
        total_ref[...] = jnp.zeros(total_ref.shape, f32)
        for h in range(heads):
            rows = pl.ds(h * HEAD_DIM, HEAD_DIM)
            turned_ref[rows] = acc_sc[rows] / sum_sc[h : h + 1]
            total_ref[h : h + 1] = top_sc[h : h + 1] + jnp.log(sum_sc[h : h + 1])
        whole = turned_ref[...].astype(bf16).T
        for slot in range(8):
            for part in range(2):
                begin = (slot * 2 + part) * half
                out_ref[slot, :, pl.ds(part * WIDTH, WIDTH)] = whole[begin : begin + half]


def pair_specs(pairs, chunk):
    specs, starts, begin = [], [], 0
    for pair in pairs:
        count = pair.shape[0] // chunk
        specs.append(
            pl.BlockSpec(
                (chunk, 2 * WIDTH),
                lambda i, begin=begin, count=count: (jnp.clip(i - begin, 0, count - 1), 0),
            )
        )
        starts.append((begin, begin + count))
        begin += count
    return specs, starts, begin


def attend(came, pairs, key_docs, query_docs):
    slots, half, columns = came.shape
    queries = slots * 2 * half
    heads = WIDTH // HEAD_DIM
    chunk = 512
    specs, starts, steps = pair_specs(pairs, chunk)
    outs = (
        result((slots, half, columns), bf16, True),
        result((WIDTH, queries), f32),
        result((8, queries), f32),
    )
    return pl.pallas_call(
        partial(forward_kernel, starts),
        grid=(steps,),
        out_shape=outs,
        in_specs=[
            whole_spec(came.shape),
            *specs,
            whole_spec(key_docs.shape),
            whole_spec(query_docs.shape),
        ],
        out_specs=tuple(whole_spec(o.shape) for o in outs),
        scratch_shapes=[
            pltpu.VMEM((heads, queries, WIDTH), bf16),
            pltpu.VMEM((queries, WIDTH), bf16),
            pltpu.VMEM((chunk, 2 * WIDTH), bf16),
            pltpu.VMEM((8, queries), f32),
            pltpu.VMEM((8, queries), f32),
            pltpu.VMEM((WIDTH, queries), f32),
        ],
        compiler_params=pltpu.CompilerParams(vmem_limit_bytes=48 << 20),
    )(*map(hbm, (came, *pairs, key_docs, query_docs)))


def backward_kernel(
    starts, came_ref, grad_ref, first_ref, second_ref, third_ref, fourth_ref, key_docs_ref, query_docs_ref,
    turned_ref, total_ref, query_out, keep_ref, keep_other, send_ref,
    query_sc, grad_sc, flat_sc, pair_sc, delta_sc, acc_sc,
):
    step = pl.program_id(0)
    heads, queries = query_sc.shape[:2]
    half = query_out.shape[1]

    @pl.when(step == 0)
    def start():
        gather_pairs(came_ref, flat_sc)
        spread_heads(flat_sc[...], query_sc)
        gather_pairs(grad_ref, flat_sc)
        spread_heads(flat_sc[...], grad_sc)
        acc_sc[...] = jnp.zeros(acc_sc.shape, f32)
        product = flat_sc[...].T.astype(f32) * turned_ref[...]
        for h in range(heads):
            rows = slice(h * HEAD_DIM, (h + 1) * HEAD_DIM)
            delta_sc[h : h + 1] = jnp.sum(product[rows], axis=0, keepdims=True)

    fetch(step, (first_ref, second_ref, third_ref, fourth_ref), starts, pair_sc)
    key_part = pair_sc[:, :WIDTH]
    value_part = pair_sc[:, WIDTH:]
    key_turned = key_part.T
    allowed = key_column(key_docs_ref, step) == query_docs_ref[...]
    raw = [dot_nt(key_part, query_sc[h]) for h in range(heads)]
    slopes = [dot_nt(value_part, grad_sc[h]) for h in range(heads)]
    probabilities = [
        jnp.exp(jnp.where(allowed, value, -1e30) - total_ref[h : h + 1])
        for h, value in enumerate(raw)
    ]
    grad_scores = [
        (p * (slope - delta_sc[h : h + 1])).astype(bf16)
        for h, (p, slope) in enumerate(zip(probabilities, slopes))
    ]
    grad_value = sum(dot(probabilities[h].astype(bf16), grad_sc[h]) for h in range(heads))
    grad_key = sum(dot(grad_scores[h], query_sc[h]) for h in range(heads))
    for h in range(heads):
        rows = pl.ds(h * HEAD_DIM, HEAD_DIM)
        acc_sc[rows] = acc_sc[rows] + dot(
            key_turned[h * HEAD_DIM : (h + 1) * HEAD_DIM], grad_scores[h]
        )
    quarter = pl.num_programs(0) // 4
    middle = 2 * quarter

    for number, ref in enumerate((keep_ref, keep_other)):
        @pl.when((step >= number * quarter) & (step < (number + 1) * quarter))
        def mine(ref=ref):
            ref[:, pl.ds(0, WIDTH)] = grad_key
            ref[:, pl.ds(WIDTH, WIDTH)] = grad_value

    @pl.when(step >= middle)
    def theirs():
        send_ref[:, pl.ds(0, WIDTH)] = grad_key.astype(bf16)
        send_ref[:, pl.ds(WIDTH, WIDTH)] = grad_value.astype(bf16)

    @pl.when(step == pl.num_programs(0) - 1)
    def finish():
        whole = (acc_sc[...] * HEAD_DIM ** (-0.5)).astype(bf16).T
        for slot in range(8):
            for part in range(2):
                begin = (slot * 2 + part) * half
                query_out[slot, :, pl.ds(part * WIDTH, WIDTH)] = whole[begin : begin + half]


def attend_back(came, grad, pairs, key_docs, query_docs, turned, total):
    slots, half, columns = came.shape
    queries = slots * 2 * half
    heads = WIDTH // HEAD_DIM
    chunk = 512
    specs, starts, steps = pair_specs(pairs, chunk)
    quarter = steps // 4
    middle = 2 * quarter
    return pl.pallas_call(
        partial(backward_kernel, starts),
        grid=(steps,),
        out_shape=(
            jax.ShapeDtypeStruct((slots, half, columns), bf16),
            jax.ShapeDtypeStruct((quarter * chunk, columns), f32),
            jax.ShapeDtypeStruct((quarter * chunk, columns), f32),
            jax.ShapeDtypeStruct((middle * chunk, columns), bf16),
        ),
        in_specs=[
            whole_spec(came.shape),
            whole_spec(grad.shape),
            *specs,
            whole_spec(key_docs.shape),
            whole_spec(query_docs.shape),
            whole_spec(turned.shape),
            whole_spec(total.shape),
        ],
        out_specs=(
            whole_spec((slots, half, columns)),
            pl.BlockSpec((chunk, columns), lambda i: (jnp.minimum(i, quarter - 1), 0)),
            pl.BlockSpec((chunk, columns), lambda i: (jnp.clip(i - quarter, 0, quarter - 1), 0)),
            pl.BlockSpec((chunk, columns), lambda i: (jnp.maximum(i - middle, 0), 0)),
        ),
        scratch_shapes=[
            pltpu.VMEM((heads, queries, WIDTH), bf16),
            pltpu.VMEM((heads, queries, WIDTH), bf16),
            pltpu.VMEM((queries, WIDTH), bf16),
            pltpu.VMEM((chunk, 2 * WIDTH), bf16),
            pltpu.VMEM((8, queries), f32),
            pltpu.VMEM((WIDTH, queries), f32),
        ],
        compiler_params=pltpu.CompilerParams(vmem_limit_bytes=48 << 20),
    )(*map(hbm, (came, grad, *pairs, key_docs, query_docs, turned, total)))


def settle_kernel(
    later_hbm, out_ref, up_ref, down_ref, block_sc, out_sc, up_sc, down_sc, sems, out_sems
):
    width = out_ref.shape[1]
    copies = [
        pltpu.make_async_copy(later_hbm.at[:, j], block_sc.at[j], sems.at[j]) for j in range(9)
    ]
    for copy in copies:
        copy.start()
    leaving = []
    for j in range(9):
        copies[j].wait()
        for i in range(32):
            value = block_sc[j, i]
            if j == 0:
                out_sc[pl.ds(i * 24, 24), :] = value
            elif j < 5:
                up_sc[pl.ds(i * 24, 24), pl.ds((j - 1) * width, width)] = value
            else:
                down_sc[pl.ds(i * 96 + (j - 5) * 24, 24), :] = value
        if j == 0:
            leaving.append(pltpu.make_async_copy(out_sc, out_ref, out_sems.at[j]))
        elif j < 5:
            columns = pl.ds((j - 1) * width, width)
            leaving.append(
                pltpu.make_async_copy(up_sc.at[:, columns], up_ref.at[:, columns], out_sems.at[j])
            )
        elif j == 8:
            leaving.append(pltpu.make_async_copy(down_sc, down_ref, out_sems.at[j]))
        if j < 5 or j == 8:
            leaving[-1].start()
    for copy in leaving:
        copy.wait()


def settle(later):
    width = later.shape[-1]
    shapes = ((width, width), (width, 4 * width), (4 * width, width))
    return pl.pallas_call(
        settle_kernel,
        out_shape=tuple(result(shape, bf16) for shape in shapes),
        in_specs=[ANY],
        out_specs=(ANY,) * 3,
        scratch_shapes=[
            pltpu.VMEM((9, 32, 24, width), bf16),
            *(pltpu.VMEM(shape, bf16) for shape in shapes),
            pltpu.SemaphoreType.DMA((9,)),
            pltpu.SemaphoreType.DMA((9,)),
        ],
        compiler_params=pltpu.CompilerParams(vmem_limit_bytes=40 << 20),
    )(hbm(later))


def middle_kernel(
    came_ref, x_ref, teacher_ref, mask_ref, mod_ref, gains_ref, up_bias_ref,
    out_hbm, up_hbm, down_hbm,
    final_ref, hidden_ref, leave_ref, pack_ref, sums_ref, out_sc, up_sc, down_sc, slope_sc, sems,
):
    seqs, tokens, width = x_ref.shape
    units = up_sc.shape[1]
    rows = seqs * tokens
    half = tokens // 2
    parts = [pl.ds(f * width, width) for f in range(units // width)]
    copies = [pltpu.make_async_copy(out_hbm, out_sc, sems.at[0])]
    for f, part in enumerate(parts):
        copies.append(
            pltpu.make_async_copy(up_hbm.at[:, part], up_sc.at[:, part], sems.at[1 + 2 * f])
        )
        copies.append(
            pltpu.make_async_copy(down_hbm.at[part, :], down_sc.at[part, :], sems.at[2 + 2 * f])
        )
    for copy in copies:
        copy.start()
    masks = mask_ref[...].T

    def wide(index):
        return jnp.concatenate(
            [
                jnp.broadcast_to(
                    mod_ref[s : s + 1, pl.ds(index * width, width)], (tokens, width)
                )
                for s in range(seqs)
            ]
        )

    def add_rows(first, value):
        for s in range(seqs):
            sums_ref[first + s : first + s + 1] = jnp.sum(
                value[s * tokens : (s + 1) * tokens], axis=0, keepdims=True
            )

    for s in range(seqs):
        for g in range(GROUPS):
            left, right = load_pairs(came_ref, s * GROUPS + g, 0, half)
            columns = pl.ds(g * WIDTH, WIDTH)
            pack_ref[pl.ds(s * tokens, half), columns] = left
            pack_ref[pl.ds(s * tokens + half, half), columns] = right
    mixed = pack_ref[:, pl.ds(0, width)]
    residual = jnp.concatenate([x_ref[s].astype(f32) for s in range(seqs)])
    copies[0].wait()
    branch = dot(mixed, out_sc[...])
    hidden = residual + wide(2) * branch
    normed, inverse = normalize(hidden)
    scaled = normed * gains_ref[1:2]
    moved = (scaled * (1.0 + wide(4)) + wide(3)).astype(bf16)
    pack_ref[:, pl.ds(width, width)] = moved
    lower = None
    for f in range(units // width):
        columns = pl.ds(f * width, width)
        copies[1 + 2 * f].wait()
        u = dot(moved, up_sc[:, columns]) + up_bias_ref[0:1, columns]
        square = u * u
        t = jnp.tanh(0.7978845608028654 * (u + 0.044715 * u * square))
        active = (0.5 * u * (1.0 + t)).astype(bf16)
        slope_sc[:, columns] = 0.5 * (1.0 + t) + 0.5 * u * (1.0 - t * t) * 0.7978845608028654 * (
            1.0 + 0.134145 * square
        )
        pack_ref[:, pl.ds(2 * width + f * width, width)] = active
        copies[2 + 2 * f].wait()
        term = dot(active, down_sc[columns, :])
        lower = term if lower is None else lower + term
    lower = lower + gains_ref[2:3]
    gate = wide(5)
    final = hidden + gate * lower
    for s in range(seqs):
        final_ref[s] = final[s * tokens : (s + 1) * tokens].astype(bf16)
    teacher = jnp.concatenate([teacher_ref[s].astype(f32) for s in range(seqs)])
    mismatch = final - teacher
    sums_ref[14:15] = jnp.sum(
        masks[:, 0:1] * mismatch * mismatch, axis=0, keepdims=True
    )
    sums_ref[15:16] = jnp.zeros((1, width), f32)
    grad_final = masks[:, 1:2] * mismatch
    add_rows(6, grad_final * lower)
    grad_lower = (gate * grad_final).astype(bf16)
    base = 2 * width + units
    pack_ref[:, pl.ds(base + width + units, width)] = grad_lower
    sums_ref[9:10] = jnp.sum(grad_lower.astype(f32), axis=0, keepdims=True)
    grad_moved = None
    for f in range(units // width):
        columns = pl.ds(f * width, width)
        grad_active = dot_nt(grad_lower, down_sc[columns, :])
        grad_upper = (grad_active * slope_sc[:, columns]).astype(bf16)
        pack_ref[:, pl.ds(base + width + f * width, width)] = grad_upper
        sums_ref[10 + f : 11 + f] = jnp.sum(grad_upper.astype(f32), axis=0, keepdims=True)
        term = dot_nt(grad_upper, up_sc[:, columns])
        grad_moved = term if grad_moved is None else grad_moved + term
    add_rows(2, grad_moved)
    add_rows(4, grad_moved * scaled)
    grad_scaled = grad_moved * (1.0 + wide(4))
    sums_ref[8:9] = jnp.sum(grad_scaled * normed, axis=0, keepdims=True)
    grad_hidden = grad_final + norm_back(grad_scaled * gains_ref[1:2], normed, inverse)
    hidden_ref[...] = grad_hidden
    add_rows(0, grad_hidden * branch)
    grad_branch = (wide(2) * grad_hidden).astype(bf16)
    pack_ref[:, pl.ds(base, width)] = grad_branch
    grad_mixed = dot_nt(grad_branch, out_sc[...]).astype(bf16)
    for s in range(seqs):
        for g in range(GROUPS):
            piece = grad_mixed[s * tokens : (s + 1) * tokens, g * WIDTH : (g + 1) * WIDTH]
            leave_ref[s * GROUPS + g, :, pl.ds(0, WIDTH)] = piece[:half]
            leave_ref[s * GROUPS + g, :, pl.ds(WIDTH, WIDTH)] = piece[half:]


def middle(came, inputs, teacher, masks, modulation, gains, up_bias, weights):
    seqs, tokens, width = inputs.shape
    units = up_bias.shape[1]
    rows = seqs * tokens
    return single(
        middle_kernel,
        [
            ((seqs, tokens, width), bf16),
            ((rows, width), f32),
            (came.shape, bf16, True),
            ((rows, 4 * width + 2 * units), bf16, True),
            ((16, width), f32),
        ],
        [came, inputs, teacher, masks, modulation, gains, up_bias],
        raw=[hbm(w) for w in weights],
        scratch=[
            pltpu.VMEM((width, width), bf16),
            pltpu.VMEM((width, units), bf16),
            pltpu.VMEM((units, width), bf16),
            pltpu.VMEM((rows, units), f32),
            pltpu.SemaphoreType.DMA((9,)),
        ],
        limit=40,
    )


def weights_kernel(
    place_ref, own_ref, other_ref, *refs
):
    *groups, left_sc, right_sc, block_sc, sems = refs
    rows, width = own_ref.shape[0], block_sc.shape[-1]
    units = 4 * width
    hc = place_ref[1]
    base = 2 * width + units
    for which, ref in enumerate((own_ref, other_ref)):
        left_sc[:, pl.ds(which * rows, rows)] = ref[:, pl.ds(0, base)].T
        right_sc[pl.ds(which * rows, rows), :] = ref[:, pl.ds(base, base)]
    for hx in range(2):
        begin = pl.multiple_of(hx * 384 + hc * 192, 64)
        for j in range(5):
            offset = 0 if j == 0 else width
            value = dot(left_sc[pl.ds(begin + offset, 192), :], right_sc[:, pl.ds(j * width, width)])
            for i in range(8):
                block_sc[hx * 8 + i, j] = value[i * 24 : (i + 1) * 24].astype(bf16)
        begin = pl.multiple_of(2 * width + hx * 1536 + hc * 768, 256)
        value = dot(left_sc[pl.ds(begin, 768), :], right_sc[:, pl.ds(width + units, width)])
        for i in range(8):
            for j in range(4):
                first = i * 96 + j * 24
                block_sc[hx * 8 + i, 5 + j] = value[first : first + 24].astype(bf16)
    copies = []
    begin = 0
    for number, (_, side) in enumerate(COLUMN_GROUPS):
        keep, send = groups[2 * number : 2 * number + 2]
        columns = pl.ds(begin, keep.shape[-1])
        copies += piece_copies(place_ref, block_sc, keep, send, sems.at[number], side, columns)
        begin += keep.shape[-1]
    for copy in copies:
        copy.wait()


def weight_terms(here, own, other, width):
    rows, total = own.shape
    return single(
        weights_kernel,
        [((2, 4, 9, 24, 128 * size), bf16) for size, _ in COLUMN_GROUPS for _ in range(2)],
        [],
        held=[own, other],
        scratch=[
            pltpu.VMEM((total // 2, 2 * rows), bf16),
            pltpu.VMEM((2 * rows, total // 2), bf16),
            pltpu.VMEM((16, 9, 24, width), bf16),
            pltpu.SemaphoreType.DMA((len(COLUMN_GROUPS), 16)),
        ],
        limit=40,
        place=here,
        raw_outs=2 * len(COLUMN_GROUPS),
    )


def flat_rows(home_ref, target, first_row, seqs, tokens, width):
    half = tokens // 2
    for s in range(seqs):
        for g in range(GROUPS):
            slot = s * GROUPS + g
            row = first_row + s * tokens
            left, right = load_pairs(home_ref, slot, tokens, half)
            target[pl.ds(row, half), pl.ds(g * WIDTH, WIDTH)] = left
            target[pl.ds(row + half, half), pl.ds(g * WIDTH, WIDTH)] = right
            left, right = load_pairs(home_ref, slot, 0, tokens)
            target[pl.ds(row, tokens), pl.ds(width + g * WIDTH, WIDTH)] = left
            target[pl.ds(row, tokens), pl.ds(2 * width + g * WIDTH, WIDTH)] = right


def qkv_kernel(
    seqs, place_ref, entered_ref, entered_other, home_ref, home_other,
    keep_a, send_a, keep_b, send_b, left_sc, right_sc, block_sc, sems,
):
    rows, width = entered_ref.shape
    hc = place_ref[1]
    for which, (left, home) in enumerate(((entered_ref, home_ref), (entered_other, home_other))):
        left_sc[:, pl.ds(which * rows, rows)] = left[...].T
        flat_rows(home, right_sc, which * rows, seqs, rows // seqs, width)
    for hx in range(2):
        begin = pl.multiple_of(hx * 384 + hc * 192, 64)
        for j in range(3):
            value = dot(left_sc[pl.ds(begin, 192), :], right_sc[:, pl.ds(j * width, width)])
            for i in range(8):
                block_sc[hx * 8 + i, :, pl.ds(j * width, width)] = value[
                    i * 24 : (i + 1) * 24
                ].astype(bf16)
    half = 3 * width // 2
    copies = piece_copies(place_ref, block_sc, keep_a, send_a, sems.at[0], 0, pl.ds(0, half))
    copies += piece_copies(place_ref, block_sc, keep_b, send_b, sems.at[1], 1, pl.ds(half, half))
    for copy in copies:
        copy.wait()


def qkv_terms(here, seqs, *values):
    rows, width = values[0].shape
    return single(
        partial(qkv_kernel, seqs),
        [((2, 4, 24, 3 * width // 2), bf16)] * 4,
        values,
        scratch=[
            pltpu.VMEM((width, 2 * rows), bf16),
            pltpu.VMEM((2 * rows, 3 * width), bf16),
            pltpu.VMEM((16, 24, 3 * width), bf16),
            pltpu.SemaphoreType.DMA((2, 16)),
        ],
        place=here,
        raw_outs=4,
    )


def leave_kernel(
    home_ref, x_ref, hidden_ref, mod_ref, gains_ref, weight_ref, middle_ref,
    grad_ref, small_ref, flat_ref,
):
    seqs, tokens, width = x_ref.shape
    devices = small_ref.shape[0]
    flat_rows(home_ref, flat_ref, 0, seqs, tokens, width)
    grad_entered = None
    for which in range(3):
        columns = pl.ds(which * width, width)
        term = dot_nt(flat_ref[:, columns], weight_ref[:, columns])
        grad_entered = term if grad_entered is None else grad_entered + term
    gain_sum = None
    sums = []
    for s in range(seqs):
        normed, inverse = normalize(x_ref[s].astype(f32))
        rows = slice(s * tokens, (s + 1) * tokens)
        grad = grad_entered[rows]
        shift_sum = jnp.sum(grad, axis=0, keepdims=True)
        scale_sum = jnp.sum(grad * (normed * gains_ref[0:1]), axis=0, keepdims=True)
        grad_scaled = grad * (1.0 + mod_ref[s : s + 1, pl.ds(width, width)])
        term = jnp.sum(grad_scaled * normed, axis=0, keepdims=True)
        gain_sum = term if gain_sum is None else gain_sum + term
        grad_ref[s] = hidden_ref[rows] + norm_back(grad_scaled * gains_ref[0:1], normed, inverse)
        later = [middle_ref[i + s : i + s + 1] for i in (0, 2, 4, 6)]
        sums.append(jnp.concatenate([shift_sum, scale_sum, *later], axis=1))
    up_bias = jnp.concatenate([middle_ref[i : i + 1] for i in range(10, 14)], axis=1)
    fields = [*sums, gain_sum, middle_ref[8:9], up_bias, middle_ref[9:10]]
    error = jnp.sum(middle_ref[14:15], axis=1, keepdims=True)
    small_ref[...] = jnp.zeros(small_ref.shape, f32)
    begin = 0
    for field in fields:
        size = field.shape[1] // devices
        for i in range(devices):
            small_ref[i : i + 1, pl.ds(begin, size)] = field[:, i * size : (i + 1) * size]
        begin += size
    small_ref[:, pl.ds(begin, 1)] = jnp.broadcast_to(error, (devices, 1))


def leave(home, inputs, grad_hidden, modulation, gains, weight, sums, devices):
    seqs, tokens, width = inputs.shape
    return single(
        leave_kernel,
        [
            ((seqs, tokens, width), f32),
            ((devices, 512), f32, True),
            ((seqs * tokens, 3 * width), bf16),
        ],
        [home, inputs, grad_hidden, modulation, gains, weight, sums],
    )


def unpack_kernel(
    parts, sizes, factor, place_ref, every_ref, valid_ref,
    mod_ref, gains_ref, up_ref, key_docs_ref, query_docs_ref, masks_ref,
):
    devices = every_ref.shape[0]
    seqs, tokens = valid_ref.shape
    size_mod, size_gain, size_up = sizes
    mod_ref[...] = jnp.zeros(mod_ref.shape, f32)
    gains_ref[...] = jnp.zeros(gains_ref.shape, f32)
    up_ref[...] = jnp.zeros(up_ref.shape, f32)
    begin = 0
    targets = [(mod_ref, s, size_mod) for s in range(seqs)]
    targets += [(gains_ref, 0, size_gain), (gains_ref, 1, size_gain)]
    targets += [(up_ref, 0, size_up), (gains_ref, 2, size_gain)]
    for target, row, size in targets:
        for i in range(devices):
            target[row : row + 1, pl.ds(i * size, size)] = every_ref[
                i : i + 1, pl.ds(begin, size)
            ]
        begin += size
    hx, hc, sz, sy, rb = (place_ref[i] for i in range(5))
    second = sz * 2 + sy >= GROUPS
    row = 0
    for core in range(2):
        for across in range(2):
            for part in range(parts):
                block = ((hx ^ across) * 2 + (hc ^ core)) * parts + part
                lines = every_ref[pl.ds(pl.multiple_of(block * 8, 8), 8), pl.ds(begin, 2 * tokens)]
                lines = jnp.where(second, lines[:, tokens:], lines[:, :tokens])
                for spot in range(8):
                    key_docs_ref[row : row + 1, pl.ds(spot * tokens, tokens)] = lines[
                        spot : spot + 1
                    ]
                row += 1
    lines = every_ref[
        pl.ds(pl.multiple_of(((hx * 2 + hc) * parts + rb) * 8, 8), 8), pl.ds(begin, 2 * tokens)
    ]
    lines = jnp.where(second, lines[:, tokens:], lines[:, :tokens])
    for spot in range(8):
        query_docs_ref[:, pl.ds(spot * tokens, tokens)] = lines[spot : spot + 1]
    begin += 2 * tokens
    count = jnp.sum(every_ref[:, pl.ds(begin, 1)], axis=0, keepdims=True)
    gains_ref[3:4, pl.ds(0, 1)] = count
    masks_ref[...] = jnp.zeros(masks_ref.shape, f32)
    for s in range(seqs):
        valid = valid_ref[s : s + 1, :].astype(f32)
        masks_ref[0:1, pl.ds(s * tokens, tokens)] = valid
        masks_ref[1:2, pl.ds(s * tokens, tokens)] = valid * (factor / count)


def unpack(here, every, valid_mask, width, units, parts, length):
    seqs, tokens = valid_mask.shape
    devices = every.shape[0]
    sizes = (6 * width // devices, width // devices, units // devices)
    return single(
        partial(unpack_kernel, parts, sizes, float(seqs * length)),
        [
            ((8, 6 * width), f32),
            ((8, width), f32),
            ((8, units), f32),
            ((4 * parts, 8 * tokens), f32),
            ((1, 8 * tokens), f32),
            ((8, seqs * tokens), f32),
        ],
        [every, valid_mask],
        place=here,
    )


def finish_kernel(width, small_ref, embed_ref, gains_ref, *refs):
    ada_ref, bias_ref, *vectors, loss_ref = refs
    seqs = embed_ref.shape[0]
    columns = ada_ref.shape[1]
    added = jnp.sum(small_ref[...], axis=0, keepdims=True)
    turned = embed_ref[...].T
    begin = 0
    ada = bias = None
    for s in range(seqs):
        grad = added[:, begin : begin + columns]
        begin += columns
        term = turned[:, s : s + 1] * grad
        ada = term if ada is None else ada + term
        bias = grad if bias is None else bias + grad
    ada_ref[...] = ada
    bias_ref[...] = bias
    for ref in vectors:
        size = ref.shape[1]
        ref[...] = added[:, begin : begin + size]
        begin += size
    loss_ref[...] = added[:, begin : begin + 1] / (gains_ref[3:4, 0:1] * width)


def finish(small, time_embed, gains, width, units):
    devices = small.shape[0]
    sizes = [6 * width // devices] + [size // devices for size in (width, width, units, width)]
    return single(
        partial(finish_kernel, float(width)),
        [((time_embed.shape[1], sizes[0]), f32)]
        + [((1, size), f32, True) for size in sizes]
        + [((1, 1), f32, True)],
        [small, time_embed, gains],
    )


def begin_kernel(embed_ref, ada_ref, vectors_ref, segments_ref, valid_ref, *refs):
    *weights, packed_ref = refs[:-1] if len(refs) > 1 else refs
    seqs, tokens = segments_ref.shape
    modulation = jnp.dot(
        embed_ref[...], ada_ref[...].astype(f32), precision=precise, preferred_element_type=f32
    )
    size = modulation.shape[1]
    modulation = modulation + vectors_ref[:, pl.ds(0, size)]
    rest = vectors_ref.shape[1] - size
    count = jnp.sum(valid_ref[...].astype(f32), axis=1, keepdims=True)
    count = jnp.sum(count, axis=0, keepdims=True)
    fields = [modulation[s : s + 1] for s in range(seqs)]
    fields.append(vectors_ref[:, pl.ds(size, rest)])
    fields += [segments_ref[s : s + 1, :].astype(f32) for s in range(seqs)]
    fields.append(count)
    packed_ref[...] = jnp.zeros(packed_ref.shape, f32)
    begin = 0
    for field in fields:
        columns = pl.ds(begin, field.shape[1])
        packed_ref[:, columns] = jnp.broadcast_to(
            field, (packed_ref.shape[0], field.shape[1])
        )
        begin += field.shape[1]
    if weights:
        out_ref, up_ref, down_ref = weights
        later_ref = refs[-1]
        width = out_ref.shape[1]
        later_ref[0] = out_ref[...]
        for j in range(4):
            later_ref[1 + j] = up_ref[:, pl.ds(j * width, width)]
            later_ref[5 + j] = down_ref[pl.ds(j * 24, 24), :]


def begin_with(time_embed, ada_weight, vectors, segments, valid_mask, weights, devices):
    seqs, tokens = segments.shape
    columns = seqs * ada_weight.shape[1] + vectors.shape[1] - ada_weight.shape[1] + seqs * tokens + 1
    outs = [((devices, columns + -columns % 128), f32, True)]
    if weights:
        outs.append(((9, 24, weights[0].shape[1]), bf16))
    return single(
        begin_kernel, outs, [time_embed, ada_weight, vectors, segments, valid_mask, *weights]
    )


def after(value, *others):
    return lax.optimization_barrier((value, others))[0]


def exchange(rows):
    return lax.all_to_all(rows, SPOT, 0, 0, tiled=True)


def on_device(
    inputs,
    time_embed,
    segments,
    valid_mask,
    teacher,
    ada_weight,
    ada_bias,
    gain_attn,
    qkv_weight,
    out_weight,
    gain_mlp,
    up_weight,
    up_bias,
    down_weight,
    down_bias,
):
    seqs, tokens, width = inputs.shape
    units = up_weight.shape[1]
    parts = lax.axis_size("rb")
    devices = 32 * parts
    length = tokens * devices
    queries = 8 * tokens
    here = place()

    vectors = jnp.concatenate([ada_bias, gain_attn, gain_mlp, up_bias, down_bias])
    vectors = vectors.astype(f32).reshape(1, -1)
    weights = [] if parts > 1 else [out_weight, up_weight, down_weight]
    packed, *later = begin_with(
        time_embed, ada_weight, vectors, segments, valid_mask, weights, devices
    )
    every = lax.all_to_all(packed, EVERY, 0, 0, tiled=True)
    if parts > 1:
        sides, *later = (
            lax.all_gather(w, EVERY, axis=0, tiled=True)
            for w in (qkv_weight, out_weight, up_weight, down_weight)
        )
    else:
        later = [lax.all_gather(later[0], EVERY, axis=0, tiled=False)]
        shard, packed = lax.optimization_barrier((qkv_weight, packed))

    def use(every):
        return unpack(here, every, valid_mask, width, units, parts, length)

    if parts > 1:
        sides = [sides]
        used = use(every)
    else:
        sides, used = gather_rows(here, shard, every, use)
    modulation, gains, full_up_bias, key_docs, query_docs, masks = used

    entered, pair, query, full_qkv = enter(here, inputs, modulation, gains, sides)
    pair = exchange(pair).reshape(queries, 2 * WIDTH)
    query = exchange(query)
    if parts > 1:
        pair = lax.all_gather(pair, "rb", axis=0, tiled=True)
    pair_x = swap(pair, "hx")
    pair_x, query = lax.optimization_barrier((pair_x, query))
    pairs = (pair, pair_x, swap(pair, "hc"), swap(pair_x, "hc"))
    attended, turned, total = attend(query, pairs, key_docs, query_docs)

    if parts == 1:
        later = settle(later[0])
    final, grad_hidden, grad_leaving, pack, sums = middle(
        exchange(attended), inputs, teacher, masks, modulation, gains, full_up_bias, later
    )
    grad_came = exchange(grad_leaving)
    if parts == 1:
        terms = weight_terms(here, pack, swap(pack, "hc"), width)
        grad_came, terms = lax.optimization_barrier((grad_came, terms))
        held = terms[::2]
        firsts = [
            swap(send, ORDERS[side][0]) for send, (_, side) in zip(terms[1::2], COLUMN_GROUPS)
        ]

    grad_query, keep, keep_x, send = attend_back(
        query, grad_came, pairs, key_docs, query_docs, turned, total
    )
    if parts == 1:
        send, firsts[0], firsts[2] = lax.optimization_barrier((send, firsts[0], firsts[2]))
    recv = swap(send, "hc")
    own_rows = keep.shape[0]
    send_x = (keep_x + recv[own_rows:].astype(f32)).astype(bf16)
    grad_pair = keep + recv[:own_rows].astype(f32) + swap(send_x, "hx").astype(f32)
    if parts > 1:
        grad_pair = lax.psum_scatter(grad_pair, "rb", scatter_dimension=0, tiled=True)
    home = jnp.concatenate(
        [grad_pair.astype(bf16).reshape(8, tokens, 2 * WIDTH), grad_query], axis=1
    )
    if parts == 1:
        home, firsts[1] = lax.optimization_barrier((home, firsts[1]))
        seconds = [
            swap(
                jnp.concatenate(
                    [
                        second_send(keep, recv)
                        for keep, recv, (_, own) in zip(held, firsts, COLUMN_GROUPS)
                        if own == side
                    ],
                    axis=3,
                ),
                ORDERS[side][1],
            )
            for side in (0, 1)
        ]
    home = exchange(home)
    if parts == 1:
        others = swap(entered, "hc"), swap(home, "hc")
        terms = qkv_terms(here, seqs, entered, others[0], home, others[1])
        seconds = after(seconds, terms)
        recvs = [swap(send, order[0]) for send, order in zip(terms[1::2], ORDERS)]
        grad_input, small, flat = leave(
            after(home, terms), inputs, grad_hidden, modulation, gains, full_qkv, sums, devices
        )
        recvs = after(recvs, small)
        nexts = [second_send(keep, recv) for keep, recv in zip(terms[::2], recvs)]
        small = after(small, nexts)
        next_recvs = [swap(value, order[1]) for value, order in zip(nexts, ORDERS)]
        totals = [
            jnp.concatenate(
                [
                    keep[0].astype(f32) + recv[0].astype(f32)
                    for keep, recv, (_, own) in zip(held, firsts, COLUMN_GROUPS)
                    if own == side
                ],
                axis=3,
            )
            + seconds[side].astype(f32)
            for side in (0, 1)
        ]
        second = jnp.concatenate(totals, axis=3)
        third = third_recvs(second)
        second_qkv = jnp.concatenate(
            [
                second_total(keep, recv, next_recv)
                for keep, recv, next_recv in zip(terms[::2], recvs, next_recvs)
            ],
            axis=2,
        )
        third_qkv = third_recvs(second_qkv)
        third, third_qkv = lax.optimization_barrier((third, third_qkv))
        owned_later = third_total(second, third)
        shard_qkv = third_total(second_qkv, third_qkv)
        shard_out = owned_later[0]
        shard_up = owned_later[1:5].transpose(1, 0, 2).reshape(24, units)
        shard_down = owned_later[5:].reshape(96, width)
    if parts > 1:
        grad_input, small, flat = leave(
            home, inputs, grad_hidden, modulation, gains, full_qkv, sums, devices
        )
        base = 2 * width + units
        ends = (base + width, base + width + units)
        shard_qkv, shard_out, shard_up, shard_down = (
            lax.psum_scatter(
                jnp.einsum("tk,tn->kn", left, right, preferred_element_type=f32),
                EVERY,
                scatter_dimension=0,
                tiled=True,
            )
            for left, right in (
                (entered, flat),
                (pack[:, :width], pack[:, base : ends[0]]),
                (pack[:, width : 2 * width], pack[:, ends[0] : ends[1]]),
                (pack[:, 2 * width : base], pack[:, ends[1] :]),
            )
        )
    small = lax.all_to_all(small, EVERY, 0, 0, tiled=True)
    if parts == 1:
        small = after(small, second_qkv)
    grads = finish(small, time_embed, gains, width, units)
    loss_value = grads[6].reshape(())
    return (
        final,
        loss_value,
        grad_input,
        grads[0],
        grads[1].reshape(-1),
        grads[2].reshape(-1),
        shard_qkv,
        shard_out,
        grads[3].reshape(-1),
        shard_up,
        grads[4].reshape(-1),
        shard_down,
        grads[5].reshape(-1),
    )


def solution(mesh):
    blocks = mesh.shape["blk"]
    fine = Mesh(mesh.devices.reshape(2, 2, blocks // 8, 4, 2), EVERY)
    tokens = ("rb", "sz", "sy", "hx", "hc")
    return jax.shard_map(
        on_device,
        mesh=fine,
        in_specs=(
            P(None, tokens, None),
            P(),
            P(None, tokens),
            P(None, tokens),
            P(None, tokens, None),
            P(None, EVERY),
            P(EVERY),
            P(EVERY),
            P(EVERY, None),
            P(EVERY, None),
            P(EVERY),
            P(EVERY, None),
            P(EVERY),
            P(EVERY, None),
            P(EVERY),
        ),
        out_specs=(
            P(None, tokens, None),
            P(),
            P(None, tokens, None),
            P(None, EVERY),
            P(EVERY),
            P(EVERY),
            P(EVERY, None),
            P(EVERY, None),
            P(EVERY),
            P(EVERY, None),
            P(EVERY),
            P(EVERY, None),
            P(EVERY),
        ),
        check_vma=False,
    )
```

```python
from functools import partial

import jax
import jax.numpy as jnp
from jax import lax
from jax.experimental import pallas as pl
from jax.experimental.pallas import tpu as pltpu
from jax.sharding import Mesh, PartitionSpec as P

HEADS = 12
HEAD_DIM = 64
GROUPS = 4
WIDTH = HEADS // GROUPS * HEAD_DIM
EVERY = ("hx", "hc", "rb", "sz", "sy")
SPOT = ("sz", "sy")
bf16 = jnp.bfloat16
f32 = jnp.float32
precise = lax.Precision.HIGHEST


def normalize(hidden):
    average = jnp.mean(hidden, axis=-1, keepdims=True)
    centred = hidden - average
    variance = jnp.mean(centred * centred, axis=-1, keepdims=True)
    inverse = lax.rsqrt(variance + 1e-05)
    return (centred * inverse, inverse)


def dot(left, right):
    return jnp.dot(left, right, preferred_element_type=f32)


def dot_nt(left, right):
    return lax.dot_general(left, right, (((1,), (1,)), ((), ())), preferred_element_type=f32)


def norm_back(upstream, normed, inverse):
    first_mean = jnp.mean(upstream, axis=-1, keepdims=True)
    second_mean = jnp.mean(upstream * normed, axis=-1, keepdims=True)
    return inverse * (upstream - first_mean - normed * second_mean)


def swap(value, axis):
    return lax.ppermute(value, axis, [(0, 1), (1, 0)])


def turn(value, axis, step):
    size = lax.axis_size(axis)
    return lax.ppermute(value, axis, [(i, (i - step) % size) for i in range(size)])


def place():
    return jnp.stack([lax.axis_index(name) for name in ("hx", "hc", "sz", "sy", "rb")]).astype(
        jnp.int32
    )


ANY = pl.BlockSpec(memory_space=pl.ANY)
SMEM = pl.BlockSpec(memory_space=pltpu.SMEM)
VMEM = pl.BlockSpec(memory_space=pltpu.VMEM)


def hbm(value):
    return pltpu.with_memory_space_constraint(value, pltpu.HBM)


def whole_spec(shape):
    return pl.BlockSpec(shape, lambda *_: (0,) * len(shape))


def result(shape, kind, free=False):
    return jax.ShapeDtypeStruct(shape, kind) if free else pltpu.HBM(shape, kind)


def single(kernel, outs, values, raw=(), held=(), scratch=(), limit=40, place=None, raw_outs=0):
    specs = [whole_spec(v.shape) for v in values] + [ANY] * len(raw) + [VMEM] * len(held)
    values = [hbm(v) for v in values] + list(raw) + list(held)
    blocked_outs = len(outs) - raw_outs
    if place is not None:
        specs, values = [SMEM] + specs, [place] + values
    return pl.pallas_call(
        kernel,
        grid=(1,),
        out_shape=tuple(result(*o) for o in outs),
        in_specs=specs,
        out_specs=tuple(
            whole_spec(o[0]) if i < blocked_outs else ANY for i, o in enumerate(outs)
        ),
        scratch_shapes=list(scratch),
        compiler_params=pltpu.CompilerParams(vmem_limit_bytes=limit << 20),
    )(*values)


def join_copies(place_ref, sides, blocks, sems):
    hx, hc, sz, sy = (place_ref[i] for i in range(4))
    half = sides[0].shape[-1]
    copies = []
    for number, pieces in enumerate(sides):
        side, core = divmod(number, 2)
        for second in range(2):
            for first in range(2):
                for deep in range(4):
                    across, down = (first, second) if side == 0 else (second, first)
                    block = (hx ^ across) * 2 + (hc ^ core)
                    spot = (block * 4 + lax.rem(sz + deep, 4)) * 2 + (sy ^ down)
                    copies.append(
                        pltpu.make_async_copy(
                            pieces.at[second, first, deep],
                            blocks.at[spot, :, pl.ds(side * half, half)],
                            sems.at[len(copies)],
                        )
                    )
    return copies


def gather_rows(here, shard, every, use):
    half = shard.shape[1] // 2
    sides = []
    deep = jnp.stack([shard] + [turn(shard, "sz", k) for k in (1, 2, 3)])
    orders = (("hx", "sy"), ("sy", "hx"))
    levels = [deep[:, :, :half], deep[:, :, half:]]
    levels = [jnp.stack([v, swap(v, order[0])]) for v, order in zip(levels, orders)]
    levels, every = lax.optimization_barrier((levels, every))
    levels = [jnp.stack([v, swap(v, order[1])]) for v, order in zip(levels, orders)]
    used = use(every)
    levels, used = lax.optimization_barrier((levels, used))
    for level in levels:
        sides += [level, swap(level, "hc")]
    return sides, used


def piece_copies(place_ref, blocks, keep, send, sems, side, columns):
    hx, sz, sy = place_ref[0], place_ref[2], place_ref[3]
    copies = []
    for second in range(2):
        for first in range(2):
            for deep in range(4):
                across, down = (first, second) if side == 0 else (second, first)
                spot = ((hx ^ across) * 4 + lax.rem(sz + deep, 4)) * 2 + (sy ^ down)
                source = blocks.at[(spot,) + (slice(None),) * (len(blocks.shape) - 2) + (columns,)]
                target = (keep, send)[second].at[first, deep]
                copies.append(pltpu.make_async_copy(source, target, sems.at[len(copies)]))
    for copy in copies:
        copy.start()
    return copies


ORDERS = (("sy", "hx"), ("hx", "sy"))
COLUMN_GROUPS = ((1, 0), (2, 0), (1, 1), (2, 1))


def second_send(keep, recv):
    return (keep[1].astype(f32) + recv[1].astype(f32)).astype(bf16)


def second_total(keep, recv, recv_second):
    return keep[0].astype(f32) + recv[0].astype(f32) + recv_second.astype(f32)


def third_recvs(total):
    return [turn(total[k].astype(bf16), "sz", -k) for k in (1, 2, 3)]


def enter_kernel(place_ref, x_ref, mod_ref, gains_ref, *refs):
    *sides, entered_ref, pair_ref, query_ref, whole_ref, block_sc, weight_sc, sems, sem = refs
    seqs, tokens, width = x_ref.shape
    half = tokens // 2
    pieced = len(sides) > 1
    if pieced:
        copies = join_copies(place_ref, sides, block_sc, sems)
    else:
        copies = [pltpu.make_async_copy(sides[0], weight_sc, sem)]
    for copy in copies:
        copy.start()
    for s in range(seqs):
        normed = normalize(x_ref[s].astype(f32))[0]
        shift, scale = (mod_ref[s : s + 1, pl.ds(i * width, width)] for i in (0, 1))
        value = normed * gains_ref[0:1] * (1.0 + scale) + shift
        entered_ref[pl.ds(s * tokens, tokens), :] = value.astype(bf16)
    entered = entered_ref[...]
    for copy in copies:
        copy.wait()
    if pieced:
        rows = block_sc.shape[1]
        for i in range(block_sc.shape[0]):
            weight_sc[pl.ds(i * rows, rows), :] = block_sc[i]
    leaving = pltpu.make_async_copy(weight_sc, whole_ref, sem)
    leaving.start()
    for which in (1, 2, 0):
        triple = dot(entered, weight_sc[:, pl.ds(which * width, width)])
        if which == 0:
            triple = triple * HEAD_DIM ** (-0.5)
        triple = triple.astype(bf16)
        for s in range(seqs):
            for g in range(GROUPS):
                rows = triple[s * tokens : (s + 1) * tokens, g * WIDTH : (g + 1) * WIDTH]
                slot = s * GROUPS + g
                if which == 0:
                    query_ref[slot, :, pl.ds(0, WIDTH)] = rows[:half]
                    query_ref[slot, :, pl.ds(WIDTH, WIDTH)] = rows[half:]
                else:
                    pair_ref[slot, :, pl.ds((which - 1) * WIDTH, WIDTH)] = rows
    leaving.wait()


def enter(here, inputs, modulation, gains, sides):
    seqs, tokens, width = inputs.shape
    rows = sides[0].shape[-2] if len(sides) > 1 else width // 32
    return single(
        enter_kernel,
        [
            ((seqs * tokens, width), bf16),
            ((8, tokens, 2 * WIDTH), bf16, True),
            ((8, tokens // 2, 2 * WIDTH), bf16, True),
            ((width, 3 * width), bf16),
        ],
        [inputs, modulation, gains],
        raw=sides,
        scratch=[
            pltpu.VMEM((32, rows, 3 * width), bf16),
            pltpu.VMEM((width, 3 * width), bf16),
            pltpu.SemaphoreType.DMA((64,)),
            pltpu.SemaphoreType.DMA,
        ],
        place=here,
        raw_outs=1,
    )


def load_pairs(pair_ref, slot, first_row, half):
    value = pair_ref[slot, pl.ds(first_row, half), :]
    return value[:, :WIDTH], value[:, WIDTH:]


def key_column(docs_ref, step):
    row = docs_ref[pl.ds(step, 1), :]
    return jnp.broadcast_to(row, (8, row.shape[1])).T[:, 0:1]


def gather_pairs(pair_ref, target):
    half = pair_ref.shape[1]
    for slot in range(pair_ref.shape[0]):
        for part, rows in enumerate(load_pairs(pair_ref, slot, 0, half)):
            target[pl.ds((slot * 2 + part) * half, half), :] = rows


def spread_heads(rows, target):
    lane = lax.broadcasted_iota(jnp.int32, (1, WIDTH), 1)
    for h in range(target.shape[0]):
        own = (lane >= h * HEAD_DIM) & (lane < (h + 1) * HEAD_DIM)
        target[h] = rows * jnp.where(own, 1.0, 0.0).astype(bf16)


def fetch(step, pair_refs, starts, pair_sc):
    for ref, (begin, end) in zip(pair_refs, starts):
        @pl.when((step >= begin) & (step < end))
        def take(ref=ref):
            pair_sc[...] = ref[...]


def forward_kernel(
    starts, came_ref, first_ref, second_ref, third_ref, fourth_ref, key_docs_ref, query_docs_ref,
    out_ref, turned_ref, total_ref, query_sc, flat_sc, pair_sc, top_sc, sum_sc, acc_sc,
):
    step = pl.program_id(0)
    heads, queries = query_sc.shape[:2]
    half = out_ref.shape[1]

    @pl.when(step == 0)
    def start():
        gather_pairs(came_ref, flat_sc)
        spread_heads(flat_sc[...], query_sc)
        top_sc[...] = jnp.full(top_sc.shape, -1e30, f32)
        sum_sc[...] = jnp.zeros(sum_sc.shape, f32)
        acc_sc[...] = jnp.zeros(acc_sc.shape, f32)

    fetch(step, (first_ref, second_ref, third_ref, fourth_ref), starts, pair_sc)
    key_part = pair_sc[:, :WIDTH]
    value_turned = pair_sc[:, WIDTH:].T
    allowed = key_column(key_docs_ref, step) == query_docs_ref[...]
    old = [top_sc[h : h + 1] for h in range(heads)]
    raw = [dot_nt(key_part, query_sc[h]) for h in range(heads)]
    scores = [jnp.where(allowed, value, -1e30) for value in raw]
    new = [jnp.maximum(o, jnp.max(v, axis=0, keepdims=True)) for o, v in zip(old, scores)]
    exponent = [jnp.exp(v - n) for v, n in zip(scores, new)]
    terms = [
        dot(value_turned[h * HEAD_DIM : (h + 1) * HEAD_DIM], exponent[h].astype(bf16))
        for h in range(heads)
    ]
    sums = [jnp.sum(v, axis=0, keepdims=True) for v in exponent]
    for h in range(heads):
        rows = pl.ds(h * HEAD_DIM, HEAD_DIM)
        fade = jnp.exp(old[h] - new[h])
        top_sc[h : h + 1] = new[h]
        sum_sc[h : h + 1] = sum_sc[h : h + 1] * fade + sums[h]
        acc_sc[rows] = acc_sc[rows] * fade + terms[h]

    @pl.when(step == pl.num_programs(0) - 1)
    def finish():
        total_ref[...] = jnp.zeros(total_ref.shape, f32)
        for h in range(heads):
            rows = pl.ds(h * HEAD_DIM, HEAD_DIM)
            turned_ref[rows] = acc_sc[rows] / sum_sc[h : h + 1]
            total_ref[h : h + 1] = top_sc[h : h + 1] + jnp.log(sum_sc[h : h + 1])
        whole = turned_ref[...].astype(bf16).T
        for slot in range(8):
            for part in range(2):
                begin = (slot * 2 + part) * half
                out_ref[slot, :, pl.ds(part * WIDTH, WIDTH)] = whole[begin : begin + half]


def pair_specs(pairs, chunk):
    specs, starts, begin = [], [], 0
    for pair in pairs:
        count = pair.shape[0] // chunk
        specs.append(
            pl.BlockSpec(
                (chunk, 2 * WIDTH),
                lambda i, begin=begin, count=count: (jnp.clip(i - begin, 0, count - 1), 0),
            )
        )
        starts.append((begin, begin + count))
        begin += count
    return specs, starts, begin


def attend(came, pairs, key_docs, query_docs):
    slots, half, columns = came.shape
    queries = slots * 2 * half
    heads = WIDTH // HEAD_DIM
    chunk = 512
    specs, starts, steps = pair_specs(pairs, chunk)
    outs = (
        result((slots, half, columns), bf16, True),
        result((WIDTH, queries), f32),
        result((8, queries), f32),
    )
    return pl.pallas_call(
        partial(forward_kernel, starts),
        grid=(steps,),
        out_shape=outs,
        in_specs=[
            whole_spec(came.shape),
            *specs,
            whole_spec(key_docs.shape),
            whole_spec(query_docs.shape),
        ],
        out_specs=tuple(whole_spec(o.shape) for o in outs),
        scratch_shapes=[
            pltpu.VMEM((heads, queries, WIDTH), bf16),
            pltpu.VMEM((queries, WIDTH), bf16),
            pltpu.VMEM((chunk, 2 * WIDTH), bf16),
            pltpu.VMEM((8, queries), f32),
            pltpu.VMEM((8, queries), f32),
            pltpu.VMEM((WIDTH, queries), f32),
        ],
        compiler_params=pltpu.CompilerParams(vmem_limit_bytes=48 << 20),
    )(*map(hbm, (came, *pairs, key_docs, query_docs)))


def backward_kernel(
    starts, came_ref, grad_ref, first_ref, second_ref, third_ref, fourth_ref, key_docs_ref, query_docs_ref,
    turned_ref, total_ref, query_out, keep_ref, keep_other, send_ref,
    query_sc, grad_sc, flat_sc, pair_sc, delta_sc, acc_sc,
):
    step = pl.program_id(0)
    heads, queries = query_sc.shape[:2]
    half = query_out.shape[1]

    @pl.when(step == 0)
    def start():
        gather_pairs(came_ref, flat_sc)
        spread_heads(flat_sc[...], query_sc)
        gather_pairs(grad_ref, flat_sc)
        spread_heads(flat_sc[...], grad_sc)
        acc_sc[...] = jnp.zeros(acc_sc.shape, f32)
        product = flat_sc[...].T.astype(f32) * turned_ref[...]
        for h in range(heads):
            rows = slice(h * HEAD_DIM, (h + 1) * HEAD_DIM)
            delta_sc[h : h + 1] = jnp.sum(product[rows], axis=0, keepdims=True)

    fetch(step, (first_ref, second_ref, third_ref, fourth_ref), starts, pair_sc)
    key_part = pair_sc[:, :WIDTH]
    value_part = pair_sc[:, WIDTH:]
    key_turned = key_part.T
    allowed = key_column(key_docs_ref, step) == query_docs_ref[...]
    raw = [dot_nt(key_part, query_sc[h]) for h in range(heads)]
    slopes = [dot_nt(value_part, grad_sc[h]) for h in range(heads)]
    probabilities = [
        jnp.exp(jnp.where(allowed, value, -1e30) - total_ref[h : h + 1])
        for h, value in enumerate(raw)
    ]
    grad_scores = [
        (p * (slope - delta_sc[h : h + 1])).astype(bf16)
        for h, (p, slope) in enumerate(zip(probabilities, slopes))
    ]
    grad_value = sum(dot(probabilities[h].astype(bf16), grad_sc[h]) for h in range(heads))
    grad_key = sum(dot(grad_scores[h], query_sc[h]) for h in range(heads))
    for h in range(heads):
        rows = pl.ds(h * HEAD_DIM, HEAD_DIM)
        acc_sc[rows] = acc_sc[rows] + dot(
            key_turned[h * HEAD_DIM : (h + 1) * HEAD_DIM], grad_scores[h]
        )
    quarter = pl.num_programs(0) // 4
    middle = 2 * quarter

    for number, ref in enumerate((keep_ref, keep_other)):
        @pl.when((step >= number * quarter) & (step < (number + 1) * quarter))
        def mine(ref=ref):
            ref[:, pl.ds(0, WIDTH)] = grad_key
            ref[:, pl.ds(WIDTH, WIDTH)] = grad_value

    @pl.when(step >= middle)
    def theirs():
        send_ref[:, pl.ds(0, WIDTH)] = grad_key.astype(bf16)
        send_ref[:, pl.ds(WIDTH, WIDTH)] = grad_value.astype(bf16)

    @pl.when(step == pl.num_programs(0) - 1)
    def finish():
        whole = (acc_sc[...] * HEAD_DIM ** (-0.5)).astype(bf16).T
        for slot in range(8):
            for part in range(2):
                begin = (slot * 2 + part) * half
                query_out[slot, :, pl.ds(part * WIDTH, WIDTH)] = whole[begin : begin + half]


def attend_back(came, grad, pairs, key_docs, query_docs, turned, total):
    slots, half, columns = came.shape
    queries = slots * 2 * half
    heads = WIDTH // HEAD_DIM
    chunk = 512
    specs, starts, steps = pair_specs(pairs, chunk)
    quarter = steps // 4
    middle = 2 * quarter
    return pl.pallas_call(
        partial(backward_kernel, starts),
        grid=(steps,),
        out_shape=(
            jax.ShapeDtypeStruct((slots, half, columns), bf16),
            jax.ShapeDtypeStruct((quarter * chunk, columns), f32),
            jax.ShapeDtypeStruct((quarter * chunk, columns), f32),
            jax.ShapeDtypeStruct((middle * chunk, columns), bf16),
        ),
        in_specs=[
            whole_spec(came.shape),
            whole_spec(grad.shape),
            *specs,
            whole_spec(key_docs.shape),
            whole_spec(query_docs.shape),
            whole_spec(turned.shape),
            whole_spec(total.shape),
        ],
        out_specs=(
            whole_spec((slots, half, columns)),
            pl.BlockSpec((chunk, columns), lambda i: (jnp.minimum(i, quarter - 1), 0)),
            pl.BlockSpec((chunk, columns), lambda i: (jnp.clip(i - quarter, 0, quarter - 1), 0)),
            pl.BlockSpec((chunk, columns), lambda i: (jnp.maximum(i - middle, 0), 0)),
        ),
        scratch_shapes=[
            pltpu.VMEM((heads, queries, WIDTH), bf16),
            pltpu.VMEM((heads, queries, WIDTH), bf16),
            pltpu.VMEM((queries, WIDTH), bf16),
            pltpu.VMEM((chunk, 2 * WIDTH), bf16),
            pltpu.VMEM((8, queries), f32),
            pltpu.VMEM((WIDTH, queries), f32),
        ],
        compiler_params=pltpu.CompilerParams(vmem_limit_bytes=48 << 20),
    )(*map(hbm, (came, grad, *pairs, key_docs, query_docs, turned, total)))


def settle_kernel(
    later_hbm, out_ref, up_ref, down_ref, block_sc, out_sc, up_sc, down_sc, sems, out_sems
):
    width = out_ref.shape[1]
    copies = [
        pltpu.make_async_copy(later_hbm.at[:, j], block_sc.at[j], sems.at[j]) for j in range(9)
    ]
    for copy in copies:
        copy.start()
    leaving = []
    for j in range(9):
        copies[j].wait()
        for i in range(32):
            value = block_sc[j, i]
            if j == 0:
                out_sc[pl.ds(i * 24, 24), :] = value
            elif j < 5:
                up_sc[pl.ds(i * 24, 24), pl.ds((j - 1) * width, width)] = value
            else:
                down_sc[pl.ds(i * 96 + (j - 5) * 24, 24), :] = value
        if j == 0:
            leaving.append(pltpu.make_async_copy(out_sc, out_ref, out_sems.at[j]))
        elif j < 5:
            columns = pl.ds((j - 1) * width, width)
            leaving.append(
                pltpu.make_async_copy(up_sc.at[:, columns], up_ref.at[:, columns], out_sems.at[j])
            )
        elif j == 8:
            leaving.append(pltpu.make_async_copy(down_sc, down_ref, out_sems.at[j]))
        if j < 5 or j == 8:
            leaving[-1].start()
    for copy in leaving:
        copy.wait()


def settle(later):
    width = later.shape[-1]
    shapes = ((width, width), (width, 4 * width), (4 * width, width))
    return pl.pallas_call(
        settle_kernel,
        out_shape=tuple(result(shape, bf16) for shape in shapes),
        in_specs=[ANY],
        out_specs=(ANY,) * 3,
        scratch_shapes=[
            pltpu.VMEM((9, 32, 24, width), bf16),
            *(pltpu.VMEM(shape, bf16) for shape in shapes),
            pltpu.SemaphoreType.DMA((9,)),
            pltpu.SemaphoreType.DMA((9,)),
        ],
        compiler_params=pltpu.CompilerParams(vmem_limit_bytes=40 << 20),
    )(hbm(later))


def middle_kernel(
    came_ref, x_ref, teacher_ref, mask_ref, mod_ref, gains_ref, up_bias_ref,
    out_hbm, up_hbm, down_hbm,
    final_ref, hidden_ref, leave_ref, pack_ref, sums_ref, out_sc, up_sc, down_sc, slope_sc, sems,
):
    seqs, tokens, width = x_ref.shape
    units = up_sc.shape[1]
    rows = seqs * tokens
    half = tokens // 2
    parts = [pl.ds(f * width, width) for f in range(units // width)]
    copies = [pltpu.make_async_copy(out_hbm, out_sc, sems.at[0])]
    for f, part in enumerate(parts):
        copies.append(
            pltpu.make_async_copy(up_hbm.at[:, part], up_sc.at[:, part], sems.at[1 + 2 * f])
        )
        copies.append(
            pltpu.make_async_copy(down_hbm.at[part, :], down_sc.at[part, :], sems.at[2 + 2 * f])
        )
    for copy in copies:
        copy.start()
    masks = mask_ref[...].T

    def wide(index):
        return jnp.concatenate(
            [
                jnp.broadcast_to(
                    mod_ref[s : s + 1, pl.ds(index * width, width)], (tokens, width)
                )
                for s in range(seqs)
            ]
        )

    def add_rows(first, value):
        for s in range(seqs):
            sums_ref[first + s : first + s + 1] = jnp.sum(
                value[s * tokens : (s + 1) * tokens], axis=0, keepdims=True
            )

    for s in range(seqs):
        for g in range(GROUPS):
            left, right = load_pairs(came_ref, s * GROUPS + g, 0, half)
            columns = pl.ds(g * WIDTH, WIDTH)
            pack_ref[pl.ds(s * tokens, half), columns] = left
            pack_ref[pl.ds(s * tokens + half, half), columns] = right
    mixed = pack_ref[:, pl.ds(0, width)]
    residual = jnp.concatenate([x_ref[s].astype(f32) for s in range(seqs)])
    copies[0].wait()
    branch = dot(mixed, out_sc[...])
    hidden = residual + wide(2) * branch
    normed, inverse = normalize(hidden)
    scaled = normed * gains_ref[1:2]
    moved = (scaled * (1.0 + wide(4)) + wide(3)).astype(bf16)
    pack_ref[:, pl.ds(width, width)] = moved
    lower = None
    for f in range(units // width):
        columns = pl.ds(f * width, width)
        copies[1 + 2 * f].wait()
        u = dot(moved, up_sc[:, columns]) + up_bias_ref[0:1, columns]
        square = u * u
        t = jnp.tanh(0.7978845608028654 * (u + 0.044715 * u * square))
        active = (0.5 * u * (1.0 + t)).astype(bf16)
        slope_sc[:, columns] = 0.5 * (1.0 + t) + 0.5 * u * (1.0 - t * t) * 0.7978845608028654 * (
            1.0 + 0.134145 * square
        )
        pack_ref[:, pl.ds(2 * width + f * width, width)] = active
        copies[2 + 2 * f].wait()
        term = dot(active, down_sc[columns, :])
        lower = term if lower is None else lower + term
    lower = lower + gains_ref[2:3]
    gate = wide(5)
    final = hidden + gate * lower
    for s in range(seqs):
        final_ref[s] = final[s * tokens : (s + 1) * tokens].astype(bf16)
    teacher = jnp.concatenate([teacher_ref[s].astype(f32) for s in range(seqs)])
    mismatch = final - teacher
    sums_ref[14:15] = jnp.sum(
        masks[:, 0:1] * mismatch * mismatch, axis=0, keepdims=True
    )
    sums_ref[15:16] = jnp.zeros((1, width), f32)
    grad_final = masks[:, 1:2] * mismatch
    add_rows(6, grad_final * lower)
    grad_lower = (gate * grad_final).astype(bf16)
    base = 2 * width + units
    pack_ref[:, pl.ds(base + width + units, width)] = grad_lower
    sums_ref[9:10] = jnp.sum(grad_lower.astype(f32), axis=0, keepdims=True)
    grad_moved = None
    for f in range(units // width):
        columns = pl.ds(f * width, width)
        grad_active = dot_nt(grad_lower, down_sc[columns, :])
        grad_upper = (grad_active * slope_sc[:, columns]).astype(bf16)
        pack_ref[:, pl.ds(base + width + f * width, width)] = grad_upper
        sums_ref[10 + f : 11 + f] = jnp.sum(grad_upper.astype(f32), axis=0, keepdims=True)
        term = dot_nt(grad_upper, up_sc[:, columns])
        grad_moved = term if grad_moved is None else grad_moved + term
    add_rows(2, grad_moved)
    add_rows(4, grad_moved * scaled)
    grad_scaled = grad_moved * (1.0 + wide(4))
    sums_ref[8:9] = jnp.sum(grad_scaled * normed, axis=0, keepdims=True)
    grad_hidden = grad_final + norm_back(grad_scaled * gains_ref[1:2], normed, inverse)
    hidden_ref[...] = grad_hidden
    add_rows(0, grad_hidden * branch)
    grad_branch = (wide(2) * grad_hidden).astype(bf16)
    pack_ref[:, pl.ds(base, width)] = grad_branch
    grad_mixed = dot_nt(grad_branch, out_sc[...]).astype(bf16)
    for s in range(seqs):
        for g in range(GROUPS):
            piece = grad_mixed[s * tokens : (s + 1) * tokens, g * WIDTH : (g + 1) * WIDTH]
            leave_ref[s * GROUPS + g, :, pl.ds(0, WIDTH)] = piece[:half]
            leave_ref[s * GROUPS + g, :, pl.ds(WIDTH, WIDTH)] = piece[half:]


def middle(came, inputs, teacher, masks, modulation, gains, up_bias, weights):
    seqs, tokens, width = inputs.shape
    units = up_bias.shape[1]
    rows = seqs * tokens
    return single(
        middle_kernel,
        [
            ((seqs, tokens, width), bf16),
            ((rows, width), f32),
            (came.shape, bf16, True),
            ((rows, 4 * width + 2 * units), bf16, True),
            ((16, width), f32),
        ],
        [came, inputs, teacher, masks, modulation, gains, up_bias],
        raw=[hbm(w) for w in weights],
        scratch=[
            pltpu.VMEM((width, width), bf16),
            pltpu.VMEM((width, units), bf16),
            pltpu.VMEM((units, width), bf16),
            pltpu.VMEM((rows, units), f32),
            pltpu.SemaphoreType.DMA((9,)),
        ],
        limit=40,
    )


def weights_kernel(
    place_ref, own_ref, other_ref, *refs
):
    *groups, left_sc, right_sc, block_sc, sems = refs
    rows, width = own_ref.shape[0], block_sc.shape[-1]
    units = 4 * width
    hc = place_ref[1]
    base = 2 * width + units
    for which, ref in enumerate((own_ref, other_ref)):
        left_sc[:, pl.ds(which * rows, rows)] = ref[:, pl.ds(0, base)].T
        right_sc[pl.ds(which * rows, rows), :] = ref[:, pl.ds(base, base)]
    for hx in range(2):
        begin = pl.multiple_of(hx * 384 + hc * 192, 64)
        for j in range(5):
            offset = 0 if j == 0 else width
            value = dot(left_sc[pl.ds(begin + offset, 192), :], right_sc[:, pl.ds(j * width, width)])
            for i in range(8):
                block_sc[hx * 8 + i, j] = value[i * 24 : (i + 1) * 24].astype(bf16)
        begin = pl.multiple_of(2 * width + hx * 1536 + hc * 768, 256)
        value = dot(left_sc[pl.ds(begin, 768), :], right_sc[:, pl.ds(width + units, width)])
        for i in range(8):
            for j in range(4):
                first = i * 96 + j * 24
                block_sc[hx * 8 + i, 5 + j] = value[first : first + 24].astype(bf16)
    copies = []
    begin = 0
    for number, (_, side) in enumerate(COLUMN_GROUPS):
        keep, send = groups[2 * number : 2 * number + 2]
        columns = pl.ds(begin, keep.shape[-1])
        copies += piece_copies(place_ref, block_sc, keep, send, sems.at[number], side, columns)
        begin += keep.shape[-1]
    for copy in copies:
        copy.wait()


def weight_terms(here, own, other, width):
    rows, total = own.shape
    return single(
        weights_kernel,
        [((2, 4, 9, 24, 128 * size), bf16) for size, _ in COLUMN_GROUPS for _ in range(2)],
        [],
        held=[own, other],
        scratch=[
            pltpu.VMEM((total // 2, 2 * rows), bf16),
            pltpu.VMEM((2 * rows, total // 2), bf16),
            pltpu.VMEM((16, 9, 24, width), bf16),
            pltpu.SemaphoreType.DMA((len(COLUMN_GROUPS), 16)),
        ],
        limit=40,
        place=here,
        raw_outs=2 * len(COLUMN_GROUPS),
    )


def flat_rows(home_ref, target, first_row, seqs, tokens, width):
    half = tokens // 2
    for s in range(seqs):
        for g in range(GROUPS):
            slot = s * GROUPS + g
            row = first_row + s * tokens
            left, right = load_pairs(home_ref, slot, tokens, half)
            target[pl.ds(row, half), pl.ds(g * WIDTH, WIDTH)] = left
            target[pl.ds(row + half, half), pl.ds(g * WIDTH, WIDTH)] = right
            left, right = load_pairs(home_ref, slot, 0, tokens)
            target[pl.ds(row, tokens), pl.ds(width + g * WIDTH, WIDTH)] = left
            target[pl.ds(row, tokens), pl.ds(2 * width + g * WIDTH, WIDTH)] = right


def qkv_kernel(
    seqs, place_ref, entered_ref, entered_other, home_ref, home_other,
    keep_a, send_a, keep_b, send_b, left_sc, right_sc, block_sc, sems,
):
    rows, width = entered_ref.shape
    hc = place_ref[1]
    for which, (left, home) in enumerate(((entered_ref, home_ref), (entered_other, home_other))):
        left_sc[:, pl.ds(which * rows, rows)] = left[...].T
        flat_rows(home, right_sc, which * rows, seqs, rows // seqs, width)
    for hx in range(2):
        begin = pl.multiple_of(hx * 384 + hc * 192, 64)
        for j in range(3):
            value = dot(left_sc[pl.ds(begin, 192), :], right_sc[:, pl.ds(j * width, width)])
            for i in range(8):
                block_sc[hx * 8 + i, :, pl.ds(j * width, width)] = value[
                    i * 24 : (i + 1) * 24
                ].astype(bf16)
    half = 3 * width // 2
    copies = piece_copies(place_ref, block_sc, keep_a, send_a, sems.at[0], 0, pl.ds(0, half))
    copies += piece_copies(place_ref, block_sc, keep_b, send_b, sems.at[1], 1, pl.ds(half, half))
    for copy in copies:
        copy.wait()


def qkv_terms(here, seqs, *values):
    rows, width = values[0].shape
    return single(
        partial(qkv_kernel, seqs),
        [((2, 4, 24, 3 * width // 2), bf16)] * 4,
        values,
        scratch=[
            pltpu.VMEM((width, 2 * rows), bf16),
            pltpu.VMEM((2 * rows, 3 * width), bf16),
            pltpu.VMEM((16, 24, 3 * width), bf16),
            pltpu.SemaphoreType.DMA((2, 16)),
        ],
        place=here,
        raw_outs=4,
    )


def leave_kernel(
    home_ref, x_ref, hidden_ref, mod_ref, gains_ref, weight_ref, middle_ref,
    grad_ref, small_ref, flat_ref,
):
    seqs, tokens, width = x_ref.shape
    devices = small_ref.shape[0]
    flat_rows(home_ref, flat_ref, 0, seqs, tokens, width)
    grad_entered = None
    for which in range(3):
        columns = pl.ds(which * width, width)
        term = dot_nt(flat_ref[:, columns], weight_ref[:, columns])
        grad_entered = term if grad_entered is None else grad_entered + term
    gain_sum = None
    sums = []
    for s in range(seqs):
        normed, inverse = normalize(x_ref[s].astype(f32))
        rows = slice(s * tokens, (s + 1) * tokens)
        grad = grad_entered[rows]
        shift_sum = jnp.sum(grad, axis=0, keepdims=True)
        scale_sum = jnp.sum(grad * (normed * gains_ref[0:1]), axis=0, keepdims=True)
        grad_scaled = grad * (1.0 + mod_ref[s : s + 1, pl.ds(width, width)])
        term = jnp.sum(grad_scaled * normed, axis=0, keepdims=True)
        gain_sum = term if gain_sum is None else gain_sum + term
        grad_ref[s] = hidden_ref[rows] + norm_back(grad_scaled * gains_ref[0:1], normed, inverse)
        later = [middle_ref[i + s : i + s + 1] for i in (0, 2, 4, 6)]
        sums.append(jnp.concatenate([shift_sum, scale_sum, *later], axis=1))
    up_bias = jnp.concatenate([middle_ref[i : i + 1] for i in range(10, 14)], axis=1)
    fields = [*sums, gain_sum, middle_ref[8:9], up_bias, middle_ref[9:10]]
    error = jnp.sum(middle_ref[14:15], axis=1, keepdims=True)
    small_ref[...] = jnp.zeros(small_ref.shape, f32)
    begin = 0
    for field in fields:
        size = field.shape[1] // devices
        for i in range(devices):
            small_ref[i, :, pl.ds(begin, size)] = field[:, i * size : (i + 1) * size]
        begin += size
    small_ref[:, :, pl.ds(begin, 1)] = jnp.broadcast_to(error[None], (devices, 1, 1))


def leave(home, inputs, grad_hidden, modulation, gains, weight, sums, devices):
    seqs, tokens, width = inputs.shape
    return single(
        leave_kernel,
        [
            ((seqs, tokens, width), f32),
            ((devices, 1, 512), f32, True),
            ((seqs * tokens, 3 * width), bf16),
        ],
        [home, inputs, grad_hidden, modulation, gains, weight, sums],
    )


def unpack_kernel(
    parts, sizes, factor, place_ref, every_ref, valid_ref,
    mod_ref, gains_ref, up_ref, key_docs_ref, query_docs_ref, masks_ref,
):
    devices = every_ref.shape[0]
    seqs, tokens = valid_ref.shape
    size_mod, size_gain, size_up = sizes
    mod_ref[...] = jnp.zeros(mod_ref.shape, f32)
    gains_ref[...] = jnp.zeros(gains_ref.shape, f32)
    up_ref[...] = jnp.zeros(up_ref.shape, f32)
    begin = 0
    targets = [(mod_ref, s, size_mod) for s in range(seqs)]
    targets += [(gains_ref, 0, size_gain), (gains_ref, 1, size_gain)]
    targets += [(up_ref, 0, size_up), (gains_ref, 2, size_gain)]
    for target, row, size in targets:
        for i in range(devices):
            target[row : row + 1, pl.ds(i * size, size)] = every_ref[i, :, pl.ds(begin, size)]
        begin += size
    hx, hc, sz, sy, rb = (place_ref[i] for i in range(5))
    second = sz * 2 + sy >= GROUPS
    row = 0
    for core in range(2):
        for across in range(2):
            for part in range(parts):
                block = ((hx ^ across) * 2 + (hc ^ core)) * parts + part
                for spot in range(8):
                    line = every_ref[block * 8 + spot, :, pl.ds(begin, 2 * tokens)]
                    key_docs_ref[row : row + 1, pl.ds(spot * tokens, tokens)] = jnp.where(
                        second, line[:, tokens:], line[:, :tokens]
                    )
                row += 1
    for spot in range(8):
        line = every_ref[((hx * 2 + hc) * parts + rb) * 8 + spot, :, pl.ds(begin, 2 * tokens)]
        query_docs_ref[:, pl.ds(spot * tokens, tokens)] = jnp.where(
            second, line[:, tokens:], line[:, :tokens]
        )
    begin += 2 * tokens
    count = jnp.sum(every_ref[:, :, pl.ds(begin, 1)], axis=0)
    gains_ref[3:4, pl.ds(0, 1)] = count
    masks_ref[...] = jnp.zeros(masks_ref.shape, f32)
    for s in range(seqs):
        valid = valid_ref[s : s + 1, :].astype(f32)
        masks_ref[0:1, pl.ds(s * tokens, tokens)] = valid
        masks_ref[1:2, pl.ds(s * tokens, tokens)] = valid * (factor / count)


def unpack(here, every, valid_mask, width, units, parts, length):
    seqs, tokens = valid_mask.shape
    devices = every.shape[0]
    sizes = (6 * width // devices, width // devices, units // devices)
    return single(
        partial(unpack_kernel, parts, sizes, float(seqs * length)),
        [
            ((8, 6 * width), f32),
            ((8, width), f32),
            ((8, units), f32),
            ((4 * parts, 8 * tokens), f32),
            ((1, 8 * tokens), f32),
            ((8, seqs * tokens), f32),
        ],
        [every, valid_mask],
        place=here,
    )


def finish_kernel(width, small_ref, embed_ref, gains_ref, *refs):
    ada_ref, bias_ref, *vectors, loss_ref = refs
    seqs = embed_ref.shape[0]
    columns = ada_ref.shape[0]
    added = jnp.sum(small_ref[...], axis=0)
    begin = 0
    ada = bias = None
    for s in range(seqs):
        grad = added[:, begin : begin + columns]
        begin += columns
        turned = jnp.broadcast_to(grad, (8, columns)).T[:, 0:1]
        term = turned * embed_ref[s : s + 1, :]
        ada = term if ada is None else ada + term
        bias = grad if bias is None else bias + grad
    ada_ref[...] = ada
    bias_ref[...] = bias
    for ref in vectors:
        size = ref.shape[1]
        ref[...] = added[:, begin : begin + size]
        begin += size
    loss_ref[...] = added[:, begin : begin + 1] / (gains_ref[3:4, 0:1] * width)


def finish(small, time_embed, gains, width, units):
    devices = small.shape[0]
    sizes = [6 * width // devices] + [size // devices for size in (width, width, units, width)]
    return single(
        partial(finish_kernel, float(width)),
        [((sizes[0], time_embed.shape[1]), f32)]
        + [((1, size), f32, True) for size in sizes]
        + [((1, 1), f32, True)],
        [small, time_embed, gains],
    )


def grads_kernel(total_ref, first_ref, second_ref, third_ref, *refs):
    qkv_total, qkv_first, qkv_second, qkv_third, out_ref, up_ref, down_ref, qkv_ref = refs
    width = out_ref.shape[1]
    for j in range(9):
        value = total_ref[0, j]
        for ref in (first_ref, second_ref, third_ref):
            value = value + ref[j].astype(f32)
        if j == 0:
            out_ref[...] = value
        elif j < 5:
            up_ref[:, pl.ds((j - 1) * width, width)] = value
        else:
            down_ref[pl.ds((j - 5) * 24, 24), :] = value
    value = qkv_total[0]
    for ref in (qkv_first, qkv_second, qkv_third):
        value = value + ref[...].astype(f32)
    qkv_ref[...] = value


def weight_grads(total, third, qkv_total, third_qkv):
    width = total.shape[-1]
    values = [total, *third, qkv_total, *third_qkv]
    specs = [
        pl.BlockSpec((1,) + v.shape[1:], lambda i, n=v.ndim: (0,) * n)
        if i in (0, 4)
        else whole_spec(v.shape)
        for i, v in enumerate(values)
    ]
    shapes = ((24, width), (24, 4 * width), (96, width), (24, 3 * width))
    return pl.pallas_call(
        grads_kernel,
        grid=(1,),
        out_shape=tuple(jax.ShapeDtypeStruct(shape, f32) for shape in shapes),
        in_specs=specs,
        out_specs=tuple(whole_spec(shape) for shape in shapes),
        compiler_params=pltpu.CompilerParams(vmem_limit_bytes=40 << 20),
    )(*values)


def begin_kernel(embed_ref, ada_ref, vectors_ref, segments_ref, valid_ref, *refs):
    *weights, packed_ref = refs[:-1] if len(refs) > 1 else refs
    seqs, tokens = segments_ref.shape
    modulation = lax.dot_general(
        embed_ref[...],
        ada_ref[...].astype(f32),
        (((1,), (1,)), ((), ())),
        precision=precise,
        preferred_element_type=f32,
    )
    size = modulation.shape[1]
    vectors = vectors_ref[...].astype(f32)
    modulation = modulation + vectors[:, :size]
    count = jnp.sum(valid_ref[...].astype(f32), axis=1, keepdims=True)
    count = jnp.sum(count, axis=0, keepdims=True)
    fields = [modulation[s : s + 1] for s in range(seqs)]
    fields.append(vectors[:, size:])
    fields += [segments_ref[s : s + 1, :].astype(f32) for s in range(seqs)]
    fields.append(count)
    fields.append(jnp.zeros((1, packed_ref.shape[2] - sum(f.shape[1] for f in fields)), f32))
    packed_ref[...] = jnp.broadcast_to(
        jnp.concatenate(fields, axis=1)[None], packed_ref.shape
    )
    if weights:
        out_ref, up_ref, down_ref = weights
        later_ref = refs[-1]
        width = out_ref.shape[1]
        later_ref[0] = out_ref[...]
        for j in range(4):
            later_ref[1 + j] = up_ref[:, pl.ds(j * width, width)]
            later_ref[5 + j] = down_ref[pl.ds(j * 24, 24), :]


def begin_with(time_embed, ada_weight, vectors, segments, valid_mask, weights, devices):
    seqs, tokens = segments.shape
    columns = (seqs - 1) * ada_weight.shape[1] + vectors.shape[1] + seqs * tokens + 1
    outs = [((devices, 1, columns + -columns % 128), f32, True)]
    if weights:
        outs.append(((9, 24, weights[0].shape[1]), bf16))
    return single(
        begin_kernel, outs, [time_embed, ada_weight.T, vectors, segments, valid_mask, *weights]
    )


def after(value, *others):
    return lax.optimization_barrier((value, others))[0]


def exchange(rows):
    return lax.all_to_all(rows, SPOT, 0, 0, tiled=True)


def on_device(
    inputs,
    time_embed,
    segments,
    valid_mask,
    teacher,
    ada_weight,
    ada_bias,
    gain_attn,
    qkv_weight,
    out_weight,
    gain_mlp,
    up_weight,
    up_bias,
    down_weight,
    down_bias,
):
    seqs, tokens, width = inputs.shape
    units = up_weight.shape[1]
    parts = lax.axis_size("rb")
    devices = 32 * parts
    length = tokens * devices
    queries = 8 * tokens
    here = place()

    vectors = [ada_bias, gain_attn, gain_mlp, up_bias, down_bias]
    vectors = jnp.concatenate([v.astype(f32) for v in vectors]).reshape(1, -1)
    weights = [] if parts > 1 else [out_weight, up_weight, down_weight]
    packed, *later = begin_with(
        time_embed, ada_weight, vectors, segments, valid_mask, weights, devices
    )
    every = lax.all_to_all(packed, EVERY, 0, 0, tiled=True)
    if parts > 1:
        sides, *later = (
            lax.all_gather(w, EVERY, axis=0, tiled=True)
            for w in (qkv_weight, out_weight, up_weight, down_weight)
        )
    else:
        later = [lax.all_gather(later[0], EVERY, axis=0, tiled=False)]
        shard, packed = lax.optimization_barrier((qkv_weight, packed))

    def use(every):
        return unpack(here, every, valid_mask, width, units, parts, length)

    if parts > 1:
        sides = [sides]
        used = use(every)
    else:
        sides, used = gather_rows(here, shard, every, use)
    modulation, gains, full_up_bias, key_docs, query_docs, masks = used

    entered, pair, query, full_qkv = enter(here, inputs, modulation, gains, sides)
    pair = exchange(pair).reshape(queries, 2 * WIDTH)
    query = exchange(query)
    if parts > 1:
        pair = lax.all_gather(pair, "rb", axis=0, tiled=True)
    pair_x = swap(pair, "hx")
    pair_x, query = lax.optimization_barrier((pair_x, query))
    pairs = (pair, pair_x, swap(pair, "hc"), swap(pair_x, "hc"))
    attended, turned, total = attend(query, pairs, key_docs, query_docs)

    if parts == 1:
        later = settle(later[0])
    final, grad_hidden, grad_leaving, pack, sums = middle(
        exchange(attended), inputs, teacher, masks, modulation, gains, full_up_bias, later
    )
    grad_came = exchange(grad_leaving)
    if parts == 1:
        terms = weight_terms(here, pack, swap(pack, "hc"), width)
        grad_came, terms = lax.optimization_barrier((grad_came, terms))
        held = terms[::2]
        firsts = [
            swap(send, ORDERS[side][0]) for send, (_, side) in zip(terms[1::2], COLUMN_GROUPS)
        ]

    grad_query, keep, keep_x, send = attend_back(
        query, grad_came, pairs, key_docs, query_docs, turned, total
    )
    if parts == 1:
        send, firsts[0], firsts[2] = lax.optimization_barrier((send, firsts[0], firsts[2]))
    recv = swap(send, "hc")
    own_rows = keep.shape[0]
    send_x = (keep_x + recv[own_rows:].astype(f32)).astype(bf16)
    grad_pair = keep + recv[:own_rows].astype(f32) + swap(send_x, "hx").astype(f32)
    if parts > 1:
        grad_pair = lax.psum_scatter(grad_pair, "rb", scatter_dimension=0, tiled=True)
    home = jnp.concatenate(
        [grad_pair.astype(bf16).reshape(8, tokens, 2 * WIDTH), grad_query], axis=1
    )
    if parts == 1:
        home, firsts[1] = lax.optimization_barrier((home, firsts[1]))
        seconds = [
            swap(
                jnp.concatenate(
                    [
                        second_send(keep, recv)
                        for keep, recv, (_, own) in zip(held, firsts, COLUMN_GROUPS)
                        if own == side
                    ],
                    axis=3,
                ),
                ORDERS[side][1],
            )
            for side in (0, 1)
        ]
    home = exchange(home)
    if parts == 1:
        others = swap(entered, "hc"), swap(home, "hc")
        terms = qkv_terms(here, seqs, entered, others[0], home, others[1])
        seconds = after(seconds, terms)
        recvs = [swap(send, order[0]) for send, order in zip(terms[1::2], ORDERS)]
        grad_input, small, flat = leave(
            after(home, terms), inputs, grad_hidden, modulation, gains, full_qkv, sums, devices
        )
        recvs = after(recvs, small)
        nexts = [second_send(keep, recv) for keep, recv in zip(terms[::2], recvs)]
        small = after(small, nexts)
        next_recvs = [swap(value, order[1]) for value, order in zip(nexts, ORDERS)]
        totals = [
            jnp.concatenate(
                [
                    keep[0].astype(f32) + recv[0].astype(f32)
                    for keep, recv, (_, own) in zip(held, firsts, COLUMN_GROUPS)
                    if own == side
                ],
                axis=3,
            )
            + seconds[side].astype(f32)
            for side in (0, 1)
        ]
        second = jnp.concatenate(totals, axis=3)
        third = third_recvs(second)
        second_qkv = jnp.concatenate(
            [
                second_total(keep, recv, next_recv)
                for keep, recv, next_recv in zip(terms[::2], recvs, next_recvs)
            ],
            axis=2,
        )
        third_qkv = third_recvs(second_qkv)
        third, third_qkv = lax.optimization_barrier((third, third_qkv))
        shard_out, shard_up, shard_down, shard_qkv = weight_grads(
            second, third, second_qkv, third_qkv
        )
    if parts > 1:
        grad_input, small, flat = leave(
            home, inputs, grad_hidden, modulation, gains, full_qkv, sums, devices
        )
        base = 2 * width + units
        ends = (base + width, base + width + units)
        shard_qkv, shard_out, shard_up, shard_down = (
            lax.psum_scatter(
                jnp.einsum("tk,tn->kn", left, right, preferred_element_type=f32),
                EVERY,
                scatter_dimension=0,
                tiled=True,
            )
            for left, right in (
                (entered, flat),
                (pack[:, :width], pack[:, base : ends[0]]),
                (pack[:, width : 2 * width], pack[:, ends[0] : ends[1]]),
                (pack[:, 2 * width : base], pack[:, ends[1] :]),
            )
        )
    small = lax.all_to_all(small, EVERY, 0, 0, tiled=True)
    if parts == 1:
        small = after(small, second_qkv)
    grads = finish(small, time_embed, gains, width, units)
    loss_value = grads[6].reshape(())
    return (
        final,
        loss_value,
        grad_input,
        grads[0].T,
        grads[1].reshape(-1),
        grads[2].reshape(-1),
        shard_qkv,
        shard_out,
        grads[3].reshape(-1),
        shard_up,
        grads[4].reshape(-1),
        shard_down,
        grads[5].reshape(-1),
    )


def solution(mesh):
    blocks = mesh.shape["blk"]
    fine = Mesh(mesh.devices.reshape(2, 2, blocks // 8, 4, 2), EVERY)
    tokens = ("rb", "sz", "sy", "hx", "hc")
    return jax.shard_map(
        on_device,
        mesh=fine,
        in_specs=(
            P(None, tokens, None),
            P(),
            P(None, tokens),
            P(None, tokens),
            P(None, tokens, None),
            P(None, EVERY),
            P(EVERY),
            P(EVERY),
            P(EVERY, None),
            P(EVERY, None),
            P(EVERY),
            P(EVERY, None),
            P(EVERY),
            P(EVERY, None),
            P(EVERY),
        ),
        out_specs=(
            P(None, tokens, None),
            P(),
            P(None, tokens, None),
            P(None, EVERY),
            P(EVERY),
            P(EVERY),
            P(EVERY, None),
            P(EVERY, None),
            P(EVERY),
            P(EVERY, None),
            P(EVERY),
            P(EVERY, None),
            P(EVERY),
        ),
        check_vma=False,
    )
```

```python
from functools import partial

import jax
import jax.numpy as jnp
from jax import lax
from jax.experimental import pallas as pl
from jax.experimental.pallas import tpu as pltpu
from jax.sharding import Mesh, PartitionSpec as P

HEADS = 12
HEAD_DIM = 64
GROUPS = 4
WIDTH = HEADS // GROUPS * HEAD_DIM
EVERY = ("hx", "hc", "rb", "sz", "sy")
SPOT = ("sz", "sy")
bf16 = jnp.bfloat16
f32 = jnp.float32
precise = lax.Precision.HIGHEST


def normalize(hidden):
    average = jnp.mean(hidden, axis=-1, keepdims=True)
    centred = hidden - average
    variance = jnp.mean(centred * centred, axis=-1, keepdims=True)
    inverse = lax.rsqrt(variance + 1e-05)
    return (centred * inverse, inverse)


def dot(left, right):
    return jnp.dot(left, right, preferred_element_type=f32)


def dot_nt(left, right):
    return lax.dot_general(left, right, (((1,), (1,)), ((), ())), preferred_element_type=f32)


def norm_back(upstream, normed, inverse):
    first_mean = jnp.mean(upstream, axis=-1, keepdims=True)
    second_mean = jnp.mean(upstream * normed, axis=-1, keepdims=True)
    return inverse * (upstream - first_mean - normed * second_mean)


def swap(value, axis):
    return lax.ppermute(value, axis, [(0, 1), (1, 0)])


def turn(value, axis, step):
    size = lax.axis_size(axis)
    return lax.ppermute(value, axis, [(i, (i - step) % size) for i in range(size)])


def place():
    return jnp.stack([lax.axis_index(name) for name in ("hx", "hc", "sz", "sy", "rb")]).astype(
        jnp.int32
    )


ANY = pl.BlockSpec(memory_space=pl.ANY)
SMEM = pl.BlockSpec(memory_space=pltpu.SMEM)
VMEM = pl.BlockSpec(memory_space=pltpu.VMEM)


def hbm(value):
    return pltpu.with_memory_space_constraint(value, pltpu.HBM)


def whole_spec(shape):
    return pl.BlockSpec(shape, lambda *_: (0,) * len(shape))


def result(shape, kind, free=False):
    return jax.ShapeDtypeStruct(shape, kind) if free else pltpu.HBM(shape, kind)


def single(kernel, outs, values, raw=(), held=(), scratch=(), limit=40, place=None, raw_outs=0):
    specs = [whole_spec(v.shape) for v in values] + [ANY] * len(raw) + [VMEM] * len(held)
    values = [hbm(v) for v in values] + list(raw) + list(held)
    blocked_outs = len(outs) - raw_outs
    if place is not None:
        specs, values = [SMEM] + specs, [place] + values
    return pl.pallas_call(
        kernel,
        grid=(1,),
        out_shape=tuple(result(*o) for o in outs),
        in_specs=specs,
        out_specs=tuple(
            whole_spec(o[0]) if i < blocked_outs else ANY for i, o in enumerate(outs)
        ),
        scratch_shapes=list(scratch),
        compiler_params=pltpu.CompilerParams(vmem_limit_bytes=limit << 20),
    )(*values)


def join_copies(place_ref, sides, blocks, sems):
    hx, hc, sz, sy = (place_ref[i] for i in range(4))
    half = sides[0].shape[-1]
    copies = []
    for number, pieces in enumerate(sides):
        side, core = divmod(number, 2)
        for second in range(2):
            for first in range(2):
                for deep in range(4):
                    across, down = (first, second) if side == 0 else (second, first)
                    block = (hx ^ across) * 2 + (hc ^ core)
                    spot = (block * 4 + lax.rem(sz + deep, 4)) * 2 + (sy ^ down)
                    copies.append(
                        pltpu.make_async_copy(
                            pieces.at[second, first, deep],
                            blocks.at[spot, :, pl.ds(side * half, half)],
                            sems.at[len(copies)],
                        )
                    )
    return copies


def gather_rows(here, shard, every, use):
    half = shard.shape[1] // 2
    sides = []
    deep = jnp.stack([shard] + [turn(shard, "sz", k) for k in (1, 2, 3)])
    orders = (("hx", "sy"), ("sy", "hx"))
    deep, every = lax.optimization_barrier((deep, every))
    levels = [deep[:, :, :half], deep[:, :, half:]]
    levels = [jnp.stack([v, swap(v, order[0])]) for v, order in zip(levels, orders)]
    levels = [jnp.stack([v, swap(v, order[1])]) for v, order in zip(levels, orders)]
    used = use(every)
    levels, used = lax.optimization_barrier((levels, used))
    for level in levels:
        sides += [level, swap(level, "hc")]
    return sides, used


def piece_copies(place_ref, blocks, keep, send, sems, side, columns):
    hx, sz, sy = place_ref[0], place_ref[2], place_ref[3]
    copies = []
    for second in range(2):
        for first in range(2):
            for deep in range(4):
                across, down = (first, second) if side == 0 else (second, first)
                spot = ((hx ^ across) * 4 + lax.rem(sz + deep, 4)) * 2 + (sy ^ down)
                source = blocks.at[(spot,) + (slice(None),) * (len(blocks.shape) - 2) + (columns,)]
                target = (keep, send)[second].at[first, deep]
                copies.append(pltpu.make_async_copy(source, target, sems.at[len(copies)]))
    for copy in copies:
        copy.start()
    return copies


ORDERS = (("sy", "hx"), ("hx", "sy"))
COLUMN_GROUPS = ((1, 0), (2, 0), (1, 1), (2, 1))


def second_send(keep, recv):
    return (keep[1].astype(f32) + recv[1].astype(f32)).astype(bf16)


def second_total(keep, recv, recv_second):
    return keep[0].astype(f32) + recv[0].astype(f32) + recv_second.astype(f32)


def third_recvs(total):
    return [turn(total[k].astype(bf16), "sz", -k) for k in (1, 2, 3)]


def enter_kernel(place_ref, x_ref, mod_ref, gains_ref, *refs):
    *sides, entered_ref, pair_ref, query_ref, whole_ref, block_sc, weight_sc, sems, sem = refs
    seqs, tokens, width = x_ref.shape
    half = tokens // 2
    pieced = len(sides) > 1
    if pieced:
        copies = join_copies(place_ref, sides, block_sc, sems)
    else:
        copies = [pltpu.make_async_copy(sides[0], weight_sc, sem)]
    for copy in copies:
        copy.start()
    for s in range(seqs):
        normed = normalize(x_ref[s].astype(f32))[0]
        shift, scale = (mod_ref[s : s + 1, pl.ds(i * width, width)] for i in (0, 1))
        value = normed * gains_ref[0:1] * (1.0 + scale) + shift
        entered_ref[pl.ds(s * tokens, tokens), :] = value.astype(bf16)
    entered = entered_ref[...]
    for copy in copies:
        copy.wait()
    if pieced:
        rows = block_sc.shape[1]
        for i in range(block_sc.shape[0]):
            weight_sc[pl.ds(i * rows, rows), :] = block_sc[i]
    leaving = pltpu.make_async_copy(weight_sc, whole_ref, sem)
    leaving.start()
    for which in (1, 2, 0):
        triple = dot(entered, weight_sc[:, pl.ds(which * width, width)])
        if which == 0:
            triple = triple * HEAD_DIM ** (-0.5)
        triple = triple.astype(bf16)
        for s in range(seqs):
            for g in range(GROUPS):
                rows = triple[s * tokens : (s + 1) * tokens, g * WIDTH : (g + 1) * WIDTH]
                slot = s * GROUPS + g
                if which == 0:
                    query_ref[slot, :, pl.ds(0, WIDTH)] = rows[:half]
                    query_ref[slot, :, pl.ds(WIDTH, WIDTH)] = rows[half:]
                else:
                    pair_ref[slot, :, pl.ds((which - 1) * WIDTH, WIDTH)] = rows
    leaving.wait()


def enter(here, inputs, modulation, gains, sides):
    seqs, tokens, width = inputs.shape
    rows = sides[0].shape[-2] if len(sides) > 1 else width // 32
    return single(
        enter_kernel,
        [
            ((seqs * tokens, width), bf16),
            ((8, tokens, 2 * WIDTH), bf16, True),
            ((8, tokens // 2, 2 * WIDTH), bf16, True),
            ((width, 3 * width), bf16),
        ],
        [inputs, modulation, gains],
        raw=sides,
        scratch=[
            pltpu.VMEM((32, rows, 3 * width), bf16),
            pltpu.VMEM((width, 3 * width), bf16),
            pltpu.SemaphoreType.DMA((64,)),
            pltpu.SemaphoreType.DMA,
        ],
        place=here,
        raw_outs=1,
    )


def load_pairs(pair_ref, slot, first_row, half):
    value = pair_ref[slot, pl.ds(first_row, half), :]
    return value[:, :WIDTH], value[:, WIDTH:]


def key_column(docs_ref, step):
    row = docs_ref[pl.ds(step, 1), :]
    return jnp.broadcast_to(row, (8, row.shape[1])).T[:, 0:1]


def gather_pairs(pair_ref, target):
    half = pair_ref.shape[1]
    for slot in range(pair_ref.shape[0]):
        for part, rows in enumerate(load_pairs(pair_ref, slot, 0, half)):
            target[pl.ds((slot * 2 + part) * half, half), :] = rows


def spread_heads(rows, target):
    lane = lax.broadcasted_iota(jnp.int32, (1, WIDTH), 1)
    for h in range(target.shape[0]):
        own = (lane >= h * HEAD_DIM) & (lane < (h + 1) * HEAD_DIM)
        target[h] = rows * jnp.where(own, 1.0, 0.0).astype(bf16)


def fetch(step, pair_refs, starts, pair_sc):
    for ref, (begin, end) in zip(pair_refs, starts):
        @pl.when((step >= begin) & (step < end))
        def take(ref=ref):
            pair_sc[...] = ref[...]


def forward_kernel(
    starts, came_ref, first_ref, second_ref, third_ref, fourth_ref, key_docs_ref, query_docs_ref,
    out_ref, turned_ref, total_ref, query_sc, flat_sc, pair_sc, top_sc, sum_sc, acc_sc,
):
    step = pl.program_id(0)
    heads, queries = query_sc.shape[:2]
    half = out_ref.shape[1]

    @pl.when(step == 0)
    def start():
        gather_pairs(came_ref, flat_sc)
        spread_heads(flat_sc[...], query_sc)
        top_sc[...] = jnp.full(top_sc.shape, -1e30, f32)
        sum_sc[...] = jnp.zeros(sum_sc.shape, f32)
        acc_sc[...] = jnp.zeros(acc_sc.shape, f32)

    fetch(step, (first_ref, second_ref, third_ref, fourth_ref), starts, pair_sc)
    key_part = pair_sc[:, :WIDTH]
    value_turned = pair_sc[:, WIDTH:].T
    allowed = key_column(key_docs_ref, step) == query_docs_ref[...]
    old = [top_sc[h : h + 1] for h in range(heads)]
    raw = [dot_nt(key_part, query_sc[h]) for h in range(heads)]
    scores = [jnp.where(allowed, value, -1e30) for value in raw]
    new = [jnp.maximum(o, jnp.max(v, axis=0, keepdims=True)) for o, v in zip(old, scores)]
    exponent = [jnp.exp(v - n) for v, n in zip(scores, new)]
    terms = [
        dot(value_turned[h * HEAD_DIM : (h + 1) * HEAD_DIM], exponent[h].astype(bf16))
        for h in range(heads)
    ]
    sums = [jnp.sum(v, axis=0, keepdims=True) for v in exponent]
    for h in range(heads):
        rows = pl.ds(h * HEAD_DIM, HEAD_DIM)
        fade = jnp.exp(old[h] - new[h])
        top_sc[h : h + 1] = new[h]
        sum_sc[h : h + 1] = sum_sc[h : h + 1] * fade + sums[h]
        acc_sc[rows] = acc_sc[rows] * fade + terms[h]

    @pl.when(step == pl.num_programs(0) - 1)
    def finish():
        total_ref[...] = jnp.zeros(total_ref.shape, f32)
        for h in range(heads):
            rows = pl.ds(h * HEAD_DIM, HEAD_DIM)
            turned_ref[rows] = acc_sc[rows] / sum_sc[h : h + 1]
            total_ref[h : h + 1] = top_sc[h : h + 1] + jnp.log(sum_sc[h : h + 1])
        whole = turned_ref[...].astype(bf16).T
        for slot in range(8):
            for part in range(2):
                begin = (slot * 2 + part) * half
                out_ref[slot, :, pl.ds(part * WIDTH, WIDTH)] = whole[begin : begin + half]


def pair_specs(pairs, chunk):
    specs, starts, begin = [], [], 0
    for pair in pairs:
        count = pair.shape[0] // chunk
        specs.append(
            pl.BlockSpec(
                (chunk, 2 * WIDTH),
                lambda i, begin=begin, count=count: (jnp.clip(i - begin, 0, count - 1), 0),
            )
        )
        starts.append((begin, begin + count))
        begin += count
    return specs, starts, begin


def attend(came, pairs, key_docs, query_docs):
    slots, half, columns = came.shape
    queries = slots * 2 * half
    heads = WIDTH // HEAD_DIM
    chunk = 512
    specs, starts, steps = pair_specs(pairs, chunk)
    outs = (
        result((slots, half, columns), bf16, True),
        result((WIDTH, queries), f32),
        result((8, queries), f32),
    )
    return pl.pallas_call(
        partial(forward_kernel, starts),
        grid=(steps,),
        out_shape=outs,
        in_specs=[
            whole_spec(came.shape),
            *specs,
            whole_spec(key_docs.shape),
            whole_spec(query_docs.shape),
        ],
        out_specs=tuple(whole_spec(o.shape) for o in outs),
        scratch_shapes=[
            pltpu.VMEM((heads, queries, WIDTH), bf16),
            pltpu.VMEM((queries, WIDTH), bf16),
            pltpu.VMEM((chunk, 2 * WIDTH), bf16),
            pltpu.VMEM((8, queries), f32),
            pltpu.VMEM((8, queries), f32),
            pltpu.VMEM((WIDTH, queries), f32),
        ],
        compiler_params=pltpu.CompilerParams(vmem_limit_bytes=48 << 20),
    )(*map(hbm, (came, *pairs, key_docs, query_docs)))


def backward_kernel(
    starts, came_ref, grad_ref, first_ref, second_ref, third_ref, fourth_ref, key_docs_ref, query_docs_ref,
    turned_ref, total_ref, query_out, keep_ref, keep_other, send_ref,
    query_sc, grad_sc, flat_sc, pair_sc, delta_sc, acc_sc,
):
    step = pl.program_id(0)
    heads, queries = query_sc.shape[:2]
    half = query_out.shape[1]

    @pl.when(step == 0)
    def start():
        gather_pairs(came_ref, flat_sc)
        spread_heads(flat_sc[...], query_sc)
        gather_pairs(grad_ref, flat_sc)
        spread_heads(flat_sc[...], grad_sc)
        acc_sc[...] = jnp.zeros(acc_sc.shape, f32)
        product = flat_sc[...].T.astype(f32) * turned_ref[...]
        for h in range(heads):
            rows = slice(h * HEAD_DIM, (h + 1) * HEAD_DIM)
            delta_sc[h : h + 1] = jnp.sum(product[rows], axis=0, keepdims=True)

    fetch(step, (first_ref, second_ref, third_ref, fourth_ref), starts, pair_sc)
    key_part = pair_sc[:, :WIDTH]
    value_part = pair_sc[:, WIDTH:]
    key_turned = key_part.T
    allowed = key_column(key_docs_ref, step) == query_docs_ref[...]
    raw = [dot_nt(key_part, query_sc[h]) for h in range(heads)]
    slopes = [dot_nt(value_part, grad_sc[h]) for h in range(heads)]
    probabilities = [
        jnp.exp(jnp.where(allowed, value, -1e30) - total_ref[h : h + 1])
        for h, value in enumerate(raw)
    ]
    grad_scores = [
        (p * (slope - delta_sc[h : h + 1])).astype(bf16)
        for h, (p, slope) in enumerate(zip(probabilities, slopes))
    ]
    grad_value = sum(dot(probabilities[h].astype(bf16), grad_sc[h]) for h in range(heads))
    grad_key = sum(dot(grad_scores[h], query_sc[h]) for h in range(heads))
    for h in range(heads):
        rows = pl.ds(h * HEAD_DIM, HEAD_DIM)
        acc_sc[rows] = acc_sc[rows] + dot(
            key_turned[h * HEAD_DIM : (h + 1) * HEAD_DIM], grad_scores[h]
        )
    quarter = pl.num_programs(0) // 4
    middle = 2 * quarter

    for number, ref in enumerate((keep_ref, keep_other)):
        @pl.when((step >= number * quarter) & (step < (number + 1) * quarter))
        def mine(ref=ref):
            ref[:, pl.ds(0, WIDTH)] = grad_key
            ref[:, pl.ds(WIDTH, WIDTH)] = grad_value

    @pl.when(step >= middle)
    def theirs():
        send_ref[:, pl.ds(0, WIDTH)] = grad_key.astype(bf16)
        send_ref[:, pl.ds(WIDTH, WIDTH)] = grad_value.astype(bf16)

    @pl.when(step == pl.num_programs(0) - 1)
    def finish():
        whole = (acc_sc[...] * HEAD_DIM ** (-0.5)).astype(bf16).T
        for slot in range(8):
            for part in range(2):
                begin = (slot * 2 + part) * half
                query_out[slot, :, pl.ds(part * WIDTH, WIDTH)] = whole[begin : begin + half]


def attend_back(came, grad, pairs, key_docs, query_docs, turned, total):
    slots, half, columns = came.shape
    queries = slots * 2 * half
    heads = WIDTH // HEAD_DIM
    chunk = 512
    specs, starts, steps = pair_specs(pairs, chunk)
    quarter = steps // 4
    middle = 2 * quarter
    return pl.pallas_call(
        partial(backward_kernel, starts),
        grid=(steps,),
        out_shape=(
            jax.ShapeDtypeStruct((slots, half, columns), bf16),
            jax.ShapeDtypeStruct((quarter * chunk, columns), f32),
            jax.ShapeDtypeStruct((quarter * chunk, columns), f32),
            jax.ShapeDtypeStruct((middle * chunk, columns), bf16),
        ),
        in_specs=[
            whole_spec(came.shape),
            whole_spec(grad.shape),
            *specs,
            whole_spec(key_docs.shape),
            whole_spec(query_docs.shape),
            whole_spec(turned.shape),
            whole_spec(total.shape),
        ],
        out_specs=(
            whole_spec((slots, half, columns)),
            pl.BlockSpec((chunk, columns), lambda i: (jnp.minimum(i, quarter - 1), 0)),
            pl.BlockSpec((chunk, columns), lambda i: (jnp.clip(i - quarter, 0, quarter - 1), 0)),
            pl.BlockSpec((chunk, columns), lambda i: (jnp.maximum(i - middle, 0), 0)),
        ),
        scratch_shapes=[
            pltpu.VMEM((heads, queries, WIDTH), bf16),
            pltpu.VMEM((heads, queries, WIDTH), bf16),
            pltpu.VMEM((queries, WIDTH), bf16),
            pltpu.VMEM((chunk, 2 * WIDTH), bf16),
            pltpu.VMEM((8, queries), f32),
            pltpu.VMEM((WIDTH, queries), f32),
        ],
        compiler_params=pltpu.CompilerParams(vmem_limit_bytes=48 << 20),
    )(*map(hbm, (came, grad, *pairs, key_docs, query_docs, turned, total)))


def settle_kernel(
    later_hbm, out_ref, up_ref, down_ref, block_sc, out_sc, up_sc, down_sc, sems, out_sems
):
    width = out_ref.shape[1]
    copies = [
        pltpu.make_async_copy(later_hbm.at[:, j], block_sc.at[j], sems.at[j]) for j in range(9)
    ]
    for copy in copies:
        copy.start()
    leaving = []
    for j in range(9):
        copies[j].wait()
        for i in range(32):
            value = block_sc[j, i]
            if j == 0:
                out_sc[pl.ds(i * 24, 24), :] = value
            elif j < 5:
                up_sc[pl.ds(i * 24, 24), pl.ds((j - 1) * width, width)] = value
            else:
                down_sc[pl.ds(i * 96 + (j - 5) * 24, 24), :] = value
        if j == 0:
            leaving.append(pltpu.make_async_copy(out_sc, out_ref, out_sems.at[j]))
        elif j < 5:
            columns = pl.ds((j - 1) * width, width)
            leaving.append(
                pltpu.make_async_copy(up_sc.at[:, columns], up_ref.at[:, columns], out_sems.at[j])
            )
        elif j == 8:
            leaving.append(pltpu.make_async_copy(down_sc, down_ref, out_sems.at[j]))
        if j < 5 or j == 8:
            leaving[-1].start()
    for copy in leaving:
        copy.wait()


def settle(later):
    width = later.shape[-1]
    shapes = ((width, width), (width, 4 * width), (4 * width, width))
    return pl.pallas_call(
        settle_kernel,
        out_shape=tuple(result(shape, bf16) for shape in shapes),
        in_specs=[ANY],
        out_specs=(ANY,) * 3,
        scratch_shapes=[
            pltpu.VMEM((9, 32, 24, width), bf16),
            *(pltpu.VMEM(shape, bf16) for shape in shapes),
            pltpu.SemaphoreType.DMA((9,)),
            pltpu.SemaphoreType.DMA((9,)),
        ],
        compiler_params=pltpu.CompilerParams(vmem_limit_bytes=40 << 20),
    )(hbm(later))


def middle_kernel(
    came_ref, x_ref, teacher_ref, mask_ref, mod_ref, gains_ref, up_bias_ref,
    out_hbm, up_hbm, down_hbm,
    final_ref, hidden_ref, leave_ref, pack_ref, sums_ref, out_sc, up_sc, down_sc, slope_sc, sems,
):
    seqs, tokens, width = x_ref.shape
    units = up_sc.shape[1]
    rows = seqs * tokens
    half = tokens // 2
    parts = [pl.ds(f * width, width) for f in range(units // width)]
    copies = [pltpu.make_async_copy(out_hbm, out_sc, sems.at[0])]
    for f, part in enumerate(parts):
        copies.append(
            pltpu.make_async_copy(up_hbm.at[:, part], up_sc.at[:, part], sems.at[1 + 2 * f])
        )
        copies.append(
            pltpu.make_async_copy(down_hbm.at[part, :], down_sc.at[part, :], sems.at[2 + 2 * f])
        )
    for copy in copies:
        copy.start()
    masks = mask_ref[...].T

    def wide(index):
        return jnp.concatenate(
            [
                jnp.broadcast_to(
                    mod_ref[s : s + 1, pl.ds(index * width, width)], (tokens, width)
                )
                for s in range(seqs)
            ]
        )

    def add_rows(first, value):
        for s in range(seqs):
            sums_ref[first + s : first + s + 1] = jnp.sum(
                value[s * tokens : (s + 1) * tokens], axis=0, keepdims=True
            )

    for s in range(seqs):
        for g in range(GROUPS):
            left, right = load_pairs(came_ref, s * GROUPS + g, 0, half)
            columns = pl.ds(g * WIDTH, WIDTH)
            pack_ref[pl.ds(s * tokens, half), columns] = left
            pack_ref[pl.ds(s * tokens + half, half), columns] = right
    mixed = pack_ref[:, pl.ds(0, width)]
    residual = jnp.concatenate([x_ref[s].astype(f32) for s in range(seqs)])
    copies[0].wait()
    branch = dot(mixed, out_sc[...])
    hidden = residual + wide(2) * branch
    normed, inverse = normalize(hidden)
    scaled = normed * gains_ref[1:2]
    moved = (scaled * (1.0 + wide(4)) + wide(3)).astype(bf16)
    pack_ref[:, pl.ds(width, width)] = moved
    lower = None
    for f in range(units // width):
        columns = pl.ds(f * width, width)
        copies[1 + 2 * f].wait()
        u = dot(moved, up_sc[:, columns]) + up_bias_ref[0:1, columns]
        square = u * u
        t = jnp.tanh(0.7978845608028654 * (u + 0.044715 * u * square))
        active = (0.5 * u * (1.0 + t)).astype(bf16)
        slope_sc[:, columns] = 0.5 * (1.0 + t) + 0.5 * u * (1.0 - t * t) * 0.7978845608028654 * (
            1.0 + 0.134145 * square
        )
        pack_ref[:, pl.ds(2 * width + f * width, width)] = active
        copies[2 + 2 * f].wait()
        term = dot(active, down_sc[columns, :])
        lower = term if lower is None else lower + term
    lower = lower + gains_ref[2:3]
    gate = wide(5)
    final = hidden + gate * lower
    for s in range(seqs):
        final_ref[s] = final[s * tokens : (s + 1) * tokens].astype(bf16)
    teacher = jnp.concatenate([teacher_ref[s].astype(f32) for s in range(seqs)])
    mismatch = final - teacher
    sums_ref[14:15] = jnp.sum(
        masks[:, 0:1] * mismatch * mismatch, axis=0, keepdims=True
    )
    sums_ref[15:16] = jnp.zeros((1, width), f32)
    grad_final = masks[:, 1:2] * mismatch
    add_rows(6, grad_final * lower)
    grad_lower = (gate * grad_final).astype(bf16)
    base = 2 * width + units
    pack_ref[:, pl.ds(base + width + units, width)] = grad_lower
    sums_ref[9:10] = jnp.sum(grad_lower.astype(f32), axis=0, keepdims=True)
    grad_moved = None
    for f in range(units // width):
        columns = pl.ds(f * width, width)
        grad_active = dot_nt(grad_lower, down_sc[columns, :])
        grad_upper = (grad_active * slope_sc[:, columns]).astype(bf16)
        pack_ref[:, pl.ds(base + width + f * width, width)] = grad_upper
        sums_ref[10 + f : 11 + f] = jnp.sum(grad_upper.astype(f32), axis=0, keepdims=True)
        term = dot_nt(grad_upper, up_sc[:, columns])
        grad_moved = term if grad_moved is None else grad_moved + term
    add_rows(2, grad_moved)
    add_rows(4, grad_moved * scaled)
    grad_scaled = grad_moved * (1.0 + wide(4))
    sums_ref[8:9] = jnp.sum(grad_scaled * normed, axis=0, keepdims=True)
    grad_hidden = grad_final + norm_back(grad_scaled * gains_ref[1:2], normed, inverse)
    hidden_ref[...] = grad_hidden
    add_rows(0, grad_hidden * branch)
    grad_branch = (wide(2) * grad_hidden).astype(bf16)
    pack_ref[:, pl.ds(base, width)] = grad_branch
    grad_mixed = dot_nt(grad_branch, out_sc[...]).astype(bf16)
    for s in range(seqs):
        for g in range(GROUPS):
            piece = grad_mixed[s * tokens : (s + 1) * tokens, g * WIDTH : (g + 1) * WIDTH]
            leave_ref[s * GROUPS + g, :, pl.ds(0, WIDTH)] = piece[:half]
            leave_ref[s * GROUPS + g, :, pl.ds(WIDTH, WIDTH)] = piece[half:]


def middle(came, inputs, teacher, masks, modulation, gains, up_bias, weights):
    seqs, tokens, width = inputs.shape
    units = up_bias.shape[1]
    rows = seqs * tokens
    return single(
        middle_kernel,
        [
            ((seqs, tokens, width), bf16),
            ((rows, width), f32),
            (came.shape, bf16, True),
            ((rows, 4 * width + 2 * units), bf16, True),
            ((16, width), f32),
        ],
        [came, inputs, teacher, masks, modulation, gains, up_bias],
        raw=[hbm(w) for w in weights],
        scratch=[
            pltpu.VMEM((width, width), bf16),
            pltpu.VMEM((width, units), bf16),
            pltpu.VMEM((units, width), bf16),
            pltpu.VMEM((rows, units), f32),
            pltpu.SemaphoreType.DMA((9,)),
        ],
        limit=40,
    )


def weights_kernel(
    place_ref, own_ref, other_ref, *refs
):
    *groups, left_sc, right_sc, block_sc, sems = refs
    rows, width = own_ref.shape[0], block_sc.shape[-1]
    units = 4 * width
    hc = place_ref[1]
    base = 2 * width + units
    for which, ref in enumerate((own_ref, other_ref)):
        left_sc[:, pl.ds(which * rows, rows)] = ref[:, pl.ds(0, base)].T
        right_sc[pl.ds(which * rows, rows), :] = ref[:, pl.ds(base, base)]
    for hx in range(2):
        begin = pl.multiple_of(hx * 384 + hc * 192, 64)
        for j in range(5):
            offset = 0 if j == 0 else width
            value = dot(left_sc[pl.ds(begin + offset, 192), :], right_sc[:, pl.ds(j * width, width)])
            for i in range(8):
                block_sc[hx * 8 + i, j] = value[i * 24 : (i + 1) * 24].astype(bf16)
        begin = pl.multiple_of(2 * width + hx * 1536 + hc * 768, 256)
        value = dot(left_sc[pl.ds(begin, 768), :], right_sc[:, pl.ds(width + units, width)])
        for i in range(8):
            for j in range(4):
                first = i * 96 + j * 24
                block_sc[hx * 8 + i, 5 + j] = value[first : first + 24].astype(bf16)
    copies = []
    begin = 0
    for number, (_, side) in enumerate(COLUMN_GROUPS):
        keep, send = groups[2 * number : 2 * number + 2]
        columns = pl.ds(begin, keep.shape[-1])
        copies += piece_copies(place_ref, block_sc, keep, send, sems.at[number], side, columns)
        begin += keep.shape[-1]
    for copy in copies:
        copy.wait()


def weight_terms(here, own, other, width):
    rows, total = own.shape
    return single(
        weights_kernel,
        [((2, 4, 9, 24, 128 * size), bf16) for size, _ in COLUMN_GROUPS for _ in range(2)],
        [],
        held=[own, other],
        scratch=[
            pltpu.VMEM((total // 2, 2 * rows), bf16),
            pltpu.VMEM((2 * rows, total // 2), bf16),
            pltpu.VMEM((16, 9, 24, width), bf16),
            pltpu.SemaphoreType.DMA((len(COLUMN_GROUPS), 16)),
        ],
        limit=40,
        place=here,
        raw_outs=2 * len(COLUMN_GROUPS),
    )


def flat_rows(home_ref, target, first_row, seqs, tokens, width):
    half = tokens // 2
    for s in range(seqs):
        for g in range(GROUPS):
            slot = s * GROUPS + g
            row = first_row + s * tokens
            left, right = load_pairs(home_ref, slot, tokens, half)
            target[pl.ds(row, half), pl.ds(g * WIDTH, WIDTH)] = left
            target[pl.ds(row + half, half), pl.ds(g * WIDTH, WIDTH)] = right
            left, right = load_pairs(home_ref, slot, 0, tokens)
            target[pl.ds(row, tokens), pl.ds(width + g * WIDTH, WIDTH)] = left
            target[pl.ds(row, tokens), pl.ds(2 * width + g * WIDTH, WIDTH)] = right


def qkv_kernel(
    seqs, place_ref, entered_ref, entered_other, home_ref, home_other,
    keep_a, send_a, keep_b, send_b, left_sc, right_sc, block_sc, sems,
):
    rows, width = entered_ref.shape
    hc = place_ref[1]
    for which, (left, home) in enumerate(((entered_ref, home_ref), (entered_other, home_other))):
        left_sc[:, pl.ds(which * rows, rows)] = left[...].T
        flat_rows(home, right_sc, which * rows, seqs, rows // seqs, width)
    for hx in range(2):
        begin = pl.multiple_of(hx * 384 + hc * 192, 64)
        for j in range(3):
            value = dot(left_sc[pl.ds(begin, 192), :], right_sc[:, pl.ds(j * width, width)])
            for i in range(8):
                block_sc[hx * 8 + i, :, pl.ds(j * width, width)] = value[
                    i * 24 : (i + 1) * 24
                ].astype(bf16)
    half = 3 * width // 2
    copies = piece_copies(place_ref, block_sc, keep_a, send_a, sems.at[0], 0, pl.ds(0, half))
    copies += piece_copies(place_ref, block_sc, keep_b, send_b, sems.at[1], 1, pl.ds(half, half))
    for copy in copies:
        copy.wait()


def qkv_terms(here, seqs, *values):
    rows, width = values[0].shape
    return single(
        partial(qkv_kernel, seqs),
        [((2, 4, 24, 3 * width // 2), bf16)] * 4,
        values,
        scratch=[
            pltpu.VMEM((width, 2 * rows), bf16),
            pltpu.VMEM((2 * rows, 3 * width), bf16),
            pltpu.VMEM((16, 24, 3 * width), bf16),
            pltpu.SemaphoreType.DMA((2, 16)),
        ],
        place=here,
        raw_outs=4,
    )


def leave_kernel(
    home_ref, x_ref, hidden_ref, mod_ref, gains_ref, weight_ref, middle_ref,
    grad_ref, small_ref, flat_ref,
):
    seqs, tokens, width = x_ref.shape
    devices = small_ref.shape[0]
    flat_rows(home_ref, flat_ref, 0, seqs, tokens, width)
    grad_entered = None
    for which in range(3):
        columns = pl.ds(which * width, width)
        term = dot_nt(flat_ref[:, columns], weight_ref[:, columns])
        grad_entered = term if grad_entered is None else grad_entered + term
    gain_sum = None
    sums = []
    for s in range(seqs):
        normed, inverse = normalize(x_ref[s].astype(f32))
        rows = slice(s * tokens, (s + 1) * tokens)
        grad = grad_entered[rows]
        shift_sum = jnp.sum(grad, axis=0, keepdims=True)
        scale_sum = jnp.sum(grad * (normed * gains_ref[0:1]), axis=0, keepdims=True)
        grad_scaled = grad * (1.0 + mod_ref[s : s + 1, pl.ds(width, width)])
        term = jnp.sum(grad_scaled * normed, axis=0, keepdims=True)
        gain_sum = term if gain_sum is None else gain_sum + term
        grad_ref[s] = hidden_ref[rows] + norm_back(grad_scaled * gains_ref[0:1], normed, inverse)
        later = [middle_ref[i + s : i + s + 1] for i in (0, 2, 4, 6)]
        sums.append(jnp.concatenate([shift_sum, scale_sum, *later], axis=1))
    up_bias = jnp.concatenate([middle_ref[i : i + 1] for i in range(10, 14)], axis=1)
    fields = [*sums, gain_sum, middle_ref[8:9], up_bias, middle_ref[9:10]]
    error = jnp.sum(middle_ref[14:15], axis=1, keepdims=True)
    small_ref[...] = jnp.zeros(small_ref.shape, f32)
    begin = 0
    for field in fields:
        size = field.shape[1] // devices
        for i in range(devices):
            small_ref[i, :, pl.ds(begin, size)] = field[:, i * size : (i + 1) * size]
        begin += size
    small_ref[:, :, pl.ds(begin, 1)] = jnp.broadcast_to(error[None], (devices, 1, 1))


def leave(home, inputs, grad_hidden, modulation, gains, weight, sums, devices):
    seqs, tokens, width = inputs.shape
    return single(
        leave_kernel,
        [
            ((seqs, tokens, width), f32),
            ((devices, 1, 512), f32, True),
            ((seqs * tokens, 3 * width), bf16),
        ],
        [home, inputs, grad_hidden, modulation, gains, weight, sums],
    )


def unpack_kernel(
    parts, sizes, factor, place_ref, every_ref, valid_ref,
    mod_ref, gains_ref, up_ref, key_docs_ref, query_docs_ref, masks_ref,
):
    devices = every_ref.shape[0]
    seqs, tokens = valid_ref.shape
    size_mod, size_gain, size_up = sizes
    mod_ref[...] = jnp.zeros(mod_ref.shape, f32)
    gains_ref[...] = jnp.zeros(gains_ref.shape, f32)
    up_ref[...] = jnp.zeros(up_ref.shape, f32)
    begin = 0
    targets = [(mod_ref, s, size_mod) for s in range(seqs)]
    targets += [(gains_ref, 0, size_gain), (gains_ref, 1, size_gain)]
    targets += [(up_ref, 0, size_up), (gains_ref, 2, size_gain)]
    for target, row, size in targets:
        for i in range(devices):
            target[row : row + 1, pl.ds(i * size, size)] = every_ref[i, :, pl.ds(begin, size)]
        begin += size
    hx, hc, sz, sy, rb = (place_ref[i] for i in range(5))
    second = sz * 2 + sy >= GROUPS
    row = 0
    for core in range(2):
        for across in range(2):
            for part in range(parts):
                block = ((hx ^ across) * 2 + (hc ^ core)) * parts + part
                for spot in range(8):
                    line = every_ref[block * 8 + spot, :, pl.ds(begin, 2 * tokens)]
                    key_docs_ref[row : row + 1, pl.ds(spot * tokens, tokens)] = jnp.where(
                        second, line[:, tokens:], line[:, :tokens]
                    )
                row += 1
    for spot in range(8):
        line = every_ref[((hx * 2 + hc) * parts + rb) * 8 + spot, :, pl.ds(begin, 2 * tokens)]
        query_docs_ref[:, pl.ds(spot * tokens, tokens)] = jnp.where(
            second, line[:, tokens:], line[:, :tokens]
        )
    begin += 2 * tokens
    count = jnp.sum(every_ref[:, :, pl.ds(begin, 1)], axis=0)
    gains_ref[3:4, pl.ds(0, 1)] = count
    masks_ref[...] = jnp.zeros(masks_ref.shape, f32)
    for s in range(seqs):
        valid = valid_ref[s : s + 1, :].astype(f32)
        masks_ref[0:1, pl.ds(s * tokens, tokens)] = valid
        masks_ref[1:2, pl.ds(s * tokens, tokens)] = valid * (factor / count)


def unpack(here, every, valid_mask, width, units, parts, length):
    seqs, tokens = valid_mask.shape
    devices = every.shape[0]
    sizes = (6 * width // devices, width // devices, units // devices)
    return single(
        partial(unpack_kernel, parts, sizes, float(seqs * length)),
        [
            ((8, 6 * width), f32),
            ((8, width), f32),
            ((8, units), f32),
            ((4 * parts, 8 * tokens), f32),
            ((1, 8 * tokens), f32),
            ((8, seqs * tokens), f32),
        ],
        [every, valid_mask],
        place=here,
    )


def finish_kernel(width, small_ref, embed_ref, gains_ref, *refs):
    ada_ref, bias_ref, *vectors, loss_ref = refs
    seqs = embed_ref.shape[0]
    columns = ada_ref.shape[0]
    added = jnp.sum(small_ref[...], axis=0)
    begin = 0
    ada = bias = None
    for s in range(seqs):
        grad = added[:, begin : begin + columns]
        begin += columns
        turned = jnp.broadcast_to(grad, (8, columns)).T[:, 0:1]
        term = turned * embed_ref[s : s + 1, :]
        ada = term if ada is None else ada + term
        bias = grad if bias is None else bias + grad
    ada_ref[...] = ada
    bias_ref[...] = bias
    for ref in vectors:
        size = ref.shape[1]
        ref[...] = added[:, begin : begin + size]
        begin += size
    loss_ref[...] = added[:, begin : begin + 1] / (gains_ref[3:4, 0:1] * width)


def finish(small, time_embed, gains, width, units):
    devices = small.shape[0]
    sizes = [6 * width // devices] + [size // devices for size in (width, width, units, width)]
    return single(
        partial(finish_kernel, float(width)),
        [((sizes[0], time_embed.shape[1]), f32)]
        + [((1, size), f32, True) for size in sizes]
        + [((1, 1), f32, True)],
        [small, time_embed, gains],
    )


def grads_kernel(total_ref, first_ref, second_ref, third_ref, *refs):
    qkv_total, qkv_first, qkv_second, qkv_third, out_ref, up_ref, down_ref, qkv_ref = refs
    width = out_ref.shape[1]
    for j in range(9):
        value = total_ref[0, j]
        for ref in (first_ref, second_ref, third_ref):
            value = value + ref[j].astype(f32)
        if j == 0:
            out_ref[...] = value
        elif j < 5:
            up_ref[:, pl.ds((j - 1) * width, width)] = value
        else:
            down_ref[pl.ds((j - 5) * 24, 24), :] = value
    value = qkv_total[0]
    for ref in (qkv_first, qkv_second, qkv_third):
        value = value + ref[...].astype(f32)
    qkv_ref[...] = value


def weight_grads(total, third, qkv_total, third_qkv):
    width = total.shape[-1]
    values = [total, *third, qkv_total, *third_qkv]
    specs = [
        pl.BlockSpec((1,) + v.shape[1:], lambda i, n=v.ndim: (0,) * n)
        if i in (0, 4)
        else whole_spec(v.shape)
        for i, v in enumerate(values)
    ]
    shapes = ((24, width), (24, 4 * width), (96, width), (24, 3 * width))
    return pl.pallas_call(
        grads_kernel,
        grid=(1,),
        out_shape=tuple(jax.ShapeDtypeStruct(shape, f32) for shape in shapes),
        in_specs=specs,
        out_specs=tuple(whole_spec(shape) for shape in shapes),
        compiler_params=pltpu.CompilerParams(vmem_limit_bytes=40 << 20),
    )(*values)


def begin_kernel(embed_ref, ada_ref, vectors_ref, segments_ref, valid_ref, *refs):
    *weights, packed_ref = refs[:-1] if len(refs) > 1 else refs
    seqs, tokens = segments_ref.shape
    modulation = lax.dot_general(
        embed_ref[...],
        ada_ref[...].astype(f32),
        (((1,), (1,)), ((), ())),
        precision=precise,
        preferred_element_type=f32,
    )
    size = modulation.shape[1]
    vectors = vectors_ref[...].astype(f32)
    modulation = modulation + vectors[:, :size]
    count = jnp.sum(valid_ref[...].astype(f32), axis=1, keepdims=True)
    count = jnp.sum(count, axis=0, keepdims=True)
    fields = [modulation[s : s + 1] for s in range(seqs)]
    fields.append(vectors[:, size:])
    fields += [segments_ref[s : s + 1, :].astype(f32) for s in range(seqs)]
    fields.append(count)
    fields.append(jnp.zeros((1, packed_ref.shape[2] - sum(f.shape[1] for f in fields)), f32))
    packed_ref[...] = jnp.broadcast_to(
        jnp.concatenate(fields, axis=1)[None], packed_ref.shape
    )
    if weights:
        out_ref, up_ref, down_ref = weights
        later_ref = refs[-1]
        width = out_ref.shape[1]
        later_ref[0] = out_ref[...]
        for j in range(4):
            later_ref[1 + j] = up_ref[:, pl.ds(j * width, width)]
            later_ref[5 + j] = down_ref[pl.ds(j * 24, 24), :]


def begin_with(time_embed, ada_weight, vectors, segments, valid_mask, weights, devices):
    seqs, tokens = segments.shape
    columns = (seqs - 1) * ada_weight.shape[1] + vectors.shape[1] + seqs * tokens + 1
    outs = [((devices, 1, columns + -columns % 128), f32, True)]
    if weights:
        outs.append(((9, 24, weights[0].shape[1]), bf16))
    return single(
        begin_kernel, outs, [time_embed, ada_weight.T, vectors, segments, valid_mask, *weights]
    )


def after(value, *others):
    return lax.optimization_barrier((value, others))[0]


def exchange(rows):
    return lax.all_to_all(rows, SPOT, 0, 0, tiled=True)


def on_device(
    inputs,
    time_embed,
    segments,
    valid_mask,
    teacher,
    ada_weight,
    ada_bias,
    gain_attn,
    qkv_weight,
    out_weight,
    gain_mlp,
    up_weight,
    up_bias,
    down_weight,
    down_bias,
):
    seqs, tokens, width = inputs.shape
    units = up_weight.shape[1]
    parts = lax.axis_size("rb")
    devices = 32 * parts
    length = tokens * devices
    queries = 8 * tokens
    here = place()

    vectors = [ada_bias, gain_attn, gain_mlp, up_bias, down_bias]
    vectors = jnp.concatenate([v.astype(f32) for v in vectors]).reshape(1, -1)
    weights = [] if parts > 1 else [out_weight, up_weight, down_weight]
    packed, *later = begin_with(
        time_embed, ada_weight, vectors, segments, valid_mask, weights, devices
    )
    every = lax.all_to_all(packed, EVERY, 0, 0, tiled=True)
    if parts > 1:
        sides, *later = (
            lax.all_gather(w, EVERY, axis=0, tiled=True)
            for w in (qkv_weight, out_weight, up_weight, down_weight)
        )
    else:
        later = [lax.all_gather(later[0], EVERY, axis=0, tiled=False)]

    def use(every):
        return unpack(here, every, valid_mask, width, units, parts, length)

    if parts > 1:
        sides = [sides]
        used = use(every)
    else:
        sides, used = gather_rows(here, qkv_weight, every, use)
    modulation, gains, full_up_bias, key_docs, query_docs, masks = used

    entered, pair, query, full_qkv = enter(here, inputs, modulation, gains, sides)
    pair = exchange(pair).reshape(queries, 2 * WIDTH)
    query = exchange(query)
    if parts > 1:
        pair = lax.all_gather(pair, "rb", axis=0, tiled=True)
    pair_x = swap(pair, "hx")
    pair_x, query = lax.optimization_barrier((pair_x, query))
    pairs = (pair, pair_x, swap(pair, "hc"), swap(pair_x, "hc"))
    attended, turned, total = attend(query, pairs, key_docs, query_docs)

    if parts == 1:
        later = settle(later[0])
    final, grad_hidden, grad_leaving, pack, sums = middle(
        exchange(attended), inputs, teacher, masks, modulation, gains, full_up_bias, later
    )
    grad_came = exchange(grad_leaving)
    if parts == 1:
        terms = weight_terms(here, pack, swap(pack, "hc"), width)
        grad_came, terms = lax.optimization_barrier((grad_came, terms))
        held = terms[::2]
        firsts = [
            swap(send, ORDERS[side][0]) for send, (_, side) in zip(terms[1::2], COLUMN_GROUPS)
        ]

    grad_query, keep, keep_x, send = attend_back(
        query, grad_came, pairs, key_docs, query_docs, turned, total
    )
    if parts == 1:
        send, firsts[0], firsts[2] = lax.optimization_barrier((send, firsts[0], firsts[2]))
    recv = swap(send, "hc")
    own_rows = keep.shape[0]
    send_x = (keep_x + recv[own_rows:].astype(f32)).astype(bf16)
    grad_pair = keep + recv[:own_rows].astype(f32) + swap(send_x, "hx").astype(f32)
    if parts > 1:
        grad_pair = lax.psum_scatter(grad_pair, "rb", scatter_dimension=0, tiled=True)
    home = jnp.concatenate(
        [grad_pair.astype(bf16).reshape(8, tokens, 2 * WIDTH), grad_query], axis=1
    )
    if parts == 1:
        seconds = [
            swap(
                jnp.concatenate(
                    [
                        second_send(keep, recv)
                        for keep, recv, (_, own) in zip(held, firsts, COLUMN_GROUPS)
                        if own == side
                    ],
                    axis=3,
                ),
                ORDERS[side][1],
            )
            for side in (0, 1)
        ]
    home = exchange(home)
    if parts == 1:
        others = swap(entered, "hc"), swap(home, "hc")
        terms = qkv_terms(here, seqs, entered, others[0], home, others[1])
        seconds = after(seconds, terms)
        recvs = [swap(send, order[0]) for send, order in zip(terms[1::2], ORDERS)]
        grad_input, small, flat = leave(
            after(home, terms), inputs, grad_hidden, modulation, gains, full_qkv, sums, devices
        )
        recvs = after(recvs, small)
        nexts = [second_send(keep, recv) for keep, recv in zip(terms[::2], recvs)]
        small = after(small, nexts)
        next_recvs = [swap(value, order[1]) for value, order in zip(nexts, ORDERS)]
        totals = [
            jnp.concatenate(
                [
                    keep[0].astype(f32) + recv[0].astype(f32)
                    for keep, recv, (_, own) in zip(held, firsts, COLUMN_GROUPS)
                    if own == side
                ],
                axis=3,
            )
            + seconds[side].astype(f32)
            for side in (0, 1)
        ]
        second = jnp.concatenate(totals, axis=3)
        third = third_recvs(second)
        second_qkv = jnp.concatenate(
            [
                second_total(keep, recv, next_recv)
                for keep, recv, next_recv in zip(terms[::2], recvs, next_recvs)
            ],
            axis=2,
        )
        third_qkv = third_recvs(second_qkv)
        third, third_qkv = lax.optimization_barrier((third, third_qkv))
        shard_out, shard_up, shard_down, shard_qkv = weight_grads(
            second, third, second_qkv, third_qkv
        )
    if parts > 1:
        grad_input, small, flat = leave(
            home, inputs, grad_hidden, modulation, gains, full_qkv, sums, devices
        )
        base = 2 * width + units
        ends = (base + width, base + width + units)
        shard_qkv, shard_out, shard_up, shard_down = (
            lax.psum_scatter(
                jnp.einsum("tk,tn->kn", left, right, preferred_element_type=f32),
                EVERY,
                scatter_dimension=0,
                tiled=True,
            )
            for left, right in (
                (entered, flat),
                (pack[:, :width], pack[:, base : ends[0]]),
                (pack[:, width : 2 * width], pack[:, ends[0] : ends[1]]),
                (pack[:, 2 * width : base], pack[:, ends[1] :]),
            )
        )
    small = lax.all_to_all(small, EVERY, 0, 0, tiled=True)
    if parts == 1:
        small = after(small, second_qkv)
    grads = finish(small, time_embed, gains, width, units)
    loss_value = grads[6].reshape(())
    return (
        final,
        loss_value,
        grad_input,
        grads[0].T,
        grads[1].reshape(-1),
        grads[2].reshape(-1),
        shard_qkv,
        shard_out,
        grads[3].reshape(-1),
        shard_up,
        grads[4].reshape(-1),
        shard_down,
        grads[5].reshape(-1),
    )


def solution(mesh):
    blocks = mesh.shape["blk"]
    fine = Mesh(mesh.devices.reshape(2, 2, blocks // 8, 4, 2), EVERY)
    tokens = ("rb", "sz", "sy", "hx", "hc")
    return jax.shard_map(
        on_device,
        mesh=fine,
        in_specs=(
            P(None, tokens, None),
            P(),
            P(None, tokens),
            P(None, tokens),
            P(None, tokens, None),
            P(None, EVERY),
            P(EVERY),
            P(EVERY),
            P(EVERY, None),
            P(EVERY, None),
            P(EVERY),
            P(EVERY, None),
            P(EVERY),
            P(EVERY, None),
            P(EVERY),
        ),
        out_specs=(
            P(None, tokens, None),
            P(),
            P(None, tokens, None),
            P(None, EVERY),
            P(EVERY),
            P(EVERY),
            P(EVERY, None),
            P(EVERY, None),
            P(EVERY),
            P(EVERY, None),
            P(EVERY),
            P(EVERY, None),
            P(EVERY),
        ),
        check_vma=False,
    )
```

```python
from functools import partial

import jax
import jax.numpy as jnp
from jax import lax
from jax.experimental import pallas as pl
from jax.experimental.pallas import tpu as pltpu
from jax.sharding import Mesh, PartitionSpec as P

HEADS = 12
HEAD_DIM = 64
GROUPS = 4
WIDTH = HEADS // GROUPS * HEAD_DIM
EVERY = ("hx", "hc", "rb", "sz", "sy")
SPOT = ("sz", "sy")
bf16 = jnp.bfloat16
f32 = jnp.float32
precise = lax.Precision.HIGHEST


def normalize(hidden):
    average = jnp.mean(hidden, axis=-1, keepdims=True)
    centred = hidden - average
    variance = jnp.mean(centred * centred, axis=-1, keepdims=True)
    inverse = lax.rsqrt(variance + 1e-05)
    return (centred * inverse, inverse)


def dot(left, right):
    return jnp.dot(left, right, preferred_element_type=f32)


def dot_nt(left, right):
    return lax.dot_general(left, right, (((1,), (1,)), ((), ())), preferred_element_type=f32)


def norm_back(upstream, normed, inverse):
    first_mean = jnp.mean(upstream, axis=-1, keepdims=True)
    second_mean = jnp.mean(upstream * normed, axis=-1, keepdims=True)
    return inverse * (upstream - first_mean - normed * second_mean)


def swap(value, axis):
    return lax.ppermute(value, axis, [(0, 1), (1, 0)])


def turn(value, axis, step):
    size = lax.axis_size(axis)
    return lax.ppermute(value, axis, [(i, (i - step) % size) for i in range(size)])


def place():
    return jnp.stack([lax.axis_index(name) for name in ("hx", "hc", "sz", "sy", "rb")]).astype(
        jnp.int32
    )


ANY = pl.BlockSpec(memory_space=pl.ANY)
SMEM = pl.BlockSpec(memory_space=pltpu.SMEM)
VMEM = pl.BlockSpec(memory_space=pltpu.VMEM)


def hbm(value):
    return pltpu.with_memory_space_constraint(value, pltpu.HBM)


def whole_spec(shape):
    return pl.BlockSpec(shape, lambda *_: (0,) * len(shape))


def result(shape, kind, free=False):
    return jax.ShapeDtypeStruct(shape, kind) if free else pltpu.HBM(shape, kind)


def single(kernel, outs, values, raw=(), held=(), scratch=(), limit=40, place=None, raw_outs=0):
    specs = [whole_spec(v.shape) for v in values] + [ANY] * len(raw) + [VMEM] * len(held)
    values = [hbm(v) for v in values] + list(raw) + list(held)
    blocked_outs = len(outs) - raw_outs
    if place is not None:
        specs, values = [SMEM] + specs, [place] + values
    return pl.pallas_call(
        kernel,
        grid=(1,),
        out_shape=tuple(result(*o) for o in outs),
        in_specs=specs,
        out_specs=tuple(
            whole_spec(o[0]) if i < blocked_outs else ANY for i, o in enumerate(outs)
        ),
        scratch_shapes=list(scratch),
        compiler_params=pltpu.CompilerParams(vmem_limit_bytes=limit << 20),
    )(*values)


def join_copies(place_ref, sides, blocks, sems):
    hx, hc, sz, sy = (place_ref[i] for i in range(4))
    half = sides[0].shape[-1]
    copies = []
    for number, pieces in enumerate(sides):
        side, core = divmod(number, 2)
        for second in range(2):
            for first in range(2):
                for deep in range(4):
                    across, down = (first, second) if side == 0 else (second, first)
                    block = (hx ^ across) * 2 + (hc ^ core)
                    spot = (block * 4 + lax.rem(sz + deep, 4)) * 2 + (sy ^ down)
                    copies.append(
                        pltpu.make_async_copy(
                            pieces.at[second, first, deep],
                            blocks.at[spot, :, pl.ds(side * half, half)],
                            sems.at[len(copies)],
                        )
                    )
    return copies


def gather_rows(here, shard, every, use):
    half = shard.shape[1] // 2
    sides = []
    deep = jnp.stack([shard] + [turn(shard, "sz", k) for k in (1, 2, 3)])
    orders = (("hx", "sy"), ("sy", "hx"))
    deep, every = lax.optimization_barrier((deep, every))
    levels = [deep[:, :, :half], deep[:, :, half:]]
    levels = [jnp.stack([v, swap(v, order[0])]) for v, order in zip(levels, orders)]
    levels = [jnp.stack([v, swap(v, order[1])]) for v, order in zip(levels, orders)]
    used = use(every)
    levels, used = lax.optimization_barrier((levels, used))
    for level in levels:
        sides += [level, swap(level, "hc")]
    return sides, used


def piece_copies(place_ref, blocks, keep, send, sems, side, columns):
    hx, sz, sy = place_ref[0], place_ref[2], place_ref[3]
    copies = []
    for second in range(2):
        for first in range(2):
            for deep in range(4):
                across, down = (first, second) if side == 0 else (second, first)
                spot = ((hx ^ across) * 4 + lax.rem(sz + deep, 4)) * 2 + (sy ^ down)
                source = blocks.at[(spot,) + (slice(None),) * (len(blocks.shape) - 2) + (columns,)]
                target = (keep, send)[second].at[first, deep]
                copies.append(pltpu.make_async_copy(source, target, sems.at[len(copies)]))
    for copy in copies:
        copy.start()
    return copies


ORDERS = (("sy", "hx"), ("hx", "sy"))
COLUMN_GROUPS = ((1, 0), (2, 0), (1, 1), (2, 1))


def second_send(keep, recv):
    return (keep[1].astype(f32) + recv[1].astype(f32)).astype(bf16)


def second_total(keep, recv, recv_second):
    return keep[0].astype(f32) + recv[0].astype(f32) + recv_second.astype(f32)


def third_recvs(total):
    return [turn(total[k].astype(bf16), "sz", -k) for k in (1, 2, 3)]


def enter_kernel(place_ref, x_ref, mod_ref, gains_ref, *refs):
    *sides, entered_ref, pair_ref, query_ref, whole_ref, block_sc, weight_sc, sems, sem = refs
    seqs, tokens, width = x_ref.shape
    half = tokens // 2
    pieced = len(sides) > 1
    if pieced:
        copies = join_copies(place_ref, sides, block_sc, sems)
    else:
        copies = [pltpu.make_async_copy(sides[0], weight_sc, sem)]
    for copy in copies:
        copy.start()
    for s in range(seqs):
        normed = normalize(x_ref[s].astype(f32))[0]
        shift, scale = (mod_ref[s : s + 1, pl.ds(i * width, width)] for i in (0, 1))
        value = normed * gains_ref[0:1] * (1.0 + scale) + shift
        entered_ref[pl.ds(s * tokens, tokens), :] = value.astype(bf16)
    entered = entered_ref[...]
    for copy in copies:
        copy.wait()
    if pieced:
        rows = block_sc.shape[1]
        for i in range(block_sc.shape[0]):
            weight_sc[pl.ds(i * rows, rows), :] = block_sc[i]
    leaving = pltpu.make_async_copy(weight_sc, whole_ref, sem)
    leaving.start()
    for which in (1, 2, 0):
        triple = dot(entered, weight_sc[:, pl.ds(which * width, width)])
        if which == 0:
            triple = triple * HEAD_DIM ** (-0.5)
        triple = triple.astype(bf16)
        for s in range(seqs):
            for g in range(GROUPS):
                rows = triple[s * tokens : (s + 1) * tokens, g * WIDTH : (g + 1) * WIDTH]
                slot = s * GROUPS + g
                if which == 0:
                    query_ref[slot, :, pl.ds(0, WIDTH)] = rows[:half]
                    query_ref[slot, :, pl.ds(WIDTH, WIDTH)] = rows[half:]
                else:
                    pair_ref[slot, :, pl.ds((which - 1) * WIDTH, WIDTH)] = rows
    leaving.wait()


def enter(here, inputs, modulation, gains, sides):
    seqs, tokens, width = inputs.shape
    rows = sides[0].shape[-2] if len(sides) > 1 else width // 32
    return single(
        enter_kernel,
        [
            ((seqs * tokens, width), bf16),
            ((8, tokens, 2 * WIDTH), bf16, True),
            ((8, tokens // 2, 2 * WIDTH), bf16, True),
            ((width, 3 * width), bf16),
        ],
        [inputs, modulation, gains],
        raw=sides,
        scratch=[
            pltpu.VMEM((32, rows, 3 * width), bf16),
            pltpu.VMEM((width, 3 * width), bf16),
            pltpu.SemaphoreType.DMA((64,)),
            pltpu.SemaphoreType.DMA,
        ],
        place=here,
        raw_outs=1,
    )


def load_pairs(pair_ref, slot, first_row, half):
    value = pair_ref[slot, pl.ds(first_row, half), :]
    return value[:, :WIDTH], value[:, WIDTH:]


def key_column(docs_ref, step):
    row = docs_ref[pl.ds(step, 1), :]
    return jnp.broadcast_to(row, (8, row.shape[1])).T[:, 0:1]


def gather_pairs(pair_ref, target):
    half = pair_ref.shape[1]
    for slot in range(pair_ref.shape[0]):
        for part, rows in enumerate(load_pairs(pair_ref, slot, 0, half)):
            target[pl.ds((slot * 2 + part) * half, half), :] = rows


def spread_heads(rows, target):
    lane = lax.broadcasted_iota(jnp.int32, (1, WIDTH), 1)
    for h in range(target.shape[0]):
        own = (lane >= h * HEAD_DIM) & (lane < (h + 1) * HEAD_DIM)
        target[h] = rows * jnp.where(own, 1.0, 0.0).astype(bf16)


def fetch(step, pair_refs, starts, pair_sc):
    for ref, (begin, end) in zip(pair_refs, starts):
        @pl.when((step >= begin) & (step < end))
        def take(ref=ref):
            pair_sc[...] = ref[...]


def forward_kernel(
    starts, came_ref, first_ref, second_ref, third_ref, fourth_ref, key_docs_ref, query_docs_ref,
    out_ref, turned_ref, total_ref, query_sc, flat_sc, pair_sc, top_sc, sum_sc, acc_sc,
):
    step = pl.program_id(0)
    heads, queries = query_sc.shape[:2]
    half = out_ref.shape[1]

    @pl.when(step == 0)
    def start():
        gather_pairs(came_ref, flat_sc)
        spread_heads(flat_sc[...], query_sc)
        top_sc[...] = jnp.full(top_sc.shape, -1e30, f32)
        sum_sc[...] = jnp.zeros(sum_sc.shape, f32)
        acc_sc[...] = jnp.zeros(acc_sc.shape, f32)

    fetch(step, (first_ref, second_ref, third_ref, fourth_ref), starts, pair_sc)
    key_part = pair_sc[:, :WIDTH]
    value_turned = pair_sc[:, WIDTH:].T
    allowed = key_column(key_docs_ref, step) == query_docs_ref[...]
    old = [top_sc[h : h + 1] for h in range(heads)]
    raw = [dot_nt(key_part, query_sc[h]) for h in range(heads)]
    scores = [jnp.where(allowed, value, -1e30) for value in raw]
    new = [jnp.maximum(o, jnp.max(v, axis=0, keepdims=True)) for o, v in zip(old, scores)]
    exponent = [jnp.exp(v - n) for v, n in zip(scores, new)]
    terms = [
        dot(value_turned[h * HEAD_DIM : (h + 1) * HEAD_DIM], exponent[h].astype(bf16))
        for h in range(heads)
    ]
    sums = [jnp.sum(v, axis=0, keepdims=True) for v in exponent]
    for h in range(heads):
        rows = pl.ds(h * HEAD_DIM, HEAD_DIM)
        fade = jnp.exp(old[h] - new[h])
        top_sc[h : h + 1] = new[h]
        sum_sc[h : h + 1] = sum_sc[h : h + 1] * fade + sums[h]
        acc_sc[rows] = acc_sc[rows] * fade + terms[h]

    @pl.when(step == pl.num_programs(0) - 1)
    def finish():
        total_ref[...] = jnp.zeros(total_ref.shape, f32)
        for h in range(heads):
            rows = pl.ds(h * HEAD_DIM, HEAD_DIM)
            turned_ref[rows] = acc_sc[rows] / sum_sc[h : h + 1]
            total_ref[h : h + 1] = top_sc[h : h + 1] + jnp.log(sum_sc[h : h + 1])
        whole = turned_ref[...].astype(bf16).T
        for slot in range(8):
            for part in range(2):
                begin = (slot * 2 + part) * half
                out_ref[slot, :, pl.ds(part * WIDTH, WIDTH)] = whole[begin : begin + half]


def pair_specs(pairs, chunk):
    specs, starts, begin = [], [], 0
    for pair in pairs:
        count = pair.shape[0] // chunk
        specs.append(
            pl.BlockSpec(
                (chunk, 2 * WIDTH),
                lambda i, begin=begin, count=count: (jnp.clip(i - begin, 0, count - 1), 0),
            )
        )
        starts.append((begin, begin + count))
        begin += count
    return specs, starts, begin


def attend(came, pairs, key_docs, query_docs):
    slots, half, columns = came.shape
    queries = slots * 2 * half
    heads = WIDTH // HEAD_DIM
    chunk = 512
    specs, starts, steps = pair_specs(pairs, chunk)
    outs = (
        result((slots, half, columns), bf16, True),
        result((WIDTH, queries), f32),
        result((8, queries), f32),
    )
    return pl.pallas_call(
        partial(forward_kernel, starts),
        grid=(steps,),
        out_shape=outs,
        in_specs=[
            whole_spec(came.shape),
            *specs,
            whole_spec(key_docs.shape),
            whole_spec(query_docs.shape),
        ],
        out_specs=tuple(whole_spec(o.shape) for o in outs),
        scratch_shapes=[
            pltpu.VMEM((heads, queries, WIDTH), bf16),
            pltpu.VMEM((queries, WIDTH), bf16),
            pltpu.VMEM((chunk, 2 * WIDTH), bf16),
            pltpu.VMEM((8, queries), f32),
            pltpu.VMEM((8, queries), f32),
            pltpu.VMEM((WIDTH, queries), f32),
        ],
        compiler_params=pltpu.CompilerParams(vmem_limit_bytes=48 << 20),
    )(*map(hbm, (came, *pairs, key_docs, query_docs)))


def backward_kernel(
    starts, came_ref, grad_ref, first_ref, second_ref, third_ref, fourth_ref, key_docs_ref, query_docs_ref,
    turned_ref, total_ref, query_out, keep_ref, keep_other, send_ref,
    query_sc, grad_sc, flat_sc, pair_sc, delta_sc, acc_sc,
):
    step = pl.program_id(0)
    heads, queries = query_sc.shape[:2]
    half = query_out.shape[1]

    @pl.when(step == 0)
    def start():
        gather_pairs(came_ref, flat_sc)
        spread_heads(flat_sc[...], query_sc)
        gather_pairs(grad_ref, flat_sc)
        spread_heads(flat_sc[...], grad_sc)
        acc_sc[...] = jnp.zeros(acc_sc.shape, f32)
        product = flat_sc[...].T.astype(f32) * turned_ref[...]
        for h in range(heads):
            rows = slice(h * HEAD_DIM, (h + 1) * HEAD_DIM)
            delta_sc[h : h + 1] = jnp.sum(product[rows], axis=0, keepdims=True)

    fetch(step, (first_ref, second_ref, third_ref, fourth_ref), starts, pair_sc)
    key_part = pair_sc[:, :WIDTH]
    value_part = pair_sc[:, WIDTH:]
    key_turned = key_part.T
    allowed = key_column(key_docs_ref, step) == query_docs_ref[...]
    raw = [dot_nt(key_part, query_sc[h]) for h in range(heads)]
    slopes = [dot_nt(value_part, grad_sc[h]) for h in range(heads)]
    probabilities = [
        jnp.exp(jnp.where(allowed, value, -1e30) - total_ref[h : h + 1])
        for h, value in enumerate(raw)
    ]
    grad_scores = [
        (p * (slope - delta_sc[h : h + 1])).astype(bf16)
        for h, (p, slope) in enumerate(zip(probabilities, slopes))
    ]
    grad_value = sum(dot(probabilities[h].astype(bf16), grad_sc[h]) for h in range(heads))
    grad_key = sum(dot(grad_scores[h], query_sc[h]) for h in range(heads))
    for h in range(heads):
        rows = pl.ds(h * HEAD_DIM, HEAD_DIM)
        acc_sc[rows] = acc_sc[rows] + dot(
            key_turned[h * HEAD_DIM : (h + 1) * HEAD_DIM], grad_scores[h]
        )
    quarter = pl.num_programs(0) // 4
    middle = 2 * quarter

    for number, ref in enumerate((keep_ref, keep_other)):
        @pl.when((step >= number * quarter) & (step < (number + 1) * quarter))
        def mine(ref=ref):
            ref[:, pl.ds(0, WIDTH)] = grad_key
            ref[:, pl.ds(WIDTH, WIDTH)] = grad_value

    @pl.when(step >= middle)
    def theirs():
        send_ref[:, pl.ds(0, WIDTH)] = grad_key.astype(bf16)
        send_ref[:, pl.ds(WIDTH, WIDTH)] = grad_value.astype(bf16)

    @pl.when(step == pl.num_programs(0) - 1)
    def finish():
        whole = (acc_sc[...] * HEAD_DIM ** (-0.5)).astype(bf16).T
        for slot in range(8):
            for part in range(2):
                begin = (slot * 2 + part) * half
                query_out[slot, :, pl.ds(part * WIDTH, WIDTH)] = whole[begin : begin + half]


def attend_back(came, grad, pairs, key_docs, query_docs, turned, total):
    slots, half, columns = came.shape
    queries = slots * 2 * half
    heads = WIDTH // HEAD_DIM
    chunk = 512
    specs, starts, steps = pair_specs(pairs, chunk)
    quarter = steps // 4
    middle = 2 * quarter
    return pl.pallas_call(
        partial(backward_kernel, starts),
        grid=(steps,),
        out_shape=(
            jax.ShapeDtypeStruct((slots, half, columns), bf16),
            jax.ShapeDtypeStruct((quarter * chunk, columns), f32),
            jax.ShapeDtypeStruct((quarter * chunk, columns), f32),
            jax.ShapeDtypeStruct((middle * chunk, columns), bf16),
        ),
        in_specs=[
            whole_spec(came.shape),
            whole_spec(grad.shape),
            *specs,
            whole_spec(key_docs.shape),
            whole_spec(query_docs.shape),
            whole_spec(turned.shape),
            whole_spec(total.shape),
        ],
        out_specs=(
            whole_spec((slots, half, columns)),
            pl.BlockSpec((chunk, columns), lambda i: (jnp.minimum(i, quarter - 1), 0)),
            pl.BlockSpec((chunk, columns), lambda i: (jnp.clip(i - quarter, 0, quarter - 1), 0)),
            pl.BlockSpec((chunk, columns), lambda i: (jnp.maximum(i - middle, 0), 0)),
        ),
        scratch_shapes=[
            pltpu.VMEM((heads, queries, WIDTH), bf16),
            pltpu.VMEM((heads, queries, WIDTH), bf16),
            pltpu.VMEM((queries, WIDTH), bf16),
            pltpu.VMEM((chunk, 2 * WIDTH), bf16),
            pltpu.VMEM((8, queries), f32),
            pltpu.VMEM((WIDTH, queries), f32),
        ],
        compiler_params=pltpu.CompilerParams(vmem_limit_bytes=48 << 20),
    )(*map(hbm, (came, grad, *pairs, key_docs, query_docs, turned, total)))


def settle_kernel(
    later_hbm, out_ref, up_ref, down_ref, block_sc, out_sc, up_sc, down_sc, sems, out_sems
):
    width = out_ref.shape[1]
    copies = [
        pltpu.make_async_copy(later_hbm.at[:, j], block_sc.at[j], sems.at[j]) for j in range(9)
    ]
    for copy in copies:
        copy.start()
    leaving = []
    for j in range(9):
        copies[j].wait()
        for i in range(32):
            value = block_sc[j, i]
            if j == 0:
                out_sc[pl.ds(i * 24, 24), :] = value
            elif j < 5:
                up_sc[pl.ds(i * 24, 24), pl.ds((j - 1) * width, width)] = value
            else:
                down_sc[pl.ds(i * 96 + (j - 5) * 24, 24), :] = value
        if j == 0:
            leaving.append(pltpu.make_async_copy(out_sc, out_ref, out_sems.at[j]))
        elif j < 5:
            columns = pl.ds((j - 1) * width, width)
            leaving.append(
                pltpu.make_async_copy(up_sc.at[:, columns], up_ref.at[:, columns], out_sems.at[j])
            )
        elif j == 8:
            leaving.append(pltpu.make_async_copy(down_sc, down_ref, out_sems.at[j]))
        if j < 5 or j == 8:
            leaving[-1].start()
    for copy in leaving:
        copy.wait()


def settle(later):
    width = later.shape[-1]
    shapes = ((width, width), (width, 4 * width), (4 * width, width))
    return pl.pallas_call(
        settle_kernel,
        out_shape=tuple(result(shape, bf16) for shape in shapes),
        in_specs=[ANY],
        out_specs=(ANY,) * 3,
        scratch_shapes=[
            pltpu.VMEM((9, 32, 24, width), bf16),
            *(pltpu.VMEM(shape, bf16) for shape in shapes),
            pltpu.SemaphoreType.DMA((9,)),
            pltpu.SemaphoreType.DMA((9,)),
        ],
        compiler_params=pltpu.CompilerParams(vmem_limit_bytes=40 << 20),
    )(hbm(later))


def middle_kernel(
    came_ref, x_ref, teacher_ref, mask_ref, mod_ref, gains_ref, up_bias_ref,
    out_hbm, up_hbm, down_hbm,
    final_ref, hidden_ref, leave_ref, pack_ref, sums_ref, out_sc, up_sc, down_sc, slope_sc, sems,
):
    seqs, tokens, width = x_ref.shape
    units = up_sc.shape[1]
    rows = seqs * tokens
    half = tokens // 2
    parts = [pl.ds(f * width, width) for f in range(units // width)]
    copies = [pltpu.make_async_copy(out_hbm, out_sc, sems.at[0])]
    for f, part in enumerate(parts):
        copies.append(
            pltpu.make_async_copy(up_hbm.at[:, part], up_sc.at[:, part], sems.at[1 + 2 * f])
        )
        copies.append(
            pltpu.make_async_copy(down_hbm.at[part, :], down_sc.at[part, :], sems.at[2 + 2 * f])
        )
    for copy in copies:
        copy.start()
    masks = mask_ref[...].T

    def wide(index):
        return jnp.concatenate(
            [
                jnp.broadcast_to(
                    mod_ref[s : s + 1, pl.ds(index * width, width)], (tokens, width)
                )
                for s in range(seqs)
            ]
        )

    def add_rows(first, value):
        for s in range(seqs):
            sums_ref[first + s : first + s + 1] = jnp.sum(
                value[s * tokens : (s + 1) * tokens], axis=0, keepdims=True
            )

    for s in range(seqs):
        for g in range(GROUPS):
            left, right = load_pairs(came_ref, s * GROUPS + g, 0, half)
            columns = pl.ds(g * WIDTH, WIDTH)
            pack_ref[pl.ds(s * tokens, half), columns] = left
            pack_ref[pl.ds(s * tokens + half, half), columns] = right
    mixed = pack_ref[:, pl.ds(0, width)]
    residual = jnp.concatenate([x_ref[s].astype(f32) for s in range(seqs)])
    copies[0].wait()
    branch = dot(mixed, out_sc[...])
    hidden = residual + wide(2) * branch
    normed, inverse = normalize(hidden)
    scaled = normed * gains_ref[1:2]
    moved = (scaled * (1.0 + wide(4)) + wide(3)).astype(bf16)
    pack_ref[:, pl.ds(width, width)] = moved
    lower = None
    for f in range(units // width):
        columns = pl.ds(f * width, width)
        copies[1 + 2 * f].wait()
        u = dot(moved, up_sc[:, columns]) + up_bias_ref[0:1, columns]
        square = u * u
        t = jnp.tanh(0.7978845608028654 * (u + 0.044715 * u * square))
        active = (0.5 * u * (1.0 + t)).astype(bf16)
        slope_sc[:, columns] = 0.5 * (1.0 + t) + 0.5 * u * (1.0 - t * t) * 0.7978845608028654 * (
            1.0 + 0.134145 * square
        )
        pack_ref[:, pl.ds(2 * width + f * width, width)] = active
        copies[2 + 2 * f].wait()
        term = dot(active, down_sc[columns, :])
        lower = term if lower is None else lower + term
    lower = lower + gains_ref[2:3]
    gate = wide(5)
    final = hidden + gate * lower
    for s in range(seqs):
        final_ref[s] = final[s * tokens : (s + 1) * tokens].astype(bf16)
    teacher = jnp.concatenate([teacher_ref[s].astype(f32) for s in range(seqs)])
    mismatch = final - teacher
    sums_ref[14:15] = jnp.sum(
        masks[:, 0:1] * mismatch * mismatch, axis=0, keepdims=True
    )
    sums_ref[15:16] = jnp.zeros((1, width), f32)
    grad_final = masks[:, 1:2] * mismatch
    add_rows(6, grad_final * lower)
    grad_lower = (gate * grad_final).astype(bf16)
    base = 2 * width + units
    pack_ref[:, pl.ds(base + width + units, width)] = grad_lower
    sums_ref[9:10] = jnp.sum(grad_lower.astype(f32), axis=0, keepdims=True)
    grad_moved = None
    for f in range(units // width):
        columns = pl.ds(f * width, width)
        grad_active = dot_nt(grad_lower, down_sc[columns, :])
        grad_upper = (grad_active * slope_sc[:, columns]).astype(bf16)
        pack_ref[:, pl.ds(base + width + f * width, width)] = grad_upper
        sums_ref[10 + f : 11 + f] = jnp.sum(grad_upper.astype(f32), axis=0, keepdims=True)
        term = dot_nt(grad_upper, up_sc[:, columns])
        grad_moved = term if grad_moved is None else grad_moved + term
    add_rows(2, grad_moved)
    add_rows(4, grad_moved * scaled)
    grad_scaled = grad_moved * (1.0 + wide(4))
    sums_ref[8:9] = jnp.sum(grad_scaled * normed, axis=0, keepdims=True)
    grad_hidden = grad_final + norm_back(grad_scaled * gains_ref[1:2], normed, inverse)
    hidden_ref[...] = grad_hidden
    add_rows(0, grad_hidden * branch)
    grad_branch = (wide(2) * grad_hidden).astype(bf16)
    pack_ref[:, pl.ds(base, width)] = grad_branch
    grad_mixed = dot_nt(grad_branch, out_sc[...]).astype(bf16)
    for s in range(seqs):
        for g in range(GROUPS):
            piece = grad_mixed[s * tokens : (s + 1) * tokens, g * WIDTH : (g + 1) * WIDTH]
            leave_ref[s * GROUPS + g, :, pl.ds(0, WIDTH)] = piece[:half]
            leave_ref[s * GROUPS + g, :, pl.ds(WIDTH, WIDTH)] = piece[half:]


def middle(came, inputs, teacher, masks, modulation, gains, up_bias, weights):
    seqs, tokens, width = inputs.shape
    units = up_bias.shape[1]
    rows = seqs * tokens
    return single(
        middle_kernel,
        [
            ((seqs, tokens, width), bf16),
            ((rows, width), f32),
            (came.shape, bf16, True),
            ((rows, 4 * width + 2 * units), bf16, True),
            ((16, width), f32),
        ],
        [came, inputs, teacher, masks, modulation, gains, up_bias],
        raw=[hbm(w) for w in weights],
        scratch=[
            pltpu.VMEM((width, width), bf16),
            pltpu.VMEM((width, units), bf16),
            pltpu.VMEM((units, width), bf16),
            pltpu.VMEM((rows, units), f32),
            pltpu.SemaphoreType.DMA((9,)),
        ],
        limit=40,
    )


def weights_kernel(
    place_ref, own_ref, other_ref, *refs
):
    *groups, left_sc, right_sc, block_sc, sems = refs
    rows, width = own_ref.shape[0], block_sc.shape[-1]
    units = 4 * width
    hc = place_ref[1]
    base = 2 * width + units
    for which, ref in enumerate((own_ref, other_ref)):
        left_sc[:, pl.ds(which * rows, rows)] = ref[:, pl.ds(0, base)].T
        right_sc[pl.ds(which * rows, rows), :] = ref[:, pl.ds(base, base)]
    for hx in range(2):
        begin = pl.multiple_of(hx * 384 + hc * 192, 64)
        for j in range(5):
            offset = 0 if j == 0 else width
            value = dot(left_sc[pl.ds(begin + offset, 192), :], right_sc[:, pl.ds(j * width, width)])
            for i in range(8):
                block_sc[hx * 8 + i, j] = value[i * 24 : (i + 1) * 24].astype(bf16)
        begin = pl.multiple_of(2 * width + hx * 1536 + hc * 768, 256)
        value = dot(left_sc[pl.ds(begin, 768), :], right_sc[:, pl.ds(width + units, width)])
        for i in range(8):
            for j in range(4):
                first = i * 96 + j * 24
                block_sc[hx * 8 + i, 5 + j] = value[first : first + 24].astype(bf16)
    copies = []
    begin = 0
    for number, (_, side) in enumerate(COLUMN_GROUPS):
        keep, send = groups[2 * number : 2 * number + 2]
        columns = pl.ds(begin, keep.shape[-1])
        copies += piece_copies(place_ref, block_sc, keep, send, sems.at[number], side, columns)
        begin += keep.shape[-1]
    for copy in copies:
        copy.wait()


def weight_terms(here, own, other, width):
    rows, total = own.shape
    return single(
        weights_kernel,
        [((2, 4, 9, 24, 128 * size), bf16) for size, _ in COLUMN_GROUPS for _ in range(2)],
        [],
        held=[own, other],
        scratch=[
            pltpu.VMEM((total // 2, 2 * rows), bf16),
            pltpu.VMEM((2 * rows, total // 2), bf16),
            pltpu.VMEM((16, 9, 24, width), bf16),
            pltpu.SemaphoreType.DMA((len(COLUMN_GROUPS), 16)),
        ],
        limit=40,
        place=here,
        raw_outs=2 * len(COLUMN_GROUPS),
    )


def flat_rows(home_ref, target, first_row, seqs, tokens, width):
    half = tokens // 2
    for s in range(seqs):
        for g in range(GROUPS):
            slot = s * GROUPS + g
            row = first_row + s * tokens
            left, right = load_pairs(home_ref, slot, tokens, half)
            target[pl.ds(row, half), pl.ds(g * WIDTH, WIDTH)] = left
            target[pl.ds(row + half, half), pl.ds(g * WIDTH, WIDTH)] = right
            left, right = load_pairs(home_ref, slot, 0, tokens)
            target[pl.ds(row, tokens), pl.ds(width + g * WIDTH, WIDTH)] = left
            target[pl.ds(row, tokens), pl.ds(2 * width + g * WIDTH, WIDTH)] = right


def qkv_kernel(
    seqs, place_ref, entered_ref, entered_other, home_ref, home_other,
    keep_a, send_a, keep_b, send_b, left_sc, right_sc, block_sc, sems,
):
    rows, width = entered_ref.shape
    hc = place_ref[1]
    for which, (left, home) in enumerate(((entered_ref, home_ref), (entered_other, home_other))):
        left_sc[:, pl.ds(which * rows, rows)] = left[...].T
        flat_rows(home, right_sc, which * rows, seqs, rows // seqs, width)
    for hx in range(2):
        begin = pl.multiple_of(hx * 384 + hc * 192, 64)
        for j in range(3):
            value = dot(left_sc[pl.ds(begin, 192), :], right_sc[:, pl.ds(j * width, width)])
            for i in range(8):
                block_sc[hx * 8 + i, :, pl.ds(j * width, width)] = value[
                    i * 24 : (i + 1) * 24
                ].astype(bf16)
    half = 3 * width // 2
    copies = piece_copies(place_ref, block_sc, keep_a, send_a, sems.at[0], 0, pl.ds(0, half))
    copies += piece_copies(place_ref, block_sc, keep_b, send_b, sems.at[1], 1, pl.ds(half, half))
    for copy in copies:
        copy.wait()


def qkv_terms(here, seqs, *values):
    rows, width = values[0].shape
    return single(
        partial(qkv_kernel, seqs),
        [((2, 4, 24, 3 * width // 2), bf16)] * 4,
        values,
        scratch=[
            pltpu.VMEM((width, 2 * rows), bf16),
            pltpu.VMEM((2 * rows, 3 * width), bf16),
            pltpu.VMEM((16, 24, 3 * width), bf16),
            pltpu.SemaphoreType.DMA((2, 16)),
        ],
        place=here,
        raw_outs=4,
    )


def leave_kernel(
    home_ref, x_ref, hidden_ref, mod_ref, gains_ref, weight_ref, middle_ref,
    grad_ref, small_ref, flat_ref,
):
    seqs, tokens, width = x_ref.shape
    devices = small_ref.shape[0]
    flat_rows(home_ref, flat_ref, 0, seqs, tokens, width)
    grad_entered = None
    for which in range(3):
        columns = pl.ds(which * width, width)
        term = dot_nt(flat_ref[:, columns], weight_ref[:, columns])
        grad_entered = term if grad_entered is None else grad_entered + term
    gain_sum = None
    sums = []
    for s in range(seqs):
        normed, inverse = normalize(x_ref[s].astype(f32))
        rows = slice(s * tokens, (s + 1) * tokens)
        grad = grad_entered[rows]
        shift_sum = jnp.sum(grad, axis=0, keepdims=True)
        scale_sum = jnp.sum(grad * (normed * gains_ref[0:1]), axis=0, keepdims=True)
        grad_scaled = grad * (1.0 + mod_ref[s : s + 1, pl.ds(width, width)])
        term = jnp.sum(grad_scaled * normed, axis=0, keepdims=True)
        gain_sum = term if gain_sum is None else gain_sum + term
        grad_ref[s] = hidden_ref[rows] + norm_back(grad_scaled * gains_ref[0:1], normed, inverse)
        later = [middle_ref[i + s : i + s + 1] for i in (0, 2, 4, 6)]
        sums.append(jnp.concatenate([shift_sum, scale_sum, *later], axis=1))
    up_bias = jnp.concatenate([middle_ref[i : i + 1] for i in range(10, 14)], axis=1)
    fields = [*sums, gain_sum, middle_ref[8:9], up_bias, middle_ref[9:10]]
    error = jnp.sum(middle_ref[14:15], axis=1, keepdims=True)
    small_ref[...] = jnp.zeros(small_ref.shape, f32)
    begin = 0
    for field in fields:
        size = field.shape[1] // devices
        for i in range(devices):
            small_ref[i, :, pl.ds(begin, size)] = field[:, i * size : (i + 1) * size]
        begin += size
    small_ref[:, :, pl.ds(begin, 1)] = jnp.broadcast_to(error[None], (devices, 1, 1))


def leave(home, inputs, grad_hidden, modulation, gains, weight, sums, devices):
    seqs, tokens, width = inputs.shape
    return single(
        leave_kernel,
        [
            ((seqs, tokens, width), f32),
            ((devices, 1, 512), f32, True),
            ((seqs * tokens, 3 * width), bf16),
        ],
        [home, inputs, grad_hidden, modulation, gains, weight, sums],
    )


def unpack_kernel(
    parts, sizes, factor, place_ref, every_ref, valid_ref,
    mod_ref, gains_ref, up_ref, key_docs_ref, query_docs_ref, masks_ref,
):
    devices = every_ref.shape[0]
    seqs, tokens = valid_ref.shape
    size_mod, size_gain, size_up = sizes
    mod_ref[...] = jnp.zeros(mod_ref.shape, f32)
    gains_ref[...] = jnp.zeros(gains_ref.shape, f32)
    up_ref[...] = jnp.zeros(up_ref.shape, f32)
    begin = 0
    targets = [(mod_ref, s, size_mod) for s in range(seqs)]
    targets += [(gains_ref, 0, size_gain), (gains_ref, 1, size_gain)]
    targets += [(up_ref, 0, size_up), (gains_ref, 2, size_gain)]
    for target, row, size in targets:
        for i in range(devices):
            target[row : row + 1, pl.ds(i * size, size)] = every_ref[i, :, pl.ds(begin, size)]
        begin += size
    hx, hc, sz, sy, rb = (place_ref[i] for i in range(5))
    second = sz * 2 + sy >= GROUPS
    row = 0
    for core in range(2):
        for across in range(2):
            for part in range(parts):
                block = ((hx ^ across) * 2 + (hc ^ core)) * parts + part
                for spot in range(8):
                    line = every_ref[block * 8 + spot, :, pl.ds(begin, 2 * tokens)]
                    key_docs_ref[row : row + 1, pl.ds(spot * tokens, tokens)] = jnp.where(
                        second, line[:, tokens:], line[:, :tokens]
                    )
                row += 1
    for spot in range(8):
        line = every_ref[((hx * 2 + hc) * parts + rb) * 8 + spot, :, pl.ds(begin, 2 * tokens)]
        query_docs_ref[:, pl.ds(spot * tokens, tokens)] = jnp.where(
            second, line[:, tokens:], line[:, :tokens]
        )
    begin += 2 * tokens
    count = jnp.sum(every_ref[:, :, pl.ds(begin, 1)], axis=0)
    gains_ref[3:4, pl.ds(0, 1)] = count
    masks_ref[...] = jnp.zeros(masks_ref.shape, f32)
    for s in range(seqs):
        valid = valid_ref[s : s + 1, :].astype(f32)
        masks_ref[0:1, pl.ds(s * tokens, tokens)] = valid
        masks_ref[1:2, pl.ds(s * tokens, tokens)] = valid * (factor / count)


def unpack(here, every, valid_mask, width, units, parts, length):
    seqs, tokens = valid_mask.shape
    devices = every.shape[0]
    sizes = (6 * width // devices, width // devices, units // devices)
    return single(
        partial(unpack_kernel, parts, sizes, float(seqs * length)),
        [
            ((8, 6 * width), f32),
            ((8, width), f32),
            ((8, units), f32),
            ((4 * parts, 8 * tokens), f32),
            ((1, 8 * tokens), f32),
            ((8, seqs * tokens), f32),
        ],
        [every, valid_mask],
        place=here,
    )


def finish_kernel(width, small_ref, embed_ref, gains_ref, *refs):
    ada_ref, bias_ref, *vectors, loss_ref = refs
    seqs = embed_ref.shape[0]
    columns = ada_ref.shape[0]
    added = jnp.sum(small_ref[...], axis=0)
    begin = 0
    ada = bias = None
    for s in range(seqs):
        grad = added[:, begin : begin + columns]
        begin += columns
        turned = jnp.broadcast_to(grad, (8, columns)).T[:, 0:1]
        term = turned * embed_ref[s : s + 1, :]
        ada = term if ada is None else ada + term
        bias = grad if bias is None else bias + grad
    ada_ref[...] = ada
    bias_ref[...] = bias
    for ref in vectors:
        size = ref.shape[1]
        ref[...] = added[:, begin : begin + size]
        begin += size
    loss_ref[...] = added[:, begin : begin + 1] / (gains_ref[3:4, 0:1] * width)


def finish(small, time_embed, gains, width, units):
    devices = small.shape[0]
    sizes = [6 * width // devices] + [size // devices for size in (width, width, units, width)]
    return single(
        partial(finish_kernel, float(width)),
        [((sizes[0], time_embed.shape[1]), f32)]
        + [((1, size), f32, True) for size in sizes]
        + [((1, 1), f32, True)],
        [small, time_embed, gains],
    )


def grads_kernel(total_ref, first_ref, second_ref, third_ref, *refs):
    qkv_total, qkv_first, qkv_second, qkv_third, out_ref, up_ref, down_ref, qkv_ref = refs
    width = out_ref.shape[1]
    for j in range(9):
        value = total_ref[0, j]
        for ref in (first_ref, second_ref, third_ref):
            value = value + ref[j].astype(f32)
        if j == 0:
            out_ref[...] = value
        elif j < 5:
            up_ref[:, pl.ds((j - 1) * width, width)] = value
        else:
            down_ref[pl.ds((j - 5) * 24, 24), :] = value
    value = qkv_total[0]
    for ref in (qkv_first, qkv_second, qkv_third):
        value = value + ref[...].astype(f32)
    qkv_ref[...] = value


def weight_grads(total, third, qkv_total, third_qkv):
    width = total.shape[-1]
    values = [total, *third, qkv_total, *third_qkv]
    specs = [
        pl.BlockSpec((1,) + v.shape[1:], lambda i, n=v.ndim: (0,) * n)
        if i in (0, 4)
        else whole_spec(v.shape)
        for i, v in enumerate(values)
    ]
    shapes = ((24, width), (24, 4 * width), (96, width), (24, 3 * width))
    return pl.pallas_call(
        grads_kernel,
        grid=(1,),
        out_shape=tuple(jax.ShapeDtypeStruct(shape, f32) for shape in shapes),
        in_specs=specs,
        out_specs=tuple(whole_spec(shape) for shape in shapes),
        compiler_params=pltpu.CompilerParams(vmem_limit_bytes=40 << 20),
    )(*values)


def begin_kernel(embed_ref, ada_ref, segments_ref, valid_ref, *refs):
    vectors, refs = [ref[...].astype(f32) for ref in refs[:5]], refs[5:]
    *weights, packed_ref = refs[:-1] if len(refs) > 1 else refs
    seqs, tokens = segments_ref.shape
    modulation = lax.dot_general(
        embed_ref[...],
        ada_ref[...].astype(f32),
        (((1,), (1,)), ((), ())),
        precision=precise,
        preferred_element_type=f32,
    )
    modulation = modulation + vectors[0]
    count = jnp.sum(valid_ref[...].astype(f32), axis=1, keepdims=True)
    count = jnp.sum(count, axis=0, keepdims=True)
    fields = [modulation[s : s + 1] for s in range(seqs)]
    fields += vectors[1:]
    fields += [segments_ref[s : s + 1, :].astype(f32) for s in range(seqs)]
    fields.append(count)
    fields.append(jnp.zeros((1, packed_ref.shape[2] - sum(f.shape[1] for f in fields)), f32))
    packed_ref[...] = jnp.broadcast_to(
        jnp.concatenate(fields, axis=1)[None], packed_ref.shape
    )
    if weights:
        out_ref, up_ref, down_ref = weights
        later_ref = refs[-1]
        width = out_ref.shape[1]
        later_ref[0] = out_ref[...]
        for j in range(4):
            later_ref[1 + j] = up_ref[:, pl.ds(j * width, width)]
            later_ref[5 + j] = down_ref[pl.ds(j * 24, 24), :]


def begin_with(time_embed, ada_weight, vectors, segments, valid_mask, weights, devices):
    seqs, tokens = segments.shape
    columns = (seqs - 1) * ada_weight.shape[1] + sum(v.shape[1] for v in vectors) + seqs * tokens + 1
    outs = [((devices, 1, columns + -columns % 128), f32, True)]
    if weights:
        outs.append(((9, 24, weights[0].shape[1]), bf16))
    return single(
        begin_kernel, outs, [time_embed, ada_weight.T, segments, valid_mask, *vectors, *weights]
    )


def after(value, *others):
    return lax.optimization_barrier((value, others))[0]


def exchange(rows):
    return lax.all_to_all(rows, SPOT, 0, 0, tiled=True)


def on_device(
    inputs,
    time_embed,
    segments,
    valid_mask,
    teacher,
    ada_weight,
    ada_bias,
    gain_attn,
    qkv_weight,
    out_weight,
    gain_mlp,
    up_weight,
    up_bias,
    down_weight,
    down_bias,
):
    seqs, tokens, width = inputs.shape
    units = up_weight.shape[1]
    parts = lax.axis_size("rb")
    devices = 32 * parts
    length = tokens * devices
    queries = 8 * tokens
    here = place()

    vectors = [v.reshape(1, -1) for v in (ada_bias, gain_attn, gain_mlp, up_bias, down_bias)]
    weights = [] if parts > 1 else [out_weight, up_weight, down_weight]
    packed, *later = begin_with(
        time_embed, ada_weight, vectors, segments, valid_mask, weights, devices
    )
    every = lax.all_to_all(packed, EVERY, 0, 0, tiled=True)
    if parts > 1:
        sides, *later = (
            lax.all_gather(w, EVERY, axis=0, tiled=True)
            for w in (qkv_weight, out_weight, up_weight, down_weight)
        )
    else:
        later = [lax.all_gather(later[0], EVERY, axis=0, tiled=False)]

    def use(every):
        return unpack(here, every, valid_mask, width, units, parts, length)

    if parts > 1:
        sides = [sides]
        used = use(every)
    else:
        sides, used = gather_rows(here, qkv_weight, every, use)
    modulation, gains, full_up_bias, key_docs, query_docs, masks = used

    entered, pair, query, full_qkv = enter(here, inputs, modulation, gains, sides)
    pair = exchange(pair).reshape(queries, 2 * WIDTH)
    query = exchange(query)
    if parts > 1:
        pair = lax.all_gather(pair, "rb", axis=0, tiled=True)
    pair_x = swap(pair, "hx")
    pair_x, query = lax.optimization_barrier((pair_x, query))
    pairs = (pair, pair_x, swap(pair, "hc"), swap(pair_x, "hc"))
    attended, turned, total = attend(query, pairs, key_docs, query_docs)

    if parts == 1:
        later = settle(later[0])
    final, grad_hidden, grad_leaving, pack, sums = middle(
        exchange(attended), inputs, teacher, masks, modulation, gains, full_up_bias, later
    )
    grad_came = exchange(grad_leaving)
    if parts == 1:
        terms = weight_terms(here, pack, swap(pack, "hc"), width)
        grad_came, terms = lax.optimization_barrier((grad_came, terms))
        held = terms[::2]
        firsts = [
            swap(send, ORDERS[side][0]) for send, (_, side) in zip(terms[1::2], COLUMN_GROUPS)
        ]

    grad_query, keep, keep_x, send = attend_back(
        query, grad_came, pairs, key_docs, query_docs, turned, total
    )
    if parts == 1:
        send, firsts[0], firsts[2] = lax.optimization_barrier((send, firsts[0], firsts[2]))
    recv = swap(send, "hc")
    own_rows = keep.shape[0]
    send_x = (keep_x + recv[own_rows:].astype(f32)).astype(bf16)
    grad_pair = keep + recv[:own_rows].astype(f32) + swap(send_x, "hx").astype(f32)
    if parts > 1:
        grad_pair = lax.psum_scatter(grad_pair, "rb", scatter_dimension=0, tiled=True)
    home = jnp.concatenate(
        [grad_pair.astype(bf16).reshape(8, tokens, 2 * WIDTH), grad_query], axis=1
    )
    if parts == 1:
        seconds = [
            swap(
                jnp.concatenate(
                    [
                        second_send(keep, recv)
                        for keep, recv, (_, own) in zip(held, firsts, COLUMN_GROUPS)
                        if own == side
                    ],
                    axis=3,
                ),
                ORDERS[side][1],
            )
            for side in (0, 1)
        ]
    home = exchange(home)
    if parts == 1:
        others = swap(entered, "hc"), swap(home, "hc")
        terms = qkv_terms(here, seqs, entered, others[0], home, others[1])
        seconds = after(seconds, terms)
        recvs = [swap(send, order[0]) for send, order in zip(terms[1::2], ORDERS)]
        grad_input, small, flat = leave(
            after(home, terms), inputs, grad_hidden, modulation, gains, full_qkv, sums, devices
        )
        recvs = after(recvs, small)
        nexts = [second_send(keep, recv) for keep, recv in zip(terms[::2], recvs)]
        small = after(small, nexts)
        next_recvs = [swap(value, order[1]) for value, order in zip(nexts, ORDERS)]
        totals = [
            jnp.concatenate(
                [
                    keep[0].astype(f32) + recv[0].astype(f32)
                    for keep, recv, (_, own) in zip(held, firsts, COLUMN_GROUPS)
                    if own == side
                ],
                axis=3,
            )
            + seconds[side].astype(f32)
            for side in (0, 1)
        ]
        second = jnp.concatenate(totals, axis=3)
        third = third_recvs(second)
        second_qkv = jnp.concatenate(
            [
                second_total(keep, recv, next_recv)
                for keep, recv, next_recv in zip(terms[::2], recvs, next_recvs)
            ],
            axis=2,
        )
        third_qkv = third_recvs(second_qkv)
        third, third_qkv = lax.optimization_barrier((third, third_qkv))
        shard_out, shard_up, shard_down, shard_qkv = weight_grads(
            second, third, second_qkv, third_qkv
        )
    if parts > 1:
        grad_input, small, flat = leave(
            home, inputs, grad_hidden, modulation, gains, full_qkv, sums, devices
        )
        base = 2 * width + units
        ends = (base + width, base + width + units)
        shard_qkv, shard_out, shard_up, shard_down = (
            lax.psum_scatter(
                jnp.einsum("tk,tn->kn", left, right, preferred_element_type=f32),
                EVERY,
                scatter_dimension=0,
                tiled=True,
            )
            for left, right in (
                (entered, flat),
                (pack[:, :width], pack[:, base : ends[0]]),
                (pack[:, width : 2 * width], pack[:, ends[0] : ends[1]]),
                (pack[:, 2 * width : base], pack[:, ends[1] :]),
            )
        )
    small = lax.all_to_all(small, EVERY, 0, 0, tiled=True)
    if parts == 1:
        small = after(small, second_qkv)
    grads = finish(small, time_embed, gains, width, units)
    loss_value = grads[6].reshape(())
    return (
        final,
        loss_value,
        grad_input,
        grads[0].T,
        grads[1].reshape(-1),
        grads[2].reshape(-1),
        shard_qkv,
        shard_out,
        grads[3].reshape(-1),
        shard_up,
        grads[4].reshape(-1),
        shard_down,
        grads[5].reshape(-1),
    )


def solution(mesh):
    blocks = mesh.shape["blk"]
    fine = Mesh(mesh.devices.reshape(2, 2, blocks // 8, 4, 2), EVERY)
    tokens = ("rb", "sz", "sy", "hx", "hc")
    return jax.shard_map(
        on_device,
        mesh=fine,
        in_specs=(
            P(None, tokens, None),
            P(),
            P(None, tokens),
            P(None, tokens),
            P(None, tokens, None),
            P(None, EVERY),
            P(EVERY),
            P(EVERY),
            P(EVERY, None),
            P(EVERY, None),
            P(EVERY),
            P(EVERY, None),
            P(EVERY),
            P(EVERY, None),
            P(EVERY),
        ),
        out_specs=(
            P(None, tokens, None),
            P(),
            P(None, tokens, None),
            P(None, EVERY),
            P(EVERY),
            P(EVERY),
            P(EVERY, None),
            P(EVERY, None),
            P(EVERY),
            P(EVERY, None),
            P(EVERY),
            P(EVERY, None),
            P(EVERY),
        ),
        check_vma=False,
    )
```

```python
from functools import partial

import jax
import jax.numpy as jnp
from jax import lax
from jax.experimental import pallas as pl
from jax.experimental.pallas import tpu as pltpu
from jax.sharding import Mesh, PartitionSpec as P

HEADS = 12
HEAD_DIM = 64
GROUPS = 4
WIDTH = HEADS // GROUPS * HEAD_DIM
EVERY = ("hx", "hc", "rb", "sz", "sy")
SPOT = ("sz", "sy")
bf16 = jnp.bfloat16
f32 = jnp.float32
precise = lax.Precision.HIGHEST


def normalize(hidden):
    average = jnp.mean(hidden, axis=-1, keepdims=True)
    centred = hidden - average
    variance = jnp.mean(centred * centred, axis=-1, keepdims=True)
    inverse = lax.rsqrt(variance + 1e-05)
    return (centred * inverse, inverse)


def dot(left, right):
    return jnp.dot(left, right, preferred_element_type=f32)


def dot_nt(left, right):
    return lax.dot_general(left, right, (((1,), (1,)), ((), ())), preferred_element_type=f32)


def norm_back(upstream, normed, inverse):
    first_mean = jnp.mean(upstream, axis=-1, keepdims=True)
    second_mean = jnp.mean(upstream * normed, axis=-1, keepdims=True)
    return inverse * (upstream - first_mean - normed * second_mean)


def swap(value, axis):
    return lax.ppermute(value, axis, [(0, 1), (1, 0)])


def turn(value, axis, step):
    size = lax.axis_size(axis)
    return lax.ppermute(value, axis, [(i, (i - step) % size) for i in range(size)])


def place():
    return jnp.stack([lax.axis_index(name) for name in ("hx", "hc", "sz", "sy", "rb")]).astype(
        jnp.int32
    )


ANY = pl.BlockSpec(memory_space=pl.ANY)
SMEM = pl.BlockSpec(memory_space=pltpu.SMEM)
VMEM = pl.BlockSpec(memory_space=pltpu.VMEM)


def hbm(value):
    return pltpu.with_memory_space_constraint(value, pltpu.HBM)


def whole_spec(shape):
    return pl.BlockSpec(shape, lambda *_: (0,) * len(shape))


def result(shape, kind, free=False):
    return jax.ShapeDtypeStruct(shape, kind) if free else pltpu.HBM(shape, kind)


def single(kernel, outs, values, raw=(), held=(), scratch=(), limit=40, place=None, raw_outs=0):
    specs = [whole_spec(v.shape) for v in values] + [ANY] * len(raw) + [VMEM] * len(held)
    values = [hbm(v) for v in values] + list(raw) + list(held)
    blocked_outs = len(outs) - raw_outs
    if place is not None:
        specs, values = [SMEM] + specs, [place] + values
    return pl.pallas_call(
        kernel,
        grid=(1,),
        out_shape=tuple(result(*o) for o in outs),
        in_specs=specs,
        out_specs=tuple(
            whole_spec(o[0]) if i < blocked_outs else ANY for i, o in enumerate(outs)
        ),
        scratch_shapes=list(scratch),
        compiler_params=pltpu.CompilerParams(vmem_limit_bytes=limit << 20),
    )(*values)


def join_copies(place_ref, sides, blocks, sems):
    hx, hc, sz, sy = (place_ref[i] for i in range(4))
    half = sides[0].shape[-1]
    copies = []
    for number, pieces in enumerate(sides):
        side, core = divmod(number, 2)
        for second in range(2):
            for first in range(2):
                for deep in range(4):
                    across, down = (first, second) if side == 0 else (second, first)
                    block = (hx ^ across) * 2 + (hc ^ core)
                    spot = (block * 4 + lax.rem(sz + deep, 4)) * 2 + (sy ^ down)
                    copies.append(
                        pltpu.make_async_copy(
                            pieces.at[second, first, deep],
                            blocks.at[spot, :, pl.ds(side * half, half)],
                            sems.at[len(copies)],
                        )
                    )
    return copies


def gather_rows(here, shard, every, use):
    half = shard.shape[1] // 2
    sides = []
    deep = jnp.stack([shard] + [turn(shard, "sz", k) for k in (1, 2, 3)])
    orders = (("hx", "sy"), ("sy", "hx"))
    deep, every = lax.optimization_barrier((deep, every))
    levels = [deep[:, :, :half], deep[:, :, half:]]
    levels = [jnp.stack([v, swap(v, order[0])]) for v, order in zip(levels, orders)]
    levels = [jnp.stack([v, swap(v, order[1])]) for v, order in zip(levels, orders)]
    used = use(every)
    levels, used = lax.optimization_barrier((levels, used))
    for level in levels:
        sides += [level, swap(level, "hc")]
    return sides, used


def piece_copies(place_ref, blocks, keep, send, sems, side, columns):
    hx, sz, sy = place_ref[0], place_ref[2], place_ref[3]
    copies = []
    for second in range(2):
        for first in range(2):
            for deep in range(4):
                across, down = (first, second) if side == 0 else (second, first)
                spot = ((hx ^ across) * 4 + lax.rem(sz + deep, 4)) * 2 + (sy ^ down)
                source = blocks.at[(spot,) + (slice(None),) * (len(blocks.shape) - 2) + (columns,)]
                target = (keep, send)[second].at[first, deep]
                copies.append(pltpu.make_async_copy(source, target, sems.at[len(copies)]))
    for copy in copies:
        copy.start()
    return copies


ORDERS = (("sy", "hx"), ("hx", "sy"))
COLUMN_GROUPS = ((1, 0), (2, 0), (1, 1), (2, 1))


def second_send(keep, recv):
    return (keep[1].astype(f32) + recv[1].astype(f32)).astype(bf16)


def second_total(keep, recv, recv_second):
    return keep[0].astype(f32) + recv[0].astype(f32) + recv_second.astype(f32)


def third_recvs(total):
    return [turn(total[k].astype(bf16), "sz", -k) for k in (1, 2, 3)]


def enter_kernel(place_ref, x_ref, mod_ref, gains_ref, *refs):
    *sides, entered_ref, pair_ref, query_ref, whole_ref, block_sc, weight_sc, sems, sem = refs
    seqs, tokens, width = x_ref.shape
    half = tokens // 2
    pieced = len(sides) > 1
    if pieced:
        copies = join_copies(place_ref, sides, block_sc, sems)
    else:
        copies = [pltpu.make_async_copy(sides[0], weight_sc, sem)]
    for copy in copies:
        copy.start()
    for s in range(seqs):
        normed = normalize(x_ref[s].astype(f32))[0]
        shift, scale = (mod_ref[s : s + 1, pl.ds(i * width, width)] for i in (0, 1))
        value = normed * gains_ref[0:1] * (1.0 + scale) + shift
        entered_ref[pl.ds(s * tokens, tokens), :] = value.astype(bf16)
    entered = entered_ref[...]
    for copy in copies:
        copy.wait()
    if pieced:
        rows = block_sc.shape[1]
        for i in range(block_sc.shape[0]):
            weight_sc[pl.ds(i * rows, rows), :] = block_sc[i]
    leaving = pltpu.make_async_copy(weight_sc, whole_ref, sem)
    leaving.start()
    for which in (1, 2, 0):
        triple = dot(entered, weight_sc[:, pl.ds(which * width, width)])
        if which == 0:
            triple = triple * HEAD_DIM ** (-0.5)
        triple = triple.astype(bf16)
        for s in range(seqs):
            for g in range(GROUPS):
                rows = triple[s * tokens : (s + 1) * tokens, g * WIDTH : (g + 1) * WIDTH]
                slot = s * GROUPS + g
                if which == 0:
                    query_ref[slot, :, pl.ds(0, WIDTH)] = rows[:half]
                    query_ref[slot, :, pl.ds(WIDTH, WIDTH)] = rows[half:]
                else:
                    pair_ref[slot, :, pl.ds((which - 1) * WIDTH, WIDTH)] = rows
    leaving.wait()


def enter(here, inputs, modulation, gains, sides):
    seqs, tokens, width = inputs.shape
    rows = sides[0].shape[-2] if len(sides) > 1 else width // 32
    return single(
        enter_kernel,
        [
            ((seqs * tokens, width), bf16),
            ((8, tokens, 2 * WIDTH), bf16, True),
            ((8, tokens // 2, 2 * WIDTH), bf16, True),
            ((width, 3 * width), bf16),
        ],
        [inputs, modulation, gains],
        raw=sides,
        scratch=[
            pltpu.VMEM((32, rows, 3 * width), bf16),
            pltpu.VMEM((width, 3 * width), bf16),
            pltpu.SemaphoreType.DMA((64,)),
            pltpu.SemaphoreType.DMA,
        ],
        place=here,
        raw_outs=1,
    )


def load_pairs(pair_ref, slot, first_row, half):
    value = pair_ref[slot, pl.ds(first_row, half), :]
    return value[:, :WIDTH], value[:, WIDTH:]


def key_column(docs_ref, step):
    row = docs_ref[pl.ds(step, 1), :]
    return jnp.broadcast_to(row, (8, row.shape[1])).T[:, 0:1]


def gather_pairs(pair_ref, target):
    half = pair_ref.shape[1]
    for slot in range(pair_ref.shape[0]):
        for part, rows in enumerate(load_pairs(pair_ref, slot, 0, half)):
            target[pl.ds((slot * 2 + part) * half, half), :] = rows


def spread_heads(rows, target):
    lane = lax.broadcasted_iota(jnp.int32, (1, WIDTH), 1)
    for h in range(target.shape[0]):
        own = (lane >= h * HEAD_DIM) & (lane < (h + 1) * HEAD_DIM)
        target[h] = rows * jnp.where(own, 1.0, 0.0).astype(bf16)


def fetch(step, pair_refs, starts, pair_sc):
    for ref, (begin, end) in zip(pair_refs, starts):
        @pl.when((step >= begin) & (step < end))
        def take(ref=ref):
            pair_sc[...] = ref[...]


def forward_kernel(
    starts, came_ref, first_ref, second_ref, third_ref, fourth_ref, key_docs_ref, query_docs_ref,
    out_ref, turned_ref, total_ref, query_sc, flat_sc, pair_sc, top_sc, sum_sc, acc_sc,
):
    step = pl.program_id(0)
    heads, queries = query_sc.shape[:2]
    half = out_ref.shape[1]

    @pl.when(step == 0)
    def start():
        gather_pairs(came_ref, flat_sc)
        spread_heads(flat_sc[...], query_sc)
        top_sc[...] = jnp.full(top_sc.shape, -1e30, f32)
        sum_sc[...] = jnp.zeros(sum_sc.shape, f32)
        acc_sc[...] = jnp.zeros(acc_sc.shape, f32)

    fetch(step, (first_ref, second_ref, third_ref, fourth_ref), starts, pair_sc)
    key_part = pair_sc[:, :WIDTH]
    value_turned = pair_sc[:, WIDTH:].T
    allowed = key_column(key_docs_ref, step) == query_docs_ref[...]
    old = [top_sc[h : h + 1] for h in range(heads)]
    raw = [dot_nt(key_part, query_sc[h]) for h in range(heads)]
    scores = [jnp.where(allowed, value, -1e30) for value in raw]
    new = [jnp.maximum(o, jnp.max(v, axis=0, keepdims=True)) for o, v in zip(old, scores)]
    exponent = [jnp.exp(v - n) for v, n in zip(scores, new)]
    terms = [
        dot(value_turned[h * HEAD_DIM : (h + 1) * HEAD_DIM], exponent[h].astype(bf16))
        for h in range(heads)
    ]
    sums = [jnp.sum(v, axis=0, keepdims=True) for v in exponent]
    for h in range(heads):
        rows = pl.ds(h * HEAD_DIM, HEAD_DIM)
        fade = jnp.exp(old[h] - new[h])
        top_sc[h : h + 1] = new[h]
        sum_sc[h : h + 1] = sum_sc[h : h + 1] * fade + sums[h]
        acc_sc[rows] = acc_sc[rows] * fade + terms[h]

    @pl.when(step == pl.num_programs(0) - 1)
    def finish():
        total_ref[...] = jnp.zeros(total_ref.shape, f32)
        for h in range(heads):
            rows = pl.ds(h * HEAD_DIM, HEAD_DIM)
            turned_ref[rows] = acc_sc[rows] / sum_sc[h : h + 1]
            total_ref[h : h + 1] = top_sc[h : h + 1] + jnp.log(sum_sc[h : h + 1])
        whole = turned_ref[...].astype(bf16).T
        for slot in range(8):
            for part in range(2):
                begin = (slot * 2 + part) * half
                out_ref[slot, :, pl.ds(part * WIDTH, WIDTH)] = whole[begin : begin + half]


def pair_specs(pairs, chunk):
    specs, starts, begin = [], [], 0
    for pair in pairs:
        count = pair.shape[0] // chunk
        specs.append(
            pl.BlockSpec(
                (chunk, 2 * WIDTH),
                lambda i, begin=begin, count=count: (jnp.clip(i - begin, 0, count - 1), 0),
            )
        )
        starts.append((begin, begin + count))
        begin += count
    return specs, starts, begin


def attend(came, pairs, key_docs, query_docs):
    slots, half, columns = came.shape
    queries = slots * 2 * half
    heads = WIDTH // HEAD_DIM
    chunk = 512
    specs, starts, steps = pair_specs(pairs, chunk)
    outs = (
        result((slots, half, columns), bf16, True),
        result((WIDTH, queries), f32),
        result((8, queries), f32),
    )
    return pl.pallas_call(
        partial(forward_kernel, starts),
        grid=(steps,),
        out_shape=outs,
        in_specs=[
            whole_spec(came.shape),
            *specs,
            whole_spec(key_docs.shape),
            whole_spec(query_docs.shape),
        ],
        out_specs=tuple(whole_spec(o.shape) for o in outs),
        scratch_shapes=[
            pltpu.VMEM((heads, queries, WIDTH), bf16),
            pltpu.VMEM((queries, WIDTH), bf16),
            pltpu.VMEM((chunk, 2 * WIDTH), bf16),
            pltpu.VMEM((8, queries), f32),
            pltpu.VMEM((8, queries), f32),
            pltpu.VMEM((WIDTH, queries), f32),
        ],
        compiler_params=pltpu.CompilerParams(vmem_limit_bytes=48 << 20),
    )(*map(hbm, (came, *pairs[:-1])), pairs[-1], *map(hbm, (key_docs, query_docs)))


def backward_kernel(
    starts, came_ref, grad_ref, first_ref, second_ref, third_ref, fourth_ref, key_docs_ref, query_docs_ref,
    turned_ref, total_ref, query_out, keep_ref, keep_other, send_ref,
    query_sc, grad_sc, flat_sc, pair_sc, delta_sc, acc_sc,
):
    step = pl.program_id(0)
    heads, queries = query_sc.shape[:2]
    half = query_out.shape[1]

    @pl.when(step == 0)
    def start():
        gather_pairs(came_ref, flat_sc)
        spread_heads(flat_sc[...], query_sc)
        gather_pairs(grad_ref, flat_sc)
        spread_heads(flat_sc[...], grad_sc)
        acc_sc[...] = jnp.zeros(acc_sc.shape, f32)
        product = flat_sc[...].T.astype(f32) * turned_ref[...]
        for h in range(heads):
            rows = slice(h * HEAD_DIM, (h + 1) * HEAD_DIM)
            delta_sc[h : h + 1] = jnp.sum(product[rows], axis=0, keepdims=True)

    fetch(step, (first_ref, second_ref, third_ref, fourth_ref), starts, pair_sc)
    key_part = pair_sc[:, :WIDTH]
    value_part = pair_sc[:, WIDTH:]
    key_turned = key_part.T
    allowed = key_column(key_docs_ref, step) == query_docs_ref[...]
    raw = [dot_nt(key_part, query_sc[h]) for h in range(heads)]
    slopes = [dot_nt(value_part, grad_sc[h]) for h in range(heads)]
    probabilities = [
        jnp.exp(jnp.where(allowed, value, -1e30) - total_ref[h : h + 1])
        for h, value in enumerate(raw)
    ]
    grad_scores = [
        (p * (slope - delta_sc[h : h + 1])).astype(bf16)
        for h, (p, slope) in enumerate(zip(probabilities, slopes))
    ]
    grad_value = sum(dot(probabilities[h].astype(bf16), grad_sc[h]) for h in range(heads))
    grad_key = sum(dot(grad_scores[h], query_sc[h]) for h in range(heads))
    for h in range(heads):
        rows = pl.ds(h * HEAD_DIM, HEAD_DIM)
        acc_sc[rows] = acc_sc[rows] + dot(
            key_turned[h * HEAD_DIM : (h + 1) * HEAD_DIM], grad_scores[h]
        )
    quarter = pl.num_programs(0) // 4
    middle = 2 * quarter

    for number, ref in enumerate((keep_ref, keep_other)):
        @pl.when((step >= number * quarter) & (step < (number + 1) * quarter))
        def mine(ref=ref):
            ref[:, pl.ds(0, WIDTH)] = grad_key
            ref[:, pl.ds(WIDTH, WIDTH)] = grad_value

    @pl.when(step >= middle)
    def theirs():
        send_ref[:, pl.ds(0, WIDTH)] = grad_key.astype(bf16)
        send_ref[:, pl.ds(WIDTH, WIDTH)] = grad_value.astype(bf16)

    @pl.when(step == pl.num_programs(0) - 1)
    def finish():
        whole = (acc_sc[...] * HEAD_DIM ** (-0.5)).astype(bf16).T
        for slot in range(8):
            for part in range(2):
                begin = (slot * 2 + part) * half
                query_out[slot, :, pl.ds(part * WIDTH, WIDTH)] = whole[begin : begin + half]


def attend_back(came, grad, pairs, key_docs, query_docs, turned, total):
    slots, half, columns = came.shape
    queries = slots * 2 * half
    heads = WIDTH // HEAD_DIM
    chunk = 512
    specs, starts, steps = pair_specs(pairs, chunk)
    quarter = steps // 4
    middle = 2 * quarter
    return pl.pallas_call(
        partial(backward_kernel, starts),
        grid=(steps,),
        out_shape=(
            jax.ShapeDtypeStruct((slots, half, columns), bf16),
            jax.ShapeDtypeStruct((quarter * chunk, columns), f32),
            jax.ShapeDtypeStruct((quarter * chunk, columns), f32),
            jax.ShapeDtypeStruct((middle * chunk, columns), bf16),
        ),
        in_specs=[
            whole_spec(came.shape),
            whole_spec(grad.shape),
            *specs,
            whole_spec(key_docs.shape),
            whole_spec(query_docs.shape),
            whole_spec(turned.shape),
            whole_spec(total.shape),
        ],
        out_specs=(
            whole_spec((slots, half, columns)),
            pl.BlockSpec((chunk, columns), lambda i: (jnp.minimum(i, quarter - 1), 0)),
            pl.BlockSpec((chunk, columns), lambda i: (jnp.clip(i - quarter, 0, quarter - 1), 0)),
            pl.BlockSpec((chunk, columns), lambda i: (jnp.maximum(i - middle, 0), 0)),
        ),
        scratch_shapes=[
            pltpu.VMEM((heads, queries, WIDTH), bf16),
            pltpu.VMEM((heads, queries, WIDTH), bf16),
            pltpu.VMEM((queries, WIDTH), bf16),
            pltpu.VMEM((chunk, 2 * WIDTH), bf16),
            pltpu.VMEM((8, queries), f32),
            pltpu.VMEM((WIDTH, queries), f32),
        ],
        compiler_params=pltpu.CompilerParams(vmem_limit_bytes=48 << 20),
    )(*map(hbm, (came, grad, *pairs, key_docs, query_docs, turned, total)))


def settle_kernel(
    later_hbm, out_ref, up_ref, down_ref, block_sc, out_sc, up_sc, down_sc, sems, out_sems
):
    width = out_ref.shape[1]
    copies = [
        pltpu.make_async_copy(later_hbm.at[:, j], block_sc.at[j], sems.at[j]) for j in range(9)
    ]
    for copy in copies:
        copy.start()
    leaving = []
    for j in range(9):
        copies[j].wait()
        for i in range(32):
            value = block_sc[j, i]
            if j == 0:
                out_sc[pl.ds(i * 24, 24), :] = value
            elif j < 5:
                up_sc[pl.ds(i * 24, 24), pl.ds((j - 1) * width, width)] = value
            else:
                down_sc[pl.ds(i * 96 + (j - 5) * 24, 24), :] = value
        if j == 0:
            leaving.append(pltpu.make_async_copy(out_sc, out_ref, out_sems.at[j]))
        elif j < 5:
            columns = pl.ds((j - 1) * width, width)
            leaving.append(
                pltpu.make_async_copy(up_sc.at[:, columns], up_ref.at[:, columns], out_sems.at[j])
            )
        elif j == 8:
            leaving.append(pltpu.make_async_copy(down_sc, down_ref, out_sems.at[j]))
        if j < 5 or j == 8:
            leaving[-1].start()
    for copy in leaving:
        copy.wait()


def settle(later):
    width = later.shape[-1]
    shapes = ((width, width), (width, 4 * width), (4 * width, width))
    return pl.pallas_call(
        settle_kernel,
        out_shape=tuple(result(shape, bf16) for shape in shapes),
        in_specs=[ANY],
        out_specs=(ANY,) * 3,
        scratch_shapes=[
            pltpu.VMEM((9, 32, 24, width), bf16),
            *(pltpu.VMEM(shape, bf16) for shape in shapes),
            pltpu.SemaphoreType.DMA((9,)),
            pltpu.SemaphoreType.DMA((9,)),
        ],
        compiler_params=pltpu.CompilerParams(vmem_limit_bytes=40 << 20),
    )(hbm(later))


def middle_kernel(
    came_ref, x_ref, teacher_ref, mask_ref, mod_ref, gains_ref, up_bias_ref,
    out_hbm, up_hbm, down_hbm,
    final_ref, hidden_ref, leave_ref, pack_ref, sums_ref, out_sc, up_sc, down_sc, slope_sc, sems,
):
    seqs, tokens, width = x_ref.shape
    units = up_sc.shape[1]
    rows = seqs * tokens
    half = tokens // 2
    parts = [pl.ds(f * width, width) for f in range(units // width)]
    copies = [pltpu.make_async_copy(out_hbm, out_sc, sems.at[0])]
    for f, part in enumerate(parts):
        copies.append(
            pltpu.make_async_copy(up_hbm.at[:, part], up_sc.at[:, part], sems.at[1 + 2 * f])
        )
        copies.append(
            pltpu.make_async_copy(down_hbm.at[part, :], down_sc.at[part, :], sems.at[2 + 2 * f])
        )
    for copy in copies:
        copy.start()
    masks = mask_ref[...].T

    def wide(index):
        return jnp.concatenate(
            [
                jnp.broadcast_to(
                    mod_ref[s : s + 1, pl.ds(index * width, width)], (tokens, width)
                )
                for s in range(seqs)
            ]
        )

    def add_rows(first, value):
        for s in range(seqs):
            sums_ref[first + s : first + s + 1] = jnp.sum(
                value[s * tokens : (s + 1) * tokens], axis=0, keepdims=True
            )

    for s in range(seqs):
        for g in range(GROUPS):
            left, right = load_pairs(came_ref, s * GROUPS + g, 0, half)
            columns = pl.ds(g * WIDTH, WIDTH)
            pack_ref[pl.ds(s * tokens, half), columns] = left
            pack_ref[pl.ds(s * tokens + half, half), columns] = right
    mixed = pack_ref[:, pl.ds(0, width)]
    residual = jnp.concatenate([x_ref[s].astype(f32) for s in range(seqs)])
    copies[0].wait()
    branch = dot(mixed, out_sc[...])
    hidden = residual + wide(2) * branch
    normed, inverse = normalize(hidden)
    scaled = normed * gains_ref[1:2]
    moved = (scaled * (1.0 + wide(4)) + wide(3)).astype(bf16)
    pack_ref[:, pl.ds(width, width)] = moved
    lower = None
    for f in range(units // width):
        columns = pl.ds(f * width, width)
        copies[1 + 2 * f].wait()
        u = dot(moved, up_sc[:, columns]) + up_bias_ref[0:1, columns]
        square = u * u
        t = jnp.tanh(0.7978845608028654 * (u + 0.044715 * u * square))
        active = (0.5 * u * (1.0 + t)).astype(bf16)
        slope_sc[:, columns] = 0.5 * (1.0 + t) + 0.5 * u * (1.0 - t * t) * 0.7978845608028654 * (
            1.0 + 0.134145 * square
        )
        pack_ref[:, pl.ds(2 * width + f * width, width)] = active
        copies[2 + 2 * f].wait()
        term = dot(active, down_sc[columns, :])
        lower = term if lower is None else lower + term
    lower = lower + gains_ref[2:3]
    gate = wide(5)
    final = hidden + gate * lower
    for s in range(seqs):
        final_ref[s] = final[s * tokens : (s + 1) * tokens].astype(bf16)
    teacher = jnp.concatenate([teacher_ref[s].astype(f32) for s in range(seqs)])
    mismatch = final - teacher
    sums_ref[14:15] = jnp.sum(
        masks[:, 0:1] * mismatch * mismatch, axis=0, keepdims=True
    )
    sums_ref[15:16] = jnp.zeros((1, width), f32)
    grad_final = masks[:, 1:2] * mismatch
    add_rows(6, grad_final * lower)
    grad_lower = (gate * grad_final).astype(bf16)
    base = 2 * width + units
    pack_ref[:, pl.ds(base + width + units, width)] = grad_lower
    sums_ref[9:10] = jnp.sum(grad_lower.astype(f32), axis=0, keepdims=True)
    grad_moved = None
    for f in range(units // width):
        columns = pl.ds(f * width, width)
        grad_active = dot_nt(grad_lower, down_sc[columns, :])
        grad_upper = (grad_active * slope_sc[:, columns]).astype(bf16)
        pack_ref[:, pl.ds(base + width + f * width, width)] = grad_upper
        sums_ref[10 + f : 11 + f] = jnp.sum(grad_upper.astype(f32), axis=0, keepdims=True)
        term = dot_nt(grad_upper, up_sc[:, columns])
        grad_moved = term if grad_moved is None else grad_moved + term
    add_rows(2, grad_moved)
    add_rows(4, grad_moved * scaled)
    grad_scaled = grad_moved * (1.0 + wide(4))
    sums_ref[8:9] = jnp.sum(grad_scaled * normed, axis=0, keepdims=True)
    grad_hidden = grad_final + norm_back(grad_scaled * gains_ref[1:2], normed, inverse)
    hidden_ref[...] = grad_hidden
    add_rows(0, grad_hidden * branch)
    grad_branch = (wide(2) * grad_hidden).astype(bf16)
    pack_ref[:, pl.ds(base, width)] = grad_branch
    grad_mixed = dot_nt(grad_branch, out_sc[...]).astype(bf16)
    for s in range(seqs):
        for g in range(GROUPS):
            piece = grad_mixed[s * tokens : (s + 1) * tokens, g * WIDTH : (g + 1) * WIDTH]
            leave_ref[s * GROUPS + g, :, pl.ds(0, WIDTH)] = piece[:half]
            leave_ref[s * GROUPS + g, :, pl.ds(WIDTH, WIDTH)] = piece[half:]


def middle(came, inputs, teacher, masks, modulation, gains, up_bias, weights):
    seqs, tokens, width = inputs.shape
    units = up_bias.shape[1]
    rows = seqs * tokens
    return single(
        middle_kernel,
        [
            ((seqs, tokens, width), bf16),
            ((rows, width), f32),
            (came.shape, bf16, True),
            ((rows, 4 * width + 2 * units), bf16, True),
            ((16, width), f32),
        ],
        [came, inputs, teacher, masks, modulation, gains, up_bias],
        raw=[hbm(w) for w in weights],
        scratch=[
            pltpu.VMEM((width, width), bf16),
            pltpu.VMEM((width, units), bf16),
            pltpu.VMEM((units, width), bf16),
            pltpu.VMEM((rows, units), f32),
            pltpu.SemaphoreType.DMA((9,)),
        ],
        limit=40,
    )


def weights_kernel(
    place_ref, own_ref, other_ref, *refs
):
    *groups, left_sc, right_sc, block_sc, sems = refs
    rows, width = own_ref.shape[0], block_sc.shape[-1]
    units = 4 * width
    hc = place_ref[1]
    base = 2 * width + units
    for which, ref in enumerate((own_ref, other_ref)):
        left_sc[:, pl.ds(which * rows, rows)] = ref[:, pl.ds(0, base)].T
        right_sc[pl.ds(which * rows, rows), :] = ref[:, pl.ds(base, base)]
    for hx in range(2):
        begin = pl.multiple_of(hx * 384 + hc * 192, 64)
        for j in range(5):
            offset = 0 if j == 0 else width
            value = dot(left_sc[pl.ds(begin + offset, 192), :], right_sc[:, pl.ds(j * width, width)])
            for i in range(8):
                block_sc[hx * 8 + i, j] = value[i * 24 : (i + 1) * 24].astype(bf16)
        begin = pl.multiple_of(2 * width + hx * 1536 + hc * 768, 256)
        value = dot(left_sc[pl.ds(begin, 768), :], right_sc[:, pl.ds(width + units, width)])
        for i in range(8):
            for j in range(4):
                first = i * 96 + j * 24
                block_sc[hx * 8 + i, 5 + j] = value[first : first + 24].astype(bf16)
    copies = []
    begin = 0
    for number, (_, side) in enumerate(COLUMN_GROUPS):
        keep, send = groups[2 * number : 2 * number + 2]
        columns = pl.ds(begin, keep.shape[-1])
        copies += piece_copies(place_ref, block_sc, keep, send, sems.at[number], side, columns)
        begin += keep.shape[-1]
    for copy in copies:
        copy.wait()


def weight_terms(here, own, other, width):
    rows, total = own.shape
    return single(
        weights_kernel,
        [((2, 4, 9, 24, 128 * size), bf16) for size, _ in COLUMN_GROUPS for _ in range(2)],
        [],
        held=[own, other],
        scratch=[
            pltpu.VMEM((total // 2, 2 * rows), bf16),
            pltpu.VMEM((2 * rows, total // 2), bf16),
            pltpu.VMEM((16, 9, 24, width), bf16),
            pltpu.SemaphoreType.DMA((len(COLUMN_GROUPS), 16)),
        ],
        limit=40,
        place=here,
        raw_outs=2 * len(COLUMN_GROUPS),
    )


def flat_rows(home_ref, target, first_row, seqs, tokens, width):
    half = tokens // 2
    for s in range(seqs):
        for g in range(GROUPS):
            slot = s * GROUPS + g
            row = first_row + s * tokens
            left, right = load_pairs(home_ref, slot, tokens, half)
            target[pl.ds(row, half), pl.ds(g * WIDTH, WIDTH)] = left
            target[pl.ds(row + half, half), pl.ds(g * WIDTH, WIDTH)] = right
            left, right = load_pairs(home_ref, slot, 0, tokens)
            target[pl.ds(row, tokens), pl.ds(width + g * WIDTH, WIDTH)] = left
            target[pl.ds(row, tokens), pl.ds(2 * width + g * WIDTH, WIDTH)] = right


def qkv_kernel(
    seqs, place_ref, entered_ref, entered_other, home_ref, home_other,
    keep_a, send_a, keep_b, send_b, left_sc, right_sc, block_sc, sems,
):
    rows, width = entered_ref.shape
    hc = place_ref[1]
    for which, (left, home) in enumerate(((entered_ref, home_ref), (entered_other, home_other))):
        left_sc[:, pl.ds(which * rows, rows)] = left[...].T
        flat_rows(home, right_sc, which * rows, seqs, rows // seqs, width)
    for hx in range(2):
        begin = pl.multiple_of(hx * 384 + hc * 192, 64)
        for j in range(3):
            value = dot(left_sc[pl.ds(begin, 192), :], right_sc[:, pl.ds(j * width, width)])
            for i in range(8):
                block_sc[hx * 8 + i, :, pl.ds(j * width, width)] = value[
                    i * 24 : (i + 1) * 24
                ].astype(bf16)
    half = 3 * width // 2
    copies = piece_copies(place_ref, block_sc, keep_a, send_a, sems.at[0], 0, pl.ds(0, half))
    copies += piece_copies(place_ref, block_sc, keep_b, send_b, sems.at[1], 1, pl.ds(half, half))
    for copy in copies:
        copy.wait()


def qkv_terms(here, seqs, *values):
    rows, width = values[0].shape
    return single(
        partial(qkv_kernel, seqs),
        [((2, 4, 24, 3 * width // 2), bf16)] * 4,
        values,
        scratch=[
            pltpu.VMEM((width, 2 * rows), bf16),
            pltpu.VMEM((2 * rows, 3 * width), bf16),
            pltpu.VMEM((16, 24, 3 * width), bf16),
            pltpu.SemaphoreType.DMA((2, 16)),
        ],
        place=here,
        raw_outs=4,
    )


def leave_kernel(
    home_ref, x_ref, hidden_ref, mod_ref, gains_ref, weight_ref, middle_ref,
    grad_ref, small_ref, flat_ref,
):
    seqs, tokens, width = x_ref.shape
    devices = small_ref.shape[0]
    flat_rows(home_ref, flat_ref, 0, seqs, tokens, width)
    grad_entered = None
    for which in range(3):
        columns = pl.ds(which * width, width)
        term = dot_nt(flat_ref[:, columns], weight_ref[:, columns])
        grad_entered = term if grad_entered is None else grad_entered + term
    gain_sum = None
    sums = []
    for s in range(seqs):
        normed, inverse = normalize(x_ref[s].astype(f32))
        rows = slice(s * tokens, (s + 1) * tokens)
        grad = grad_entered[rows]
        shift_sum = jnp.sum(grad, axis=0, keepdims=True)
        scale_sum = jnp.sum(grad * (normed * gains_ref[0:1]), axis=0, keepdims=True)
        grad_scaled = grad * (1.0 + mod_ref[s : s + 1, pl.ds(width, width)])
        term = jnp.sum(grad_scaled * normed, axis=0, keepdims=True)
        gain_sum = term if gain_sum is None else gain_sum + term
        grad_ref[s] = hidden_ref[rows] + norm_back(grad_scaled * gains_ref[0:1], normed, inverse)
        later = [middle_ref[i + s : i + s + 1] for i in (0, 2, 4, 6)]
        sums.append(jnp.concatenate([shift_sum, scale_sum, *later], axis=1))
    up_bias = jnp.concatenate([middle_ref[i : i + 1] for i in range(10, 14)], axis=1)
    fields = [*sums, gain_sum, middle_ref[8:9], up_bias, middle_ref[9:10]]
    error = jnp.sum(middle_ref[14:15], axis=1, keepdims=True)
    small_ref[...] = jnp.zeros(small_ref.shape, f32)
    begin = 0
    for field in fields:
        size = field.shape[1] // devices
        for i in range(devices):
            small_ref[i, :, pl.ds(begin, size)] = field[:, i * size : (i + 1) * size]
        begin += size
    small_ref[:, :, pl.ds(begin, 1)] = jnp.broadcast_to(error[None], (devices, 1, 1))


def leave(home, inputs, grad_hidden, modulation, gains, weight, sums, devices):
    seqs, tokens, width = inputs.shape
    return single(
        leave_kernel,
        [
            ((seqs, tokens, width), f32),
            ((devices, 1, 512), f32, True),
            ((seqs * tokens, 3 * width), bf16),
        ],
        [home, inputs, grad_hidden, modulation, gains, weight, sums],
    )


def unpack_kernel(
    parts, sizes, factor, place_ref, every_ref, valid_ref,
    mod_ref, gains_ref, up_ref, key_docs_ref, query_docs_ref, masks_ref,
):
    devices = every_ref.shape[0]
    seqs, tokens = valid_ref.shape
    size_mod, size_gain, size_up = sizes
    mod_ref[...] = jnp.zeros(mod_ref.shape, f32)
    gains_ref[...] = jnp.zeros(gains_ref.shape, f32)
    up_ref[...] = jnp.zeros(up_ref.shape, f32)
    begin = 0
    targets = [(mod_ref, s, size_mod) for s in range(seqs)]
    targets += [(gains_ref, 0, size_gain), (gains_ref, 1, size_gain)]
    targets += [(up_ref, 0, size_up), (gains_ref, 2, size_gain)]
    for target, row, size in targets:
        for i in range(devices):
            target[row : row + 1, pl.ds(i * size, size)] = every_ref[i, :, pl.ds(begin, size)]
        begin += size
    hx, hc, sz, sy, rb = (place_ref[i] for i in range(5))
    second = sz * 2 + sy >= GROUPS
    row = 0
    for core in range(2):
        for across in range(2):
            for part in range(parts):
                block = ((hx ^ across) * 2 + (hc ^ core)) * parts + part
                for spot in range(8):
                    line = every_ref[block * 8 + spot, :, pl.ds(begin, 2 * tokens)]
                    key_docs_ref[row : row + 1, pl.ds(spot * tokens, tokens)] = jnp.where(
                        second, line[:, tokens:], line[:, :tokens]
                    )
                row += 1
    for spot in range(8):
        line = every_ref[((hx * 2 + hc) * parts + rb) * 8 + spot, :, pl.ds(begin, 2 * tokens)]
        query_docs_ref[:, pl.ds(spot * tokens, tokens)] = jnp.where(
            second, line[:, tokens:], line[:, :tokens]
        )
    begin += 2 * tokens
    count = jnp.sum(every_ref[:, :, pl.ds(begin, 1)], axis=0)
    gains_ref[3:4, pl.ds(0, 1)] = count
    masks_ref[...] = jnp.zeros(masks_ref.shape, f32)
    for s in range(seqs):
        valid = valid_ref[s : s + 1, :].astype(f32)
        masks_ref[0:1, pl.ds(s * tokens, tokens)] = valid
        masks_ref[1:2, pl.ds(s * tokens, tokens)] = valid * (factor / count)


def unpack(here, every, valid_mask, width, units, parts, length):
    seqs, tokens = valid_mask.shape
    devices = every.shape[0]
    sizes = (6 * width // devices, width // devices, units // devices)
    return single(
        partial(unpack_kernel, parts, sizes, float(seqs * length)),
        [
            ((8, 6 * width), f32),
            ((8, width), f32),
            ((8, units), f32),
            ((4 * parts, 8 * tokens), f32),
            ((1, 8 * tokens), f32),
            ((8, seqs * tokens), f32),
        ],
        [every, valid_mask],
        place=here,
    )


def finish_kernel(width, small_ref, embed_ref, gains_ref, *refs):
    ada_ref, bias_ref, *vectors, loss_ref = refs
    seqs = embed_ref.shape[0]
    columns = ada_ref.shape[0]
    added = jnp.sum(small_ref[...], axis=0)
    begin = 0
    ada = bias = None
    for s in range(seqs):
        grad = added[:, begin : begin + columns]
        begin += columns
        turned = jnp.broadcast_to(grad, (8, columns)).T[:, 0:1]
        term = turned * embed_ref[s : s + 1, :]
        ada = term if ada is None else ada + term
        bias = grad if bias is None else bias + grad
    ada_ref[...] = ada
    bias_ref[...] = bias
    for ref in vectors:
        size = ref.shape[1]
        ref[...] = added[:, begin : begin + size]
        begin += size
    loss_ref[...] = added[:, begin : begin + 1] / (gains_ref[3:4, 0:1] * width)


def finish(small, time_embed, gains, width, units):
    devices = small.shape[0]
    sizes = [6 * width // devices] + [size // devices for size in (width, width, units, width)]
    return single(
        partial(finish_kernel, float(width)),
        [((sizes[0], time_embed.shape[1]), f32)]
        + [((1, size), f32, True) for size in sizes]
        + [((1, 1), f32, True)],
        [small, time_embed, gains],
    )


def grads_kernel(total_ref, first_ref, second_ref, third_ref, *refs):
    qkv_total, qkv_first, qkv_second, qkv_third, out_ref, up_ref, down_ref, qkv_ref = refs
    width = out_ref.shape[1]
    for j in range(9):
        value = total_ref[0, j]
        for ref in (first_ref, second_ref, third_ref):
            value = value + ref[j].astype(f32)
        if j == 0:
            out_ref[...] = value
        elif j < 5:
            up_ref[:, pl.ds((j - 1) * width, width)] = value
        else:
            down_ref[pl.ds((j - 5) * 24, 24), :] = value
    value = qkv_total[0]
    for ref in (qkv_first, qkv_second, qkv_third):
        value = value + ref[...].astype(f32)
    qkv_ref[...] = value


def weight_grads(total, third, qkv_total, third_qkv):
    width = total.shape[-1]
    values = [total, *third, qkv_total, *third_qkv]
    specs = [
        pl.BlockSpec((1,) + v.shape[1:], lambda i, n=v.ndim: (0,) * n)
        if i in (0, 4)
        else whole_spec(v.shape)
        for i, v in enumerate(values)
    ]
    shapes = ((24, width), (24, 4 * width), (96, width), (24, 3 * width))
    return pl.pallas_call(
        grads_kernel,
        grid=(1,),
        out_shape=tuple(jax.ShapeDtypeStruct(shape, f32) for shape in shapes),
        in_specs=specs,
        out_specs=tuple(whole_spec(shape) for shape in shapes),
        compiler_params=pltpu.CompilerParams(vmem_limit_bytes=40 << 20),
    )(*values)


def begin_kernel(embed_ref, ada_ref, segments_ref, valid_ref, *refs):
    vectors, refs = [ref[...].astype(f32) for ref in refs[:5]], refs[5:]
    *weights, packed_ref = refs[:-1] if len(refs) > 1 else refs
    seqs, tokens = segments_ref.shape
    modulation = lax.dot_general(
        embed_ref[...],
        ada_ref[...].astype(f32),
        (((1,), (1,)), ((), ())),
        precision=precise,
        preferred_element_type=f32,
    )
    modulation = modulation + vectors[0]
    count = jnp.sum(valid_ref[...].astype(f32), axis=1, keepdims=True)
    count = jnp.sum(count, axis=0, keepdims=True)
    fields = [modulation[s : s + 1] for s in range(seqs)]
    fields += vectors[1:]
    fields += [segments_ref[s : s + 1, :].astype(f32) for s in range(seqs)]
    fields.append(count)
    fields.append(jnp.zeros((1, packed_ref.shape[2] - sum(f.shape[1] for f in fields)), f32))
    packed_ref[...] = jnp.broadcast_to(
        jnp.concatenate(fields, axis=1)[None], packed_ref.shape
    )
    if weights:
        out_ref, up_ref, down_ref = weights
        later_ref = refs[-1]
        width = out_ref.shape[1]
        later_ref[0] = out_ref[...]
        for j in range(4):
            later_ref[1 + j] = up_ref[:, pl.ds(j * width, width)]
            later_ref[5 + j] = down_ref[pl.ds(j * 24, 24), :]


def begin_with(time_embed, ada_weight, vectors, segments, valid_mask, weights, devices):
    seqs, tokens = segments.shape
    columns = (seqs - 1) * ada_weight.shape[1] + sum(v.shape[1] for v in vectors) + seqs * tokens + 1
    outs = [((devices, 1, columns + -columns % 128), f32, True)]
    if weights:
        outs.append(((9, 24, weights[0].shape[1]), bf16))
    return single(
        begin_kernel, outs, [time_embed, ada_weight.T, segments, valid_mask, *vectors, *weights]
    )


def after(value, *others):
    return lax.optimization_barrier((value, others))[0]


def exchange(rows):
    return lax.all_to_all(rows, SPOT, 0, 0, tiled=True)


def on_device(
    inputs,
    time_embed,
    segments,
    valid_mask,
    teacher,
    ada_weight,
    ada_bias,
    gain_attn,
    qkv_weight,
    out_weight,
    gain_mlp,
    up_weight,
    up_bias,
    down_weight,
    down_bias,
):
    seqs, tokens, width = inputs.shape
    units = up_weight.shape[1]
    parts = lax.axis_size("rb")
    devices = 32 * parts
    length = tokens * devices
    queries = 8 * tokens
    here = place()

    vectors = [v.reshape(1, -1) for v in (ada_bias, gain_attn, gain_mlp, up_bias, down_bias)]
    weights = [] if parts > 1 else [out_weight, up_weight, down_weight]
    packed, *later = begin_with(
        time_embed, ada_weight, vectors, segments, valid_mask, weights, devices
    )
    every = lax.all_to_all(packed, EVERY, 0, 0, tiled=True)
    if parts > 1:
        sides, *later = (
            lax.all_gather(w, EVERY, axis=0, tiled=True)
            for w in (qkv_weight, out_weight, up_weight, down_weight)
        )
    else:
        later = [lax.all_gather(later[0], EVERY, axis=0, tiled=False)]

    def use(every):
        return unpack(here, every, valid_mask, width, units, parts, length)

    if parts > 1:
        sides = [sides]
        used = use(every)
    else:
        sides, used = gather_rows(here, qkv_weight, every, use)
    modulation, gains, full_up_bias, key_docs, query_docs, masks = used

    entered, pair, query, full_qkv = enter(here, inputs, modulation, gains, sides)
    pair = exchange(pair).reshape(queries, 2 * WIDTH)
    query = exchange(query)
    if parts > 1:
        pair = lax.all_gather(pair, "rb", axis=0, tiled=True)
    pair_x = swap(pair, "hx")
    pair_x, query = lax.optimization_barrier((pair_x, query))
    pairs = (pair, pair_x, swap(pair, "hc"), swap(pair_x, "hc"))
    attended, turned, total = attend(query, pairs, key_docs, query_docs)

    if parts == 1:
        later = settle(later[0])
    final, grad_hidden, grad_leaving, pack, sums = middle(
        exchange(attended), inputs, teacher, masks, modulation, gains, full_up_bias, later
    )
    grad_came = exchange(grad_leaving)
    if parts == 1:
        terms = weight_terms(here, pack, swap(pack, "hc"), width)
        grad_came, terms = lax.optimization_barrier((grad_came, terms))
        held = terms[::2]
        firsts = [
            swap(send, ORDERS[side][0]) for send, (_, side) in zip(terms[1::2], COLUMN_GROUPS)
        ]

    grad_query, keep, keep_x, send = attend_back(
        query, grad_came, pairs, key_docs, query_docs, turned, total
    )
    if parts == 1:
        send, firsts[0], firsts[2] = lax.optimization_barrier((send, firsts[0], firsts[2]))
    recv = swap(send, "hc")
    own_rows = keep.shape[0]
    send_x = (keep_x + recv[own_rows:].astype(f32)).astype(bf16)
    grad_pair = keep + recv[:own_rows].astype(f32) + swap(send_x, "hx").astype(f32)
    if parts > 1:
        grad_pair = lax.psum_scatter(grad_pair, "rb", scatter_dimension=0, tiled=True)
    home = jnp.concatenate(
        [grad_pair.astype(bf16).reshape(8, tokens, 2 * WIDTH), grad_query], axis=1
    )
    if parts == 1:
        seconds = [
            swap(
                jnp.concatenate(
                    [
                        second_send(keep, recv)
                        for keep, recv, (_, own) in zip(held, firsts, COLUMN_GROUPS)
                        if own == side
                    ],
                    axis=3,
                ),
                ORDERS[side][1],
            )
            for side in (0, 1)
        ]
    home = exchange(home)
    if parts == 1:
        others = swap(entered, "hc"), swap(home, "hc")
        terms = qkv_terms(here, seqs, entered, others[0], home, others[1])
        seconds = after(seconds, terms)
        recvs = [swap(send, order[0]) for send, order in zip(terms[1::2], ORDERS)]
        grad_input, small, flat = leave(
            after(home, terms), inputs, grad_hidden, modulation, gains, full_qkv, sums, devices
        )
        recvs = after(recvs, small)
        nexts = [second_send(keep, recv) for keep, recv in zip(terms[::2], recvs)]
        small = after(small, nexts)
        next_recvs = [swap(value, order[1]) for value, order in zip(nexts, ORDERS)]
        totals = [
            jnp.concatenate(
                [
                    keep[0].astype(f32) + recv[0].astype(f32)
                    for keep, recv, (_, own) in zip(held, firsts, COLUMN_GROUPS)
                    if own == side
                ],
                axis=3,
            )
            + seconds[side].astype(f32)
            for side in (0, 1)
        ]
        second = jnp.concatenate(totals, axis=3)
        third = third_recvs(second)
        second_qkv = jnp.concatenate(
            [
                second_total(keep, recv, next_recv)
                for keep, recv, next_recv in zip(terms[::2], recvs, next_recvs)
            ],
            axis=2,
        )
        third_qkv = third_recvs(second_qkv)
        third, third_qkv = lax.optimization_barrier((third, third_qkv))
        shard_out, shard_up, shard_down, shard_qkv = weight_grads(
            second, third, second_qkv, third_qkv
        )
    if parts > 1:
        grad_input, small, flat = leave(
            home, inputs, grad_hidden, modulation, gains, full_qkv, sums, devices
        )
        base = 2 * width + units
        ends = (base + width, base + width + units)
        shard_qkv, shard_out, shard_up, shard_down = (
            lax.psum_scatter(
                jnp.einsum("tk,tn->kn", left, right, preferred_element_type=f32),
                EVERY,
                scatter_dimension=0,
                tiled=True,
            )
            for left, right in (
                (entered, flat),
                (pack[:, :width], pack[:, base : ends[0]]),
                (pack[:, width : 2 * width], pack[:, ends[0] : ends[1]]),
                (pack[:, 2 * width : base], pack[:, ends[1] :]),
            )
        )
    small = lax.all_to_all(small, EVERY, 0, 0, tiled=True)
    if parts == 1:
        small = after(small, second_qkv)
    grads = finish(small, time_embed, gains, width, units)
    loss_value = grads[6].reshape(())
    return (
        final,
        loss_value,
        grad_input,
        grads[0].T,
        grads[1].reshape(-1),
        grads[2].reshape(-1),
        shard_qkv,
        shard_out,
        grads[3].reshape(-1),
        shard_up,
        grads[4].reshape(-1),
        shard_down,
        grads[5].reshape(-1),
    )


def solution(mesh):
    blocks = mesh.shape["blk"]
    fine = Mesh(mesh.devices.reshape(2, 2, blocks // 8, 4, 2), EVERY)
    tokens = ("rb", "sz", "sy", "hx", "hc")
    return jax.shard_map(
        on_device,
        mesh=fine,
        in_specs=(
            P(None, tokens, None),
            P(),
            P(None, tokens),
            P(None, tokens),
            P(None, tokens, None),
            P(None, EVERY),
            P(EVERY),
            P(EVERY),
            P(EVERY, None),
            P(EVERY, None),
            P(EVERY),
            P(EVERY, None),
            P(EVERY),
            P(EVERY, None),
            P(EVERY),
        ),
        out_specs=(
            P(None, tokens, None),
            P(),
            P(None, tokens, None),
            P(None, EVERY),
            P(EVERY),
            P(EVERY),
            P(EVERY, None),
            P(EVERY, None),
            P(EVERY),
            P(EVERY, None),
            P(EVERY),
            P(EVERY, None),
            P(EVERY),
        ),
        check_vma=False,
    )
```
